32 devices in a mesh: dp: 16 (over z, x, core), tensor: 2 (over y).
Axes of the slice: x: 2, y: 2, z: 4, core: 2. Of those that a mesh axis runs over, the one named last changes fastest.
Arguments:
- block_input: bfloat16 [8192, 1024], P(('dp', 'tensor')), may hold values from -6 to 6
- cotangent: bfloat16 [8192, 1024], P(('dp', 'tensor')), may hold values from -6 to 6
- segment_ids: int32 [16, 512], P('dp'), may hold values from 0 to 2, never falling along the last dimension, each value on 1 to 384 neighbouring positions
- positions: int32 [16, 512], P('dp'), may hold values from 0 to 8191
- norm_gains: bfloat16 [2, 1024], P(None, 'dp'), may hold values from 0.25 to 1.75
- qk_gains: bfloat16 [2, 64], P(None, 'dp'), may hold values from 0.6 to 1.6
- w_query: bfloat16 [1024, 1024], P('dp', 'tensor'), may hold values from -0.1875 to 0.1875
- w_keyval: bfloat16 [2, 1024, 512], P(None, 'dp', 'tensor'), may hold values from -0.1875 to 0.1875
- w_output: bfloat16 [1024, 1024], P('tensor', 'dp'), may hold values from -0.75 to 0.75
- w_gate_up: bfloat16 [2, 1024, 4608], P(None, 'dp', 'tensor'), may hold values from -0.1875 to 0.1875
- w_down: bfloat16 [4608, 1024], P('tensor', 'dp'), may hold values from -0.09375 to 0.09375
Outputs:
- block_output: bfloat16 [8192, 1024], P(('dp', 'tensor'))
- grad_input: float32 [8192, 1024], P(('dp', 'tensor'))
- grad_norm_gains: float32 [2, 1024], P(None, 'dp')
- grad_qk_gains: float32 [2, 64], P(None, 'dp')
- grad_query: float32 [1024, 1024], P('dp', 'tensor')
- grad_keyval: float32 [2, 1024, 512], P(None, 'dp', 'tensor')
- grad_output: float32 [1024, 1024], P('tensor', 'dp')
- grad_gate_up: float32 [2, 1024, 4608], P(None, 'dp', 'tensor')
- grad_down: float32 [4608, 1024], P('tensor', 'dp')
The draws below stay inside these ranges and needn't reach their ends.
Inputs may be any that keep to these rules, and one draw needn't show every extreme that they name: `segment_ids`: ids never fall along a row; each document spans 1 to 384 tokens and one spans exactly that many.
All inputs are finite; a program needn't handle non-finite values.
Results may differ from the reference program's by a relative error of at most 0.028.
Values may be sent and summed in bfloat16 or wider, within the bound.
A program may use at most 128 MiB of HBM per device.

```python
import math
import jax
import jax.numpy as jnp
import numpy as np
from jax import lax

D = 1024
H = 16
KV = 8
HD = 64
FF = 4608
ROW_LEN = 512
ROWS = 16
TOKENS = 8192


def draw_qk_gains(key, part):
    values = jnp.exp(jax.random.uniform(key, (2, HD), jnp.float32, math.log(0.6), math.log(1.6)))
    return values.astype(jnp.bfloat16)


def touch_ends(array, rng, least, largest):
    longest = array.shape.index(max(array.shape))
    spots = []
    for shift in (0, 1):
        where = [jax.random.randint(jax.random.fold_in(rng, axis), (), 0, length) for axis, length in enumerate(array.shape)]
        where[longest] = (where[longest] + shift) % array.shape[longest]
        spots.append(tuple(where))
    return array.at[spots[0]].set(least).at[spots[1]].set(largest)


def raised(drawn, own_key, source, target, blocks, factor):
    def block_of(position):
        return (jnp.arange(drawn.shape[position]) // (drawn.shape[position] // blocks)).reshape((-1,) + (1,) * (drawn.ndim - 1 - position))

    one_side = jax.random.permutation(own_key, blocks)[block_of(target)]
    other_side = (block_of(target) + blocks // 2) % blocks
    return jnp.where((block_of(source) == one_side) | (block_of(source) == other_side), factor * drawn, drawn)


def block_levels(stream_key, dims, pieces, low, top_value):
    factor_of, own = 1.0, jax.random.fold_in(stream_key, 6)
    for position, parts in pieces:
        draws = jnp.exp(jax.random.uniform(jax.random.fold_in(own, position), (parts,), jnp.float32, low / len(pieces), top_value / len(pieces)))
        factor_of = factor_of * jnp.repeat(draws, dims[position] // parts).reshape([-1 if axis == position else 1 for axis in range(len(dims))])
    return factor_of


def split_up(amount, total, reach, slope):
    weights = [(1 << 20) // math.isqrt(standing ** slope) + 1 for standing in range(2, amount + 1)]
    surplus, counts = total - reach - (amount - 1), [1] * (amount - 1)
    while surplus > 0:
        movable = [i for i in range(amount - 1) if counts[i] < reach]
        pool, remaining = sum([weights[i] for i in movable]), surplus
        for i in movable:
            addition = min(reach - counts[i], max(1, remaining * weights[i] // pool), surplus)
            counts[i] = counts[i] + addition
            surplus = surplus - addition
    return np.array([reach] + counts)


def uneven_parts(own_key, number_of, total, bound, skew):
    if number_of == 2:
        one = jax.random.randint(own_key, (), max(1, total - bound), min(bound, total - 1) + 1)
        return jnp.stack([one, total - one])
    sizes = jnp.asarray(split_up(number_of, total, bound, skew), jnp.int32)
    couples = (number_of - 1) // 2
    giver, receiver = sizes[1:1 + 2 * couples:2], sizes[2:2 + 2 * couples:2]
    margin = jnp.minimum(giver - 1, bound - receiver)
    moved = jax.random.randint(jax.random.fold_in(own_key, 1), (couples,), 0, 1 << 20) % (margin + 1)
    sizes = sizes.at[1:1 + 2 * couples:2].set(giver - moved).at[2:2 + 2 * couples:2].set(receiver + moved)
    return sizes[jax.random.permutation(jax.random.fold_in(own_key, 2), number_of)]


def centred(own_key, shape, scale, most, shards=(), kind=jnp.bfloat16):
    result = jax.random.normal(own_key, shape, jnp.float32) * scale
    if len(shards) > 0:
        result = block_levels(own_key, shape, shards, -0.22, 0.18) * result
    return jnp.clip(result, min=-most, max=most).astype(kind)


def heavy_noise(stream_key, extent, spread, bound, shards, heavy, held_as=jnp.bfloat16):
    values = spread * jax.random.normal(stream_key, extent, jnp.float32)
    if shards:
        values = values * block_levels(stream_key, extent, shards, -0.22, 0.18)
    return jnp.clip(raised(values, jax.random.fold_in(stream_key, 3), *heavy), -bound, bound).astype(held_as)


def setup_inputs(seed: int = 0) -> dict:
    seeds = jax.random.split(jax.random.key(seed), 12)
    block_input = centred(seeds[0], (TOKENS, D), 1.0, 6.0, ((0, 32),))
    cotangent = heavy_noise(seeds[1], (TOKENS, D), 1.0, 6.0, ((0, 32),), (0, 1, 32, 2.75))
    segment_ids = jax.vmap(lambda own: jnp.searchsorted(jnp.cumsum(uneven_parts(own, 3, ROW_LEN, ROW_LEN * 3 // 4, 0)), jnp.arange(ROW_LEN), side="right"))(jax.random.split(seeds[2], ROWS)).reshape((ROWS, ROW_LEN)).astype(jnp.int32)
    positions = touch_ends(jax.random.randint(seeds[3], (ROWS, ROW_LEN), 0, 8192), jax.random.fold_in(seeds[3], 1), 0, 8191).astype(jnp.int32)
    norm_gains = jnp.clip(1.0 + 0.15 * jax.random.normal(seeds[4], (2, D), jnp.float32), 0.25, 1.75).astype(jnp.bfloat16)
    qk_gains = draw_qk_gains(jax.random.fold_in(seeds[11], 71), 0)
    w_query = centred(seeds[6], (D, H * HD), D ** -0.5, 0.1875, ((0, 16), (1, 2)))
    w_keyval = centred(seeds[7], (2, D, KV * HD), D ** -0.5, 0.1875, ((1, 16), (2, 2)))
    w_output = centred(seeds[8], (H * HD, D), (H * HD // 16) ** -0.5, 0.75, ((0, 2), (1, 16)))
    w_gate_up = centred(seeds[9], (2, D, FF), D ** -0.5, 0.1875, ((1, 16), (2, 2)))
    w_down = centred(seeds[10], (FF, D), FF ** -0.5, 0.09375, ((0, 2), (1, 16)))
    return dict(block_input=block_input, cotangent=cotangent, segment_ids=segment_ids, positions=positions, norm_gains=norm_gains, qk_gains=qk_gains, w_query=w_query, w_keyval=w_keyval, w_output=w_output, w_gate_up=w_gate_up, w_down=w_down)


EPSILON = 1e-05
ROPE_BASE = 1000000.0
NEG_FILL = -1e+30

def rms_forward(values, gain):
    scale = lax.rsqrt(lax.optimization_barrier(jnp.mean(values * values, axis=-1, keepdims=True)) + EPSILON)
    return (values * scale * gain, scale)

def rms_backward(values, scale, gain, grad):
    weighted = grad * gain
    inner = lax.optimization_barrier(jnp.mean(weighted * values, axis=-1, keepdims=True))
    return scale * (weighted - values * scale * scale * inner)

def rope_tables(places):
    freqs = ROPE_BASE ** (-jnp.arange(0, HD, 2).astype(jnp.float32) / HD)
    angles = places.astype(jnp.float32)[..., None] * freqs
    angles = jnp.concatenate([angles, angles], axis=-1)
    return (jnp.cos(angles), jnp.sin(angles))

def rotate_half(values):
    half = values.shape[-1] // 2
    return jnp.concatenate([-values[..., half:], values[..., :half]], axis=-1)

def rotate_back(values):
    half = values.shape[-1] // 2
    return jnp.concatenate([values[..., half:], -values[..., :half]], axis=-1)

def allowed_mask(segs):
    length = segs.shape[0]
    index = jnp.arange(length, dtype=jnp.int32)
    return (segs[:, None] == segs[None, :]) & (index[None, :] <= index[:, None])

def row_scores(q_rot, k_rot):
    kv_heads = k_rot.shape[1]
    groups = q_rot.shape[1] // kv_heads
    q_four = q_rot.reshape(q_rot.shape[0], kv_heads, groups, HD)
    scores = jnp.einsum('ikgd,jkd->kgij', q_four.astype(jnp.float32), k_rot.astype(jnp.float32))
    return (scores / math.sqrt(HD), q_four)

def attend_row(q_rot, k_rot, values, segs):
    scores, q_four = row_scores(q_rot, k_rot)
    allowed = allowed_mask(segs)[None, None]
    masked = jnp.where(allowed, scores, NEG_FILL)
    top = lax.optimization_barrier(jnp.max(masked, axis=-1, keepdims=True))
    expd = jnp.where(allowed, jnp.exp(masked - top), 0.0)
    total = lax.optimization_barrier(jnp.sum(expd, axis=-1, keepdims=True))
    probs = (expd / total).astype(jnp.bfloat16)
    log_total = top[..., 0] + jnp.log(total[..., 0])
    attended = jnp.einsum('kgij,jkd->ikgd', probs.astype(jnp.float32), values.astype(jnp.float32))
    return (attended.reshape(q_rot.shape).astype(jnp.bfloat16), log_total)

def back_row(q_rot, k_rot, values, grad_att, log_total, segs):
    scores, q_four = row_scores(q_rot, k_rot)
    allowed = allowed_mask(segs)[None, None]
    masked = jnp.where(allowed, scores, NEG_FILL)
    probs = jnp.where(allowed, jnp.exp(masked - log_total[..., None]), 0.0)
    probs_b = probs.astype(jnp.bfloat16)
    grad_four = grad_att.reshape(q_four.shape).astype(jnp.float32)
    grad_values = jnp.einsum('kgij,ikgd->jkd', probs_b.astype(jnp.float32), grad_four)
    grad_p = jnp.einsum('ikgd,jkd->kgij', grad_four, values.astype(jnp.float32))
    delta = lax.optimization_barrier(jnp.sum(probs * grad_p, axis=-1, keepdims=True))
    d_scores = (probs * (grad_p - delta) / math.sqrt(HD)).astype(jnp.bfloat16).astype(jnp.float32)
    grad_q = jnp.einsum('kgij,jkd->ikgd', d_scores, k_rot.astype(jnp.float32)).reshape(q_rot.shape)
    grad_k = jnp.einsum('kgij,ikgd->jkd', d_scores, q_four.astype(jnp.float32))
    return (grad_q, grad_k, grad_values)

def fdot(left, right):
    return jnp.dot(left, right, preferred_element_type=jnp.float32)

def run_block(x_blk, dy_blk, seg_blk, pos_blk, params):
    gain_attn, gain_ffn, gain_q, gain_k, w_q, w_k, w_v, w_o, w_g, w_u, w_d = params
    rows_n = seg_blk.shape[0]
    tokens_n = rows_n * ROW_LEN
    xfull = x_blk.astype(jnp.float32)
    normed_f, scale1 = rms_forward(xfull, gain_attn)
    normed1 = normed_f.astype(jnp.bfloat16)
    query = fdot(normed1, w_q).reshape(rows_n, ROW_LEN, H, HD)
    keys = fdot(normed1, w_k).reshape(rows_n, ROW_LEN, KV, HD)
    values = fdot(normed1, w_v).astype(jnp.bfloat16).reshape(rows_n, ROW_LEN, KV, HD)
    q_norm, q_scale = rms_forward(query, gain_q)
    k_norm, k_scale = rms_forward(keys, gain_k)
    cosv, sinv = rope_tables(pos_blk)
    cosv = cosv[:, :, None, :]
    sinv = sinv[:, :, None, :]
    q_rot = (q_norm * cosv + rotate_half(q_norm) * sinv).astype(jnp.bfloat16)
    k_rot = (k_norm * cosv + rotate_half(k_norm) * sinv).astype(jnp.bfloat16)
    attended, log_total = jax.vmap(attend_row)(q_rot, k_rot, values, seg_blk)
    att_flat = attended.reshape(tokens_n, H * HD)
    hidden = xfull + fdot(att_flat, w_o)
    normed_g, scale2 = rms_forward(hidden, gain_ffn)
    normed2 = normed_g.astype(jnp.bfloat16)
    gate_proj = fdot(normed2, w_g)
    up_proj = fdot(normed2, w_u)
    sigmoid_gate = jax.nn.sigmoid(gate_proj)
    silu_gate = gate_proj * sigmoid_gate
    act = (silu_gate * up_proj).astype(jnp.bfloat16)
    out_blk = (hidden + fdot(act, w_d)).astype(jnp.bfloat16)
    grad_act = fdot(dy_blk, w_d.T)
    grad_down = fdot(act.T, dy_blk)
    d_gate = (grad_act * up_proj * sigmoid_gate * (1.0 + gate_proj * (1.0 - sigmoid_gate))).astype(jnp.bfloat16)
    d_up = (grad_act * silu_gate).astype(jnp.bfloat16)
    grad_gate = fdot(normed2.T, d_gate)
    grad_up = fdot(normed2.T, d_up)
    grad_n2 = fdot(d_gate, w_g.T) + fdot(d_up, w_u.T)
    gain_ffn_grad = lax.optimization_barrier(jnp.sum(grad_n2 * hidden * scale2, axis=0))
    grad_hidden = dy_blk.astype(jnp.float32) + rms_backward(hidden, scale2, gain_ffn, grad_n2)
    grad_hidden_b = grad_hidden.astype(jnp.bfloat16)
    grad_att = fdot(grad_hidden_b, w_o.T).astype(jnp.bfloat16).reshape(rows_n, ROW_LEN, H, HD)
    grad_out = fdot(att_flat.T, grad_hidden_b)
    grad_qrot, grad_krot, grad_vals = jax.vmap(back_row)(q_rot, k_rot, values, grad_att, log_total, seg_blk)
    grad_qn = grad_qrot * cosv + rotate_back(grad_qrot * sinv)
    grad_kn = grad_krot * cosv + rotate_back(grad_krot * sinv)
    gain_q_grad = lax.optimization_barrier(jnp.sum(grad_qn * query * q_scale, axis=(0, 1, 2)))
    gain_k_grad = lax.optimization_barrier(jnp.sum(grad_kn * keys * k_scale, axis=(0, 1, 2)))
    d_query = rms_backward(query, q_scale, gain_q, grad_qn).astype(jnp.bfloat16).reshape(tokens_n, H * HD)
    d_keys = rms_backward(keys, k_scale, gain_k, grad_kn).astype(jnp.bfloat16).reshape(tokens_n, KV * HD)
    d_values = grad_vals.astype(jnp.bfloat16).reshape(tokens_n, KV * HD)
    grad_wq = fdot(normed1.T, d_query)
    grad_wk = fdot(normed1.T, d_keys)
    grad_wv = fdot(normed1.T, d_values)
    grad_n1 = fdot(d_query, w_q.T) + fdot(d_keys, w_k.T) + fdot(d_values, w_v.T)
    gain_attn_grad = lax.optimization_barrier(jnp.sum(grad_n1 * xfull * scale1, axis=0))
    grad_x = grad_hidden + rms_backward(xfull, scale1, gain_attn, grad_n1)
    grads = (gain_attn_grad, gain_ffn_grad, gain_q_grad, gain_k_grad, grad_wq, grad_wk, grad_wv, grad_out, grad_gate, grad_up, grad_down)
    return (out_blk, grad_x, grads)

def reference(block_input, cotangent, segment_ids, positions, norm_gains, qk_gains, w_query, w_keyval, w_output, w_gate_up, w_down):
    block_rows = math.gcd(ROWS, 8)
    blocks = ROWS // block_rows
    params = (norm_gains[0].astype(jnp.float32), norm_gains[1].astype(jnp.float32), qk_gains[0].astype(jnp.float32), qk_gains[1].astype(jnp.float32), w_query, w_keyval[0], w_keyval[1], w_output, w_gate_up[0], w_gate_up[1], w_down)
    inputs_b = block_input.reshape(blocks, block_rows * ROW_LEN, D)
    cotan_b = cotangent.reshape(blocks, block_rows * ROW_LEN, D)
    segs_b = segment_ids.reshape(blocks, block_rows, ROW_LEN)
    places_b = positions.reshape(blocks, block_rows, ROW_LEN)
    shapes = [(D,), (D,), (HD,), (HD,), (D, H * HD), (D, KV * HD), (D, KV * HD), (H * HD, D), (D, FF), (D, FF), (FF, D)]
    start = tuple((jnp.zeros(shape, jnp.float32) for shape in shapes))

    def advance(carry, items):
        x_blk, dy_blk, seg_blk, pos_blk = items
        out_blk, grad_x, grads = run_block(x_blk, dy_blk, seg_blk, pos_blk, params)
        return (tuple((total + term for total, term in zip(carry, grads))), (out_blk, grad_x))
    totals, (outputs, grads_x) = lax.scan(advance, start, (inputs_b, cotan_b, segs_b, places_b))
    grad_norm = jnp.stack([totals[0], totals[1]])
    grad_qk = jnp.stack([totals[2], totals[3]])
    grad_kv = jnp.stack([totals[5], totals[6]])
    grad_gu = jnp.stack([totals[8], totals[9]])
    return (outputs.reshape(TOKENS, D), grads_x.reshape(TOKENS, D), grad_norm, grad_qk, totals[4], grad_kv, totals[7], grad_gu, totals[10])
```

```python
import functools
import math

import jax
import jax.numpy as jnp
from jax import lax
from jax.experimental import pallas as pl
from jax.experimental.pallas import tpu as pltpu
from jax.sharding import PartitionSpec as P

HD = 64


EPSILON = 1e-05
ROPE_BASE = 1000000.0
NEG_FILL = -1e30


def rms_forward(values, gain):
    scale = lax.rsqrt(jnp.mean(values * values, axis=-1, keepdims=True) + EPSILON)
    return (values * scale * gain, scale)


def rms_backward(values, scale, gain, grad):
    weighted = grad * gain
    inner = jnp.mean(weighted * values, axis=-1, keepdims=True)
    return scale * (weighted - values * scale * scale * inner)


def rope_tables(places):
    freqs = ROPE_BASE ** (-jnp.arange(0, HD, 2).astype(jnp.float32) / HD)
    angles = places.astype(jnp.float32)[..., None] * freqs
    angles = jnp.concatenate([angles, angles], axis=-1)
    return (jnp.cos(angles), jnp.sin(angles))


def rotate_half(values):
    half = values.shape[-1] // 2
    return jnp.concatenate([-values[..., half:], values[..., :half]], axis=-1)


def rotate_back(values):
    half = values.shape[-1] // 2
    return jnp.concatenate([values[..., half:], -values[..., :half]], axis=-1)


def allowed_mask(segs):
    length = segs.shape[0]
    index = jnp.arange(length, dtype=jnp.int32)
    return (segs[:, None] == segs[None, :]) & (index[None, :] <= index[:, None])


def contract(left, right, left_dim, right_dim):
    return lax.dot_general(
        left, right, (((left_dim,), (right_dim,)), ((), ())), preferred_element_type=jnp.float32
    )


def fdot(left, right):
    return jnp.dot(left, right, preferred_element_type=jnp.float32)


def row_scores(q_rot, k_rot):
    kv_heads = k_rot.shape[1]
    groups = q_rot.shape[1] // kv_heads
    q_four = q_rot.reshape(q_rot.shape[0], kv_heads, groups, HD)
    scores = jnp.einsum("ikgd,jkd->kgij", q_four, k_rot, preferred_element_type=jnp.float32)
    return (scores / math.sqrt(HD), q_four)


def attend_row(q_rot, k_rot, values, segs):
    scores, q_four = row_scores(q_rot, k_rot)
    allowed = allowed_mask(segs)[None, None]
    masked = jnp.where(allowed, scores, NEG_FILL)
    top = jnp.max(masked, axis=-1, keepdims=True)
    expd = jnp.where(allowed, jnp.exp(masked - top), 0.0)
    total = jnp.sum(expd, axis=-1, keepdims=True)
    probs = (expd / total).astype(jnp.bfloat16)
    log_total = top[..., 0] + jnp.log(total[..., 0])
    attended = jnp.einsum("kgij,jkd->ikgd", probs, values, preferred_element_type=jnp.float32)
    return (attended.reshape(q_rot.shape).astype(jnp.bfloat16), log_total)


def back_row(q_rot, k_rot, values, grad_att, log_total, segs):
    scores, q_four = row_scores(q_rot, k_rot)
    allowed = allowed_mask(segs)[None, None]
    masked = jnp.where(allowed, scores, NEG_FILL)
    probs = jnp.where(allowed, jnp.exp(masked - log_total[..., None]), 0.0)
    probs_b = probs.astype(jnp.bfloat16)
    grad_four = grad_att.reshape(q_four.shape)
    grad_values = jnp.einsum(
        "kgij,ikgd->jkd", probs_b, grad_four, preferred_element_type=jnp.float32
    )
    grad_p = jnp.einsum("ikgd,jkd->kgij", grad_four, values, preferred_element_type=jnp.float32)
    delta = jnp.sum(probs * grad_p, axis=-1, keepdims=True)
    d_scores = (probs * (grad_p - delta) / math.sqrt(HD)).astype(jnp.bfloat16)
    grad_q = jnp.einsum(
        "kgij,jkd->ikgd", d_scores, k_rot, preferred_element_type=jnp.float32
    ).reshape(q_rot.shape)
    grad_k = jnp.einsum("kgij,ikgd->jkd", d_scores, q_four, preferred_element_type=jnp.float32)
    return (grad_q, grad_k, grad_values)


def layout_of(dp):
    if dp == 16:
        return (4, 4, 2)
    return (dp // 4, 2, dp // 2)


class Place:
    def __init__(self, dp):
        self.length, self.zs, self.xs = layout_of(dp)
        me = lax.axis_index("dp")
        self.z = lax.rem(me // self.zs, self.length)
        self.x = lax.rem(me // self.xs, 2)
        self.c = lax.rem(me, 2)

    def device(self, z, x, c):
        return z * self.zs + x * self.xs + c

    def greet(self):
        z, x, c = self.z, self.x, self.c
        barrier = pltpu.get_barrier_semaphore()

        def signal(target):
            pl.semaphore_signal(
                barrier, inc=1, device_id={"dp": target}, device_id_type=pl.DeviceIdType.MESH
            )

        signal(self.device(z, x, 1 - c))
        signal(self.device(z, 1 - x, c))
        pl.when(z > 0)(lambda: signal(self.device(z - 1, x, c)))
        pl.when(z < self.length - 1)(lambda: signal(self.device(z + 1, x, c)))
        ends = jnp.where(z > 0, 1, 0) + jnp.where(z < self.length - 1, 1, 0)
        pl.semaphore_wait(barrier, 2 + ends)


def remote(src, dst, send, recv, target):
    return pltpu.make_async_remote_copy(
        src_ref=src,
        dst_ref=dst,
        send_sem=send,
        recv_sem=recv,
        device_id={"dp": target},
        device_id_type=pl.DeviceIdType.MESH,
    )


def gather_kernel(dp, count, rows, *refs):
    ins, outs = refs[:count], refs[count : 2 * count]
    send, recv, local = refs[2 * count :]
    at = Place(dp)
    z, x, c, length = at.z, at.x, at.c, at.length
    below, above = at.device(z - 1, x, c), at.device(z + 1, x, c)
    beside, sibling = at.device(z, 1 - x, c), at.device(z, x, 1 - c)
    at.greet()
    own = at.device(z, x, c)

    def slab(k, o):
        return outs[k].at[pl.ds(pl.multiple_of(o * rows, rows), rows)]

    for k in range(count):
        pltpu.make_async_copy(ins[k], slab(k, own), local.at[k]).start()

    def move(k, oz, ox, way, target, first):
        o = at.device(oz, ox, c)
        src = ins[k] if first else slab(k, o)
        return remote(src, slab(k, o), send.at[k, oz * 2 + ox, way], recv.at[k, o], target)

    def arrived(k, o):
        remote(slab(k, o), slab(k, o), send.at[k, 0, 0], recv.at[k, o], sibling).wait_recv()

    def steps(act):
        for s in range(length):
            for sign in (1, -1) if s else (0,):
                oz = z - s * sign

                def event(oz=oz, s=s, sign=sign):
                    for k in range(count):
                        act(k, oz, s, sign)

                if s:
                    pl.when((oz >= 0) & (oz < length))(event)
                else:
                    event()
            if s:
                side(s - 1, act)
        side(length - 1, act)

    def side(s, act):
        for sign in (1, -1) if s else (0,):
            oz = z - s * sign

            def event(oz=oz):
                for k in range(count):
                    act(k, oz, None, 0)

            if s:
                pl.when((oz >= 0) & (oz < length))(event)
            else:
                event()

    def begin(k, oz, s, sign):
        if s is None:
            arrived(k, at.device(oz, 1 - x, c))
            move(k, oz, 1 - x, 3, sibling, False).start()
            return
        first = s == 0
        if not first:
            arrived(k, at.device(oz, x, c))
        if sign >= 0:
            pl.when(z < length - 1)(lambda: move(k, oz, x, 0, above, first).start())
        if sign <= 0:
            pl.when(z > 0)(lambda: move(k, oz, x, 1, below, first).start())
        move(k, oz, x, 2, beside, first).start()
        move(k, oz, x, 3, sibling, first).start()

    def finish(k, oz, s, sign):
        if s is None:
            move(k, oz, 1 - x, 3, sibling, False).wait_send()
            return
        first = s == 0
        if sign >= 0:
            pl.when(z < length - 1)(lambda: move(k, oz, x, 0, above, first).wait_send())
        if sign <= 0:
            pl.when(z > 0)(lambda: move(k, oz, x, 1, below, first).wait_send())
        move(k, oz, x, 2, beside, first).wait_send()
        move(k, oz, x, 3, sibling, first).wait_send()

    steps(begin)
    for oz in range(length):
        for ox in range(2):
            for k in range(count):
                arrived(k, at.device(oz, ox, 1 - c))
    steps(finish)
    for k in range(count):
        pltpu.make_async_copy(ins[k], slab(k, own), local.at[k]).wait()


def gather_rows(arrays, dp):
    count, rows = len(arrays), arrays[0].shape[0]
    return pl.pallas_call(
        functools.partial(gather_kernel, dp, count, rows),
        out_shape=[jax.ShapeDtypeStruct((dp * rows, a.shape[1]), a.dtype) for a in arrays],
        in_specs=[pl.BlockSpec(memory_space=pltpu.VMEM)] * count,
        out_specs=[pl.BlockSpec(memory_space=pl.ANY)] * count,
        scratch_shapes=[
            pltpu.SemaphoreType.DMA((count, dp // 2, 4)),
            pltpu.SemaphoreType.DMA((count, dp)),
            pltpu.SemaphoreType.DMA((count,)),
        ],
        compiler_params=pltpu.CompilerParams(collective_id=1, has_side_effects=True),
        name="gather_rows",
    )(*arrays)


def scatter_kernel(dp, count, rows, *refs):
    parts, outs = refs[:count], refs[count : 2 * count]
    mine, first, second, upward, downward = (
        refs[(2 + i) * count : (3 + i) * count] for i in range(5)
    )
    sent1, sent2, sent4, got1, got2, got_up, got_down, local = refs[7 * count :]
    at = Place(dp)
    z, x, c, length = at.z, at.x, at.c, at.length
    below, above = at.device(z - 1, x, c), at.device(z + 1, x, c)
    beside, sibling = at.device(z, 1 - x, c), at.device(z, x, 1 - c)
    at.greet()

    def slab(k, o):
        return parts[k].at[pl.ds(pl.multiple_of(o * rows, rows), rows)]

    def swap(k, t, ox):
        q = t * 2 + ox
        return remote(
            slab(k, at.device(t, ox, 1 - c)), first[k].at[q], sent1.at[k, q], got1.at[k, q], sibling
        )

    def keep(k, t, ox):
        q = t * 2 + ox
        return pltpu.make_async_copy(slab(k, at.device(t, ox, c)), mine[k].at[q], local.at[k, q])

    def cross(k, t):
        q = t * 2 + 1 - x
        return remote(first[k].at[q], second[k].at[t], sent2.at[k, t], got2.at[k, t], beside)

    def rise(k, t):
        return remote(second[k].at[t], upward[k].at[t], sent4.at[k, t], got_up.at[k, t], above)

    def fall(k, t):
        return remote(second[k].at[t], downward[k].at[t], sent4.at[k, t], got_down.at[k, t], below)

    def targets(act):
        for d in range(length - 1, -1, -1):
            for sign in (1, -1) if d else (0,):
                t = z + d * sign

                def event(t=t, sign=sign):
                    for k in range(count):
                        act(k, t, sign)

                if d:
                    pl.when((t >= 0) & (t < length))(event)
                else:
                    event()

    def wide(value):
        return value.astype(jnp.float32)

    def start(k, t, sign):
        for ox in (1 - x, x):
            swap(k, t, ox).start()
            keep(k, t, ox).start()

    def chip_sum(k, t, sign):
        for ox in (1 - x, x):
            q = t * 2 + ox
            keep(k, t, ox).wait()
            swap(k, t, ox).wait_recv()
            first[k][q] = (wide(first[k][q]) + wide(mine[k][q])).astype(jnp.bfloat16)
            if ox is not x:
                cross(k, t).start()

    def chain(k, t, sign):
        cross(k, t).wait_recv()
        if sign == 0:
            outs[k][...] = wide(second[k][t]) + wide(first[k][t * 2 + x])

            def add_up():
                rise(k, t).wait_recv()
                outs[k][...] += wide(upward[k][t])

            def add_down():
                fall(k, t).wait_recv()
                outs[k][...] += wide(downward[k][t])

            pl.when(z > 0)(add_up)
            pl.when(z < length - 1)(add_down)
            return
        base, move = (upward, rise) if sign > 0 else (downward, fall)
        inner = z > 0 if sign > 0 else z < length - 1

        def middle():
            move(k, t).wait_recv()
            second[k][t] = (
                wide(second[k][t]) + wide(first[k][t * 2 + x]) + wide(base[k][t])
            ).astype(jnp.bfloat16)

        def edge():
            second[k][t] = (wide(second[k][t]) + wide(first[k][t * 2 + x])).astype(jnp.bfloat16)

        pl.when(inner)(middle)
        pl.when(jnp.logical_not(inner))(edge)
        move(k, t).start()

    def finish(k, t, sign):
        swap(k, t, 0).wait_send()
        swap(k, t, 1).wait_send()
        cross(k, t).wait_send()
        if sign:
            (rise if sign > 0 else fall)(k, t).wait_send()

    targets(start)
    targets(chip_sum)
    targets(chain)
    targets(finish)


def scatter_rows(arrays, dp):
    count, rows = len(arrays), arrays[0].shape[0] // dp
    length = layout_of(dp)[0]
    slots = [dp // 2, dp // 2, length, length, length]
    return pl.pallas_call(
        functools.partial(scatter_kernel, dp, count, rows),
        out_shape=[jax.ShapeDtypeStruct((rows, a.shape[1]), jnp.float32) for a in arrays],
        in_specs=[pl.BlockSpec(memory_space=pl.ANY)] * count,
        out_specs=[pl.BlockSpec(memory_space=pltpu.VMEM)] * count,
        scratch_shapes=[
            pltpu.VMEM((n, rows, a.shape[1]), a.dtype) for n in slots for a in arrays
        ]
        + [
            pltpu.SemaphoreType.DMA((count, n))
            for n in (dp // 2, length, length, dp // 2, length, length, length, dp // 2)
        ],
        compiler_params=pltpu.CompilerParams(
            collective_id=2, has_side_effects=True, vmem_limit_bytes=60 * 1024 * 1024
        ),
        name="scatter_rows",
    )(*arrays)


def exchange(values):
    return lax.ppermute(values, "tensor", ((0, 1), (1, 0)))


def collect(values):
    if lax.axis_size("tensor") != 2:
        return lax.all_gather(values, "tensor", axis=0, tiled=True)
    other = exchange(values)
    low = lax.axis_index("tensor") == 0
    return jnp.concatenate([jnp.where(low, values, other), jnp.where(low, other, values)])


def spread(values):
    if lax.axis_size("tensor") != 2:
        return lax.psum_scatter(values, "tensor", scatter_dimension=0, tiled=True)
    half = values.shape[0] // 2
    low = lax.axis_index("tensor") == 0
    head, tail = values[:half], values[half:]
    other = exchange(jnp.where(low, tail, head).astype(jnp.bfloat16))
    return jnp.where(low, head, tail) + other.astype(jnp.float32)


def total(values):
    if lax.axis_size("tensor") != 2:
        return lax.psum(values, "tensor")
    return values + exchange(values)


def on_device(
    block_input,
    cotangent,
    segment_ids,
    positions,
    norm_gains,
    qk_gains,
    w_query,
    w_keyval,
    w_output,
    w_gate_up,
    w_down,
):
    dp = lax.axis_size("dp")
    rows_here, row_len = segment_ids.shape
    tokens_here = rows_here * row_len
    shard, q_wide = w_query.shape
    kv_wide, ff_wide = w_keyval.shape[2], w_gate_up.shape[2]
    qk_shard = qk_gains.shape[1]
    gains = jnp.concatenate(
        [norm_gains.T, jnp.pad(qk_gains.T, ((0, shard - qk_shard), (0, 0)))], axis=1
    )
    gains = jnp.pad(gains, ((0, 0), (0, 124)))
    attn_pack = jnp.concatenate([w_query, w_keyval[0], w_keyval[1], w_output.T, gains], axis=1)
    gate_up_pack = jnp.concatenate([w_gate_up[0], w_gate_up[1]], axis=1)
    attn_full, gate_up_full, down_full = gather_rows([attn_pack, gate_up_pack, w_down.T], dp)
    qkv_wide = q_wide + 2 * kv_wide
    qkv_full = attn_full[:, :qkv_wide]
    output_full = attn_full[:, qkv_wide : qkv_wide + q_wide]
    gain_cols = attn_full[:, qkv_wide + q_wide :].astype(jnp.float32)
    gain_attn, gain_ffn = gain_cols[:, 0], gain_cols[:, 1]
    qk_cols = gain_cols.reshape(dp, shard, 128)[:, :qk_shard, 2:4].reshape(dp * qk_shard, 2)
    gain_q, gain_k = qk_cols[:, 0], qk_cols[:, 1]
    heads_here = q_wide // HD
    kv_here = kv_wide // HD
    dy_rows = collect(cotangent)
    xlocal = block_input.astype(jnp.float32)
    normed_f, scale1 = rms_forward(xlocal, gain_attn)
    normed1 = collect(normed_f.astype(jnp.bfloat16))
    qkv = fdot(normed1, qkv_full)
    query = qkv[:, :q_wide].reshape(rows_here, row_len, heads_here, HD)
    keys = qkv[:, q_wide : q_wide + kv_wide].reshape(rows_here, row_len, kv_here, HD)
    values = (
        qkv[:, q_wide + kv_wide :].astype(jnp.bfloat16).reshape(rows_here, row_len, kv_here, HD)
    )
    q_norm, q_scale = rms_forward(query, gain_q)
    k_norm, k_scale = rms_forward(keys, gain_k)
    cosv, sinv = rope_tables(positions)
    cosv = cosv[:, :, None, :]
    sinv = sinv[:, :, None, :]
    q_rot = (q_norm * cosv + rotate_half(q_norm) * sinv).astype(jnp.bfloat16)
    k_rot = (k_norm * cosv + rotate_half(k_norm) * sinv).astype(jnp.bfloat16)
    attended, log_total = jax.vmap(attend_row)(q_rot, k_rot, values, segment_ids)
    att_flat = attended.reshape(tokens_here, heads_here * HD)
    hidden = xlocal + spread(contract(att_flat, output_full, 1, 1))
    normed_g, scale2 = rms_forward(hidden, gain_ffn)
    normed2 = collect(normed_g.astype(jnp.bfloat16))
    gate_up = fdot(normed2, gate_up_full)
    gate_proj, up_proj = gate_up[:, :ff_wide], gate_up[:, ff_wide:]
    sigmoid_gate = jax.nn.sigmoid(gate_proj)
    silu_gate = gate_proj * sigmoid_gate
    act = (silu_gate * up_proj).astype(jnp.bfloat16)
    block_output = (hidden + spread(contract(act, down_full, 1, 1))).astype(jnp.bfloat16)
    grad_act = fdot(dy_rows, down_full)
    grad_down = contract(dy_rows, act, 0, 0).astype(jnp.bfloat16)
    d_gate = grad_act * up_proj * sigmoid_gate * (1.0 + gate_proj * (1.0 - sigmoid_gate))
    d_gate_up = jnp.concatenate(
        [d_gate.astype(jnp.bfloat16), (grad_act * silu_gate).astype(jnp.bfloat16)], axis=1
    )
    grad_gate_up = contract(normed2, d_gate_up, 0, 0).astype(jnp.bfloat16)
    grad_n2 = spread(contract(d_gate_up, gate_up_full, 1, 1))
    gain_ffn_grad = jnp.sum(grad_n2 * hidden * scale2, axis=0)
    grad_hidden = cotangent.astype(jnp.float32) + rms_backward(hidden, scale2, gain_ffn, grad_n2)
    grad_rows = collect(grad_hidden.astype(jnp.bfloat16))
    grad_att = (
        fdot(grad_rows, output_full)
        .astype(jnp.bfloat16)
        .reshape(rows_here, row_len, heads_here, HD)
    )
    grad_out = contract(grad_rows, att_flat, 0, 0).astype(jnp.bfloat16)
    grad_qrot, grad_krot, grad_vals = jax.vmap(back_row)(
        q_rot, k_rot, values, grad_att, log_total, segment_ids
    )
    grad_qn = grad_qrot * cosv + rotate_back(grad_qrot * sinv)
    grad_kn = grad_krot * cosv + rotate_back(grad_krot * sinv)
    gain_q_grad = jnp.sum(grad_qn * query * q_scale, axis=(0, 1, 2))
    gain_k_grad = jnp.sum(grad_kn * keys * k_scale, axis=(0, 1, 2))
    d_query = rms_backward(query, q_scale, gain_q, grad_qn).astype(jnp.bfloat16)
    d_keys = rms_backward(keys, k_scale, gain_k, grad_kn).astype(jnp.bfloat16)
    d_qkv = jnp.concatenate(
        [
            d_query.reshape(tokens_here, q_wide),
            d_keys.reshape(tokens_here, kv_wide),
            grad_vals.astype(jnp.bfloat16).reshape(tokens_here, kv_wide),
        ],
        axis=1,
    )
    grad_qkv = contract(normed1, d_qkv, 0, 0).astype(jnp.bfloat16)
    grad_n1 = spread(contract(d_qkv, qkv_full, 1, 1))
    gain_attn_grad = jnp.sum(grad_n1 * xlocal * scale1, axis=0)
    grad_input = grad_hidden + rms_backward(xlocal, scale1, gain_attn, grad_n1)
    gain_terms = total(
        jnp.concatenate([gain_attn_grad, gain_ffn_grad, gain_q_grad, gain_k_grad])[None]
    )[0]
    wide = dp * shard
    norm_terms = gain_terms[: 2 * wide].reshape(2, wide).T
    qk_terms = gain_terms[2 * wide :].reshape(2, dp, qk_shard).transpose(1, 2, 0)
    qk_terms = jnp.pad(qk_terms, ((0, 0), (0, shard - qk_shard), (0, 0))).reshape(wide, 2)
    gain_pack = jnp.concatenate([norm_terms, qk_terms], axis=1).astype(jnp.bfloat16)
    gain_pack = jnp.pad(gain_pack, ((0, 0), (0, 124)))
    grad_attn = jnp.concatenate([grad_qkv, grad_out, gain_pack], axis=1)
    attn_sum, gate_up_sum, down_sum = scatter_rows([grad_attn, grad_gate_up, grad_down], dp)
    gain_sum = attn_sum[:, qkv_wide + q_wide :]
    return (
        block_output,
        grad_input,
        gain_sum[:, 0:2].T,
        gain_sum[:qk_shard, 2:4].T,
        attn_sum[:, :q_wide],
        jnp.stack([attn_sum[:, q_wide : q_wide + kv_wide], attn_sum[:, q_wide + kv_wide : qkv_wide]]),
        attn_sum[:, qkv_wide : qkv_wide + q_wide].T,
        jnp.stack([gate_up_sum[:, :ff_wide], gate_up_sum[:, ff_wide:]]),
        down_sum.T,
    )


MESH = pl.DeviceIdType.MESH
LANES = 128
F32, BF16 = jnp.float32, jnp.bfloat16


def dot_nn(a, b):
    return lax.dot_general(a, b, (((1,), (0,)), ((), ())), preferred_element_type=F32)


def dot_nt(a, b):
    return lax.dot_general(a, b, (((1,), (1,)), ((), ())), preferred_element_type=F32)


def dot_tn(a, b):
    return lax.dot_general(a, b, (((0,), (0,)), ((), ())), preferred_element_type=F32)


def lane_of(shape):
    return lax.broadcasted_iota(jnp.int32, shape, len(shape) - 1)


def head_mean(values):
    row = lax.broadcasted_iota(jnp.int32, (LANES, LANES), 0) // HD
    ones = jnp.where(row == lane_of((LANES, LANES)) // HD, 1.0 / HD, 0.0).astype(BF16)
    high = values.astype(BF16)
    low = (values - high.astype(F32)).astype(BF16)
    return dot_nn(high, ones) + dot_nn(low, ones)


def low_half(shape):
    return lane_of(shape) < HD


def first_quarter(shape):
    return lax.rem(lane_of(shape), HD) < HD // 2


def ds(start, size):
    if isinstance(start, int):
        return pl.ds(start, size)
    return pl.ds(pl.multiple_of(start, size), size)


class Gather:
    def __init__(self, at, rows, slabs, send, recv):
        self.at, self.rows, self.slabs, self.send, self.recv = at, rows, slabs, send, recv

    def slab(self, k, o):
        return self.slabs[k](ds(o * self.rows, self.rows))

    def move(self, k, oz, ox, way, target):
        at = self.at
        o = at.device(oz, ox, at.c)
        return remote(
            self.slab(k, o), self.slab(k, o), self.send.at[k, oz * 2 + ox, way], self.recv.at[k, o], target
        )

    def arrived(self, k, o):
        at = self.at
        slab = self.slab(k, o)
        remote(slab, slab, self.send.at[k, 0, 0], self.recv.at[k, o], at.sibling).wait_recv()

    def sources(self, s, act):
        at = self.at
        for sign in (1, -1) if s else (0,):
            oz = at.z - s * sign
            if s:
                pl.when((oz >= 0) & (oz < at.length))(lambda oz=oz, sign=sign: act(oz, sign))
            else:
                act(oz, 0)

    def outgoing(self, k, oz, sign, act):
        at = self.at
        if sign >= 0:
            pl.when(at.z < at.length - 1)(lambda: act(self.move(k, oz, at.x, 0, at.above)))
        if sign <= 0:
            pl.when(at.z > 0)(lambda: act(self.move(k, oz, at.x, 1, at.below)))
        act(self.move(k, oz, at.x, 2, at.beside))
        act(self.move(k, oz, at.x, 3, at.sibling))

    def main(self, k, s):
        at = self.at

        def act(oz, sign):
            if s:
                self.arrived(k, at.device(oz, at.x, at.c))
            self.outgoing(k, oz, sign, lambda m: m.start())

        self.sources(s, act)

    def side(self, k, s):
        at = self.at

        def act(oz, sign):
            self.arrived(k, at.device(oz, 1 - at.x, at.c))
            self.move(k, oz, 1 - at.x, 3, at.sibling).start()

        self.sources(s, act)

    def final(self, k):
        at = self.at
        for oz in range(at.length):
            for ox in range(2):
                self.arrived(k, at.device(oz, ox, 1 - at.c))

    def finish(self, k):
        at = self.at
        for s in range(at.length):
            self.sources(s, lambda oz, sign: self.outgoing(k, oz, sign, lambda m: m.wait_send()))
            self.sources(s, lambda oz, sign: self.move(k, oz, 1 - at.x, 3, at.sibling).wait_send())


class Spot(Place):
    def __init__(self, dp):
        super().__init__(dp)
        z, x, c = self.z, self.x, self.c
        self.below, self.above = self.device(z - 1, x, c), self.device(z + 1, x, c)
        self.beside, self.sibling = self.device(z, 1 - x, c), self.device(z, x, 1 - c)
        self.own = self.device(z, x, c)
        self.t = lax.axis_index("tensor")

    def greet(self):
        barrier = pltpu.get_barrier_semaphore()

        def signal(target):
            pl.semaphore_signal(barrier, inc=1, device_id=target, device_id_type=MESH)

        signal({"dp": self.sibling})
        signal({"dp": self.beside})
        signal({"tensor": 1 - self.t})
        pl.when(self.z > 0)(lambda: signal({"dp": self.below}))
        pl.when(self.z < self.length - 1)(lambda: signal({"dp": self.above}))
        ends = jnp.where(self.z > 0, 1, 0) + jnp.where(self.z < self.length - 1, 1, 0)
        pl.semaphore_wait(barrier, 3 + ends)


def partner(at, src, dst, sems):
    return pltpu.make_async_remote_copy(
        src_ref=src,
        dst_ref=dst,
        send_sem=sems.at[0],
        recv_sem=sems.at[1],
        device_id={"tensor": 1 - at.t},
        device_id_type=MESH,
    )


CHUNKS = 3


def fwd_kernel(
    dp, rows, half, x_ref, dy_ref, seg_ref, pos_ref, freq_ref, gains_ref, wq_ref, wkv_ref, wo_ref,
    wgu_ref, wd_ref,
    wa_out, n1_out, raw_out, p_out, qrot_out, kdup_out, vdup_out, att_out, hidden_out, n2_out,
    dyf_out, act_out, dg_out, du_out, cos_out, sin_out, gnm_out, gno_out, om_out, oo_out,
    wa, wf, xf, dyf, n1, n2, raw, prob, qrot, kdup, vdup, att, hidden, act, dg, du, cos, sin,
    segc, gn, op, part_out, part_in, gno, oo, om, gain_rows,
    send, recv, ysem, outsem,
):
    at = Spot(dp)
    wide = dp * rows
    tokens = 2 * half
    q_wide, kv_wide, ff_wide = wq_ref.shape[1], wkv_ref.shape[2], wd_ref.shape[1]
    chunk = ff_wide // CHUNKS
    o_at, g_at = q_wide + 2 * kv_wide, 2 * q_wide + 2 * kv_wide
    groups = q_wide // LANES
    mine, theirs = at.t * half, (1 - at.t) * half
    own_rows = ds(at.own * rows, rows)
    outs = []

    def put(src, dst):
        copy = pltpu.make_async_copy(src, dst, outsem.at[len(outs)])
        copy.start()
        outs.append(copy)

    at.greet()
    gather = Gather(
        at,
        rows,
        [lambda r: wa.at[r]] + [lambda r, j=j: wf.at[j, r] for j in range(CHUNKS)],
        send,
        recv,
    )
    wa[own_rows, 0:q_wide] = wq_ref[...]
    wa[own_rows, q_wide : q_wide + kv_wide] = wkv_ref[0]
    wa[own_rows, q_wide + kv_wide : o_at] = wkv_ref[1]
    wa[own_rows, o_at:g_at] = wo_ref[...]
    wa[own_rows, g_at:] = gains_ref[...]
    gather.main(0, 0)
    x_copy = partner(at, x_ref, xf.at[ds(mine, half)], ysem.at[0])
    x_copy.start()
    for j in range(CHUNKS):
        cols = slice(j * chunk, (j + 1) * chunk)
        wf[j, own_rows, 0:chunk] = wgu_ref[0, :, cols]
        wf[j, own_rows, chunk : 2 * chunk] = wgu_ref[1, :, cols]
        wf[j, own_rows, 2 * chunk :] = wd_ref[:, cols]
    gather.main(1, 0)
    dy_copy = partner(at, dy_ref, dyf.at[ds(mine, half)], ysem.at[1])
    dy_copy.start()
    xf[ds(mine, half)] = x_ref[...]
    dyf[ds(mine, half)] = dy_ref[...]

    segc[...] = jnp.broadcast_to(seg_ref[...].astype(F32), (LANES, tokens)).T
    cos[...] = jnp.broadcast_to(pos_ref[...].astype(F32), (LANES, tokens)).T

    @pl.loop(0, tokens // 64)
    def _(i):
        r = ds(i * 64, 64)
        angles = cos[r] * freq_ref[...]
        cos[r] = jnp.cos(angles)
        sin[r] = jnp.sin(angles)

    gather.main(0, 1)
    gather.side(0, 0)
    gather.main(0, 2)
    gather.side(0, 1)
    gather.main(0, 3)
    gather.side(0, 2)
    gather.side(0, 3)
    gather.final(0)
    put(wa, wa_out)
    gather.main(2, 0)
    gather.main(3, 0)
    put(cos, cos_out)
    put(sin, sin_out)

    gain_rows[...] = wa[:, g_at : g_at + LANES].astype(F32).T[:8]
    qk_gain = jnp.sum(wa[:, g_at + LANES :].astype(F32), axis=0, keepdims=True)
    lows = low_half((1, LANES))
    gain_q = jnp.where(lows, qk_gain, pltpu.roll(qk_gain, HD, 1))
    gain_k = jnp.where(lows, pltpu.roll(qk_gain, HD, 1), qk_gain)
    gain_attn, gain_ffn = gain_rows[0:1, :], gain_rows[1:2, :]
    x_copy.wait_recv()

    @pl.loop(0, tokens // 64)
    def _(i):
        r = ds(i * 64, 64)
        values = xf[r].astype(F32)
        n1[r] = rms_forward(values, gain_attn)[0].astype(BF16)

    put(n1, n1_out)
    gather.main(1, 1)
    gather.side(1, 0)

    @pl.loop(0, o_at // 256)
    def _(n):
        tile = dot_nn(n1[...], wa[:, ds(n * 256, 256)])
        raw[2 * n] = tile[:, :LANES]
        raw[2 * n + 1] = tile[:, LANES:]

    put(raw, raw_out)
    blk = 128

    def rope(n, gain, r):
        values = raw[n, r]
        normed = values * lax.rsqrt(head_mean(values * values) + EPSILON) * gain
        early = first_quarter(normed.shape)
        turned = jnp.where(early, -pltpu.roll(normed, LANES - HD // 2, 1), pltpu.roll(normed, HD // 2, 1))
        return normed * cos[r] + turned * sin[r]

    def doubled(tile):
        swapped = pltpu.roll(tile, HD, 1)
        lows = low_half(tile.shape)
        return jnp.where(lows, tile, swapped).astype(BF16), jnp.where(lows, swapped, tile).astype(BF16)

    @pl.loop(0, tokens // blk)
    def _(i):
        r = ds(i * blk, blk)
        for n in range(groups):
            qrot[n, r] = rope(n, gain_q, r).astype(BF16)
        for n in range(groups // 2):
            kdup[2 * n, r], kdup[2 * n + 1, r] = doubled(rope(groups + n, gain_k, r))
            vdup[2 * n, r], vdup[2 * n + 1, r] = doubled(raw[groups + groups // 2 + n, r])

    put(qrot, qrot_out)
    put(kdup, kdup_out)
    put(vdup, vdup_out)
    gather.main(1, 2)
    gather.side(1, 1)
    gather.main(2, 1)
    gather.side(2, 0)

    def attend(base):
        @pl.loop(0, groups * (half // blk))
        def _(step):
            g = step // (half // blk)
            start = base + lax.rem(step, half // blk) * blk
            r = ds(start, blk)
            q = qrot[g, r]
            lows = low_half(q.shape)
            index = lax.broadcasted_iota(jnp.int32, (blk, tokens), 0) + start
            allowed = (segc[r, 0:1] == seg_ref[...].astype(F32)) & (lane_of((blk, tokens)) <= index)
            result = []
            for hh in range(2):
                picked = jnp.where(lows if hh == 0 else jnp.logical_not(lows), q, jnp.zeros_like(q))
                scores = dot_nt(picked, kdup[g]) * (1.0 / math.sqrt(HD))
                scores = jnp.where(allowed, scores, NEG_FILL)
                e = jnp.exp(scores - jnp.max(scores, axis=1, keepdims=True))
                p = (e / jnp.sum(e, axis=1, keepdims=True)).astype(BF16)
                prob[g, hh, r] = p
                result.append(dot_nn(p, vdup[g]))
            att[r, ds(g * LANES, LANES)] = jnp.where(lows, result[0], result[1]).astype(BF16)

    attend(theirs)

    @pl.loop(0, wide // 256)
    def _(n):
        cols = ds(n * 256, 256)
        part_out[:, cols] = dot_nt(att[ds(theirs, half)], wa[cols, o_at:g_at]).astype(BF16)

    out_copy = partner(at, part_out, part_in, ysem.at[2])
    out_copy.start()
    gather.main(1, 3)
    gather.side(1, 2)
    gather.side(1, 3)
    gather.main(3, 1)
    gather.side(3, 0)
    attend(mine)
    put(prob, p_out)
    put(att, att_out)
    gather.main(2, 2)
    gather.side(2, 1)

    @pl.loop(0, wide // 256)
    def _(n):
        cols = ds(n * 256, 256)
        hidden[:, cols] = x_ref[:, cols].astype(F32) + dot_nt(att[ds(mine, half)], wa[cols, o_at:g_at])

    out_copy.wait_recv()

    @pl.loop(0, half // 64)
    def _(i):
        r = ds(i * 64, 64)
        values = hidden[r] + part_in[r].astype(F32)
        hidden[r] = values
        n2[ds(mine + i * 64, 64)] = rms_forward(values, gain_ffn)[0].astype(BF16)

    put(hidden, hidden_out)
    n2_copy = partner(at, n2.at[ds(mine, half)], n2.at[ds(mine, half)], ysem.at[3])
    n2_copy.start()
    gather.main(2, 3)
    gather.side(2, 2)
    gather.side(2, 3)
    gather.main(3, 2)
    gather.side(3, 1)
    dy_copy.wait_recv()
    put(dyf, dyf_out)
    n2_copy.wait_recv()
    put(n2, n2_out)

    for j in range(CHUNKS):
        gather.final(j + 1)

        @pl.loop(0, chunk // 256)
        def _(n, j=j):
            for m in range(2):
                r = slice(m * half, (m + 1) * half)
                gate = dot_nn(n2[r], wf[j, :, ds(n * 256, 256)])
                up = dot_nn(n2[r], wf[j, :, ds(chunk + n * 256, 256)])
                gact = dot_nn(dyf[r], wf[j, :, ds(2 * chunk + n * 256, 256)])
                sig = jax.nn.sigmoid(gate)
                silu = gate * sig
                cols = ds(j * chunk + n * 256, 256)
                act[r, cols] = (silu * up).astype(BF16)
                dg[r, cols] = (gact * up * sig * (1.0 + gate * (1.0 - sig))).astype(BF16)
                du[r, cols] = (gact * silu).astype(BF16)

        cols = slice(j * chunk, (j + 1) * chunk)
        if j == 0:
            gather.main(3, 3)
            gather.side(3, 2)
            gather.side(3, 3)

        @pl.loop(0, wide // 256)
        def _(n, j=j, cols=cols):
            r = ds(n * 256, 256)
            down = dot_nt(act[:, cols], wf[j, r, 2 * chunk :])
            back = dot_nt(dg[:, cols], wf[j, r, :chunk]) + dot_nt(du[:, cols], wf[j, r, chunk : 2 * chunk])
            if j == 0:
                op[:, r] = down
                gn[:, r] = back
            else:
                op[:, r] += down
                gn[:, r] += back

    put(act, act_out)
    put(dg, dg_out)
    put(du, du_out)
    put(gn.at[ds(mine, half)], gnm_out)

    @pl.loop(0, half // 64)
    def _(i):
        r = ds(i * 64, 64)
        gno[r] = gn[ds(theirs + i * 64, 64)].astype(BF16)
        oo[r] = op[ds(theirs + i * 64, 64)].astype(BF16)
        om[r] = op[ds(mine + i * 64, 64)] + hidden[r]

    put(gno, gno_out)
    put(oo, oo_out)
    put(om, om_out)
    for copy in (x_copy, dy_copy, out_copy, n2_copy):
        copy.wait_send()
    for k in range(CHUNKS + 1):
        gather.finish(k)
    for copy in outs:
        copy.wait()


def forward(dp, x, dy, seg, pos, freq, gains, wq, wkv, wo_t, wgu, wd_t):
    rows, half = wq.shape[0], x.shape[0]
    tokens, wide = 2 * half, dp * rows
    q_wide, kv_wide, ff_wide = wq.shape[1], wkv.shape[2], wd_t.shape[1]
    groups = q_wide // LANES
    attn_wide = 2 * q_wide + 2 * kv_wide + 2 * LANES
    shapes = [
        ((wide, attn_wide), BF16),
        ((tokens, wide), BF16),
        ((2 * groups, tokens, LANES), F32),
        ((groups, 2, tokens, tokens), BF16),
        ((groups, tokens, LANES), BF16),
        ((groups, tokens, LANES), BF16),
        ((groups, tokens, LANES), BF16),
        ((tokens, q_wide), BF16),
        ((half, wide), F32),
        ((tokens, wide), BF16),
        ((tokens, wide), BF16),
        ((tokens, ff_wide), BF16),
        ((tokens, ff_wide), BF16),
        ((tokens, ff_wide), BF16),
        ((tokens, LANES), F32),
        ((tokens, LANES), F32),
        ((half, wide), F32),
        ((half, wide), BF16),
        ((half, wide), F32),
        ((half, wide), BF16),
    ]
    (wa, n1, raw, p, qrot, kdup, vdup, att, hidden, n2, dyf, act, dg, du, cos, sin, gnm, gno, om, oo) = shapes
    vmem = [
        wa, ((CHUNKS, wide, 3 * ff_wide // CHUNKS), BF16), n2, dyf, n1, n2, raw, p, qrot, kdup, vdup, att,
        hidden, act, dg, du, cos, sin, cos, ((tokens, wide), F32), ((tokens, wide), F32), oo, oo, gno, oo, om,
        ((8, wide), F32),
    ]
    return pl.pallas_call(
        functools.partial(fwd_kernel, dp, rows, half),
        out_shape=[jax.ShapeDtypeStruct(*s) for s in shapes],
        in_specs=[pl.BlockSpec(memory_space=pltpu.VMEM)] * 11,
        out_specs=[pl.BlockSpec(memory_space=pl.ANY)] * len(shapes),
        scratch_shapes=[pltpu.VMEM(*s) for s in vmem]
        + [
            pltpu.SemaphoreType.DMA((CHUNKS + 1, dp // 2, 4)),
            pltpu.SemaphoreType.DMA((CHUNKS + 1, dp)),
            pltpu.SemaphoreType.DMA((4, 2)),
            pltpu.SemaphoreType.DMA((len(shapes),)),
        ],
        compiler_params=pltpu.CompilerParams(
            collective_id=3, has_side_effects=True, vmem_limit_bytes=62 * 1024 * 1024
        ),
        name="forward",
    )(x, dy, seg, pos, freq, gains, wq, wkv, wo_t, wgu, wd_t)


def untile(tiles):
    return tiles.transpose(1, 0, 2).reshape(tiles.shape[1], -1)


def pack_gains(norm_gains, qk_gains, shard):
    o = lax.axis_index("dp")
    qk_shard = qk_gains.shape[1]
    cols = jnp.pad(norm_gains.T, ((0, 0), (0, LANES - 2)))
    row = jnp.zeros((1, LANES), BF16)
    for i in range(2):
        row = lax.dynamic_update_slice(row, qk_gains[i : i + 1], (0, i * HD + o * qk_shard))
    return jnp.concatenate([cols, jnp.pad(row, ((0, shard - 1), (0, 0)))], axis=1)


def fast_device(
    block_input, cotangent, segment_ids, positions, norm_gains, qk_gains, w_query, w_keyval, w_output,
    w_gate_up, w_down,
):
    dp = lax.axis_size("dp")
    tokens = segment_ids.shape[1]
    shard, q_wide = w_query.shape
    kv_wide, ff_wide = w_keyval.shape[2], w_gate_up.shape[2]
    qk_shard = qk_gains.shape[1]
    freqs = ROPE_BASE ** (-jnp.arange(0, HD, 2).astype(F32) / HD)
    freq = jnp.tile(freqs, 4)[None]
    (wa, n1, raw, p, qrot, kdup, vdup, att, hidden, n2, dyf, act, dg, du, cos, sin, gnm, gno, om, oo) = forward(
        dp, block_input, cotangent, segment_ids, positions, freq, pack_gains(norm_gains, qk_gains, shard),
        w_query, w_keyval, w_output.T, w_gate_up, w_down.T,
    )
    qkv_wide = q_wide + 2 * kv_wide
    qkv_full, output_full = wa[:, :qkv_wide], wa[:, qkv_wide : qkv_wide + q_wide]
    gain_cols = wa[:, qkv_wide + q_wide :].astype(F32)
    gain_attn, gain_ffn = gain_cols[:, 0], gain_cols[:, 1]
    qk_sum = jnp.sum(gain_cols[:, LANES:], axis=0)
    gain_q, gain_k = qk_sum[:HD], qk_sum[HD:]
    heads_here, kv_here = q_wide // HD, kv_wide // HD
    xlocal = block_input.astype(F32)
    _, scale1 = rms_forward(xlocal, gain_attn)
    _, scale2 = rms_forward(hidden, gain_ffn)
    full = untile(raw)
    query = full[:, :q_wide].reshape(1, tokens, heads_here, HD)
    keys = full[:, q_wide : q_wide + kv_wide].reshape(1, tokens, kv_here, HD)
    values = full[:, q_wide + kv_wide :].astype(BF16).reshape(1, tokens, kv_here, HD)
    _, q_scale = rms_forward(query, gain_q)
    k_norm, k_scale = rms_forward(keys, gain_k)
    cosv, sinv = cos[None, :, None, :HD], sin[None, :, None, :HD]
    q_rot = untile(qrot).reshape(1, tokens, heads_here, HD)
    k_rot = kdup[:, :, :HD].transpose(1, 0, 2)[None]
    block_output = (om + exchange(oo).astype(F32)).astype(BF16)
    grad_down = contract(dyf, act, 0, 0).astype(BF16)
    d_gate_up = jnp.concatenate([dg, du], axis=1)
    grad_gate_up = contract(n2, d_gate_up, 0, 0).astype(BF16)
    grad_n2 = gnm + exchange(gno).astype(F32)
    gain_ffn_grad = jnp.sum(grad_n2 * hidden * scale2, axis=0)
    grad_hidden = cotangent.astype(F32) + rms_backward(hidden, scale2, gain_ffn, grad_n2)
    grad_rows = collect(grad_hidden.astype(BF16))
    grad_att = fdot(grad_rows, output_full).astype(BF16).reshape(tokens, kv_here, 2, HD)
    grad_out = contract(grad_rows, att, 0, 0).astype(BF16)
    q_four = q_rot.reshape(tokens, kv_here, 2, HD)
    grad_vals = jnp.einsum("kgij,ikgd->jkd", p, grad_att, preferred_element_type=F32)
    grad_p = jnp.einsum("ikgd,jkd->kgij", grad_att, values[0], preferred_element_type=F32)
    pf = p.astype(F32)
    delta = jnp.sum(pf * grad_p, axis=-1, keepdims=True)
    d_scores = (pf * (grad_p - delta) / math.sqrt(HD)).astype(BF16)
    grad_qrot = jnp.einsum("kgij,jkd->ikgd", d_scores, k_rot[0], preferred_element_type=F32).reshape(q_rot.shape)
    grad_krot = jnp.einsum("kgij,ikgd->jkd", d_scores, q_four, preferred_element_type=F32)[None]
    grad_qn = grad_qrot * cosv + rotate_back(grad_qrot * sinv)
    grad_kn = grad_krot * cosv + rotate_back(grad_krot * sinv)
    gain_q_grad = jnp.sum(grad_qn * query * q_scale, axis=(0, 1, 2))
    gain_k_grad = jnp.sum(grad_kn * keys * k_scale, axis=(0, 1, 2))
    d_query = rms_backward(query, q_scale, gain_q, grad_qn).astype(BF16)
    d_keys = rms_backward(keys, k_scale, gain_k, grad_kn).astype(BF16)
    d_qkv = jnp.concatenate(
        [d_query.reshape(tokens, q_wide), d_keys.reshape(tokens, kv_wide), grad_vals.astype(BF16).reshape(tokens, kv_wide)],
        axis=1,
    )
    grad_qkv = contract(n1, d_qkv, 0, 0).astype(BF16)
    grad_n1 = spread(contract(d_qkv, qkv_full, 1, 1))
    gain_attn_grad = jnp.sum(grad_n1 * xlocal * scale1, axis=0)
    grad_input = grad_hidden + rms_backward(xlocal, scale1, gain_attn, grad_n1)
    gain_terms = total(jnp.concatenate([gain_attn_grad, gain_ffn_grad, gain_q_grad, gain_k_grad])[None])[0]
    wide = dp * shard
    norm_terms = gain_terms[: 2 * wide].reshape(2, wide).T
    qk_terms = gain_terms[2 * wide :].reshape(2, dp, qk_shard).transpose(1, 2, 0)
    qk_terms = jnp.pad(qk_terms, ((0, 0), (0, shard - qk_shard), (0, 0))).reshape(wide, 2)
    gain_pack = jnp.concatenate([norm_terms, qk_terms], axis=1).astype(BF16)
    gain_pack = jnp.pad(gain_pack, ((0, 0), (0, 124)))
    grad_attn = jnp.concatenate([grad_qkv, grad_out, gain_pack], axis=1)
    attn_sum, gate_up_sum, down_sum = scatter_rows([grad_attn, grad_gate_up, grad_down], dp)
    gain_sum = attn_sum[:, qkv_wide + q_wide :]
    return (
        block_output,
        grad_input,
        gain_sum[:, 0:2].T,
        gain_sum[:qk_shard, 2:4].T,
        attn_sum[:, :q_wide],
        jnp.stack([attn_sum[:, q_wide : q_wide + kv_wide], attn_sum[:, q_wide + kv_wide : qkv_wide]]),
        attn_sum[:, qkv_wide : qkv_wide + q_wide].T,
        jnp.stack([gate_up_sum[:, :ff_wide], gate_up_sum[:, ff_wide:]]),
        down_sum.T,
    )


def solution(mesh):
    return jax.shard_map(
        fast_device if mesh.shape["tensor"] == 2 and mesh.shape["dp"] == 16 else on_device,
        mesh=mesh,
        in_specs=(
            P(("dp", "tensor"), None),
            P(("dp", "tensor"), None),
            P("dp", None),
            P("dp", None),
            P(None, "dp"),
            P(None, "dp"),
            P("dp", "tensor"),
            P(None, "dp", "tensor"),
            P("tensor", "dp"),
            P(None, "dp", "tensor"),
            P("tensor", "dp"),
        ),
        out_specs=(
            P(("dp", "tensor"), None),
            P(("dp", "tensor"), None),
            P(None, "dp"),
            P(None, "dp"),
            P("dp", "tensor"),
            P(None, "dp", "tensor"),
            P("tensor", "dp"),
            P(None, "dp", "tensor"),
            P("tensor", "dp"),
        ),
        check_vma=False,
    )
```

```python
import functools
import math

import jax
import jax.numpy as jnp
from jax import lax
from jax.experimental import pallas as pl
from jax.experimental.pallas import tpu as pltpu
from jax.sharding import PartitionSpec as P

HD = 64


EPSILON = 1e-05
ROPE_BASE = 1000000.0
NEG_FILL = -1e30


def rms_forward(values, gain):
    scale = lax.rsqrt(jnp.mean(values * values, axis=-1, keepdims=True) + EPSILON)
    return (values * scale * gain, scale)


def rms_backward(values, scale, gain, grad):
    weighted = grad * gain
    inner = jnp.mean(weighted * values, axis=-1, keepdims=True)
    return scale * (weighted - values * scale * scale * inner)


def rope_tables(places):
    freqs = ROPE_BASE ** (-jnp.arange(0, HD, 2).astype(jnp.float32) / HD)
    angles = places.astype(jnp.float32)[..., None] * freqs
    angles = jnp.concatenate([angles, angles], axis=-1)
    return (jnp.cos(angles), jnp.sin(angles))


def rotate_half(values):
    half = values.shape[-1] // 2
    return jnp.concatenate([-values[..., half:], values[..., :half]], axis=-1)


def rotate_back(values):
    half = values.shape[-1] // 2
    return jnp.concatenate([values[..., half:], -values[..., :half]], axis=-1)


def allowed_mask(segs):
    length = segs.shape[0]
    index = jnp.arange(length, dtype=jnp.int32)
    return (segs[:, None] == segs[None, :]) & (index[None, :] <= index[:, None])


def contract(left, right, left_dim, right_dim):
    return lax.dot_general(
        left, right, (((left_dim,), (right_dim,)), ((), ())), preferred_element_type=jnp.float32
    )


def fdot(left, right):
    return jnp.dot(left, right, preferred_element_type=jnp.float32)


def row_scores(q_rot, k_rot):
    kv_heads = k_rot.shape[1]
    groups = q_rot.shape[1] // kv_heads
    q_four = q_rot.reshape(q_rot.shape[0], kv_heads, groups, HD)
    scores = jnp.einsum("ikgd,jkd->kgij", q_four, k_rot, preferred_element_type=jnp.float32)
    return (scores / math.sqrt(HD), q_four)


def attend_row(q_rot, k_rot, values, segs):
    scores, q_four = row_scores(q_rot, k_rot)
    allowed = allowed_mask(segs)[None, None]
    masked = jnp.where(allowed, scores, NEG_FILL)
    top = jnp.max(masked, axis=-1, keepdims=True)
    expd = jnp.where(allowed, jnp.exp(masked - top), 0.0)
    total = jnp.sum(expd, axis=-1, keepdims=True)
    probs = (expd / total).astype(jnp.bfloat16)
    log_total = top[..., 0] + jnp.log(total[..., 0])
    attended = jnp.einsum("kgij,jkd->ikgd", probs, values, preferred_element_type=jnp.float32)
    return (attended.reshape(q_rot.shape).astype(jnp.bfloat16), log_total)


def back_row(q_rot, k_rot, values, grad_att, log_total, segs):
    scores, q_four = row_scores(q_rot, k_rot)
    allowed = allowed_mask(segs)[None, None]
    masked = jnp.where(allowed, scores, NEG_FILL)
    probs = jnp.where(allowed, jnp.exp(masked - log_total[..., None]), 0.0)
    probs_b = probs.astype(jnp.bfloat16)
    grad_four = grad_att.reshape(q_four.shape)
    grad_values = jnp.einsum(
        "kgij,ikgd->jkd", probs_b, grad_four, preferred_element_type=jnp.float32
    )
    grad_p = jnp.einsum("ikgd,jkd->kgij", grad_four, values, preferred_element_type=jnp.float32)
    delta = jnp.sum(probs * grad_p, axis=-1, keepdims=True)
    d_scores = (probs * (grad_p - delta) / math.sqrt(HD)).astype(jnp.bfloat16)
    grad_q = jnp.einsum(
        "kgij,jkd->ikgd", d_scores, k_rot, preferred_element_type=jnp.float32
    ).reshape(q_rot.shape)
    grad_k = jnp.einsum("kgij,ikgd->jkd", d_scores, q_four, preferred_element_type=jnp.float32)
    return (grad_q, grad_k, grad_values)


def layout_of(dp):
    if dp == 16:
        return (4, 4, 2)
    return (dp // 4, 2, dp // 2)


class Place:
    def __init__(self, dp):
        self.length, self.zs, self.xs = layout_of(dp)
        me = lax.axis_index("dp")
        self.z = lax.rem(me // self.zs, self.length)
        self.x = lax.rem(me // self.xs, 2)
        self.c = lax.rem(me, 2)

    def device(self, z, x, c):
        return z * self.zs + x * self.xs + c

    def greet(self):
        z, x, c = self.z, self.x, self.c
        barrier = pltpu.get_barrier_semaphore()

        def signal(target):
            pl.semaphore_signal(
                barrier, inc=1, device_id={"dp": target}, device_id_type=pl.DeviceIdType.MESH
            )

        signal(self.device(z, x, 1 - c))
        signal(self.device(z, 1 - x, c))
        pl.when(z > 0)(lambda: signal(self.device(z - 1, x, c)))
        pl.when(z < self.length - 1)(lambda: signal(self.device(z + 1, x, c)))
        ends = jnp.where(z > 0, 1, 0) + jnp.where(z < self.length - 1, 1, 0)
        pl.semaphore_wait(barrier, 2 + ends)


def remote(src, dst, send, recv, target):
    return pltpu.make_async_remote_copy(
        src_ref=src,
        dst_ref=dst,
        send_sem=send,
        recv_sem=recv,
        device_id={"dp": target},
        device_id_type=pl.DeviceIdType.MESH,
    )


def gather_kernel(dp, count, rows, *refs):
    ins, outs = refs[:count], refs[count : 2 * count]
    send, recv, local = refs[2 * count :]
    at = Place(dp)
    z, x, c, length = at.z, at.x, at.c, at.length
    below, above = at.device(z - 1, x, c), at.device(z + 1, x, c)
    beside, sibling = at.device(z, 1 - x, c), at.device(z, x, 1 - c)
    at.greet()
    own = at.device(z, x, c)

    def slab(k, o):
        return outs[k].at[pl.ds(pl.multiple_of(o * rows, rows), rows)]

    for k in range(count):
        pltpu.make_async_copy(ins[k], slab(k, own), local.at[k]).start()

    def move(k, oz, ox, way, target, first):
        o = at.device(oz, ox, c)
        src = ins[k] if first else slab(k, o)
        return remote(src, slab(k, o), send.at[k, oz * 2 + ox, way], recv.at[k, o], target)

    def arrived(k, o):
        remote(slab(k, o), slab(k, o), send.at[k, 0, 0], recv.at[k, o], sibling).wait_recv()

    def steps(act):
        for s in range(length):
            for sign in (1, -1) if s else (0,):
                oz = z - s * sign

                def event(oz=oz, s=s, sign=sign):
                    for k in range(count):
                        act(k, oz, s, sign)

                if s:
                    pl.when((oz >= 0) & (oz < length))(event)
                else:
                    event()
            if s:
                side(s - 1, act)
        side(length - 1, act)

    def side(s, act):
        for sign in (1, -1) if s else (0,):
            oz = z - s * sign

            def event(oz=oz):
                for k in range(count):
                    act(k, oz, None, 0)

            if s:
                pl.when((oz >= 0) & (oz < length))(event)
            else:
                event()

    def begin(k, oz, s, sign):
        if s is None:
            arrived(k, at.device(oz, 1 - x, c))
            move(k, oz, 1 - x, 3, sibling, False).start()
            return
        first = s == 0
        if not first:
            arrived(k, at.device(oz, x, c))
        if sign >= 0:
            pl.when(z < length - 1)(lambda: move(k, oz, x, 0, above, first).start())
        if sign <= 0:
            pl.when(z > 0)(lambda: move(k, oz, x, 1, below, first).start())
        move(k, oz, x, 2, beside, first).start()
        move(k, oz, x, 3, sibling, first).start()

    def finish(k, oz, s, sign):
        if s is None:
            move(k, oz, 1 - x, 3, sibling, False).wait_send()
            return
        first = s == 0
        if sign >= 0:
            pl.when(z < length - 1)(lambda: move(k, oz, x, 0, above, first).wait_send())
        if sign <= 0:
            pl.when(z > 0)(lambda: move(k, oz, x, 1, below, first).wait_send())
        move(k, oz, x, 2, beside, first).wait_send()
        move(k, oz, x, 3, sibling, first).wait_send()

    steps(begin)
    for oz in range(length):
        for ox in range(2):
            for k in range(count):
                arrived(k, at.device(oz, ox, 1 - c))
    steps(finish)
    for k in range(count):
        pltpu.make_async_copy(ins[k], slab(k, own), local.at[k]).wait()


def gather_rows(arrays, dp):
    count, rows = len(arrays), arrays[0].shape[0]
    return pl.pallas_call(
        functools.partial(gather_kernel, dp, count, rows),
        out_shape=[jax.ShapeDtypeStruct((dp * rows, a.shape[1]), a.dtype) for a in arrays],
        in_specs=[pl.BlockSpec(memory_space=pltpu.VMEM)] * count,
        out_specs=[pl.BlockSpec(memory_space=pl.ANY)] * count,
        scratch_shapes=[
            pltpu.SemaphoreType.DMA((count, dp // 2, 4)),
            pltpu.SemaphoreType.DMA((count, dp)),
            pltpu.SemaphoreType.DMA((count,)),
        ],
        compiler_params=pltpu.CompilerParams(collective_id=1, has_side_effects=True),
        name="gather_rows",
    )(*arrays)


def scatter_kernel(dp, count, rows, *refs):
    parts, outs = refs[:count], refs[count : 2 * count]
    mine, first, second, upward, downward = (
        refs[(2 + i) * count : (3 + i) * count] for i in range(5)
    )
    sent1, sent2, sent4, got1, got2, got_up, got_down, local = refs[7 * count :]
    at = Place(dp)
    z, x, c, length = at.z, at.x, at.c, at.length
    below, above = at.device(z - 1, x, c), at.device(z + 1, x, c)
    beside, sibling = at.device(z, 1 - x, c), at.device(z, x, 1 - c)
    at.greet()

    def slab(k, o):
        return parts[k].at[pl.ds(pl.multiple_of(o * rows, rows), rows)]

    def swap(k, t, ox):
        q = t * 2 + ox
        return remote(
            slab(k, at.device(t, ox, 1 - c)), first[k].at[q], sent1.at[k, q], got1.at[k, q], sibling
        )

    def keep(k, t, ox):
        q = t * 2 + ox
        return pltpu.make_async_copy(slab(k, at.device(t, ox, c)), mine[k].at[q], local.at[k, q])

    def cross(k, t):
        q = t * 2 + 1 - x
        return remote(first[k].at[q], second[k].at[t], sent2.at[k, t], got2.at[k, t], beside)

    def rise(k, t):
        return remote(second[k].at[t], upward[k].at[t], sent4.at[k, t], got_up.at[k, t], above)

    def fall(k, t):
        return remote(second[k].at[t], downward[k].at[t], sent4.at[k, t], got_down.at[k, t], below)

    def targets(act):
        for d in range(length - 1, -1, -1):
            for sign in (1, -1) if d else (0,):
                t = z + d * sign

                def event(t=t, sign=sign):
                    for k in range(count):
                        act(k, t, sign)

                if d:
                    pl.when((t >= 0) & (t < length))(event)
                else:
                    event()

    def wide(value):
        return value.astype(jnp.float32)

    def start(k, t, sign):
        for ox in (1 - x, x):
            swap(k, t, ox).start()
            keep(k, t, ox).start()

    def chip_sum(k, t, sign):
        for ox in (1 - x, x):
            q = t * 2 + ox
            keep(k, t, ox).wait()
            swap(k, t, ox).wait_recv()
            first[k][q] = (wide(first[k][q]) + wide(mine[k][q])).astype(jnp.bfloat16)
            if ox is not x:
                cross(k, t).start()

    def chain(k, t, sign):
        cross(k, t).wait_recv()
        if sign == 0:
            outs[k][...] = wide(second[k][t]) + wide(first[k][t * 2 + x])

            def add_up():
                rise(k, t).wait_recv()
                outs[k][...] += wide(upward[k][t])

            def add_down():
                fall(k, t).wait_recv()
                outs[k][...] += wide(downward[k][t])

            pl.when(z > 0)(add_up)
            pl.when(z < length - 1)(add_down)
            return
        base, move = (upward, rise) if sign > 0 else (downward, fall)
        inner = z > 0 if sign > 0 else z < length - 1

        def middle():
            move(k, t).wait_recv()
            second[k][t] = (
                wide(second[k][t]) + wide(first[k][t * 2 + x]) + wide(base[k][t])
            ).astype(jnp.bfloat16)

        def edge():
            second[k][t] = (wide(second[k][t]) + wide(first[k][t * 2 + x])).astype(jnp.bfloat16)

        pl.when(inner)(middle)
        pl.when(jnp.logical_not(inner))(edge)
        move(k, t).start()

    def finish(k, t, sign):
        swap(k, t, 0).wait_send()
        swap(k, t, 1).wait_send()
        cross(k, t).wait_send()
        if sign:
            (rise if sign > 0 else fall)(k, t).wait_send()

    targets(start)
    targets(chip_sum)
    targets(chain)
    targets(finish)


def scatter_rows(arrays, dp):
    count, rows = len(arrays), arrays[0].shape[0] // dp
    length = layout_of(dp)[0]
    slots = [dp // 2, dp // 2, length, length, length]
    return pl.pallas_call(
        functools.partial(scatter_kernel, dp, count, rows),
        out_shape=[jax.ShapeDtypeStruct((rows, a.shape[1]), jnp.float32) for a in arrays],
        in_specs=[pl.BlockSpec(memory_space=pl.ANY)] * count,
        out_specs=[pl.BlockSpec(memory_space=pltpu.VMEM)] * count,
        scratch_shapes=[
            pltpu.VMEM((n, rows, a.shape[1]), a.dtype) for n in slots for a in arrays
        ]
        + [
            pltpu.SemaphoreType.DMA((count, n))
            for n in (dp // 2, length, length, dp // 2, length, length, length, dp // 2)
        ],
        compiler_params=pltpu.CompilerParams(
            collective_id=2, has_side_effects=True, vmem_limit_bytes=60 * 1024 * 1024
        ),
        name="scatter_rows",
    )(*arrays)


def exchange(values):
    return lax.ppermute(values, "tensor", ((0, 1), (1, 0)))


def collect(values):
    if lax.axis_size("tensor") != 2:
        return lax.all_gather(values, "tensor", axis=0, tiled=True)
    other = exchange(values)
    low = lax.axis_index("tensor") == 0
    return jnp.concatenate([jnp.where(low, values, other), jnp.where(low, other, values)])


def spread(values):
    if lax.axis_size("tensor") != 2:
        return lax.psum_scatter(values, "tensor", scatter_dimension=0, tiled=True)
    half = values.shape[0] // 2
    low = lax.axis_index("tensor") == 0
    head, tail = values[:half], values[half:]
    other = exchange(jnp.where(low, tail, head).astype(jnp.bfloat16))
    return jnp.where(low, head, tail) + other.astype(jnp.float32)


def total(values):
    if lax.axis_size("tensor") != 2:
        return lax.psum(values, "tensor")
    return values + exchange(values)


def on_device(
    block_input,
    cotangent,
    segment_ids,
    positions,
    norm_gains,
    qk_gains,
    w_query,
    w_keyval,
    w_output,
    w_gate_up,
    w_down,
):
    dp = lax.axis_size("dp")
    rows_here, row_len = segment_ids.shape
    tokens_here = rows_here * row_len
    shard, q_wide = w_query.shape
    kv_wide, ff_wide = w_keyval.shape[2], w_gate_up.shape[2]
    qk_shard = qk_gains.shape[1]
    gains = jnp.concatenate(
        [norm_gains.T, jnp.pad(qk_gains.T, ((0, shard - qk_shard), (0, 0)))], axis=1
    )
    gains = jnp.pad(gains, ((0, 0), (0, 124)))
    attn_pack = jnp.concatenate([w_query, w_keyval[0], w_keyval[1], w_output.T, gains], axis=1)
    gate_up_pack = jnp.concatenate([w_gate_up[0], w_gate_up[1]], axis=1)
    attn_full, gate_up_full, down_full = gather_rows([attn_pack, gate_up_pack, w_down.T], dp)
    qkv_wide = q_wide + 2 * kv_wide
    qkv_full = attn_full[:, :qkv_wide]
    output_full = attn_full[:, qkv_wide : qkv_wide + q_wide]
    gain_cols = attn_full[:, qkv_wide + q_wide :].astype(jnp.float32)
    gain_attn, gain_ffn = gain_cols[:, 0], gain_cols[:, 1]
    qk_cols = gain_cols.reshape(dp, shard, 128)[:, :qk_shard, 2:4].reshape(dp * qk_shard, 2)
    gain_q, gain_k = qk_cols[:, 0], qk_cols[:, 1]
    heads_here = q_wide // HD
    kv_here = kv_wide // HD
    dy_rows = collect(cotangent)
    xlocal = block_input.astype(jnp.float32)
    normed_f, scale1 = rms_forward(xlocal, gain_attn)
    normed1 = collect(normed_f.astype(jnp.bfloat16))
    qkv = fdot(normed1, qkv_full)
    query = qkv[:, :q_wide].reshape(rows_here, row_len, heads_here, HD)
    keys = qkv[:, q_wide : q_wide + kv_wide].reshape(rows_here, row_len, kv_here, HD)
    values = (
        qkv[:, q_wide + kv_wide :].astype(jnp.bfloat16).reshape(rows_here, row_len, kv_here, HD)
    )
    q_norm, q_scale = rms_forward(query, gain_q)
    k_norm, k_scale = rms_forward(keys, gain_k)
    cosv, sinv = rope_tables(positions)
    cosv = cosv[:, :, None, :]
    sinv = sinv[:, :, None, :]
    q_rot = (q_norm * cosv + rotate_half(q_norm) * sinv).astype(jnp.bfloat16)
    k_rot = (k_norm * cosv + rotate_half(k_norm) * sinv).astype(jnp.bfloat16)
    attended, log_total = jax.vmap(attend_row)(q_rot, k_rot, values, segment_ids)
    att_flat = attended.reshape(tokens_here, heads_here * HD)
    hidden = xlocal + spread(contract(att_flat, output_full, 1, 1))
    normed_g, scale2 = rms_forward(hidden, gain_ffn)
    normed2 = collect(normed_g.astype(jnp.bfloat16))
    gate_up = fdot(normed2, gate_up_full)
    gate_proj, up_proj = gate_up[:, :ff_wide], gate_up[:, ff_wide:]
    sigmoid_gate = jax.nn.sigmoid(gate_proj)
    silu_gate = gate_proj * sigmoid_gate
    act = (silu_gate * up_proj).astype(jnp.bfloat16)
    block_output = (hidden + spread(contract(act, down_full, 1, 1))).astype(jnp.bfloat16)
    grad_act = fdot(dy_rows, down_full)
    grad_down = contract(dy_rows, act, 0, 0).astype(jnp.bfloat16)
    d_gate = grad_act * up_proj * sigmoid_gate * (1.0 + gate_proj * (1.0 - sigmoid_gate))
    d_gate_up = jnp.concatenate(
        [d_gate.astype(jnp.bfloat16), (grad_act * silu_gate).astype(jnp.bfloat16)], axis=1
    )
    grad_gate_up = contract(normed2, d_gate_up, 0, 0).astype(jnp.bfloat16)
    grad_n2 = spread(contract(d_gate_up, gate_up_full, 1, 1))
    gain_ffn_grad = jnp.sum(grad_n2 * hidden * scale2, axis=0)
    grad_hidden = cotangent.astype(jnp.float32) + rms_backward(hidden, scale2, gain_ffn, grad_n2)
    grad_rows = collect(grad_hidden.astype(jnp.bfloat16))
    grad_att = (
        fdot(grad_rows, output_full)
        .astype(jnp.bfloat16)
        .reshape(rows_here, row_len, heads_here, HD)
    )
    grad_out = contract(grad_rows, att_flat, 0, 0).astype(jnp.bfloat16)
    grad_qrot, grad_krot, grad_vals = jax.vmap(back_row)(
        q_rot, k_rot, values, grad_att, log_total, segment_ids
    )
    grad_qn = grad_qrot * cosv + rotate_back(grad_qrot * sinv)
    grad_kn = grad_krot * cosv + rotate_back(grad_krot * sinv)
    gain_q_grad = jnp.sum(grad_qn * query * q_scale, axis=(0, 1, 2))
    gain_k_grad = jnp.sum(grad_kn * keys * k_scale, axis=(0, 1, 2))
    d_query = rms_backward(query, q_scale, gain_q, grad_qn).astype(jnp.bfloat16)
    d_keys = rms_backward(keys, k_scale, gain_k, grad_kn).astype(jnp.bfloat16)
    d_qkv = jnp.concatenate(
        [
            d_query.reshape(tokens_here, q_wide),
            d_keys.reshape(tokens_here, kv_wide),
            grad_vals.astype(jnp.bfloat16).reshape(tokens_here, kv_wide),
        ],
        axis=1,
    )
    grad_qkv = contract(normed1, d_qkv, 0, 0).astype(jnp.bfloat16)
    grad_n1 = spread(contract(d_qkv, qkv_full, 1, 1))
    gain_attn_grad = jnp.sum(grad_n1 * xlocal * scale1, axis=0)
    grad_input = grad_hidden + rms_backward(xlocal, scale1, gain_attn, grad_n1)
    gain_terms = total(
        jnp.concatenate([gain_attn_grad, gain_ffn_grad, gain_q_grad, gain_k_grad])[None]
    )[0]
    wide = dp * shard
    norm_terms = gain_terms[: 2 * wide].reshape(2, wide).T
    qk_terms = gain_terms[2 * wide :].reshape(2, dp, qk_shard).transpose(1, 2, 0)
    qk_terms = jnp.pad(qk_terms, ((0, 0), (0, shard - qk_shard), (0, 0))).reshape(wide, 2)
    gain_pack = jnp.concatenate([norm_terms, qk_terms], axis=1).astype(jnp.bfloat16)
    gain_pack = jnp.pad(gain_pack, ((0, 0), (0, 124)))
    grad_attn = jnp.concatenate([grad_qkv, grad_out, gain_pack], axis=1)
    attn_sum, gate_up_sum, down_sum = scatter_rows([grad_attn, grad_gate_up, grad_down], dp)
    gain_sum = attn_sum[:, qkv_wide + q_wide :]
    return (
        block_output,
        grad_input,
        gain_sum[:, 0:2].T,
        gain_sum[:qk_shard, 2:4].T,
        attn_sum[:, :q_wide],
        jnp.stack([attn_sum[:, q_wide : q_wide + kv_wide], attn_sum[:, q_wide + kv_wide : qkv_wide]]),
        attn_sum[:, qkv_wide : qkv_wide + q_wide].T,
        jnp.stack([gate_up_sum[:, :ff_wide], gate_up_sum[:, ff_wide:]]),
        down_sum.T,
    )


MESH = pl.DeviceIdType.MESH
LANES = 128
F32, BF16 = jnp.float32, jnp.bfloat16


def dot_nn(a, b):
    return lax.dot_general(a, b, (((1,), (0,)), ((), ())), preferred_element_type=F32)


def dot_nt(a, b):
    return lax.dot_general(a, b, (((1,), (1,)), ((), ())), preferred_element_type=F32)


def dot_tn(a, b):
    return lax.dot_general(a, b, (((0,), (0,)), ((), ())), preferred_element_type=F32)


def lane_of(shape):
    return lax.broadcasted_iota(jnp.int32, shape, len(shape) - 1)


def head_mean(values):
    row = lax.broadcasted_iota(jnp.int32, (LANES, LANES), 0) // HD
    ones = jnp.where(row == lane_of((LANES, LANES)) // HD, 1.0 / HD, 0.0).astype(BF16)
    high = values.astype(BF16)
    low = (values - high.astype(F32)).astype(BF16)
    return dot_nn(high, ones) + dot_nn(low, ones)


def low_half(shape):
    return lane_of(shape) < HD


def first_quarter(shape):
    return lax.rem(lane_of(shape), HD) < HD // 2


def ds(start, size):
    if isinstance(start, int):
        return pl.ds(start, size)
    return pl.ds(pl.multiple_of(start, size), size)


class Gather:
    def __init__(self, at, rows, slabs, send, recv):
        self.at, self.rows, self.slabs, self.send, self.recv = at, rows, slabs, send, recv

    def slab(self, k, o):
        return self.slabs[k](ds(o * self.rows, self.rows))

    def move(self, k, oz, ox, way, target):
        at = self.at
        o = at.device(oz, ox, at.c)
        return remote(
            self.slab(k, o), self.slab(k, o), self.send.at[k, oz * 2 + ox, way], self.recv.at[k, o], target
        )

    def arrived(self, k, o):
        at = self.at
        slab = self.slab(k, o)
        remote(slab, slab, self.send.at[k, 0, 0], self.recv.at[k, o], at.sibling).wait_recv()

    def sources(self, s, act):
        at = self.at
        for sign in (1, -1) if s else (0,):
            oz = at.z - s * sign
            if s:
                pl.when((oz >= 0) & (oz < at.length))(lambda oz=oz, sign=sign: act(oz, sign))
            else:
                act(oz, 0)

    def outgoing(self, k, oz, sign, act):
        at = self.at
        if sign >= 0:
            pl.when(at.z < at.length - 1)(lambda: act(self.move(k, oz, at.x, 0, at.above)))
        if sign <= 0:
            pl.when(at.z > 0)(lambda: act(self.move(k, oz, at.x, 1, at.below)))
        act(self.move(k, oz, at.x, 2, at.beside))
        act(self.move(k, oz, at.x, 3, at.sibling))

    def main(self, k, s):
        at = self.at

        def act(oz, sign):
            if s:
                self.arrived(k, at.device(oz, at.x, at.c))
            self.outgoing(k, oz, sign, lambda m: m.start())

        self.sources(s, act)

    def side(self, k, s):
        at = self.at

        def act(oz, sign):
            self.arrived(k, at.device(oz, 1 - at.x, at.c))
            self.move(k, oz, 1 - at.x, 3, at.sibling).start()

        self.sources(s, act)

    def final(self, k):
        at = self.at
        for oz in range(at.length):
            for ox in range(2):
                self.arrived(k, at.device(oz, ox, 1 - at.c))

    def finish(self, k):
        at = self.at
        for s in range(at.length):
            self.sources(s, lambda oz, sign: self.outgoing(k, oz, sign, lambda m: m.wait_send()))
            self.sources(s, lambda oz, sign: self.move(k, oz, 1 - at.x, 3, at.sibling).wait_send())


class Spot(Place):
    def __init__(self, dp):
        super().__init__(dp)
        z, x, c = self.z, self.x, self.c
        self.below, self.above = self.device(z - 1, x, c), self.device(z + 1, x, c)
        self.beside, self.sibling = self.device(z, 1 - x, c), self.device(z, x, 1 - c)
        self.own = self.device(z, x, c)
        self.t = lax.axis_index("tensor")

    def greet(self):
        barrier = pltpu.get_barrier_semaphore()

        def signal(target):
            pl.semaphore_signal(barrier, inc=1, device_id=target, device_id_type=MESH)

        signal({"dp": self.sibling})
        signal({"dp": self.beside})
        signal({"tensor": 1 - self.t})
        pl.when(self.z > 0)(lambda: signal({"dp": self.below}))
        pl.when(self.z < self.length - 1)(lambda: signal({"dp": self.above}))
        ends = jnp.where(self.z > 0, 1, 0) + jnp.where(self.z < self.length - 1, 1, 0)
        pl.semaphore_wait(barrier, 3 + ends)


def partner(at, src, dst, sems):
    return pltpu.make_async_remote_copy(
        src_ref=src,
        dst_ref=dst,
        send_sem=sems.at[0],
        recv_sem=sems.at[1],
        device_id={"tensor": 1 - at.t},
        device_id_type=MESH,
    )


CHUNKS = 3


def fwd_kernel(
    dp, rows, half, x_ref, dy_ref, seg_ref, pos_ref, freq_ref, gains_ref, wq_ref, wkv_ref, wo_ref,
    wgu_ref, wd_ref,
    wa_out, n1_out, raw_out, p_out, qrot_out, kdup_out, vdup_out, att_out, hidden_out, n2_out,
    dyf_out, act_out, dg_out, du_out, cos_out, sin_out, gnm_out, gno_out, om_out, oo_out,
    wa, wf, xf, dyf, n1, n2, raw, prob, qrot, kdup, vdup, att, hidden, act, dg, du, cos, sin,
    segc, gn, op, part_out, part_in, gno, oo, om, gain_rows,
    send, recv, ysem, outsem,
):
    at = Spot(dp)
    wide = dp * rows
    tokens = 2 * half
    q_wide, kv_wide, ff_wide = wq_ref.shape[1], wkv_ref.shape[2], wd_ref.shape[1]
    chunk = ff_wide // CHUNKS
    o_at, g_at = q_wide + 2 * kv_wide, 2 * q_wide + 2 * kv_wide
    groups = q_wide // LANES
    mine, theirs = at.t * half, (1 - at.t) * half
    own_rows = ds(at.own * rows, rows)
    outs = []

    def put(src, dst):
        copy = pltpu.make_async_copy(src, dst, outsem.at[len(outs)])
        copy.start()
        outs.append(copy)

    at.greet()
    gather = Gather(
        at,
        rows,
        [lambda r: wa.at[r]] + [lambda r, j=j: wf.at[j, r] for j in range(CHUNKS)],
        send,
        recv,
    )
    wa[own_rows, 0:q_wide] = wq_ref[...]
    wa[own_rows, q_wide : q_wide + kv_wide] = wkv_ref[0]
    wa[own_rows, q_wide + kv_wide : o_at] = wkv_ref[1]
    wa[own_rows, o_at:g_at] = wo_ref[...]
    wa[own_rows, g_at:] = gains_ref[...]
    gather.main(0, 0)
    x_copy = partner(at, x_ref, xf.at[ds(mine, half)], ysem.at[0])
    x_copy.start()
    for j in range(CHUNKS):
        cols = slice(j * chunk, (j + 1) * chunk)
        wf[j, own_rows, 0:chunk] = wgu_ref[0, :, cols]
        wf[j, own_rows, chunk : 2 * chunk] = wgu_ref[1, :, cols]
        wf[j, own_rows, 2 * chunk :] = wd_ref[:, cols]
    gather.main(1, 0)
    dy_copy = partner(at, dy_ref, dyf.at[ds(mine, half)], ysem.at[1])
    dy_copy.start()
    xf[ds(mine, half)] = x_ref[...]
    dyf[ds(mine, half)] = dy_ref[...]

    segc[...] = jnp.broadcast_to(seg_ref[...].astype(F32), (LANES, tokens)).T
    cos[...] = jnp.broadcast_to(pos_ref[...].astype(F32), (LANES, tokens)).T

    @pl.loop(0, tokens // 64)
    def _(i):
        r = ds(i * 64, 64)
        angles = cos[r] * freq_ref[...]
        cos[r] = jnp.cos(angles)
        sin[r] = jnp.sin(angles)

    gather.main(0, 1)
    gather.side(0, 0)
    gather.main(0, 2)
    gather.side(0, 1)
    gather.main(0, 3)
    gather.side(0, 2)
    gather.side(0, 3)
    gather.final(0)
    put(wa, wa_out)
    gather.main(2, 0)
    gather.main(3, 0)
    put(cos, cos_out)
    put(sin, sin_out)

    gain_rows[...] = wa[:, g_at : g_at + LANES].astype(F32).T[:8]
    qk_gain = jnp.sum(wa[:, g_at + LANES :].astype(F32), axis=0, keepdims=True)
    lows = low_half((1, LANES))
    gain_q = jnp.where(lows, qk_gain, pltpu.roll(qk_gain, HD, 1))
    gain_k = jnp.where(lows, pltpu.roll(qk_gain, HD, 1), qk_gain)
    gain_attn, gain_ffn = gain_rows[0:1, :], gain_rows[1:2, :]
    x_copy.wait_recv()

    @pl.loop(0, tokens // 64)
    def _(i):
        r = ds(i * 64, 64)
        values = xf[r].astype(F32)
        n1[r] = rms_forward(values, gain_attn)[0].astype(BF16)

    put(n1, n1_out)
    gather.main(1, 1)
    gather.side(1, 0)

    @pl.loop(0, o_at // 256)
    def _(n):
        tile = dot_nn(n1[...], wa[:, ds(n * 256, 256)])
        raw[2 * n] = tile[:, :LANES]
        raw[2 * n + 1] = tile[:, LANES:]

    put(raw, raw_out)
    blk = 128

    def rope(n, gain, r):
        values = raw[n, r]
        normed = values * lax.rsqrt(head_mean(values * values) + EPSILON) * gain
        early = first_quarter(normed.shape)
        turned = jnp.where(early, -pltpu.roll(normed, LANES - HD // 2, 1), pltpu.roll(normed, HD // 2, 1))
        return normed * cos[r] + turned * sin[r]

    def doubled(tile):
        swapped = pltpu.roll(tile, HD, 1)
        lows = low_half(tile.shape)
        return jnp.where(lows, tile, swapped).astype(BF16), jnp.where(lows, swapped, tile).astype(BF16)

    @pl.loop(0, tokens // blk)
    def _(i):
        r = ds(i * blk, blk)
        for n in range(groups):
            qrot[n, r] = rope(n, gain_q, r).astype(BF16)
        for n in range(groups // 2):
            kdup[2 * n, r], kdup[2 * n + 1, r] = doubled(rope(groups + n, gain_k, r))
            vdup[2 * n, r], vdup[2 * n + 1, r] = doubled(raw[groups + groups // 2 + n, r])

    put(qrot, qrot_out)
    put(kdup, kdup_out)
    put(vdup, vdup_out)
    gather.main(1, 2)
    gather.side(1, 1)
    gather.main(2, 1)
    gather.side(2, 0)

    def attend(base):
        @pl.loop(0, groups * (half // blk))
        def _(step):
            g = step // (half // blk)
            start = base + lax.rem(step, half // blk) * blk
            r = ds(start, blk)
            q = qrot[g, r]
            lows = low_half(q.shape)
            index = lax.broadcasted_iota(jnp.int32, (blk, tokens), 0) + start
            allowed = (segc[r, 0:1] == seg_ref[...].astype(F32)) & (lane_of((blk, tokens)) <= index)
            result = []
            for hh in range(2):
                picked = jnp.where(lows if hh == 0 else jnp.logical_not(lows), q, jnp.zeros_like(q))
                scores = dot_nt(picked, kdup[g]) * (1.0 / math.sqrt(HD))
                scores = jnp.where(allowed, scores, NEG_FILL)
                e = jnp.exp(scores - jnp.max(scores, axis=1, keepdims=True))
                p = (e / jnp.sum(e, axis=1, keepdims=True)).astype(BF16)
                prob[g, ds(hh * tokens + start, blk)] = p
                result.append(dot_nn(p, vdup[g]))
            att[r, ds(g * LANES, LANES)] = jnp.where(lows, result[0], result[1]).astype(BF16)

    attend(theirs)

    @pl.loop(0, wide // 256)
    def _(n):
        cols = ds(n * 256, 256)
        part_out[:, cols] = dot_nt(att[ds(theirs, half)], wa[cols, o_at:g_at]).astype(BF16)

    out_copy = partner(at, part_out, part_in, ysem.at[2])
    out_copy.start()
    gather.main(1, 3)
    gather.side(1, 2)
    gather.side(1, 3)
    gather.main(3, 1)
    gather.side(3, 0)
    attend(mine)
    put(prob, p_out)
    put(att, att_out)
    gather.main(2, 2)
    gather.side(2, 1)

    @pl.loop(0, wide // 256)
    def _(n):
        cols = ds(n * 256, 256)
        hidden[:, cols] = x_ref[:, cols].astype(F32) + dot_nt(att[ds(mine, half)], wa[cols, o_at:g_at])

    out_copy.wait_recv()

    @pl.loop(0, half // 64)
    def _(i):
        r = ds(i * 64, 64)
        values = hidden[r] + part_in[r].astype(F32)
        hidden[r] = values
        n2[ds(mine + i * 64, 64)] = rms_forward(values, gain_ffn)[0].astype(BF16)

    put(hidden, hidden_out)
    n2_copy = partner(at, n2.at[ds(mine, half)], n2.at[ds(mine, half)], ysem.at[3])
    n2_copy.start()
    gather.main(2, 3)
    gather.side(2, 2)
    gather.side(2, 3)
    gather.main(3, 2)
    gather.side(3, 1)
    dy_copy.wait_recv()
    put(dyf, dyf_out)
    n2_copy.wait_recv()
    put(n2, n2_out)

    for j in range(CHUNKS):
        gather.final(j + 1)

        @pl.loop(0, chunk // 256)
        def _(n, j=j):
            for m in range(2):
                r = slice(m * half, (m + 1) * half)
                gate = dot_nn(n2[r], wf[j, :, ds(n * 256, 256)])
                up = dot_nn(n2[r], wf[j, :, ds(chunk + n * 256, 256)])
                gact = dot_nn(dyf[r], wf[j, :, ds(2 * chunk + n * 256, 256)])
                sig = jax.nn.sigmoid(gate)
                silu = gate * sig
                cols = ds(j * chunk + n * 256, 256)
                act[r, cols] = (silu * up).astype(BF16)
                dg[r, cols] = (gact * up * sig * (1.0 + gate * (1.0 - sig))).astype(BF16)
                du[r, cols] = (gact * silu).astype(BF16)

        cols = slice(j * chunk, (j + 1) * chunk)
        if j == 0:
            gather.main(3, 3)
            gather.side(3, 2)
            gather.side(3, 3)

        @pl.loop(0, wide // 256)
        def _(n, j=j, cols=cols):
            r = ds(n * 256, 256)
            down = dot_nt(act[:, cols], wf[j, r, 2 * chunk :])
            back = dot_nt(dg[:, cols], wf[j, r, :chunk]) + dot_nt(du[:, cols], wf[j, r, chunk : 2 * chunk])
            if j == 0:
                op[:, r] = down
                gn[:, r] = back
            else:
                op[:, r] += down
                gn[:, r] += back

    put(act, act_out)
    put(dg, dg_out)
    put(du, du_out)
    put(gn.at[ds(mine, half)], gnm_out)

    @pl.loop(0, half // 64)
    def _(i):
        r = ds(i * 64, 64)
        gno[r] = gn[ds(theirs + i * 64, 64)].astype(BF16)
        oo[r] = op[ds(theirs + i * 64, 64)].astype(BF16)
        om[r] = op[ds(mine + i * 64, 64)] + hidden[r]

    put(gno, gno_out)
    put(oo, oo_out)
    put(om, om_out)
    for copy in (x_copy, dy_copy, out_copy, n2_copy):
        copy.wait_send()
    for k in range(CHUNKS + 1):
        gather.finish(k)
    for copy in outs:
        copy.wait()


def forward(dp, x, dy, seg, pos, freq, gains, wq, wkv, wo_t, wgu, wd_t):
    rows, half = wq.shape[0], x.shape[0]
    tokens, wide = 2 * half, dp * rows
    q_wide, kv_wide, ff_wide = wq.shape[1], wkv.shape[2], wd_t.shape[1]
    groups = q_wide // LANES
    attn_wide = 2 * q_wide + 2 * kv_wide + 2 * LANES
    shapes = [
        ((wide, attn_wide), BF16),
        ((tokens, wide), BF16),
        ((2 * groups, tokens, LANES), F32),
        ((groups, 2 * tokens, tokens), BF16),
        ((groups, tokens, LANES), BF16),
        ((groups, tokens, LANES), BF16),
        ((groups, tokens, LANES), BF16),
        ((tokens, q_wide), BF16),
        ((half, wide), F32),
        ((tokens, wide), BF16),
        ((tokens, wide), BF16),
        ((tokens, ff_wide), BF16),
        ((tokens, ff_wide), BF16),
        ((tokens, ff_wide), BF16),
        ((tokens, LANES), F32),
        ((tokens, LANES), F32),
        ((half, wide), F32),
        ((half, wide), BF16),
        ((half, wide), F32),
        ((half, wide), BF16),
    ]
    (wa, n1, raw, p, qrot, kdup, vdup, att, hidden, n2, dyf, act, dg, du, cos, sin, gnm, gno, om, oo) = shapes
    vmem = [
        wa, ((CHUNKS, wide, 3 * ff_wide // CHUNKS), BF16), n2, dyf, n1, n2, raw, p, qrot, kdup, vdup, att,
        hidden, act, dg, du, cos, sin, cos, ((tokens, wide), F32), ((tokens, wide), F32), oo, oo, gno, oo, om,
        ((8, wide), F32),
    ]
    return pl.pallas_call(
        functools.partial(fwd_kernel, dp, rows, half),
        out_shape=[jax.ShapeDtypeStruct(*s) for s in shapes],
        in_specs=[pl.BlockSpec(memory_space=pltpu.VMEM)] * 11,
        out_specs=[pl.BlockSpec(memory_space=pl.ANY)] * len(shapes),
        scratch_shapes=[pltpu.VMEM(*s) for s in vmem]
        + [
            pltpu.SemaphoreType.DMA((CHUNKS + 1, dp // 2, 4)),
            pltpu.SemaphoreType.DMA((CHUNKS + 1, dp)),
            pltpu.SemaphoreType.DMA((4, 2)),
            pltpu.SemaphoreType.DMA((len(shapes),)),
        ],
        compiler_params=pltpu.CompilerParams(
            collective_id=3, has_side_effects=True, vmem_limit_bytes=62 * 1024 * 1024
        ),
        name="forward",
    )(x, dy, seg, pos, freq, gains, wq, wkv, wo_t, wgu, wd_t)


class Scatter:
    def __init__(self, at, rows, slabs, first, second, chained, emit, sems):
        self.at, self.rows, self.slabs, self.emit = at, rows, slabs, emit
        self.first, self.second, self.chained = first, second, chained
        self.sent1, self.sent2, self.sent4, self.got1, self.got2, self.got_up, self.got_down = sems

    def slab(self, k, o):
        return self.slabs[k](ds(o * self.rows, self.rows))

    def swap(self, k, t, ox):
        at, q = self.at, t * 2 + ox
        src = self.slab(k, at.device(t, ox, 1 - at.c))
        return remote(src, self.first[k].at[q], self.sent1.at[k, q], self.got1.at[k, q], at.sibling)

    def cross(self, k, t):
        at = self.at
        q = t * 2 + 1 - at.x
        return remote(
            self.first[k].at[q], self.second[k].at[t], self.sent2.at[k, t], self.got2.at[k, t], at.beside
        )

    def rise(self, k, t):
        slot = self.chained[k].at[t]
        return remote(self.second[k].at[t], slot, self.sent4.at[k, t], self.got_up.at[k, t], self.at.above)

    def fall(self, k, t, distance):
        slot = self.chained[k].at[self.at.length if distance == 1 else t]
        return remote(self.second[k].at[t], slot, self.sent4.at[k, t], self.got_down.at[k, t], self.at.below)

    def targets(self, act, distances=None):
        at = self.at
        for d in range(at.length - 1, -1, -1) if distances is None else distances:
            for sign in (1, -1) if d else (0,):
                t = at.z + d * sign
                if d:
                    pl.when((t >= 0) & (t < at.length))(lambda t=t, sign=sign, d=d: act(t, sign, d))
                else:
                    act(t, 0, 0)

    def each(self, act):
        @pl.loop(0, self.rows // 16)
        def _(i):
            act(ds(i * 16, 16))

    def start(self, k):
        def act(t, sign, d):
            for ox in (1 - self.at.x, self.at.x):
                self.swap(k, t, ox).start()

        self.targets(act)

    def chip(self, k):
        at, first = self.at, self.first[k]

        def act(t, sign, d):
            for ox in (1 - at.x, at.x):
                q = t * 2 + ox
                self.swap(k, t, ox).wait_recv()
                base = at.device(t, ox, at.c) * self.rows

                @pl.loop(0, self.rows // 16)
                def _(i, q=q, base=base):
                    r = ds(i * 16, 16)
                    first[q, r] = first[q, r] + self.slabs[k](ds(base + i * 16, 16))[...]

                if ox is not at.x:
                    self.cross(k, t).start()

        self.targets(act)

    def chain(self, k, d):
        at, first, second, chained = self.at, self.first[k], self.second[k], self.chained[k]

        def arrive(t, up, last):
            slot = chained.at[at.length if last and not up else t]
            got = self.got_up if up else self.got_down
            remote(second.at[t], slot, self.sent4.at[k, t], got.at[k, t], at.above).wait_recv()

        def act(t, sign, d):
            q = t * 2 + at.x
            self.cross(k, t).wait_recv()
            if sign == 0:
                pl.when(at.z > 0)(lambda: arrive(t, True, True))
                pl.when(at.z < at.length - 1)(lambda: arrive(t, False, True))

                def sums(up, down):
                    def row(r):
                        value = second[t, r].astype(F32) + first[q, r].astype(F32)
                        if up:
                            value += chained[t, r].astype(F32)
                        if down:
                            value += chained[at.length, r].astype(F32)
                        self.emit(k, r, value)

                    self.each(row)

                inner = (at.z > 0) & (at.z < at.length - 1)
                pl.when(inner)(lambda: sums(True, True))
                pl.when(at.z == 0)(lambda: sums(False, True))
                pl.when(at.z == at.length - 1)(lambda: sums(True, False))
                return
            up = sign > 0
            inner = at.z > 0 if up else at.z < at.length - 1

            def middle():
                arrive(t, up, False)

                def row(r):
                    value = second[t, r].astype(F32) + first[q, r].astype(F32) + chained[t, r].astype(F32)
                    second[t, r] = value.astype(BF16)

                self.each(row)

            def edge():
                def row(r):
                    second[t, r] = second[t, r] + first[q, r]

                self.each(row)

            pl.when(inner)(middle)
            pl.when(jnp.logical_not(inner))(edge)
            (self.rise(k, t) if up else self.fall(k, t, d)).start()

        self.targets(act, (d,))

    def swapped(self, k):
        def act(t, sign, d):
            for ox in range(2):
                self.swap(k, t, ox).wait_send()

        self.targets(act)

    def finish(self, k):
        def act(t, sign, d):
            self.cross(k, t).wait_send()
            if sign:
                (self.rise(k, t) if sign > 0 else self.fall(k, t, d)).wait_send()

        self.targets(act)


def bwd_kernel(
    dp, rows, half, x_ref, dy_ref,
    wa_in, n1_in, raw_in, p_in, qrot_in, kdup_in, vdup_in, att_in, hidden_in, n2_in,
    dyf_in, act_in, dg_in, du_in, cos_in, sin_in, gnm_in, gno_in, om_in, oo_in,
    bo_out, gi_out, gain_out, gq_out, gkv_out, go_out, ggu_out, gdn_out,
    parts, pa, stage, turned, turned2, tiles, prob, raw, qrot, kdup, vdup, att, weights, gains, cos, sin,
    hidden, gh, grecv, orecv, grows, n1recv, n1send, ga, qs, dos, dq, dk, dv, dqkv, terms, terms_in,
    *rest,
):
    count = CHUNKS + 3
    first, second, chained = rest[:count], rest[count : 2 * count], rest[2 * count : 3 * count]
    sems = rest[3 * count : 3 * count + 7]
    ysem, loads, tilesem = rest[3 * count + 7 :]
    at = Spot(dp)
    wide, tokens = dp * rows, 2 * half
    q_wide, kv_wide, ff_wide = gq_out.shape[1], gkv_out.shape[2], gdn_out.shape[1]
    chunk = ff_wide // CHUNKS
    o_at, g_at = q_wide + 2 * kv_wide, 2 * q_wide + 2 * kv_wide
    groups = q_wide // LANES
    mine, theirs = at.t * half, (1 - at.t) * half
    used = []

    def load(src, dst):
        copy = pltpu.make_async_copy(src, dst, loads.at[len(used)])
        copy.start()
        used.append(copy)
        return copy

    def emit(k, r, value):
        if k < CHUNKS:
            cols = slice(k * chunk, (k + 1) * chunk)
            ggu_out[0, r, cols] = value[:, :chunk]
            ggu_out[1, r, cols] = value[:, chunk : 2 * chunk]
            gdn_out[r, cols] = value[:, 2 * chunk :]
        elif k == CHUNKS:
            go_out[r] = value
        elif k == CHUNKS + 1:
            gq_out[r] = value[:, :q_wide]
            gkv_out[0, r] = value[:, q_wide : q_wide + kv_wide]
            gkv_out[1, r] = value[:, q_wide + kv_wide :]
        else:
            gain_out[r] = value

    slabs = [lambda r, j=j: parts.at[j % 2, r] for j in range(CHUNKS)]
    slabs += [lambda r: pa.at[r, o_at:g_at], lambda r: pa.at[r, 0:o_at], lambda r: pa.at[r, g_at:]]
    scatter = Scatter(at, rows, slabs, first, second, chained, emit, sems)

    at.greet()
    g_copy = partner(at, gno_in, grecv, ysem.at[0])
    g_copy.start()
    o_copy = partner(at, oo_in, orecv, ysem.at[1])
    o_copy.start()
    dy_load = load(dyf_in, stage.at[0])
    n2_load = load(n2_in, stage.at[1])

    def tile_copies(i, slot):
        cols = ds(i * 256, 256)
        return [
            pltpu.make_async_copy(src.at[:, cols], tiles.at[slot, n], tilesem.at[slot, n])
            for n, src in enumerate((act_in, dg_in, du_in))
        ]

    for copy in tile_copies(0, 0):
        copy.start()
    wo_load = load(wa_in.at[:, o_at:g_at], weights.at[:, : g_at - o_at])
    gain_load = load(wa_in.at[:, g_at:], gains)
    hidden_load = load(hidden_in, hidden)
    gnm_load = load(gnm_in, gh)
    cos_load, sin_load = load(cos_in, cos), load(sin_in, sin)
    att_load, raw_load = load(att_in, att), load(raw_in.at[0 : groups + groups // 2], raw)
    q_load, k_load, v_load = load(qrot_in, qrot), load(kdup_in, kdup), load(vdup_in, vdup)
    om_load = load(om_in, gi_out)
    p_loads = [load(p_in.at[0], prob.at[0])]

    def transpose(src, dst):
        @pl.loop(0, wide // 128)
        def _(i):
            c = ds(i * 128, 128)
            dst[c] = src[:, c].T

    dy_load.wait()
    transpose(stage.at[0], turned)
    n2_load.wait()
    transpose(stage.at[1], turned2)
    n1_load = load(n1_in, stage.at[0])

    last = ff_wide // 256 - 1

    def weight_grads(j):
        for n in range(chunk // 256):
            i = j * (chunk // 256) + n
            slot = i % 2
            if i < last:
                for copy in tile_copies(i + 1, 1 - slot):
                    copy.start()
            for copy in tile_copies(i, slot):
                copy.wait()

            @pl.loop(0, wide // 256)
            def _(m, n=n, slot=slot):
                r = ds(m * 256, 256)
                for part, left, which in ((0, turned2, 1), (1, turned2, 2), (2, turned, 0)):
                    cols = slice(part * chunk + n * 256, part * chunk + (n + 1) * 256)
                    parts[j % 2, r, cols] = dot_nn(left[r], tiles[slot, which]).astype(BF16)

        scatter.start(j)

    weight_grads(0)
    weight_grads(1)
    scatter.chip(0)

    gain_load.wait()
    gain_rows = gains[:, :LANES].astype(F32).T[:8]
    qk_gain = jnp.sum(gains[:, LANES:].astype(F32), axis=0, keepdims=True)
    lows1 = low_half((1, LANES))
    gain_q = jnp.where(lows1, qk_gain, pltpu.roll(qk_gain, HD, 1))
    gain_k = jnp.where(lows1, pltpu.roll(qk_gain, HD, 1), qk_gain)
    gain_attn, gain_ffn = gain_rows[0:1, :], gain_rows[1:2, :]
    hidden_load.wait()
    gnm_load.wait()
    g_copy.wait_recv()
    terms[...] = jnp.zeros_like(terms)

    @pl.loop(0, half // 32)
    def _(i):
        r = ds(i * 32, 32)
        grad = gh[r] + grecv[r].astype(F32)
        values = hidden[r]
        scale = lax.rsqrt(jnp.mean(values * values, axis=-1, keepdims=True) + EPSILON)
        terms[1:2, :wide] += jnp.sum(grad * values * scale, axis=0, keepdims=True)
        result = dy_ref[r].astype(F32) + rms_backward(values, scale, gain_ffn, grad)
        gh[r] = result
        grows[ds(mine + i * 32, 32)] = result.astype(BF16)

    r_copy = partner(at, grows.at[ds(mine, half)], grows.at[ds(mine, half)], ysem.at[2])
    r_copy.start()
    scatter.chain(0, 3)
    scatter.swapped(0)
    weight_grads(2)
    scatter.chip(1)
    scatter.chain(0, 2)
    scatter.chain(1, 3)

    om_load.wait()
    o_copy.wait_recv()

    @pl.loop(0, half // 64)
    def _(i):
        r = ds(i * 64, 64)
        bo_out[r] = (gi_out[r] + orecv[r].astype(F32)).astype(BF16)

    scatter.chain(0, 1)
    wo_load.wait()
    r_copy.wait_recv()

    @pl.loop(0, q_wide // 256)
    def _(n):
        tile = dot_nn(grows[...], weights[:, ds(n * 256, 256)]).astype(BF16)
        ga[2 * n] = tile[:, :LANES]
        ga[2 * n + 1] = tile[:, LANES:]

    weight_load = load(wa_in.at[:, :o_at], weights)
    transpose(grows, turned)
    att_load.wait()

    @pl.loop(0, wide // 256)
    def _(m):
        r = ds(m * 256, 256)
        pa[r, o_at:g_at] = dot_nn(turned[r], att[...]).astype(BF16)

    scatter.start(3)
    scatter.chip(2)
    scatter.chain(1, 2)
    scatter.chain(0, 0)
    scatter.chain(2, 3)
    q_load.wait()
    k_load.wait()
    v_load.wait()
    blk = 128
    polls = [
        [(scatter.chain, 1, 1), (scatter.chain, 2, 2)],
        [(scatter.chip, 3), (scatter.chain, 1, 0), (scatter.chain, 2, 1)],
        [(scatter.chain, 3, 3), (scatter.chain, 2, 0)],
        [(scatter.chain, 3, 2)],
    ]
    for g in range(groups):
        if g + 1 < groups:
            p_loads.append(load(p_in.at[g + 1], prob.at[(g + 1) % 2]))
        p_loads[g].wait()
        pg = prob.at[g % 2]

        @pl.loop(0, tokens // blk)
        def _(i, g=g):
            r, r2 = ds(i * blk, blk), ds(tokens + i * blk, blk)
            lows = low_half((blk, LANES))
            q, do = qrot[g, r], ga[g, r]
            zero = jnp.zeros_like(q)
            qs[r], qs[r2] = jnp.where(lows, q, zero), jnp.where(lows, zero, q)
            dos[r], dos[r2] = jnp.where(lows, do, zero), jnp.where(lows, zero, do)

        dv[g] = dot_tn(pg[...], dos[...])

        @pl.loop(0, tokens // blk)
        def _(i, g=g, pg=pg):
            lows = low_half((blk, LANES))
            result = []
            for hh in range(2):
                r = ds(hh * tokens + i * blk, blk)
                p = pg[r].astype(F32)
                grad_p = dot_nt(dos[r], vdup[g])
                delta = jnp.sum(p * grad_p, axis=1, keepdims=True)
                scores = (p * (grad_p - delta) * (1.0 / math.sqrt(HD))).astype(BF16)
                pg[r] = scores
                result.append(dot_nn(scores, kdup[g]))
            dq[g, ds(i * blk, blk)] = jnp.where(lows, result[0], result[1])

        dk[g] = dot_tn(pg[...], qs[...])
        for poll in polls[g]:
            poll[0](*poll[1:])

    cos_load.wait()
    sin_load.wait()
    raw_load.wait()

    def fold(value):
        return value + pltpu.roll(value, HD, 1)

    def turn_back(values, grad_rot, gain, r):
        u = grad_rot * sin[r]
        early = first_quarter(u.shape)
        grad = grad_rot * cos[r] + jnp.where(
            early, pltpu.roll(u, LANES - HD // 2, 1), -pltpu.roll(u, HD // 2, 1)
        )
        scale = lax.rsqrt(head_mean(values * values) + EPSILON)
        weighted = grad * gain
        inner = head_mean(weighted * values)
        term = jnp.sum(grad * values * scale, axis=0, keepdims=True)
        return scale * (weighted - values * scale * scale * inner), fold(term)

    @pl.loop(0, tokens // blk)
    def _(i):
        r = ds(i * blk, blk)
        lows = low_half((blk, LANES))
        q_term = k_term = jnp.zeros((1, LANES), F32)
        for n in range(groups):
            grad, term = turn_back(raw[n, r], dq[n, r], gain_q, r)
            dqkv[r, n * LANES : (n + 1) * LANES] = grad.astype(BF16)
            q_term += term
        for n in range(groups // 2):
            pair = jnp.where(lows, fold(dk[2 * n, r]), fold(dk[2 * n + 1, r]))
            grad, term = turn_back(raw[groups + n, r], pair, gain_k, r)
            dqkv[r, q_wide + n * LANES : q_wide + (n + 1) * LANES] = grad.astype(BF16)
            k_term += term
            pair = jnp.where(lows, fold(dv[2 * n, r]), fold(dv[2 * n + 1, r]))
            dqkv[r, q_wide + kv_wide + n * LANES : q_wide + kv_wide + (n + 1) * LANES] = pair.astype(BF16)
        terms[0:1, wide:] += jnp.where(low_half((1, LANES)), q_term, k_term)

    weight_load.wait()

    @pl.loop(0, wide // 256)
    def _(n):
        r = ds(n * 256, 256)
        n1send[:, r] = dot_nt(dqkv[ds(theirs, half)], weights[r]).astype(BF16)

    n_copy = partner(at, n1send, n1recv, ysem.at[3])
    n_copy.start()
    n1_load.wait()
    transpose(stage.at[0], turned2)

    @pl.loop(0, wide // 256)
    def _(m):
        r = ds(m * 256, 256)
        for n in range(o_at // 256):
            cols = slice(n * 256, (n + 1) * 256)
            pa[r, cols] = dot_nn(turned2[r], dqkv[:, cols]).astype(BF16)

    scatter.start(4)
    scatter.chain(3, 1)

    @pl.loop(0, wide // 256)
    def _(n):
        r = ds(n * 256, 256)
        gi_out[:, r] = dot_nt(dqkv[ds(mine, half)], weights[r])

    scatter.chip(4)
    scatter.chain(3, 0)
    n_copy.wait_recv()

    @pl.loop(0, half // 32)
    def _(i):
        r = ds(i * 32, 32)
        grad = gi_out[r] + n1recv[r].astype(F32)
        values = x_ref[r].astype(F32)
        scale = lax.rsqrt(jnp.mean(values * values, axis=-1, keepdims=True) + EPSILON)
        terms[0:1, :wide] += jnp.sum(grad * values * scale, axis=0, keepdims=True)
        gi_out[r] = gh[r] + rms_backward(values, scale, gain_attn, grad)

    t_copy = partner(at, terms, terms_in, ysem.at[4])
    t_copy.start()
    scatter.chain(4, 3)
    t_copy.wait_recv()

    both = terms[...] + terms_in[...]
    padded = jnp.concatenate([both[:, :wide], jnp.zeros((LANES - 8, wide), F32)], axis=0)
    pa[:, g_at : g_at + LANES] = padded.T.astype(BF16)
    head = lax.rem(lax.broadcasted_iota(jnp.int32, (wide, LANES), 0), rows) == 0
    pa[:, g_at + LANES :] = jnp.where(head, both[0:1, wide:], 0.0).astype(BF16)
    scatter.start(5)
    scatter.chain(4, 2)
    scatter.chip(5)
    scatter.chain(5, 3)
    scatter.chain(4, 1)
    scatter.chain(5, 2)
    scatter.chain(4, 0)
    scatter.chain(5, 1)
    scatter.chain(5, 0)
    for copy in (g_copy, o_copy, r_copy, n_copy, t_copy):
        copy.wait_send()
    for k in range(count):
        if k:
            scatter.swapped(k)
        scatter.finish(k)


def backward(dp, x, dy, saved, q_wide, kv_wide, ff_wide):
    half, wide = x.shape
    rows, tokens = wide // dp, 2 * half
    groups = q_wide // LANES
    length = layout_of(dp)[0]
    chunk = ff_wide // CHUNKS
    widths = [3 * chunk] * CHUNKS + [q_wide, q_wide + 2 * kv_wide, 2 * LANES]
    shapes = [
        ((half, wide), BF16),
        ((half, wide), F32),
        ((rows, 2 * LANES), F32),
        ((rows, q_wide), F32),
        ((2, rows, kv_wide), F32),
        ((rows, q_wide), F32),
        ((2, rows, ff_wide), F32),
        ((rows, ff_wide), F32),
    ]
    vmem = [
        ((2, wide, 3 * chunk), BF16),
        ((wide, sum(widths[CHUNKS:])), BF16),
        ((2, tokens, wide), BF16),
        ((wide, tokens), BF16),
        ((wide, tokens), BF16),
        ((2, 3, tokens, 256), BF16),
        ((2, 2 * tokens, tokens), BF16),
        ((groups + groups // 2, tokens, LANES), F32),
        ((groups, tokens, LANES), BF16),
        ((groups, tokens, LANES), BF16),
        ((groups, tokens, LANES), BF16),
        ((tokens, q_wide), BF16),
        ((wide, q_wide + 2 * kv_wide), BF16),
        ((wide, 2 * LANES), BF16),
        ((tokens, LANES), F32),
        ((tokens, LANES), F32),
        ((half, wide), F32),
        ((half, wide), F32),
        ((half, wide), BF16),
        ((half, wide), BF16),
        ((tokens, wide), BF16),
        ((half, wide), BF16),
        ((half, wide), BF16),
        ((groups, tokens, LANES), BF16),
        ((2 * tokens, LANES), BF16),
        ((2 * tokens, LANES), BF16),
        ((groups, tokens, LANES), F32),
        ((groups, tokens, LANES), F32),
        ((groups, tokens, LANES), F32),
        ((tokens, q_wide + 2 * kv_wide), BF16),
        ((8, wide + LANES), F32),
        ((8, wide + LANES), F32),
    ]
    for slots in (dp // 2, length, length + 1):
        vmem += [((slots, rows, w), BF16) for w in widths]
    count = len(widths)
    return pl.pallas_call(
        functools.partial(bwd_kernel, dp, rows, half),
        out_shape=[jax.ShapeDtypeStruct(*s) for s in shapes],
        in_specs=[pl.BlockSpec(memory_space=pltpu.VMEM)] * 2
        + [pl.BlockSpec(memory_space=pl.ANY)] * len(saved),
        out_specs=[pl.BlockSpec(memory_space=pltpu.VMEM)] * len(shapes),
        scratch_shapes=[pltpu.VMEM(*s) for s in vmem]
        + [
            pltpu.SemaphoreType.DMA((count, n))
            for n in (dp // 2, length, length, dp // 2, length, length, length)
        ]
        + [
            pltpu.SemaphoreType.DMA((5, 2)),
            pltpu.SemaphoreType.DMA((24,)),
            pltpu.SemaphoreType.DMA((2, 3)),
        ],
        compiler_params=pltpu.CompilerParams(
            collective_id=4, has_side_effects=True, vmem_limit_bytes=63 * 1024 * 1024
        ),
        name="backward",
    )(x, dy, *saved)


def pack_gains(norm_gains, qk_gains, shard):
    o = lax.axis_index("dp")
    qk_shard = qk_gains.shape[1]
    cols = jnp.pad(norm_gains.T, ((0, 0), (0, LANES - 2)))
    row = jnp.zeros((1, LANES), BF16)
    for i in range(2):
        row = lax.dynamic_update_slice(row, qk_gains[i : i + 1], (0, i * HD + o * qk_shard))
    return jnp.concatenate([cols, jnp.pad(row, ((0, shard - 1), (0, 0)))], axis=1)


def fast_device(
    block_input, cotangent, segment_ids, positions, norm_gains, qk_gains, w_query, w_keyval, w_output,
    w_gate_up, w_down,
):
    dp = lax.axis_size("dp")
    shard, q_wide = w_query.shape
    kv_wide, ff_wide = w_keyval.shape[2], w_gate_up.shape[2]
    qk_shard = qk_gains.shape[1]
    freqs = ROPE_BASE ** (-jnp.arange(0, HD, 2).astype(F32) / HD)
    freq = jnp.tile(freqs, 4)[None]
    saved = forward(
        dp, block_input, cotangent, segment_ids, positions, freq, pack_gains(norm_gains, qk_gains, shard),
        w_query, w_keyval, w_output.T, w_gate_up, w_down.T,
    )
    block_output, grad_input, gains, grad_query, grad_keyval, grad_out, grad_gate_up, grad_down = backward(
        dp, block_input, cotangent, saved, q_wide, kv_wide, ff_wide
    )
    o = lax.axis_index("dp")
    qk = [lax.dynamic_slice(gains, (0, LANES + i * HD + o * qk_shard), (1, qk_shard)) for i in range(2)]
    return (
        block_output,
        grad_input,
        gains[:, 0:2].T,
        jnp.concatenate(qk),
        grad_query,
        grad_keyval,
        grad_out.T,
        grad_gate_up,
        grad_down.T,
    )


def solution(mesh):
    return jax.shard_map(
        fast_device if mesh.shape["tensor"] == 2 and mesh.shape["dp"] == 16 else on_device,
        mesh=mesh,
        in_specs=(
            P(("dp", "tensor"), None),
            P(("dp", "tensor"), None),
            P("dp", None),
            P("dp", None),
            P(None, "dp"),
            P(None, "dp"),
            P("dp", "tensor"),
            P(None, "dp", "tensor"),
            P("tensor", "dp"),
            P(None, "dp", "tensor"),
            P("tensor", "dp"),
        ),
        out_specs=(
            P(("dp", "tensor"), None),
            P(("dp", "tensor"), None),
            P(None, "dp"),
            P(None, "dp"),
            P("dp", "tensor"),
            P(None, "dp", "tensor"),
            P("tensor", "dp"),
            P(None, "dp", "tensor"),
            P("tensor", "dp"),
        ),
        check_vma=False,
    )
```

```python
import functools
import math

import jax
import jax.numpy as jnp
from jax import lax
from jax.experimental import pallas as pl
from jax.experimental.pallas import tpu as pltpu
from jax.sharding import PartitionSpec as P

HD = 64


EPSILON = 1e-05
ROPE_BASE = 1000000.0
NEG_FILL = -1e30


def rms_forward(values, gain):
    scale = lax.rsqrt(jnp.mean(values * values, axis=-1, keepdims=True) + EPSILON)
    return (values * scale * gain, scale)


def rms_backward(values, scale, gain, grad):
    weighted = grad * gain
    inner = jnp.mean(weighted * values, axis=-1, keepdims=True)
    return scale * (weighted - values * scale * scale * inner)


def rope_tables(places):
    freqs = ROPE_BASE ** (-jnp.arange(0, HD, 2).astype(jnp.float32) / HD)
    angles = places.astype(jnp.float32)[..., None] * freqs
    angles = jnp.concatenate([angles, angles], axis=-1)
    return (jnp.cos(angles), jnp.sin(angles))


def rotate_half(values):
    half = values.shape[-1] // 2
    return jnp.concatenate([-values[..., half:], values[..., :half]], axis=-1)


def rotate_back(values):
    half = values.shape[-1] // 2
    return jnp.concatenate([values[..., half:], -values[..., :half]], axis=-1)


def allowed_mask(segs):
    length = segs.shape[0]
    index = jnp.arange(length, dtype=jnp.int32)
    return (segs[:, None] == segs[None, :]) & (index[None, :] <= index[:, None])


def contract(left, right, left_dim, right_dim):
    return lax.dot_general(
        left, right, (((left_dim,), (right_dim,)), ((), ())), preferred_element_type=jnp.float32
    )


def fdot(left, right):
    return jnp.dot(left, right, preferred_element_type=jnp.float32)


def row_scores(q_rot, k_rot):
    kv_heads = k_rot.shape[1]
    groups = q_rot.shape[1] // kv_heads
    q_four = q_rot.reshape(q_rot.shape[0], kv_heads, groups, HD)
    scores = jnp.einsum("ikgd,jkd->kgij", q_four, k_rot, preferred_element_type=jnp.float32)
    return (scores / math.sqrt(HD), q_four)


def attend_row(q_rot, k_rot, values, segs):
    scores, q_four = row_scores(q_rot, k_rot)
    allowed = allowed_mask(segs)[None, None]
    masked = jnp.where(allowed, scores, NEG_FILL)
    top = jnp.max(masked, axis=-1, keepdims=True)
    expd = jnp.where(allowed, jnp.exp(masked - top), 0.0)
    total = jnp.sum(expd, axis=-1, keepdims=True)
    probs = (expd / total).astype(jnp.bfloat16)
    log_total = top[..., 0] + jnp.log(total[..., 0])
    attended = jnp.einsum("kgij,jkd->ikgd", probs, values, preferred_element_type=jnp.float32)
    return (attended.reshape(q_rot.shape).astype(jnp.bfloat16), log_total)


def back_row(q_rot, k_rot, values, grad_att, log_total, segs):
    scores, q_four = row_scores(q_rot, k_rot)
    allowed = allowed_mask(segs)[None, None]
    masked = jnp.where(allowed, scores, NEG_FILL)
    probs = jnp.where(allowed, jnp.exp(masked - log_total[..., None]), 0.0)
    probs_b = probs.astype(jnp.bfloat16)
    grad_four = grad_att.reshape(q_four.shape)
    grad_values = jnp.einsum(
        "kgij,ikgd->jkd", probs_b, grad_four, preferred_element_type=jnp.float32
    )
    grad_p = jnp.einsum("ikgd,jkd->kgij", grad_four, values, preferred_element_type=jnp.float32)
    delta = jnp.sum(probs * grad_p, axis=-1, keepdims=True)
    d_scores = (probs * (grad_p - delta) / math.sqrt(HD)).astype(jnp.bfloat16)
    grad_q = jnp.einsum(
        "kgij,jkd->ikgd", d_scores, k_rot, preferred_element_type=jnp.float32
    ).reshape(q_rot.shape)
    grad_k = jnp.einsum("kgij,ikgd->jkd", d_scores, q_four, preferred_element_type=jnp.float32)
    return (grad_q, grad_k, grad_values)


def layout_of(dp):
    if dp == 16:
        return (4, 4, 2)
    return (dp // 4, 2, dp // 2)


class Place:
    def __init__(self, dp):
        self.length, self.zs, self.xs = layout_of(dp)
        me = lax.axis_index("dp")
        self.z = lax.rem(me // self.zs, self.length)
        self.x = lax.rem(me // self.xs, 2)
        self.c = lax.rem(me, 2)

    def device(self, z, x, c):
        return z * self.zs + x * self.xs + c

    def greet(self):
        z, x, c = self.z, self.x, self.c
        barrier = pltpu.get_barrier_semaphore()

        def signal(target):
            pl.semaphore_signal(
                barrier, inc=1, device_id={"dp": target}, device_id_type=pl.DeviceIdType.MESH
            )

        signal(self.device(z, x, 1 - c))
        signal(self.device(z, 1 - x, c))
        pl.when(z > 0)(lambda: signal(self.device(z - 1, x, c)))
        pl.when(z < self.length - 1)(lambda: signal(self.device(z + 1, x, c)))
        ends = jnp.where(z > 0, 1, 0) + jnp.where(z < self.length - 1, 1, 0)
        pl.semaphore_wait(barrier, 2 + ends)


def remote(src, dst, send, recv, target):
    return pltpu.make_async_remote_copy(
        src_ref=src,
        dst_ref=dst,
        send_sem=send,
        recv_sem=recv,
        device_id={"dp": target},
        device_id_type=pl.DeviceIdType.MESH,
    )


def gather_kernel(dp, count, rows, *refs):
    ins, outs = refs[:count], refs[count : 2 * count]
    send, recv, local = refs[2 * count :]
    at = Place(dp)
    z, x, c, length = at.z, at.x, at.c, at.length
    below, above = at.device(z - 1, x, c), at.device(z + 1, x, c)
    beside, sibling = at.device(z, 1 - x, c), at.device(z, x, 1 - c)
    at.greet()
    own = at.device(z, x, c)

    def slab(k, o):
        return outs[k].at[pl.ds(pl.multiple_of(o * rows, rows), rows)]

    for k in range(count):
        pltpu.make_async_copy(ins[k], slab(k, own), local.at[k]).start()

    def move(k, oz, ox, way, target, first):
        o = at.device(oz, ox, c)
        src = ins[k] if first else slab(k, o)
        return remote(src, slab(k, o), send.at[k, oz * 2 + ox, way], recv.at[k, o], target)

    def arrived(k, o):
        remote(slab(k, o), slab(k, o), send.at[k, 0, 0], recv.at[k, o], sibling).wait_recv()

    def steps(act):
        for s in range(length):
            for sign in (1, -1) if s else (0,):
                oz = z - s * sign

                def event(oz=oz, s=s, sign=sign):
                    for k in range(count):
                        act(k, oz, s, sign)

                if s:
                    pl.when((oz >= 0) & (oz < length))(event)
                else:
                    event()
            if s:
                side(s - 1, act)
        side(length - 1, act)

    def side(s, act):
        for sign in (1, -1) if s else (0,):
            oz = z - s * sign

            def event(oz=oz):
                for k in range(count):
                    act(k, oz, None, 0)

            if s:
                pl.when((oz >= 0) & (oz < length))(event)
            else:
                event()

    def begin(k, oz, s, sign):
        if s is None:
            arrived(k, at.device(oz, 1 - x, c))
            move(k, oz, 1 - x, 3, sibling, False).start()
            return
        first = s == 0
        if not first:
            arrived(k, at.device(oz, x, c))
        if sign >= 0:
            pl.when(z < length - 1)(lambda: move(k, oz, x, 0, above, first).start())
        if sign <= 0:
            pl.when(z > 0)(lambda: move(k, oz, x, 1, below, first).start())
        move(k, oz, x, 2, beside, first).start()
        move(k, oz, x, 3, sibling, first).start()

    def finish(k, oz, s, sign):
        if s is None:
            move(k, oz, 1 - x, 3, sibling, False).wait_send()
            return
        first = s == 0
        if sign >= 0:
            pl.when(z < length - 1)(lambda: move(k, oz, x, 0, above, first).wait_send())
        if sign <= 0:
            pl.when(z > 0)(lambda: move(k, oz, x, 1, below, first).wait_send())
        move(k, oz, x, 2, beside, first).wait_send()
        move(k, oz, x, 3, sibling, first).wait_send()

    steps(begin)
    for oz in range(length):
        for ox in range(2):
            for k in range(count):
                arrived(k, at.device(oz, ox, 1 - c))
    steps(finish)
    for k in range(count):
        pltpu.make_async_copy(ins[k], slab(k, own), local.at[k]).wait()


def gather_rows(arrays, dp):
    count, rows = len(arrays), arrays[0].shape[0]
    return pl.pallas_call(
        functools.partial(gather_kernel, dp, count, rows),
        out_shape=[jax.ShapeDtypeStruct((dp * rows, a.shape[1]), a.dtype) for a in arrays],
        in_specs=[pl.BlockSpec(memory_space=pltpu.VMEM)] * count,
        out_specs=[pl.BlockSpec(memory_space=pl.ANY)] * count,
        scratch_shapes=[
            pltpu.SemaphoreType.DMA((count, dp // 2, 4)),
            pltpu.SemaphoreType.DMA((count, dp)),
            pltpu.SemaphoreType.DMA((count,)),
        ],
        compiler_params=pltpu.CompilerParams(collective_id=1, has_side_effects=True),
        name="gather_rows",
    )(*arrays)


def scatter_kernel(dp, count, rows, *refs):
    parts, outs = refs[:count], refs[count : 2 * count]
    mine, first, second, upward, downward = (
        refs[(2 + i) * count : (3 + i) * count] for i in range(5)
    )
    sent1, sent2, sent4, got1, got2, got_up, got_down, local = refs[7 * count :]
    at = Place(dp)
    z, x, c, length = at.z, at.x, at.c, at.length
    below, above = at.device(z - 1, x, c), at.device(z + 1, x, c)
    beside, sibling = at.device(z, 1 - x, c), at.device(z, x, 1 - c)
    at.greet()

    def slab(k, o):
        return parts[k].at[pl.ds(pl.multiple_of(o * rows, rows), rows)]

    def swap(k, t, ox):
        q = t * 2 + ox
        return remote(
            slab(k, at.device(t, ox, 1 - c)), first[k].at[q], sent1.at[k, q], got1.at[k, q], sibling
        )

    def keep(k, t, ox):
        q = t * 2 + ox
        return pltpu.make_async_copy(slab(k, at.device(t, ox, c)), mine[k].at[q], local.at[k, q])

    def cross(k, t):
        q = t * 2 + 1 - x
        return remote(first[k].at[q], second[k].at[t], sent2.at[k, t], got2.at[k, t], beside)

    def rise(k, t):
        return remote(second[k].at[t], upward[k].at[t], sent4.at[k, t], got_up.at[k, t], above)

    def fall(k, t):
        return remote(second[k].at[t], downward[k].at[t], sent4.at[k, t], got_down.at[k, t], below)

    def targets(act):
        for d in range(length - 1, -1, -1):
            for sign in (1, -1) if d else (0,):
                t = z + d * sign

                def event(t=t, sign=sign):
                    for k in range(count):
                        act(k, t, sign)

                if d:
                    pl.when((t >= 0) & (t < length))(event)
                else:
                    event()

    def wide(value):
        return value.astype(jnp.float32)

    def start(k, t, sign):
        for ox in (1 - x, x):
            swap(k, t, ox).start()
            keep(k, t, ox).start()

    def chip_sum(k, t, sign):
        for ox in (1 - x, x):
            q = t * 2 + ox
            keep(k, t, ox).wait()
            swap(k, t, ox).wait_recv()
            first[k][q] = (wide(first[k][q]) + wide(mine[k][q])).astype(jnp.bfloat16)
            if ox is not x:
                cross(k, t).start()

    def chain(k, t, sign):
        cross(k, t).wait_recv()
        if sign == 0:
            outs[k][...] = wide(second[k][t]) + wide(first[k][t * 2 + x])

            def add_up():
                rise(k, t).wait_recv()
                outs[k][...] += wide(upward[k][t])

            def add_down():
                fall(k, t).wait_recv()
                outs[k][...] += wide(downward[k][t])

            pl.when(z > 0)(add_up)
            pl.when(z < length - 1)(add_down)
            return
        base, move = (upward, rise) if sign > 0 else (downward, fall)
        inner = z > 0 if sign > 0 else z < length - 1

        def middle():
            move(k, t).wait_recv()
            second[k][t] = (
                wide(second[k][t]) + wide(first[k][t * 2 + x]) + wide(base[k][t])
            ).astype(jnp.bfloat16)

        def edge():
            second[k][t] = (wide(second[k][t]) + wide(first[k][t * 2 + x])).astype(jnp.bfloat16)

        pl.when(inner)(middle)
        pl.when(jnp.logical_not(inner))(edge)
        move(k, t).start()

    def finish(k, t, sign):
        swap(k, t, 0).wait_send()
        swap(k, t, 1).wait_send()
        cross(k, t).wait_send()
        if sign:
            (rise if sign > 0 else fall)(k, t).wait_send()

    targets(start)
    targets(chip_sum)
    targets(chain)
    targets(finish)


def scatter_rows(arrays, dp):
    count, rows = len(arrays), arrays[0].shape[0] // dp
    length = layout_of(dp)[0]
    slots = [dp // 2, dp // 2, length, length, length]
    return pl.pallas_call(
        functools.partial(scatter_kernel, dp, count, rows),
        out_shape=[jax.ShapeDtypeStruct((rows, a.shape[1]), jnp.float32) for a in arrays],
        in_specs=[pl.BlockSpec(memory_space=pl.ANY)] * count,
        out_specs=[pl.BlockSpec(memory_space=pltpu.VMEM)] * count,
        scratch_shapes=[
            pltpu.VMEM((n, rows, a.shape[1]), a.dtype) for n in slots for a in arrays
        ]
        + [
            pltpu.SemaphoreType.DMA((count, n))
            for n in (dp // 2, length, length, dp // 2, length, length, length, dp // 2)
        ],
        compiler_params=pltpu.CompilerParams(
            collective_id=2, has_side_effects=True, vmem_limit_bytes=60 * 1024 * 1024
        ),
        name="scatter_rows",
    )(*arrays)


def exchange(values):
    return lax.ppermute(values, "tensor", ((0, 1), (1, 0)))


def collect(values):
    if lax.axis_size("tensor") != 2:
        return lax.all_gather(values, "tensor", axis=0, tiled=True)
    other = exchange(values)
    low = lax.axis_index("tensor") == 0
    return jnp.concatenate([jnp.where(low, values, other), jnp.where(low, other, values)])


def spread(values):
    if lax.axis_size("tensor") != 2:
        return lax.psum_scatter(values, "tensor", scatter_dimension=0, tiled=True)
    half = values.shape[0] // 2
    low = lax.axis_index("tensor") == 0
    head, tail = values[:half], values[half:]
    other = exchange(jnp.where(low, tail, head).astype(jnp.bfloat16))
    return jnp.where(low, head, tail) + other.astype(jnp.float32)


def total(values):
    if lax.axis_size("tensor") != 2:
        return lax.psum(values, "tensor")
    return values + exchange(values)


def on_device(
    block_input,
    cotangent,
    segment_ids,
    positions,
    norm_gains,
    qk_gains,
    w_query,
    w_keyval,
    w_output,
    w_gate_up,
    w_down,
):
    dp = lax.axis_size("dp")
    rows_here, row_len = segment_ids.shape
    tokens_here = rows_here * row_len
    shard, q_wide = w_query.shape
    kv_wide, ff_wide = w_keyval.shape[2], w_gate_up.shape[2]
    qk_shard = qk_gains.shape[1]
    gains = jnp.concatenate(
        [norm_gains.T, jnp.pad(qk_gains.T, ((0, shard - qk_shard), (0, 0)))], axis=1
    )
    gains = jnp.pad(gains, ((0, 0), (0, 124)))
    attn_pack = jnp.concatenate([w_query, w_keyval[0], w_keyval[1], w_output.T, gains], axis=1)
    gate_up_pack = jnp.concatenate([w_gate_up[0], w_gate_up[1]], axis=1)
    attn_full, gate_up_full, down_full = gather_rows([attn_pack, gate_up_pack, w_down.T], dp)
    qkv_wide = q_wide + 2 * kv_wide
    qkv_full = attn_full[:, :qkv_wide]
    output_full = attn_full[:, qkv_wide : qkv_wide + q_wide]
    gain_cols = attn_full[:, qkv_wide + q_wide :].astype(jnp.float32)
    gain_attn, gain_ffn = gain_cols[:, 0], gain_cols[:, 1]
    qk_cols = gain_cols.reshape(dp, shard, 128)[:, :qk_shard, 2:4].reshape(dp * qk_shard, 2)
    gain_q, gain_k = qk_cols[:, 0], qk_cols[:, 1]
    heads_here = q_wide // HD
    kv_here = kv_wide // HD
    dy_rows = collect(cotangent)
    xlocal = block_input.astype(jnp.float32)
    normed_f, scale1 = rms_forward(xlocal, gain_attn)
    normed1 = collect(normed_f.astype(jnp.bfloat16))
    qkv = fdot(normed1, qkv_full)
    query = qkv[:, :q_wide].reshape(rows_here, row_len, heads_here, HD)
    keys = qkv[:, q_wide : q_wide + kv_wide].reshape(rows_here, row_len, kv_here, HD)
    values = (
        qkv[:, q_wide + kv_wide :].astype(jnp.bfloat16).reshape(rows_here, row_len, kv_here, HD)
    )
    q_norm, q_scale = rms_forward(query, gain_q)
    k_norm, k_scale = rms_forward(keys, gain_k)
    cosv, sinv = rope_tables(positions)
    cosv = cosv[:, :, None, :]
    sinv = sinv[:, :, None, :]
    q_rot = (q_norm * cosv + rotate_half(q_norm) * sinv).astype(jnp.bfloat16)
    k_rot = (k_norm * cosv + rotate_half(k_norm) * sinv).astype(jnp.bfloat16)
    attended, log_total = jax.vmap(attend_row)(q_rot, k_rot, values, segment_ids)
    att_flat = attended.reshape(tokens_here, heads_here * HD)
    hidden = xlocal + spread(contract(att_flat, output_full, 1, 1))
    normed_g, scale2 = rms_forward(hidden, gain_ffn)
    normed2 = collect(normed_g.astype(jnp.bfloat16))
    gate_up = fdot(normed2, gate_up_full)
    gate_proj, up_proj = gate_up[:, :ff_wide], gate_up[:, ff_wide:]
    sigmoid_gate = jax.nn.sigmoid(gate_proj)
    silu_gate = gate_proj * sigmoid_gate
    act = (silu_gate * up_proj).astype(jnp.bfloat16)
    block_output = (hidden + spread(contract(act, down_full, 1, 1))).astype(jnp.bfloat16)
    grad_act = fdot(dy_rows, down_full)
    grad_down = contract(dy_rows, act, 0, 0).astype(jnp.bfloat16)
    d_gate = grad_act * up_proj * sigmoid_gate * (1.0 + gate_proj * (1.0 - sigmoid_gate))
    d_gate_up = jnp.concatenate(
        [d_gate.astype(jnp.bfloat16), (grad_act * silu_gate).astype(jnp.bfloat16)], axis=1
    )
    grad_gate_up = contract(normed2, d_gate_up, 0, 0).astype(jnp.bfloat16)
    grad_n2 = spread(contract(d_gate_up, gate_up_full, 1, 1))
    gain_ffn_grad = jnp.sum(grad_n2 * hidden * scale2, axis=0)
    grad_hidden = cotangent.astype(jnp.float32) + rms_backward(hidden, scale2, gain_ffn, grad_n2)
    grad_rows = collect(grad_hidden.astype(jnp.bfloat16))
    grad_att = (
        fdot(grad_rows, output_full)
        .astype(jnp.bfloat16)
        .reshape(rows_here, row_len, heads_here, HD)
    )
    grad_out = contract(grad_rows, att_flat, 0, 0).astype(jnp.bfloat16)
    grad_qrot, grad_krot, grad_vals = jax.vmap(back_row)(
        q_rot, k_rot, values, grad_att, log_total, segment_ids
    )
    grad_qn = grad_qrot * cosv + rotate_back(grad_qrot * sinv)
    grad_kn = grad_krot * cosv + rotate_back(grad_krot * sinv)
    gain_q_grad = jnp.sum(grad_qn * query * q_scale, axis=(0, 1, 2))
    gain_k_grad = jnp.sum(grad_kn * keys * k_scale, axis=(0, 1, 2))
    d_query = rms_backward(query, q_scale, gain_q, grad_qn).astype(jnp.bfloat16)
    d_keys = rms_backward(keys, k_scale, gain_k, grad_kn).astype(jnp.bfloat16)
    d_qkv = jnp.concatenate(
        [
            d_query.reshape(tokens_here, q_wide),
            d_keys.reshape(tokens_here, kv_wide),
            grad_vals.astype(jnp.bfloat16).reshape(tokens_here, kv_wide),
        ],
        axis=1,
    )
    grad_qkv = contract(normed1, d_qkv, 0, 0).astype(jnp.bfloat16)
    grad_n1 = spread(contract(d_qkv, qkv_full, 1, 1))
    gain_attn_grad = jnp.sum(grad_n1 * xlocal * scale1, axis=0)
    grad_input = grad_hidden + rms_backward(xlocal, scale1, gain_attn, grad_n1)
    gain_terms = total(
        jnp.concatenate([gain_attn_grad, gain_ffn_grad, gain_q_grad, gain_k_grad])[None]
    )[0]
    wide = dp * shard
    norm_terms = gain_terms[: 2 * wide].reshape(2, wide).T
    qk_terms = gain_terms[2 * wide :].reshape(2, dp, qk_shard).transpose(1, 2, 0)
    qk_terms = jnp.pad(qk_terms, ((0, 0), (0, shard - qk_shard), (0, 0))).reshape(wide, 2)
    gain_pack = jnp.concatenate([norm_terms, qk_terms], axis=1).astype(jnp.bfloat16)
    gain_pack = jnp.pad(gain_pack, ((0, 0), (0, 124)))
    grad_attn = jnp.concatenate([grad_qkv, grad_out, gain_pack], axis=1)
    attn_sum, gate_up_sum, down_sum = scatter_rows([grad_attn, grad_gate_up, grad_down], dp)
    gain_sum = attn_sum[:, qkv_wide + q_wide :]
    return (
        block_output,
        grad_input,
        gain_sum[:, 0:2].T,
        gain_sum[:qk_shard, 2:4].T,
        attn_sum[:, :q_wide],
        jnp.stack([attn_sum[:, q_wide : q_wide + kv_wide], attn_sum[:, q_wide + kv_wide : qkv_wide]]),
        attn_sum[:, qkv_wide : qkv_wide + q_wide].T,
        jnp.stack([gate_up_sum[:, :ff_wide], gate_up_sum[:, ff_wide:]]),
        down_sum.T,
    )


MESH = pl.DeviceIdType.MESH
LANES = 128
F32, BF16 = jnp.float32, jnp.bfloat16


def dot_nn(a, b):
    return lax.dot_general(a, b, (((1,), (0,)), ((), ())), preferred_element_type=F32)


def dot_nt(a, b):
    return lax.dot_general(a, b, (((1,), (1,)), ((), ())), preferred_element_type=F32)


def dot_tn(a, b):
    return lax.dot_general(a, b, (((0,), (0,)), ((), ())), preferred_element_type=F32)


def lane_of(shape):
    return lax.broadcasted_iota(jnp.int32, shape, len(shape) - 1)


def head_mean(values):
    row = lax.broadcasted_iota(jnp.int32, (LANES, LANES), 0) // HD
    ones = jnp.where(row == lane_of((LANES, LANES)) // HD, 1.0 / HD, 0.0).astype(BF16)
    high = values.astype(BF16)
    low = (values - high.astype(F32)).astype(BF16)
    return dot_nn(high, ones) + dot_nn(low, ones)


def low_half(shape):
    return lane_of(shape) < HD


def first_quarter(shape):
    return lax.rem(lane_of(shape), HD) < HD // 2


def ds(start, size):
    if isinstance(start, int):
        return pl.ds(start, size)
    return pl.ds(pl.multiple_of(start, size), size)


class Gather:
    def __init__(self, at, rows, slabs, flipped, send, recv):
        self.at, self.rows, self.slabs, self.flipped = at, rows, slabs, flipped
        self.send, self.recv = send, recv

    def slab(self, k, o):
        return self.slabs[k](ds(o * self.rows, self.rows))

    def move(self, k, oz, ox, way, target):
        at = self.at
        o = at.device(oz, ox, at.c)
        return remote(
            self.slab(k, o), self.slab(k, o), self.send.at[k, oz * 2 + ox, way], self.recv.at[k, o], target
        )

    def arrived(self, k, o):
        at = self.at
        slab = self.slab(k, o)
        remote(slab, slab, self.send.at[k, 0, 0], self.recv.at[k, o], at.sibling).wait_recv()

    def sources(self, s, act):
        at = self.at
        for sign in (1, -1) if s else (0,):
            oz = at.z - s * sign
            if s:
                pl.when((oz >= 0) & (oz < at.length))(lambda oz=oz, sign=sign: act(oz, sign))
            else:
                act(oz, 0)

    def along(self, k, oz, ox, sign, act):
        at = self.at
        if sign >= 0:
            pl.when(at.z < at.length - 1)(lambda: act(self.move(k, oz, ox, 0, at.above)))
        if sign <= 0:
            pl.when(at.z > 0)(lambda: act(self.move(k, oz, ox, 1, at.below)))

    def outgoing(self, k, s, oz, sign, act):
        at = self.at
        self.along(k, oz, at.x, sign, act)
        if not s or k not in self.flipped:
            act(self.move(k, oz, at.x, 2, at.beside))
        act(self.move(k, oz, at.x, 3, at.sibling))

    def onward(self, k, oz, sign, act):
        at = self.at
        if k in self.flipped:
            self.along(k, oz, 1 - at.x, sign, act)
        act(self.move(k, oz, 1 - at.x, 3, at.sibling))

    def main(self, k, s):
        at = self.at

        def act(oz, sign):
            if s:
                self.arrived(k, at.device(oz, at.x, at.c))
            self.outgoing(k, s, oz, sign, lambda m: m.start())

        self.sources(s, act)

    def side(self, k, s):
        at = self.at

        def act(oz, sign):
            self.arrived(k, at.device(oz, 1 - at.x, at.c))
            self.onward(k, oz, sign, lambda m: m.start())

        self.sources(s, act)

    def final(self, k):
        at = self.at
        for oz in range(at.length):
            for ox in range(2):
                self.arrived(k, at.device(oz, ox, 1 - at.c))

    def finish(self, k):
        at = self.at
        for s in range(at.length):
            self.sources(s, lambda oz, sign: self.outgoing(k, s, oz, sign, lambda m: m.wait_send()))
            self.sources(s, lambda oz, sign: self.onward(k, oz, sign, lambda m: m.wait_send()))


class Spot(Place):
    def __init__(self, dp):
        super().__init__(dp)
        z, x, c = self.z, self.x, self.c
        self.below, self.above = self.device(z - 1, x, c), self.device(z + 1, x, c)
        self.beside, self.sibling = self.device(z, 1 - x, c), self.device(z, x, 1 - c)
        self.own = self.device(z, x, c)
        self.t = lax.axis_index("tensor")

    def greet(self):
        barrier = pltpu.get_barrier_semaphore()

        def signal(target):
            pl.semaphore_signal(barrier, inc=1, device_id=target, device_id_type=MESH)

        signal({"dp": self.sibling})
        signal({"dp": self.beside})
        signal({"tensor": 1 - self.t})
        pl.when(self.z > 0)(lambda: signal({"dp": self.below}))
        pl.when(self.z < self.length - 1)(lambda: signal({"dp": self.above}))
        ends = jnp.where(self.z > 0, 1, 0) + jnp.where(self.z < self.length - 1, 1, 0)
        pl.semaphore_wait(barrier, 3 + ends)


def partner(at, src, dst, sems):
    return pltpu.make_async_remote_copy(
        src_ref=src,
        dst_ref=dst,
        send_sem=sems.at[0],
        recv_sem=sems.at[1],
        device_id={"tensor": 1 - at.t},
        device_id_type=MESH,
    )


CHUNKS = 3
FLIPPED = 1


def chunk_widths(ff_wide):
    tiles = ff_wide // 256
    sizes = [tiles * 4 // 9, tiles * 2 // 9]
    return [256 * n for n in sizes + [tiles - sum(sizes)]]


FORWARD_ORDER = (
    ("M", 0, 0), ("fill",), ("M", 2, 0), ("tables",), ("M", 0, 1), ("M", 3, 0), ("M", 0, 2), ("M", 2, 1),
    ("D", 0, 0), ("M", 0, 3), ("D", 0, 1), ("M", 1, 0), ("D", 0, 2), ("D", 0, 3), ("F", 0), ("gains",),
    ("M", 3, 1), ("norm1",), ("project",), ("rotate",), ("M", 1, 1), ("attend0",), ("partial0",), ("D", 2, 0),
    ("attend1",), ("M", 1, 2), ("D", 3, 0), ("partial1",), ("M", 1, 3), ("norm2",), ("D", 1, 0), ("D", 2, 1),
    ("D", 1, 1), ("M", 2, 2), ("D", 3, 1), ("M", 3, 2), ("D", 2, 2), ("M", 2, 3), ("D", 1, 2), ("D", 1, 3),
    ("F", 1), ("own", 0), ("M", 3, 3), ("other", 0), ("combine", 0), ("D", 2, 3), ("D", 3, 2), ("D", 3, 3),
    ("F", 2), ("own", 1), ("other", 1), ("combine", 1), ("F", 3), ("own", 2), ("other", 2), ("combine", 2),
    ("close",),
)


def fwd_kernel(
    dp, rows, half, x_ref, dy_ref, seg_ref, pos_ref, freq_ref, gains_ref, wq_ref, wkv_ref, wo_ref,
    wgu_ref, wd_ref,
    wa_out, n1_out, raw_out, p_out, qrot_out, kdup_out, vdup_out, att_out, hidden_out, n2_out,
    dyf_out, act_out, dg_out, du_out, cos_out, sin_out, gnm_out, gno_out, om_out, oo_out,
    wa, wf0, wf1, wf2, xf, dyf, n1, n2, raw, prob, qrot, kdup, vdup, att, hidden, act, dg, du, cos, sin,
    segc, gn, op, part_out, part_in, gno, oo, om, gain_rows,
    send, recv, ysem, outsem,
):
    at = Spot(dp)
    wide = dp * rows
    tokens = 2 * half
    q_wide, kv_wide, ff_wide = wq_ref.shape[1], wkv_ref.shape[2], wd_ref.shape[1]
    chunks = chunk_widths(ff_wide)
    wf = (wf0, wf1, wf2)
    o_at, g_at = q_wide + 2 * kv_wide, 2 * q_wide + 2 * kv_wide
    groups = q_wide // LANES
    mine, theirs = at.t * half, (1 - at.t) * half
    own_rows = ds(at.own * rows, rows)
    outs = []

    def put(src, dst):
        copy = pltpu.make_async_copy(src, dst, outsem.at[len(outs)])
        copy.start()
        outs.append(copy)

    at.greet()
    gather = Gather(
        at,
        rows,
        [lambda r: wa.at[r]] + [lambda r, j=j: wf[j].at[r] for j in range(CHUNKS)],
        (1 + FLIPPED,),
        send,
        recv,
    )
    wa[own_rows, 0:q_wide] = wq_ref[...]
    wa[own_rows, q_wide : q_wide + kv_wide] = wkv_ref[0]
    wa[own_rows, q_wide + kv_wide : o_at] = wkv_ref[1]
    wa[own_rows, o_at:g_at] = wo_ref[...]
    wa[own_rows, g_at:] = gains_ref[...]
    x_copy = partner(at, x_ref, xf.at[ds(mine, half)], ysem.at[0])
    dy_copy = partner(at, dy_ref, dyf.at[ds(mine, half)], ysem.at[1])
    out_copy = partner(at, part_out, part_in, ysem.at[2])
    n2_copy = partner(at, n2.at[ds(mine, half)], n2.at[ds(mine, half)], ysem.at[3])
    gain = {}
    blk = 128

    def fill():
        x_copy.start()
        dy_copy.start()
        for j, chunk in enumerate(chunks):
            cols = slice(sum(chunks[:j]), sum(chunks[: j + 1]))
            wf[j][own_rows, 0:chunk] = wgu_ref[0, :, cols]
            wf[j][own_rows, chunk : 2 * chunk] = wgu_ref[1, :, cols]
            wf[j][own_rows, 2 * chunk :] = wd_ref[:, cols]

    def tables():
        xf[ds(mine, half)] = x_ref[...]
        dyf[ds(mine, half)] = dy_ref[...]
        segc[...] = jnp.broadcast_to(seg_ref[...].astype(F32), (LANES, tokens)).T
        cos[...] = jnp.broadcast_to(pos_ref[...].astype(F32), (LANES, tokens)).T

        @pl.loop(0, tokens // 64)
        def _(i):
            r = ds(i * 64, 64)
            angles = cos[r] * freq_ref[...]
            cos[r] = jnp.cos(angles)
            sin[r] = jnp.sin(angles)

        put(cos, cos_out)
        put(sin, sin_out)

    def gains():
        put(wa, wa_out)
        gain_rows[...] = wa[:, g_at : g_at + LANES].astype(F32).T[:8]
        qk = jnp.sum(wa[:, g_at + LANES :].astype(F32), axis=0, keepdims=True)
        lows = low_half((1, LANES))
        gain["q"] = jnp.where(lows, qk, pltpu.roll(qk, HD, 1))
        gain["k"] = jnp.where(lows, pltpu.roll(qk, HD, 1), qk)
        x_copy.wait_recv()

    def norm1():
        @pl.loop(0, tokens // 64)
        def _(i):
            r = ds(i * 64, 64)
            values = xf[r].astype(F32)
            n1[r] = rms_forward(values, gain_rows[0:1, :])[0].astype(BF16)

        put(n1, n1_out)

    def project():
        @pl.loop(0, o_at // 256)
        def _(n):
            tile = dot_nn(n1[...], wa[:, ds(n * 256, 256)])
            raw[2 * n] = tile[:, :LANES]
            raw[2 * n + 1] = tile[:, LANES:]

        put(raw, raw_out)

    def rope(n, gain_row, r):
        values = raw[n, r]
        normed = values * lax.rsqrt(head_mean(values * values) + EPSILON) * gain_row
        early = first_quarter(normed.shape)
        turned = jnp.where(early, -pltpu.roll(normed, LANES - HD // 2, 1), pltpu.roll(normed, HD // 2, 1))
        return normed * cos[r] + turned * sin[r]

    def doubled(tile):
        swapped = pltpu.roll(tile, HD, 1)
        lows = low_half(tile.shape)
        return jnp.where(lows, tile, swapped).astype(BF16), jnp.where(lows, swapped, tile).astype(BF16)

    def rotate():
        @pl.loop(0, tokens // blk)
        def _(i):
            r = ds(i * blk, blk)
            for n in range(groups):
                qrot[n, r] = rope(n, gain["q"], r).astype(BF16)
            for n in range(groups // 2):
                kdup[2 * n, r], kdup[2 * n + 1, r] = doubled(rope(groups + n, gain["k"], r))
                vdup[2 * n, r], vdup[2 * n + 1, r] = doubled(raw[groups + groups // 2 + n, r])

        put(qrot, qrot_out)
        put(kdup, kdup_out)
        put(vdup, vdup_out)

    def attend(base):
        @pl.loop(0, groups * (half // blk))
        def _(step):
            g = step // (half // blk)
            start = base + lax.rem(step, half // blk) * blk
            r = ds(start, blk)
            q = qrot[g, r]
            lows = low_half(q.shape)
            index = lax.broadcasted_iota(jnp.int32, (blk, tokens), 0) + start
            allowed = (segc[r, 0:1] == seg_ref[...].astype(F32)) & (lane_of((blk, tokens)) <= index)
            result = []
            for hh in range(2):
                picked = jnp.where(lows if hh == 0 else jnp.logical_not(lows), q, jnp.zeros_like(q))
                scores = dot_nt(picked, kdup[g]) * (1.0 / math.sqrt(HD))
                scores = jnp.where(allowed, scores, NEG_FILL)
                e = jnp.exp(scores - jnp.max(scores, axis=1, keepdims=True))
                p = (e / jnp.sum(e, axis=1, keepdims=True)).astype(BF16)
                prob[g, ds(hh * tokens + start, blk)] = p
                result.append(dot_nn(p, vdup[g]))
            att[r, ds(g * LANES, LANES)] = jnp.where(lows, result[0], result[1]).astype(BF16)

    def send_partial():
        @pl.loop(0, wide // 256)
        def _(n):
            cols = ds(n * 256, 256)
            part_out[:, cols] = dot_nt(att[ds(theirs, half)], wa[cols, o_at:g_at]).astype(BF16)

        out_copy.start()

    def attend_mine():
        attend(mine)
        put(prob, p_out)
        put(att, att_out)

    def own_partial():
        @pl.loop(0, wide // 256)
        def _(n):
            cols = ds(n * 256, 256)
            hidden[:, cols] = x_ref[:, cols].astype(F32) + dot_nt(att[ds(mine, half)], wa[cols, o_at:g_at])

        out_copy.wait_recv()

    def norm2():
        @pl.loop(0, half // 64)
        def _(i):
            r = ds(i * 64, 64)
            values = hidden[r] + part_in[r].astype(F32)
            hidden[r] = values
            n2[ds(mine + i * 64, 64)] = rms_forward(values, gain_rows[1:2, :])[0].astype(BF16)

        put(hidden, hidden_out)
        n2_copy.start()

    def hidden_units(j, base):
        chunk, before = chunks[j], sum(chunks[:j])

        @pl.loop(0, chunk // 256)
        def _(n):
            r = ds(base, half)
            gate = dot_nn(n2[r], wf[j][:, ds(n * 256, 256)])
            up = dot_nn(n2[r], wf[j][:, ds(chunk + n * 256, 256)])
            gact = dot_nn(dyf[r], wf[j][:, ds(2 * chunk + n * 256, 256)])
            sig = jax.nn.sigmoid(gate)
            silu = gate * sig
            cols = ds(before + n * 256, 256)
            act[r, cols] = (silu * up).astype(BF16)
            dg[r, cols] = (gact * up * sig * (1.0 + gate * (1.0 - sig))).astype(BF16)
            du[r, cols] = (gact * silu).astype(BF16)

    def partner_units(j):
        if j == 0:
            dy_copy.wait_recv()
            put(dyf, dyf_out)
            n2_copy.wait_recv()
            put(n2, n2_out)
        hidden_units(j, theirs)

    def combine(j):
        chunk = chunks[j]
        cols = slice(sum(chunks[:j]), sum(chunks[: j + 1]))

        @pl.loop(0, wide // 256)
        def _(n):
            r = ds(n * 256, 256)
            down = dot_nt(act[:, cols], wf[j][r, 2 * chunk :])
            back = dot_nt(dg[:, cols], wf[j][r, :chunk]) + dot_nt(du[:, cols], wf[j][r, chunk : 2 * chunk])
            if j == 0:
                op[:, r] = down
                gn[:, r] = back
            else:
                op[:, r] += down
                gn[:, r] += back

    def close():
        put(act, act_out)
        put(dg, dg_out)
        put(du, du_out)
        put(gn.at[ds(mine, half)], gnm_out)

        @pl.loop(0, half // 64)
        def _(i):
            r = ds(i * 64, 64)
            gno[r] = gn[ds(theirs + i * 64, 64)].astype(BF16)
            oo[r] = op[ds(theirs + i * 64, 64)].astype(BF16)
            om[r] = op[ds(mine + i * 64, 64)] + hidden[r]

        put(gno, gno_out)
        put(oo, oo_out)
        put(om, om_out)

    steps = {
        "fill": fill, "tables": tables, "gains": gains, "norm1": norm1, "project": project, "rotate": rotate,
        "attend0": lambda: attend(theirs), "partial0": send_partial, "attend1": attend_mine,
        "partial1": own_partial, "norm2": norm2, "own": lambda j: hidden_units(j, mine),
        "other": partner_units, "combine": combine, "close": close,
        "M": gather.main, "D": gather.side, "F": gather.final,
    }
    for name, *which in FORWARD_ORDER:
        steps[name](*which)
    for copy in (x_copy, dy_copy, out_copy, n2_copy):
        copy.wait_send()
    for k in range(CHUNKS + 1):
        gather.finish(k)
    for copy in outs:
        copy.wait()


def forward(dp, x, dy, seg, pos, freq, gains, wq, wkv, wo_t, wgu, wd_t):
    rows, half = wq.shape[0], x.shape[0]
    tokens, wide = 2 * half, dp * rows
    q_wide, kv_wide, ff_wide = wq.shape[1], wkv.shape[2], wd_t.shape[1]
    groups = q_wide // LANES
    attn_wide = 2 * q_wide + 2 * kv_wide + 2 * LANES
    shapes = [
        ((wide, attn_wide), BF16),
        ((tokens, wide), BF16),
        ((2 * groups, tokens, LANES), F32),
        ((groups, 2 * tokens, tokens), BF16),
        ((groups, tokens, LANES), BF16),
        ((groups, tokens, LANES), BF16),
        ((groups, tokens, LANES), BF16),
        ((tokens, q_wide), BF16),
        ((half, wide), F32),
        ((tokens, wide), BF16),
        ((tokens, wide), BF16),
        ((tokens, ff_wide), BF16),
        ((tokens, ff_wide), BF16),
        ((tokens, ff_wide), BF16),
        ((tokens, LANES), F32),
        ((tokens, LANES), F32),
        ((half, wide), F32),
        ((half, wide), BF16),
        ((half, wide), F32),
        ((half, wide), BF16),
    ]
    (wa, n1, raw, p, qrot, kdup, vdup, att, hidden, n2, dyf, act, dg, du, cos, sin, gnm, gno, om, oo) = shapes
    vmem = [
        wa, *[((wide, 3 * w), BF16) for w in chunk_widths(ff_wide)], n2, dyf, n1, n2, raw, p, qrot, kdup, vdup, att,
        hidden, act, dg, du, cos, sin, cos, ((tokens, wide), F32), ((tokens, wide), F32), oo, oo, gno, oo, om,
        ((8, wide), F32),
    ]
    return pl.pallas_call(
        functools.partial(fwd_kernel, dp, rows, half),
        out_shape=[jax.ShapeDtypeStruct(*s) for s in shapes],
        in_specs=[pl.BlockSpec(memory_space=pltpu.VMEM)] * 11,
        out_specs=[pl.BlockSpec(memory_space=pl.ANY)] * len(shapes),
        scratch_shapes=[pltpu.VMEM(*s) for s in vmem]
        + [
            pltpu.SemaphoreType.DMA((CHUNKS + 1, dp // 2, 4)),
            pltpu.SemaphoreType.DMA((CHUNKS + 1, dp)),
            pltpu.SemaphoreType.DMA((4, 2)),
            pltpu.SemaphoreType.DMA((len(shapes),)),
        ],
        compiler_params=pltpu.CompilerParams(
            collective_id=3, has_side_effects=True, vmem_limit_bytes=62 * 1024 * 1024
        ),
        name="forward",
    )(x, dy, seg, pos, freq, gains, wq, wkv, wo_t, wgu, wd_t)


class Scatter:
    def __init__(self, at, rows, slabs, flipped, first, second, chained, emit, sems):
        self.at, self.rows, self.slabs, self.flipped, self.emit = at, rows, slabs, flipped, emit
        self.first, self.second, self.chained = first, second, chained
        self.sent1, self.sent2, self.sent4, self.got1, self.got2, self.got_up, self.got_down = sems

    def slab(self, k, o):
        return self.slabs[k](ds(o * self.rows, self.rows))

    def swap(self, k, t, ox):
        at, q = self.at, t * 2 + ox
        src = self.slab(k, at.device(t, ox, 1 - at.c))
        return remote(src, self.first[k].at[q], self.sent1.at[k, q], self.got1.at[k, q], at.sibling)

    def cross(self, k, t):
        at = self.at
        q, slot = t * 2 + 1 - at.x, 0 if k in self.flipped else t
        return remote(
            self.first[k].at[q], self.second[k].at[slot], self.sent2.at[k, t], self.got2.at[k, slot], at.beside
        )

    def crossed(self, k, t):
        at = self.at
        slot = 0 if k in self.flipped else t
        block = self.second[k].at[slot]
        remote(block, block, self.sent2.at[k, t], self.got2.at[k, slot], at.beside).wait_recv()

    def slot(self, t, ox, last_down):
        return ox * (self.at.length + 1) + (self.at.length if last_down else t)

    def along(self, k, t, ox, up, distance):
        at, lane = self.at, ox * self.at.length + t
        src = self.first[k].at[t * 2 + ox] if k in self.flipped else self.second[k].at[t]
        dst = self.chained[k].at[self.slot(t, ox, distance == 1 and not up)]
        got = self.got_up if up else self.got_down
        return remote(src, dst, self.sent4.at[k, lane], got.at[k, lane], at.above if up else at.below)

    def arrive(self, k, t, ox, up, last):
        at, lane = self.at, ox * self.at.length + t
        block = self.chained[k].at[self.slot(t, ox, last and not up)]
        got = self.got_up if up else self.got_down
        remote(block, block, self.sent4.at[k, lane], got.at[k, lane], at.above).wait_recv()

    def lanes(self, k):
        return (1 - self.at.x, self.at.x) if k in self.flipped else (0,)

    def targets(self, act, distances=None):
        at = self.at
        for d in range(at.length - 1, -1, -1) if distances is None else distances:
            for sign in (1, -1) if d else (0,):
                t = at.z + d * sign
                if d:
                    pl.when((t >= 0) & (t < at.length))(lambda t=t, sign=sign, d=d: act(t, sign, d))
                else:
                    act(t, 0, 0)

    def each(self, act):
        @pl.loop(0, self.rows // 16)
        def _(i):
            act(ds(i * 16, 16))

    def start(self, k):
        def act(t, sign, d):
            for ox in (1 - self.at.x, self.at.x):
                self.swap(k, t, ox).start()

        self.targets(act)

    def chip(self, k):
        at, first = self.at, self.first[k]

        def act(t, sign, d):
            for ox in (1 - at.x, at.x):
                q = t * 2 + ox
                self.swap(k, t, ox).wait_recv()
                base = at.device(t, ox, at.c) * self.rows

                @pl.loop(0, self.rows // 16)
                def _(i, q=q, base=base):
                    r = ds(i * 16, 16)
                    first[q, r] = first[q, r] + self.slabs[k](ds(base + i * 16, 16))[...]

                if ox is not at.x and k not in self.flipped:
                    self.cross(k, t).start()

        self.targets(act)

    def chain(self, k, d):
        at, first, second, chained = self.at, self.first[k], self.second[k], self.chained[k]
        flipped = k in self.flipped

        def ends(up, down, q, t, ox, other, put):
            def row(r):
                value = first[q, r].astype(F32)
                if other is not None:
                    value += second[other, r].astype(F32)
                if up:
                    value += chained[self.slot(t, ox, False), r].astype(F32)
                if down:
                    value += chained[self.slot(t, ox, True), r].astype(F32)
                put(r, value)

            self.each(row)

        def sums(*args):
            pl.when((at.z > 0) & (at.z < at.length - 1))(lambda: ends(True, True, *args))
            pl.when(at.z == 0)(lambda: ends(False, True, *args))
            pl.when(at.z == at.length - 1)(lambda: ends(True, False, *args))

        def last(t, ox):
            pl.when(at.z > 0)(lambda: self.arrive(k, t, ox, True, True))
            pl.when(at.z < at.length - 1)(lambda: self.arrive(k, t, ox, False, True))

        def out(r, value):
            self.emit(k, r, value)

        def act(t, sign, d):
            if d == 0 and flipped:
                q = t * 2 + 1 - at.x

                def keep(r, value):
                    first[q, r] = value.astype(BF16)

                last(t, 1 - at.x)
                sums(q, t, 1 - at.x, None, keep)
                self.cross(k, t).start()
                return
            if d < 0:
                last(t, at.x)
                self.crossed(k, t)
                sums(t * 2 + at.x, t, at.x, 0, out)
                return
            if not flipped:
                self.crossed(k, t)
            if d == 0:
                last(t, 0)
                sums(t * 2 + at.x, t, 0, t, out)
                return
            up = sign > 0
            inner = at.z > 0 if up else at.z < at.length - 1
            for ox in self.lanes(k):
                q = t * 2 + (ox if flipped else at.x)

                def middle(ox=ox, q=q):
                    self.arrive(k, t, ox, up, False)

                    def row(r):
                        value = first[q, r].astype(F32) + chained[self.slot(t, ox, False), r].astype(F32)
                        if flipped:
                            first[q, r] = value.astype(BF16)
                        else:
                            second[t, r] = (value + second[t, r].astype(F32)).astype(BF16)

                    self.each(row)

                def edge(q=q):
                    def row(r):
                        second[t, r] = second[t, r] + first[q, r]

                    self.each(row)

                pl.when(inner)(middle)
                if not flipped:
                    pl.when(jnp.logical_not(inner))(edge)
                self.along(k, t, ox, up, d).start()

        if d < 0:
            act(at.z, 0, d)
        else:
            self.targets(act, (d,))

    def swapped(self, k):
        def act(t, sign, d):
            for ox in range(2):
                self.swap(k, t, ox).wait_send()

        self.targets(act)

    def finish(self, k):
        def act(t, sign, d):
            if k not in self.flipped or d == 0:
                self.cross(k, t).wait_send()
            if sign:
                for ox in self.lanes(k):
                    self.along(k, t, ox, sign > 0, d).wait_send()

        self.targets(act)


BACKWARD_ORDER = (
    ("weights", 1), ("S", 1), ("weights", 0), ("S", 0), ("P", 1), ("C", 1, 3), ("P", 0), ("C", 1, 2),
    ("residual",), ("weights", 2), ("S", 2), ("C", 0, 3), ("C", 1, 1), ("P", 2), ("attended",), ("S", 3),
    ("heads", 0), ("C", 0, 2), ("heads", 1), ("heads", 2), ("heads", 3), ("C", 2, 3), ("unrotate",),
    ("send",), ("C", 2, 2), ("projection",), ("S", 4), ("P", 3), ("C", 0, 1), ("output",), ("own",), ("P", 4),
    ("input",), ("C", 2, 1), ("C", 0, 0), ("C", 4, 3), ("C", 3, 3), ("C", 4, 2), ("gains",), ("S", 5),
    ("C", 2, 0), ("C", 3, 2), ("P", 5), ("C", 5, 3), ("C", 1, 0), ("C", 4, 1), ("C", 5, 2), ("C", 3, 1),
    ("C", 4, 0), ("C", 5, 1), ("C", 1, -1), ("C", 3, 0), ("C", 5, 0),
)


def bwd_kernel(
    dp, rows, half, x_ref, dy_ref,
    wa_in, n1_in, raw_in, p_in, qrot_in, kdup_in, vdup_in, att_in, hidden_in, n2_in,
    dyf_in, act_in, dg_in, du_in, cos_in, sin_in, gnm_in, gno_in, om_in, oo_in,
    bo_out, gi_out, gain_out, gq_out, gkv_out, go_out, ggu_out, gdn_out,
    parts0, parts1, pa, stage, turned, turned2, tiles, prob, raw, qrot, kdup, vdup, att, weights, gains, cos, sin,
    hidden, gh, grecv, orecv, grows, n1recv, n1send, ga, qs, dos, dq, dk, dv, dqkv, terms, terms_in,
    *rest,
):
    count = CHUNKS + 3
    first, second, chained = rest[:count], rest[count : 2 * count], rest[2 * count : 3 * count]
    sems = rest[3 * count : 3 * count + 7]
    ysem, loads, tilesem = rest[3 * count + 7 :]
    at = Spot(dp)
    wide, tokens = dp * rows, 2 * half
    q_wide, kv_wide, ff_wide = gq_out.shape[1], gkv_out.shape[2], gdn_out.shape[1]
    chunks = chunk_widths(ff_wide)
    parts = (parts0, parts1, parts1)
    o_at, g_at = q_wide + 2 * kv_wide, 2 * q_wide + 2 * kv_wide
    groups = q_wide // LANES
    mine, theirs = at.t * half, (1 - at.t) * half
    used = []

    def load(src, dst):
        copy = pltpu.make_async_copy(src, dst, loads.at[len(used)])
        copy.start()
        used.append(copy)
        return copy

    def emit(k, r, value):
        if k < CHUNKS:
            chunk = chunks[k]
            cols = slice(sum(chunks[:k]), sum(chunks[: k + 1]))
            ggu_out[0, r, cols] = value[:, :chunk]
            ggu_out[1, r, cols] = value[:, chunk : 2 * chunk]
            gdn_out[r, cols] = value[:, 2 * chunk :]
        elif k == CHUNKS:
            go_out[r] = value
        elif k == CHUNKS + 1:
            gq_out[r] = value[:, :q_wide]
            gkv_out[0, r] = value[:, q_wide : q_wide + kv_wide]
            gkv_out[1, r] = value[:, q_wide + kv_wide :]
        else:
            gain_out[r] = value

    slabs = [lambda r, j=j: parts[j].at[r, : 3 * chunks[j]] for j in range(CHUNKS)]
    slabs += [lambda r: pa.at[r, o_at:g_at], lambda r: pa.at[r, 0:o_at], lambda r: pa.at[r, g_at:]]
    scatter = Scatter(at, rows, slabs, (FLIPPED,), first, second, chained, emit, sems)

    at.greet()
    g_copy = partner(at, gno_in, grecv, ysem.at[0])
    g_copy.start()
    o_copy = partner(at, oo_in, orecv, ysem.at[1])
    dy_load = load(dyf_in, stage.at[0])
    n2_load = load(n2_in, stage.at[1])

    def tile_copies(i, slot):
        cols = ds(i * 256, 256)
        return [
            pltpu.make_async_copy(src.at[:, cols], tiles.at[slot, n], tilesem.at[slot, n])
            for n, src in enumerate((act_in, dg_in, du_in))
        ]

    order = [FLIPPED, 0, 2]
    sequence = [(j, n) for j in order for n in range(chunks[j] // 256)]

    def tile_of(i):
        j, n = sequence[i]
        return sum(chunks[:j]) // 256 + n

    for copy in tile_copies(tile_of(0), 0):
        copy.start()
    wo_load = load(wa_in.at[:, o_at:g_at], weights.at[:, : g_at - o_at])
    gain_load = load(wa_in.at[:, g_at:], gains)
    hidden_load = load(hidden_in, hidden)
    gnm_load = load(gnm_in, gh)
    cos_load, sin_load = load(cos_in, cos), load(sin_in, sin)
    att_load, raw_load = load(att_in, att), load(raw_in.at[0 : groups + groups // 2], raw)
    q_load, k_load, v_load = load(qrot_in, qrot), load(kdup_in, kdup), load(vdup_in, vdup)
    om_load = load(om_in, gi_out)
    p_loads = [load(p_in.at[0], prob.at[0])]

    def transpose(src, dst):
        @pl.loop(0, wide // 128)
        def _(i):
            c = ds(i * 128, 128)
            dst[c] = src[:, c].T

    dy_load.wait()
    transpose(stage.at[0], turned)
    n2_load.wait()
    transpose(stage.at[1], turned2)
    n1_load = load(n1_in, stage.at[0])

    def weight_grads(j):
        chunk = chunks[j]
        for n in range(chunk // 256):
            i = sequence.index((j, n))
            slot = i % 2
            if i + 1 < len(sequence):
                for copy in tile_copies(tile_of(i + 1), 1 - slot):
                    copy.start()
            for copy in tile_copies(tile_of(i), slot):
                copy.wait()

            @pl.loop(0, wide // 256)
            def _(m, n=n, slot=slot):
                r = ds(m * 256, 256)
                for part, left, which in ((0, turned2, 1), (1, turned2, 2), (2, turned, 0)):
                    cols = slice(part * chunk + n * 256, part * chunk + (n + 1) * 256)
                    parts[j][r, cols] = dot_nn(left[r], tiles[slot, which]).astype(BF16)


    r_copy = partner(at, grows.at[ds(mine, half)], grows.at[ds(mine, half)], ysem.at[2])
    n_copy = partner(at, n1send, n1recv, ysem.at[3])
    t_copy = partner(at, terms, terms_in, ysem.at[4])
    blk = 128
    gain = {}

    def residual():
        gain_load.wait()
        gain_rows = gains[:, :LANES].astype(F32).T[:8]
        qk_gain = jnp.sum(gains[:, LANES:].astype(F32), axis=0, keepdims=True)
        lows1 = low_half((1, LANES))
        gain["q"] = jnp.where(lows1, qk_gain, pltpu.roll(qk_gain, HD, 1))
        gain["k"] = jnp.where(lows1, pltpu.roll(qk_gain, HD, 1), qk_gain)
        gain["attn"], gain["ffn"] = gain_rows[0:1, :], gain_rows[1:2, :]
        hidden_load.wait()
        gnm_load.wait()
        g_copy.wait_recv()
        terms[...] = jnp.zeros_like(terms)

        @pl.loop(0, half // 32)
        def _(i):
            r = ds(i * 32, 32)
            grad = gh[r] + grecv[r].astype(F32)
            values = hidden[r]
            scale = lax.rsqrt(jnp.mean(values * values, axis=-1, keepdims=True) + EPSILON)
            terms[1:2, :wide] += jnp.sum(grad * values * scale, axis=0, keepdims=True)
            result = dy_ref[r].astype(F32) + rms_backward(values, scale, gain["ffn"], grad)
            gh[r] = result
            grows[ds(mine + i * 32, 32)] = result.astype(BF16)

        r_copy.start()
        o_copy.start()

    def attended_grads():
        wo_load.wait()
        r_copy.wait_recv()

        @pl.loop(0, q_wide // 256)
        def _(n):
            tile = dot_nn(grows[...], weights[:, ds(n * 256, 256)]).astype(BF16)
            ga[2 * n] = tile[:, :LANES]
            ga[2 * n + 1] = tile[:, LANES:]

        gain["weights"] = load(wa_in.at[:, :o_at], weights)
        transpose(grows, turned)
        att_load.wait()

        @pl.loop(0, wide // 256)
        def _(m):
            r = ds(m * 256, 256)
            pa[r, o_at:g_at] = dot_nn(turned[r], att[...]).astype(BF16)

        q_load.wait()
        k_load.wait()
        v_load.wait()

    def heads(g):
        if g + 1 < groups:
            p_loads.append(load(p_in.at[g + 1], prob.at[(g + 1) % 2]))
        p_loads[g].wait()
        pg = prob.at[g % 2]

        @pl.loop(0, tokens // blk)
        def _(i, g=g):
            r, r2 = ds(i * blk, blk), ds(tokens + i * blk, blk)
            lows = low_half((blk, LANES))
            q, do = qrot[g, r], ga[g, r]
            zero = jnp.zeros_like(q)
            qs[r], qs[r2] = jnp.where(lows, q, zero), jnp.where(lows, zero, q)
            dos[r], dos[r2] = jnp.where(lows, do, zero), jnp.where(lows, zero, do)

        dv[g] = dot_tn(pg[...], dos[...])

        @pl.loop(0, tokens // blk)
        def _(i, g=g, pg=pg):
            lows = low_half((blk, LANES))
            result = []
            for hh in range(2):
                r = ds(hh * tokens + i * blk, blk)
                p = pg[r].astype(F32)
                grad_p = dot_nt(dos[r], vdup[g])
                delta = jnp.sum(p * grad_p, axis=1, keepdims=True)
                scores = (p * (grad_p - delta) * (1.0 / math.sqrt(HD))).astype(BF16)
                pg[r] = scores
                result.append(dot_nn(scores, kdup[g]))
            dq[g, ds(i * blk, blk)] = jnp.where(lows, result[0], result[1])

        dk[g] = dot_tn(pg[...], qs[...])

    def fold(value):
        return value + pltpu.roll(value, HD, 1)

    def turn_back(values, grad_rot, gain, r):
        u = grad_rot * sin[r]
        early = first_quarter(u.shape)
        grad = grad_rot * cos[r] + jnp.where(
            early, pltpu.roll(u, LANES - HD // 2, 1), -pltpu.roll(u, HD // 2, 1)
        )
        scale = lax.rsqrt(head_mean(values * values) + EPSILON)
        weighted = grad * gain
        inner = head_mean(weighted * values)
        term = jnp.sum(grad * values * scale, axis=0, keepdims=True)
        return scale * (weighted - values * scale * scale * inner), fold(term)

    def unrotate():
        cos_load.wait()
        sin_load.wait()
        raw_load.wait()

        @pl.loop(0, tokens // blk)
        def _(i):
            r = ds(i * blk, blk)
            lows = low_half((blk, LANES))
            q_term = k_term = jnp.zeros((1, LANES), F32)
            for n in range(groups):
                grad, term = turn_back(raw[n, r], dq[n, r], gain["q"], r)
                dqkv[r, n * LANES : (n + 1) * LANES] = grad.astype(BF16)
                q_term += term
            for n in range(groups // 2):
                pair = jnp.where(lows, fold(dk[2 * n, r]), fold(dk[2 * n + 1, r]))
                grad, term = turn_back(raw[groups + n, r], pair, gain["k"], r)
                dqkv[r, q_wide + n * LANES : q_wide + (n + 1) * LANES] = grad.astype(BF16)
                k_term += term
                pair = jnp.where(lows, fold(dv[2 * n, r]), fold(dv[2 * n + 1, r]))
                dqkv[r, q_wide + kv_wide + n * LANES : q_wide + kv_wide + (n + 1) * LANES] = pair.astype(BF16)
            terms[0:1, wide:] += jnp.where(low_half((1, LANES)), q_term, k_term)

    def send_input():
        gain["weights"].wait()

        @pl.loop(0, wide // 256)
        def _(n):
            r = ds(n * 256, 256)
            n1send[:, r] = dot_nt(dqkv[ds(theirs, half)], weights[r]).astype(BF16)

        n_copy.start()

    def projection_grads():
        n1_load.wait()
        transpose(stage.at[0], turned2)

        @pl.loop(0, wide // 256)
        def _(m):
            r = ds(m * 256, 256)
            for n in range(o_at // 256):
                cols = slice(n * 256, (n + 1) * 256)
                pa[r, cols] = dot_nn(turned2[r], dqkv[:, cols]).astype(BF16)

    def output():
        om_load.wait()
        o_copy.wait_recv()

        @pl.loop(0, half // 64)
        def _(i):
            r = ds(i * 64, 64)
            bo_out[r] = (gi_out[r] + orecv[r].astype(F32)).astype(BF16)

    def own_input():
        @pl.loop(0, wide // 256)
        def _(n):
            r = ds(n * 256, 256)
            gi_out[:, r] = dot_nt(dqkv[ds(mine, half)], weights[r])

    def input_grads():
        n_copy.wait_recv()

        @pl.loop(0, half // 32)
        def _(i):
            r = ds(i * 32, 32)
            grad = gi_out[r] + n1recv[r].astype(F32)
            values = x_ref[r].astype(F32)
            scale = lax.rsqrt(jnp.mean(values * values, axis=-1, keepdims=True) + EPSILON)
            terms[0:1, :wide] += jnp.sum(grad * values * scale, axis=0, keepdims=True)
            gi_out[r] = gh[r] + rms_backward(values, scale, gain["attn"], grad)

        t_copy.start()

    def gain_grads():
        t_copy.wait_recv()

        both = terms[...] + terms_in[...]
        padded = jnp.concatenate([both[:, :wide], jnp.zeros((LANES - 8, wide), F32)], axis=0)
        pa[:, g_at : g_at + LANES] = padded.T.astype(BF16)
        head = lax.rem(lax.broadcasted_iota(jnp.int32, (wide, LANES), 0), rows) == 0
        pa[:, g_at + LANES :] = jnp.where(head, both[0:1, wide:], 0.0).astype(BF16)
    steps = {
        "weights": weight_grads, "residual": residual, "attended": attended_grads, "heads": heads,
        "unrotate": unrotate, "send": send_input, "projection": projection_grads, "output": output,
        "own": own_input, "input": input_grads, "gains": gain_grads,
        "S": scatter.start, "P": scatter.chip, "C": scatter.chain,
    }
    waited = set()
    for name, *which in BACKWARD_ORDER:
        if name == "weights" and which[0] == 2:
            scatter.swapped(FLIPPED)
            waited.add(FLIPPED)
        steps[name](*which)
    for copy in (g_copy, o_copy, r_copy, n_copy, t_copy):
        copy.wait_send()
    for k in range(count):
        if k not in waited:
            scatter.swapped(k)
        scatter.finish(k)


def backward(dp, x, dy, saved, q_wide, kv_wide, ff_wide):
    half, wide = x.shape
    rows, tokens = wide // dp, 2 * half
    groups = q_wide // LANES
    length = layout_of(dp)[0]
    chunks = chunk_widths(ff_wide)
    widths = [3 * w for w in chunks] + [q_wide, q_wide + 2 * kv_wide, 2 * LANES]
    shapes = [
        ((half, wide), BF16),
        ((half, wide), F32),
        ((rows, 2 * LANES), F32),
        ((rows, q_wide), F32),
        ((2, rows, kv_wide), F32),
        ((rows, q_wide), F32),
        ((2, rows, ff_wide), F32),
        ((rows, ff_wide), F32),
    ]
    vmem = [
        ((wide, widths[0]), BF16),
        ((wide, max(widths[1:3])), BF16),
        ((wide, sum(widths[CHUNKS:])), BF16),
        ((2, tokens, wide), BF16),
        ((wide, tokens), BF16),
        ((wide, tokens), BF16),
        ((2, 3, tokens, 256), BF16),
        ((2, 2 * tokens, tokens), BF16),
        ((groups + groups // 2, tokens, LANES), F32),
        ((groups, tokens, LANES), BF16),
        ((groups, tokens, LANES), BF16),
        ((groups, tokens, LANES), BF16),
        ((tokens, q_wide), BF16),
        ((wide, q_wide + 2 * kv_wide), BF16),
        ((wide, 2 * LANES), BF16),
        ((tokens, LANES), F32),
        ((tokens, LANES), F32),
        ((half, wide), F32),
        ((half, wide), F32),
        ((half, wide), BF16),
        ((half, wide), BF16),
        ((tokens, wide), BF16),
        ((half, wide), BF16),
        ((half, wide), BF16),
        ((groups, tokens, LANES), BF16),
        ((2 * tokens, LANES), BF16),
        ((2 * tokens, LANES), BF16),
        ((groups, tokens, LANES), F32),
        ((groups, tokens, LANES), F32),
        ((groups, tokens, LANES), F32),
        ((tokens, q_wide + 2 * kv_wide), BF16),
        ((8, wide + LANES), F32),
        ((8, wide + LANES), F32),
    ]
    for slots, turned in ((dp // 2, dp // 2), (length, 1), (length + 1, 2 * length + 2)):
        vmem += [((turned if k == FLIPPED else slots, rows, w), BF16) for k, w in enumerate(widths)]
    count = len(widths)
    return pl.pallas_call(
        functools.partial(bwd_kernel, dp, rows, half),
        out_shape=[jax.ShapeDtypeStruct(*s) for s in shapes],
        in_specs=[pl.BlockSpec(memory_space=pltpu.VMEM)] * 2
        + [pl.BlockSpec(memory_space=pl.ANY)] * len(saved),
        out_specs=[pl.BlockSpec(memory_space=pltpu.VMEM)] * len(shapes),
        scratch_shapes=[pltpu.VMEM(*s) for s in vmem]
        + [
            pltpu.SemaphoreType.DMA((count, n))
            for n in (dp // 2, length, 2 * length, dp // 2, length, 2 * length, 2 * length)
        ]
        + [
            pltpu.SemaphoreType.DMA((5, 2)),
            pltpu.SemaphoreType.DMA((24,)),
            pltpu.SemaphoreType.DMA((2, 3)),
        ],
        compiler_params=pltpu.CompilerParams(
            collective_id=4, has_side_effects=True, vmem_limit_bytes=63 * 1024 * 1024
        ),
        name="backward",
    )(x, dy, *saved)


def pack_gains(norm_gains, qk_gains, shard):
    o = lax.axis_index("dp")
    qk_shard = qk_gains.shape[1]
    cols = jnp.pad(norm_gains.T, ((0, 0), (0, LANES - 2)))
    row = jnp.zeros((1, LANES), BF16)
    for i in range(2):
        row = lax.dynamic_update_slice(row, qk_gains[i : i + 1], (0, i * HD + o * qk_shard))
    return jnp.concatenate([cols, jnp.pad(row, ((0, shard - 1), (0, 0)))], axis=1)


def fast_device(
    block_input, cotangent, segment_ids, positions, norm_gains, qk_gains, w_query, w_keyval, w_output,
    w_gate_up, w_down,
):
    dp = lax.axis_size("dp")
    shard, q_wide = w_query.shape
    kv_wide, ff_wide = w_keyval.shape[2], w_gate_up.shape[2]
    qk_shard = qk_gains.shape[1]
    freqs = ROPE_BASE ** (-jnp.arange(0, HD, 2).astype(F32) / HD)
    freq = jnp.tile(freqs, 4)[None]
    saved = forward(
        dp, block_input, cotangent, segment_ids, positions, freq, pack_gains(norm_gains, qk_gains, shard),
        w_query, w_keyval, w_output.T, w_gate_up, w_down.T,
    )
    block_output, grad_input, gains, grad_query, grad_keyval, grad_out, grad_gate_up, grad_down = backward(
        dp, block_input, cotangent, saved, q_wide, kv_wide, ff_wide
    )
    o = lax.axis_index("dp")
    qk = [lax.dynamic_slice(gains, (0, LANES + i * HD + o * qk_shard), (1, qk_shard)) for i in range(2)]
    return (
        block_output,
        grad_input,
        gains[:, 0:2].T,
        jnp.concatenate(qk),
        grad_query,
        grad_keyval,
        grad_out.T,
        grad_gate_up,
        grad_down.T,
    )


def solution(mesh):
    return jax.shard_map(
        fast_device if mesh.shape["tensor"] == 2 and mesh.shape["dp"] == 16 else on_device,
        mesh=mesh,
        in_specs=(
            P(("dp", "tensor"), None),
            P(("dp", "tensor"), None),
            P("dp", None),
            P("dp", None),
            P(None, "dp"),
            P(None, "dp"),
            P("dp", "tensor"),
            P(None, "dp", "tensor"),
            P("tensor", "dp"),
            P(None, "dp", "tensor"),
            P("tensor", "dp"),
        ),
        out_specs=(
            P(("dp", "tensor"), None),
            P(("dp", "tensor"), None),
            P(None, "dp"),
            P(None, "dp"),
            P("dp", "tensor"),
            P(None, "dp", "tensor"),
            P("tensor", "dp"),
            P(None, "dp", "tensor"),
            P("tensor", "dp"),
        ),
        check_vma=False,
    )
```

```python
import functools
import math

import jax
import jax.numpy as jnp
import numpy as np
from jax import lax
from jax.experimental import pallas as pl
from jax.experimental.pallas import tpu as pltpu
from jax.sharding import PartitionSpec as P

HD = 64


EPSILON = 1e-05
ROPE_BASE = 1000000.0
NEG_FILL = -1e30


def rms_forward(values, gain):
    scale = lax.rsqrt(jnp.mean(values * values, axis=-1, keepdims=True) + EPSILON)
    return (values * scale * gain, scale)


def rms_backward(values, scale, gain, grad):
    weighted = grad * gain
    inner = jnp.mean(weighted * values, axis=-1, keepdims=True)
    return scale * (weighted - values * scale * scale * inner)


def rope_tables(places):
    freqs = ROPE_BASE ** (-jnp.arange(0, HD, 2).astype(jnp.float32) / HD)
    angles = places.astype(jnp.float32)[..., None] * freqs
    angles = jnp.concatenate([angles, angles], axis=-1)
    return (jnp.cos(angles), jnp.sin(angles))


def rotate_half(values):
    half = values.shape[-1] // 2
    return jnp.concatenate([-values[..., half:], values[..., :half]], axis=-1)


def rotate_back(values):
    half = values.shape[-1] // 2
    return jnp.concatenate([values[..., half:], -values[..., :half]], axis=-1)


def allowed_mask(segs):
    length = segs.shape[0]
    index = jnp.arange(length, dtype=jnp.int32)
    return (segs[:, None] == segs[None, :]) & (index[None, :] <= index[:, None])


def contract(left, right, left_dim, right_dim):
    return lax.dot_general(
        left, right, (((left_dim,), (right_dim,)), ((), ())), preferred_element_type=jnp.float32
    )


def fdot(left, right):
    return jnp.dot(left, right, preferred_element_type=jnp.float32)


def row_scores(q_rot, k_rot):
    kv_heads = k_rot.shape[1]
    groups = q_rot.shape[1] // kv_heads
    q_four = q_rot.reshape(q_rot.shape[0], kv_heads, groups, HD)
    scores = jnp.einsum("ikgd,jkd->kgij", q_four, k_rot, preferred_element_type=jnp.float32)
    return (scores / math.sqrt(HD), q_four)


def attend_row(q_rot, k_rot, values, segs):
    scores, q_four = row_scores(q_rot, k_rot)
    allowed = allowed_mask(segs)[None, None]
    masked = jnp.where(allowed, scores, NEG_FILL)
    top = jnp.max(masked, axis=-1, keepdims=True)
    expd = jnp.where(allowed, jnp.exp(masked - top), 0.0)
    total = jnp.sum(expd, axis=-1, keepdims=True)
    probs = (expd / total).astype(jnp.bfloat16)
    log_total = top[..., 0] + jnp.log(total[..., 0])
    attended = jnp.einsum("kgij,jkd->ikgd", probs, values, preferred_element_type=jnp.float32)
    return (attended.reshape(q_rot.shape).astype(jnp.bfloat16), log_total)


def back_row(q_rot, k_rot, values, grad_att, log_total, segs):
    scores, q_four = row_scores(q_rot, k_rot)
    allowed = allowed_mask(segs)[None, None]
    masked = jnp.where(allowed, scores, NEG_FILL)
    probs = jnp.where(allowed, jnp.exp(masked - log_total[..., None]), 0.0)
    probs_b = probs.astype(jnp.bfloat16)
    grad_four = grad_att.reshape(q_four.shape)
    grad_values = jnp.einsum(
        "kgij,ikgd->jkd", probs_b, grad_four, preferred_element_type=jnp.float32
    )
    grad_p = jnp.einsum("ikgd,jkd->kgij", grad_four, values, preferred_element_type=jnp.float32)
    delta = jnp.sum(probs * grad_p, axis=-1, keepdims=True)
    d_scores = (probs * (grad_p - delta) / math.sqrt(HD)).astype(jnp.bfloat16)
    grad_q = jnp.einsum(
        "kgij,jkd->ikgd", d_scores, k_rot, preferred_element_type=jnp.float32
    ).reshape(q_rot.shape)
    grad_k = jnp.einsum("kgij,ikgd->jkd", d_scores, q_four, preferred_element_type=jnp.float32)
    return (grad_q, grad_k, grad_values)


def layout_of(dp):
    if dp == 16:
        return (4, 4, 2)
    return (dp // 4, 2, dp // 2)


class Place:
    def __init__(self, dp):
        self.length, self.zs, self.xs = layout_of(dp)
        me = lax.axis_index("dp")
        self.z = lax.rem(me // self.zs, self.length)
        self.x = lax.rem(me // self.xs, 2)
        self.c = lax.rem(me, 2)

    def device(self, z, x, c):
        return z * self.zs + x * self.xs + c

    def greet(self):
        z, x, c = self.z, self.x, self.c
        barrier = pltpu.get_barrier_semaphore()

        def signal(target):
            pl.semaphore_signal(
                barrier, inc=1, device_id={"dp": target}, device_id_type=pl.DeviceIdType.MESH
            )

        signal(self.device(z, x, 1 - c))
        signal(self.device(z, 1 - x, c))
        pl.when(z > 0)(lambda: signal(self.device(z - 1, x, c)))
        pl.when(z < self.length - 1)(lambda: signal(self.device(z + 1, x, c)))
        ends = jnp.where(z > 0, 1, 0) + jnp.where(z < self.length - 1, 1, 0)
        pl.semaphore_wait(barrier, 2 + ends)


def remote(src, dst, send, recv, target):
    return pltpu.make_async_remote_copy(
        src_ref=src,
        dst_ref=dst,
        send_sem=send,
        recv_sem=recv,
        device_id={"dp": target},
        device_id_type=pl.DeviceIdType.MESH,
    )


def gather_kernel(dp, count, rows, *refs):
    ins, outs = refs[:count], refs[count : 2 * count]
    send, recv, local = refs[2 * count :]
    at = Place(dp)
    z, x, c, length = at.z, at.x, at.c, at.length
    below, above = at.device(z - 1, x, c), at.device(z + 1, x, c)
    beside, sibling = at.device(z, 1 - x, c), at.device(z, x, 1 - c)
    at.greet()
    own = at.device(z, x, c)

    def slab(k, o):
        return outs[k].at[pl.ds(pl.multiple_of(o * rows, rows), rows)]

    for k in range(count):
        pltpu.make_async_copy(ins[k], slab(k, own), local.at[k]).start()

    def move(k, oz, ox, way, target, first):
        o = at.device(oz, ox, c)
        src = ins[k] if first else slab(k, o)
        return remote(src, slab(k, o), send.at[k, oz * 2 + ox, way], recv.at[k, o], target)

    def arrived(k, o):
        remote(slab(k, o), slab(k, o), send.at[k, 0, 0], recv.at[k, o], sibling).wait_recv()

    def steps(act):
        for s in range(length):
            for sign in (1, -1) if s else (0,):
                oz = z - s * sign

                def event(oz=oz, s=s, sign=sign):
                    for k in range(count):
                        act(k, oz, s, sign)

                if s:
                    pl.when((oz >= 0) & (oz < length))(event)
                else:
                    event()
            if s:
                side(s - 1, act)
        side(length - 1, act)

    def side(s, act):
        for sign in (1, -1) if s else (0,):
            oz = z - s * sign

            def event(oz=oz):
                for k in range(count):
                    act(k, oz, None, 0)

            if s:
                pl.when((oz >= 0) & (oz < length))(event)
            else:
                event()

    def begin(k, oz, s, sign):
        if s is None:
            arrived(k, at.device(oz, 1 - x, c))
            move(k, oz, 1 - x, 3, sibling, False).start()
            return
        first = s == 0
        if not first:
            arrived(k, at.device(oz, x, c))
        if sign >= 0:
            pl.when(z < length - 1)(lambda: move(k, oz, x, 0, above, first).start())
        if sign <= 0:
            pl.when(z > 0)(lambda: move(k, oz, x, 1, below, first).start())
        move(k, oz, x, 2, beside, first).start()
        move(k, oz, x, 3, sibling, first).start()

    def finish(k, oz, s, sign):
        if s is None:
            move(k, oz, 1 - x, 3, sibling, False).wait_send()
            return
        first = s == 0
        if sign >= 0:
            pl.when(z < length - 1)(lambda: move(k, oz, x, 0, above, first).wait_send())
        if sign <= 0:
            pl.when(z > 0)(lambda: move(k, oz, x, 1, below, first).wait_send())
        move(k, oz, x, 2, beside, first).wait_send()
        move(k, oz, x, 3, sibling, first).wait_send()

    steps(begin)
    for oz in range(length):
        for ox in range(2):
            for k in range(count):
                arrived(k, at.device(oz, ox, 1 - c))
    steps(finish)
    for k in range(count):
        pltpu.make_async_copy(ins[k], slab(k, own), local.at[k]).wait()


def gather_rows(arrays, dp):
    count, rows = len(arrays), arrays[0].shape[0]
    return pl.pallas_call(
        functools.partial(gather_kernel, dp, count, rows),
        out_shape=[jax.ShapeDtypeStruct((dp * rows, a.shape[1]), a.dtype) for a in arrays],
        in_specs=[pl.BlockSpec(memory_space=pltpu.VMEM)] * count,
        out_specs=[pl.BlockSpec(memory_space=pl.ANY)] * count,
        scratch_shapes=[
            pltpu.SemaphoreType.DMA((count, dp // 2, 4)),
            pltpu.SemaphoreType.DMA((count, dp)),
            pltpu.SemaphoreType.DMA((count,)),
        ],
        compiler_params=pltpu.CompilerParams(collective_id=1, has_side_effects=True),
        name="gather_rows",
    )(*arrays)


def scatter_kernel(dp, count, rows, *refs):
    parts, outs = refs[:count], refs[count : 2 * count]
    mine, first, second, upward, downward = (
        refs[(2 + i) * count : (3 + i) * count] for i in range(5)
    )
    sent1, sent2, sent4, got1, got2, got_up, got_down, local = refs[7 * count :]
    at = Place(dp)
    z, x, c, length = at.z, at.x, at.c, at.length
    below, above = at.device(z - 1, x, c), at.device(z + 1, x, c)
    beside, sibling = at.device(z, 1 - x, c), at.device(z, x, 1 - c)
    at.greet()

    def slab(k, o):
        return parts[k].at[pl.ds(pl.multiple_of(o * rows, rows), rows)]

    def swap(k, t, ox):
        q = t * 2 + ox
        return remote(
            slab(k, at.device(t, ox, 1 - c)), first[k].at[q], sent1.at[k, q], got1.at[k, q], sibling
        )

    def keep(k, t, ox):
        q = t * 2 + ox
        return pltpu.make_async_copy(slab(k, at.device(t, ox, c)), mine[k].at[q], local.at[k, q])

    def cross(k, t):
        q = t * 2 + 1 - x
        return remote(first[k].at[q], second[k].at[t], sent2.at[k, t], got2.at[k, t], beside)

    def rise(k, t):
        return remote(second[k].at[t], upward[k].at[t], sent4.at[k, t], got_up.at[k, t], above)

    def fall(k, t):
        return remote(second[k].at[t], downward[k].at[t], sent4.at[k, t], got_down.at[k, t], below)

    def targets(act):
        for d in range(length - 1, -1, -1):
            for sign in (1, -1) if d else (0,):
                t = z + d * sign

                def event(t=t, sign=sign):
                    for k in range(count):
                        act(k, t, sign)

                if d:
                    pl.when((t >= 0) & (t < length))(event)
                else:
                    event()

    def wide(value):
        return value.astype(jnp.float32)

    def start(k, t, sign):
        for ox in (1 - x, x):
            swap(k, t, ox).start()
            keep(k, t, ox).start()

    def chip_sum(k, t, sign):
        for ox in (1 - x, x):
            q = t * 2 + ox
            keep(k, t, ox).wait()
            swap(k, t, ox).wait_recv()
            first[k][q] = (wide(first[k][q]) + wide(mine[k][q])).astype(jnp.bfloat16)
            if ox is not x:
                cross(k, t).start()

    def chain(k, t, sign):
        cross(k, t).wait_recv()
        if sign == 0:
            outs[k][...] = wide(second[k][t]) + wide(first[k][t * 2 + x])

            def add_up():
                rise(k, t).wait_recv()
                outs[k][...] += wide(upward[k][t])

            def add_down():
                fall(k, t).wait_recv()
                outs[k][...] += wide(downward[k][t])

            pl.when(z > 0)(add_up)
            pl.when(z < length - 1)(add_down)
            return
        base, move = (upward, rise) if sign > 0 else (downward, fall)
        inner = z > 0 if sign > 0 else z < length - 1

        def middle():
            move(k, t).wait_recv()
            second[k][t] = (
                wide(second[k][t]) + wide(first[k][t * 2 + x]) + wide(base[k][t])
            ).astype(jnp.bfloat16)

        def edge():
            second[k][t] = (wide(second[k][t]) + wide(first[k][t * 2 + x])).astype(jnp.bfloat16)

        pl.when(inner)(middle)
        pl.when(jnp.logical_not(inner))(edge)
        move(k, t).start()

    def finish(k, t, sign):
        swap(k, t, 0).wait_send()
        swap(k, t, 1).wait_send()
        cross(k, t).wait_send()
        if sign:
            (rise if sign > 0 else fall)(k, t).wait_send()

    targets(start)
    targets(chip_sum)
    targets(chain)
    targets(finish)


def scatter_rows(arrays, dp):
    count, rows = len(arrays), arrays[0].shape[0] // dp
    length = layout_of(dp)[0]
    slots = [dp // 2, dp // 2, length, length, length]
    return pl.pallas_call(
        functools.partial(scatter_kernel, dp, count, rows),
        out_shape=[jax.ShapeDtypeStruct((rows, a.shape[1]), jnp.float32) for a in arrays],
        in_specs=[pl.BlockSpec(memory_space=pl.ANY)] * count,
        out_specs=[pl.BlockSpec(memory_space=pltpu.VMEM)] * count,
        scratch_shapes=[
            pltpu.VMEM((n, rows, a.shape[1]), a.dtype) for n in slots for a in arrays
        ]
        + [
            pltpu.SemaphoreType.DMA((count, n))
            for n in (dp // 2, length, length, dp // 2, length, length, length, dp // 2)
        ],
        compiler_params=pltpu.CompilerParams(
            collective_id=2, has_side_effects=True, vmem_limit_bytes=60 * 1024 * 1024
        ),
        name="scatter_rows",
    )(*arrays)


def exchange(values):
    return lax.ppermute(values, "tensor", ((0, 1), (1, 0)))


def collect(values):
    if lax.axis_size("tensor") != 2:
        return lax.all_gather(values, "tensor", axis=0, tiled=True)
    other = exchange(values)
    low = lax.axis_index("tensor") == 0
    return jnp.concatenate([jnp.where(low, values, other), jnp.where(low, other, values)])


def spread(values):
    if lax.axis_size("tensor") != 2:
        return lax.psum_scatter(values, "tensor", scatter_dimension=0, tiled=True)
    half = values.shape[0] // 2
    low = lax.axis_index("tensor") == 0
    head, tail = values[:half], values[half:]
    other = exchange(jnp.where(low, tail, head).astype(jnp.bfloat16))
    return jnp.where(low, head, tail) + other.astype(jnp.float32)


def total(values):
    if lax.axis_size("tensor") != 2:
        return lax.psum(values, "tensor")
    return values + exchange(values)


def on_device(
    block_input,
    cotangent,
    segment_ids,
    positions,
    norm_gains,
    qk_gains,
    w_query,
    w_keyval,
    w_output,
    w_gate_up,
    w_down,
):
    dp = lax.axis_size("dp")
    rows_here, row_len = segment_ids.shape
    tokens_here = rows_here * row_len
    shard, q_wide = w_query.shape
    kv_wide, ff_wide = w_keyval.shape[2], w_gate_up.shape[2]
    qk_shard = qk_gains.shape[1]
    gains = jnp.concatenate(
        [norm_gains.T, jnp.pad(qk_gains.T, ((0, shard - qk_shard), (0, 0)))], axis=1
    )
    gains = jnp.pad(gains, ((0, 0), (0, 124)))
    attn_pack = jnp.concatenate([w_query, w_keyval[0], w_keyval[1], w_output.T, gains], axis=1)
    gate_up_pack = jnp.concatenate([w_gate_up[0], w_gate_up[1]], axis=1)
    attn_full, gate_up_full, down_full = gather_rows([attn_pack, gate_up_pack, w_down.T], dp)
    qkv_wide = q_wide + 2 * kv_wide
    qkv_full = attn_full[:, :qkv_wide]
    output_full = attn_full[:, qkv_wide : qkv_wide + q_wide]
    gain_cols = attn_full[:, qkv_wide + q_wide :].astype(jnp.float32)
    gain_attn, gain_ffn = gain_cols[:, 0], gain_cols[:, 1]
    qk_cols = gain_cols.reshape(dp, shard, 128)[:, :qk_shard, 2:4].reshape(dp * qk_shard, 2)
    gain_q, gain_k = qk_cols[:, 0], qk_cols[:, 1]
    heads_here = q_wide // HD
    kv_here = kv_wide // HD
    dy_rows = collect(cotangent)
    xlocal = block_input.astype(jnp.float32)
    normed_f, scale1 = rms_forward(xlocal, gain_attn)
    normed1 = collect(normed_f.astype(jnp.bfloat16))
    qkv = fdot(normed1, qkv_full)
    query = qkv[:, :q_wide].reshape(rows_here, row_len, heads_here, HD)
    keys = qkv[:, q_wide : q_wide + kv_wide].reshape(rows_here, row_len, kv_here, HD)
    values = (
        qkv[:, q_wide + kv_wide :].astype(jnp.bfloat16).reshape(rows_here, row_len, kv_here, HD)
    )
    q_norm, q_scale = rms_forward(query, gain_q)
    k_norm, k_scale = rms_forward(keys, gain_k)
    cosv, sinv = rope_tables(positions)
    cosv = cosv[:, :, None, :]
    sinv = sinv[:, :, None, :]
    q_rot = (q_norm * cosv + rotate_half(q_norm) * sinv).astype(jnp.bfloat16)
    k_rot = (k_norm * cosv + rotate_half(k_norm) * sinv).astype(jnp.bfloat16)
    attended, log_total = jax.vmap(attend_row)(q_rot, k_rot, values, segment_ids)
    att_flat = attended.reshape(tokens_here, heads_here * HD)
    hidden = xlocal + spread(contract(att_flat, output_full, 1, 1))
    normed_g, scale2 = rms_forward(hidden, gain_ffn)
    normed2 = collect(normed_g.astype(jnp.bfloat16))
    gate_up = fdot(normed2, gate_up_full)
    gate_proj, up_proj = gate_up[:, :ff_wide], gate_up[:, ff_wide:]
    sigmoid_gate = jax.nn.sigmoid(gate_proj)
    silu_gate = gate_proj * sigmoid_gate
    act = (silu_gate * up_proj).astype(jnp.bfloat16)
    block_output = (hidden + spread(contract(act, down_full, 1, 1))).astype(jnp.bfloat16)
    grad_act = fdot(dy_rows, down_full)
    grad_down = contract(dy_rows, act, 0, 0).astype(jnp.bfloat16)
    d_gate = grad_act * up_proj * sigmoid_gate * (1.0 + gate_proj * (1.0 - sigmoid_gate))
    d_gate_up = jnp.concatenate(
        [d_gate.astype(jnp.bfloat16), (grad_act * silu_gate).astype(jnp.bfloat16)], axis=1
    )
    grad_gate_up = contract(normed2, d_gate_up, 0, 0).astype(jnp.bfloat16)
    grad_n2 = spread(contract(d_gate_up, gate_up_full, 1, 1))
    gain_ffn_grad = jnp.sum(grad_n2 * hidden * scale2, axis=0)
    grad_hidden = cotangent.astype(jnp.float32) + rms_backward(hidden, scale2, gain_ffn, grad_n2)
    grad_rows = collect(grad_hidden.astype(jnp.bfloat16))
    grad_att = (
        fdot(grad_rows, output_full)
        .astype(jnp.bfloat16)
        .reshape(rows_here, row_len, heads_here, HD)
    )
    grad_out = contract(grad_rows, att_flat, 0, 0).astype(jnp.bfloat16)
    grad_qrot, grad_krot, grad_vals = jax.vmap(back_row)(
        q_rot, k_rot, values, grad_att, log_total, segment_ids
    )
    grad_qn = grad_qrot * cosv + rotate_back(grad_qrot * sinv)
    grad_kn = grad_krot * cosv + rotate_back(grad_krot * sinv)
    gain_q_grad = jnp.sum(grad_qn * query * q_scale, axis=(0, 1, 2))
    gain_k_grad = jnp.sum(grad_kn * keys * k_scale, axis=(0, 1, 2))
    d_query = rms_backward(query, q_scale, gain_q, grad_qn).astype(jnp.bfloat16)
    d_keys = rms_backward(keys, k_scale, gain_k, grad_kn).astype(jnp.bfloat16)
    d_qkv = jnp.concatenate(
        [
            d_query.reshape(tokens_here, q_wide),
            d_keys.reshape(tokens_here, kv_wide),
            grad_vals.astype(jnp.bfloat16).reshape(tokens_here, kv_wide),
        ],
        axis=1,
    )
    grad_qkv = contract(normed1, d_qkv, 0, 0).astype(jnp.bfloat16)
    grad_n1 = spread(contract(d_qkv, qkv_full, 1, 1))
    gain_attn_grad = jnp.sum(grad_n1 * xlocal * scale1, axis=0)
    grad_input = grad_hidden + rms_backward(xlocal, scale1, gain_attn, grad_n1)
    gain_terms = total(
        jnp.concatenate([gain_attn_grad, gain_ffn_grad, gain_q_grad, gain_k_grad])[None]
    )[0]
    wide = dp * shard
    norm_terms = gain_terms[: 2 * wide].reshape(2, wide).T
    qk_terms = gain_terms[2 * wide :].reshape(2, dp, qk_shard).transpose(1, 2, 0)
    qk_terms = jnp.pad(qk_terms, ((0, 0), (0, shard - qk_shard), (0, 0))).reshape(wide, 2)
    gain_pack = jnp.concatenate([norm_terms, qk_terms], axis=1).astype(jnp.bfloat16)
    gain_pack = jnp.pad(gain_pack, ((0, 0), (0, 124)))
    grad_attn = jnp.concatenate([grad_qkv, grad_out, gain_pack], axis=1)
    attn_sum, gate_up_sum, down_sum = scatter_rows([grad_attn, grad_gate_up, grad_down], dp)
    gain_sum = attn_sum[:, qkv_wide + q_wide :]
    return (
        block_output,
        grad_input,
        gain_sum[:, 0:2].T,
        gain_sum[:qk_shard, 2:4].T,
        attn_sum[:, :q_wide],
        jnp.stack([attn_sum[:, q_wide : q_wide + kv_wide], attn_sum[:, q_wide + kv_wide : qkv_wide]]),
        attn_sum[:, qkv_wide : qkv_wide + q_wide].T,
        jnp.stack([gate_up_sum[:, :ff_wide], gate_up_sum[:, ff_wide:]]),
        down_sum.T,
    )


MESH = pl.DeviceIdType.MESH
LANES = 128
F32, BF16 = jnp.float32, jnp.bfloat16


def dot_nn(a, b):
    return lax.dot_general(a, b, (((1,), (0,)), ((), ())), preferred_element_type=F32)


def dot_nt(a, b):
    return lax.dot_general(a, b, (((1,), (1,)), ((), ())), preferred_element_type=F32)


def dot_tn(a, b):
    return lax.dot_general(a, b, (((0,), (0,)), ((), ())), preferred_element_type=F32)


def lane_of(shape):
    return lax.broadcasted_iota(jnp.int32, shape, len(shape) - 1)


def head_mean(values):
    row = lax.broadcasted_iota(jnp.int32, (LANES, LANES), 0) // HD
    ones = jnp.where(row == lane_of((LANES, LANES)) // HD, 1.0 / HD, 0.0).astype(BF16)
    high = values.astype(BF16)
    low = (values - high.astype(F32)).astype(BF16)
    return dot_nn(high, ones) + dot_nn(low, ones)


def low_half(shape):
    return lane_of(shape) < HD


def first_quarter(shape):
    return lax.rem(lane_of(shape), HD) < HD // 2


def ds(start, size):
    if isinstance(start, int):
        return pl.ds(start, size)
    return pl.ds(pl.multiple_of(start, size), size)


class Gather:
    def __init__(self, at, rows, slabs, flipped, send, recv):
        self.at, self.rows, self.slabs, self.flipped = at, rows, slabs, flipped
        self.send, self.recv = send, recv

    def slab(self, k, o):
        return self.slabs[k](ds(o * self.rows[k], self.rows[k]))

    def move(self, k, oz, ox, way, target):
        at = self.at
        o = at.device(oz, ox, at.c)
        return remote(
            self.slab(k, o), self.slab(k, o), self.send.at[k, oz * 2 + ox, way], self.recv.at[k, o], target
        )

    def arrived(self, k, o):
        at = self.at
        slab = self.slab(k, o)
        remote(slab, slab, self.send.at[k, 0, 0], self.recv.at[k, o], at.sibling).wait_recv()

    def sources(self, s, act):
        at = self.at
        for sign in (1, -1) if s else (0,):
            oz = at.z - s * sign
            if s:
                pl.when((oz >= 0) & (oz < at.length))(lambda oz=oz, sign=sign: act(oz, sign))
            else:
                act(oz, 0)

    def along(self, k, oz, ox, sign, act):
        at = self.at
        if sign >= 0:
            pl.when(at.z < at.length - 1)(lambda: act(self.move(k, oz, ox, 0, at.above)))
        if sign <= 0:
            pl.when(at.z > 0)(lambda: act(self.move(k, oz, ox, 1, at.below)))

    def outgoing(self, k, s, oz, sign, act):
        at = self.at
        self.along(k, oz, at.x, sign, act)
        if not s or k not in self.flipped:
            act(self.move(k, oz, at.x, 2, at.beside))
        act(self.move(k, oz, at.x, 3, at.sibling))

    def onward(self, k, oz, sign, act):
        at = self.at
        if k in self.flipped:
            self.along(k, oz, 1 - at.x, sign, act)
        act(self.move(k, oz, 1 - at.x, 3, at.sibling))

    def main(self, k, s):
        at = self.at

        def act(oz, sign):
            if s:
                self.arrived(k, at.device(oz, at.x, at.c))
            self.outgoing(k, s, oz, sign, lambda m: m.start())

        self.sources(s, act)

    def side(self, k, s):
        at = self.at

        def act(oz, sign):
            self.arrived(k, at.device(oz, 1 - at.x, at.c))
            self.onward(k, oz, sign, lambda m: m.start())

        self.sources(s, act)

    def final(self, k):
        at = self.at
        for oz in range(at.length):
            for ox in range(2):
                self.arrived(k, at.device(oz, ox, 1 - at.c))

    def finish(self, k):
        at = self.at
        for s in range(at.length):
            self.sources(s, lambda oz, sign: self.outgoing(k, s, oz, sign, lambda m: m.wait_send()))
            self.sources(s, lambda oz, sign: self.onward(k, oz, sign, lambda m: m.wait_send()))


class Spot(Place):
    def __init__(self, dp):
        super().__init__(dp)
        z, x, c = self.z, self.x, self.c
        self.below, self.above = self.device(z - 1, x, c), self.device(z + 1, x, c)
        self.beside, self.sibling = self.device(z, 1 - x, c), self.device(z, x, 1 - c)
        self.own = self.device(z, x, c)
        self.t = lax.axis_index("tensor")

    def greet(self):
        barrier = pltpu.get_barrier_semaphore()

        def signal(target):
            pl.semaphore_signal(barrier, inc=1, device_id=target, device_id_type=MESH)

        signal({"dp": self.sibling})
        signal({"dp": self.beside})
        signal({"tensor": 1 - self.t})
        pl.when(self.z > 0)(lambda: signal({"dp": self.below}))
        pl.when(self.z < self.length - 1)(lambda: signal({"dp": self.above}))
        ends = jnp.where(self.z > 0, 1, 0) + jnp.where(self.z < self.length - 1, 1, 0)
        pl.semaphore_wait(barrier, 3 + ends)


def partner(at, src, dst, sems):
    return pltpu.make_async_remote_copy(
        src_ref=src,
        dst_ref=dst,
        send_sem=sems.at[0],
        recv_sem=sems.at[1],
        device_id={"tensor": 1 - at.t},
        device_id_type=MESH,
    )


CHUNKS = 3
GAIN_ROWS = 16
FLIPPED = 1


def chunk_widths(ff_wide):
    tiles = ff_wide // 256
    sizes = [tiles * 4 // 9, tiles * 2 // 9]
    return [256 * n for n in sizes + [tiles - sum(sizes)]]


FORWARD_ORDER = (
    ("M", 0, 0), ("fill",), ("M", 2, 0), ("D", 0, 0), ("M", 0, 1), ("D", 2, 0), ("M", 0, 2), ("M", 3, 0),
    ("tables",), ("M", 0, 3), ("D", 0, 1), ("M", 1, 0), ("D", 0, 2), ("M", 3, 1), ("D", 0, 3), ("F", 0),
    ("gains",), ("norm1",), ("project",), ("M", 1, 1), ("rotate",), ("attend0",), ("partial0",), ("M", 1, 2),
    ("attend1",), ("partial1",), ("D", 1, 0), ("M", 1, 3), ("norm2",), ("D", 2, 1), ("D", 3, 0), ("M", 3, 2),
    ("M", 2, 1), ("D", 1, 1), ("D", 2, 2), ("D", 1, 2), ("D", 1, 3), ("M", 3, 3), ("M", 2, 2), ("D", 3, 1),
    ("F", 1), ("own", 0), ("other", 0), ("D", 2, 3), ("combine", 0), ("M", 2, 3), ("D", 3, 2), ("D", 3, 3),
    ("F", 2), ("own", 1), ("other", 1), ("combine", 1), ("F", 3), ("own", 2), ("other", 2), ("combine", 2),
    ("close",),
)


def spread_gains(packed, dp, gain_rows):
    lows = low_half((1, LANES))
    qk = jnp.zeros((1, LANES), F32)
    for i in range(dp // 2):
        even = packed[2 * i * GAIN_ROWS : (2 * i + 1) * GAIN_ROWS].astype(F32)
        odd = packed[(2 * i + 1) * GAIN_ROWS : (2 * i + 2) * GAIN_ROWS].astype(F32)
        cols = slice(i * LANES, (i + 1) * LANES)
        gain_rows[0:1, cols] = jnp.where(lows, even[0:1], pltpu.roll(odd, HD, 1)[0:1])
        gain_rows[1:2, cols] = jnp.where(lows, pltpu.roll(even, HD, 1)[0:1], odd[0:1])
        qk += even[1:2] + odd[1:2]
    return qk


def fwd_kernel(
    dp, rows, half, x_ref, dy_ref, seg_ref, pos_ref, freq_ref, norm_ref, qk_ref, wq_ref, wkv_ref, wo_ref,
    wgu_ref, wd_ref,
    wa_out, wg_out, n1_out, raw_out, p_out, qrot_out, kdup_out, vdup_out, att_out, hidden_out, n2_out,
    dyf_out, act_out, dg_out, du_out, cos_out, sin_out, gnm_out, gno_out, om_out, oo_out,
    wa, wg, wf0, wf1, wf2, xf, dyf, n1, n2, raw, prob, qrot, kdup, vdup, att, hidden, act, dg, du, cos, sin,
    segc, gn, op, part_out, part_in, gno, oo, om, gain_rows,
    send, recv, ysem, outsem,
):
    at = Spot(dp)
    wide = dp * rows
    tokens = 2 * half
    q_wide, kv_wide, ff_wide = wq_ref.shape[1], wkv_ref.shape[2], wd_ref.shape[1]
    chunks = chunk_widths(ff_wide)
    wf = (wf0, wf1, wf2)
    o_at, g_at = q_wide + 2 * kv_wide, 2 * q_wide + 2 * kv_wide
    groups = q_wide // LANES
    mine, theirs = at.t * half, (1 - at.t) * half
    own_rows = ds(at.own * rows, rows)
    outs = []

    def put(src, dst):
        copy = pltpu.make_async_copy(src, dst, outsem.at[len(outs)])
        copy.start()
        outs.append(copy)

    at.greet()
    gather = Gather(
        at,
        [rows] * (CHUNKS + 1) + [GAIN_ROWS],
        [lambda r: wa.at[r]] + [lambda r, j=j: wf[j].at[r] for j in range(CHUNKS)] + [lambda r: wg.at[r]],
        (1 + FLIPPED,),
        send,
        recv,
    )
    wa[own_rows, 0:q_wide] = wq_ref[...]
    wa[own_rows, q_wide : q_wide + kv_wide] = wkv_ref[0]
    wa[own_rows, q_wide + kv_wide : o_at] = wkv_ref[1]
    wa[own_rows, o_at:g_at] = wo_ref[...]
    norms = jnp.concatenate([norm_ref[...].astype(F32), jnp.zeros((2, LANES - rows), F32)], axis=1)
    norms = jnp.concatenate([norms, jnp.zeros((6, LANES), F32)], axis=0)
    qk_shard = qk_ref.shape[1]
    qk = jnp.concatenate([qk_ref[...].astype(F32), jnp.zeros((2, LANES - qk_shard), F32)], axis=1)
    qk = jnp.concatenate([qk, jnp.zeros((6, LANES), F32)], axis=0)
    wg[ds(at.own * GAIN_ROWS, GAIN_ROWS)] = jnp.concatenate(
        [
            norms[0:1] + pltpu.roll(norms, rows, 1)[1:2],
            pltpu.roll(qk, at.own * qk_shard, 1)[0:1] + pltpu.roll(qk, at.own * qk_shard + HD, 1)[1:2],
            jnp.zeros((GAIN_ROWS - 2, LANES), F32),
        ],
        axis=0,
    ).astype(BF16)
    x_copy = partner(at, x_ref, xf.at[ds(mine, half)], ysem.at[0])
    dy_copy = partner(at, dy_ref, dyf.at[ds(mine, half)], ysem.at[1])
    out_copy = partner(at, part_out, part_in, ysem.at[2])
    n2_copy = partner(at, n2.at[ds(mine, half)], n2.at[ds(mine, half)], ysem.at[3])
    gain = {}
    blk = 128

    def fill():
        x_copy.start()
        dy_copy.start()
        for j, chunk in enumerate(chunks):
            cols = slice(sum(chunks[:j]), sum(chunks[: j + 1]))
            wf[j][own_rows, 0:chunk] = wgu_ref[0, :, cols]
            wf[j][own_rows, chunk : 2 * chunk] = wgu_ref[1, :, cols]
            wf[j][own_rows, 2 * chunk :] = wd_ref[:, cols]

    def tables():
        xf[ds(mine, half)] = x_ref[...]
        dyf[ds(mine, half)] = dy_ref[...]
        segc[...] = jnp.broadcast_to(seg_ref[...].astype(F32), (LANES, tokens)).T
        cos[...] = jnp.broadcast_to(pos_ref[...].astype(F32), (LANES, tokens)).T

        @pl.loop(0, tokens // 64)
        def _(i):
            r = ds(i * 64, 64)
            angles = cos[r] * freq_ref[...]
            cos[r] = jnp.cos(angles)
            sin[r] = jnp.sin(angles)

        put(cos, cos_out)
        put(sin, sin_out)

    def gains():
        put(wa, wa_out)
        put(wg, wg_out)
        qk = spread_gains(wg, dp, gain_rows)
        lows = low_half((1, LANES))
        gain["q"] = jnp.where(lows, qk, pltpu.roll(qk, HD, 1))
        gain["k"] = jnp.where(lows, pltpu.roll(qk, HD, 1), qk)
        x_copy.wait_recv()

    def norm1():
        @pl.loop(0, tokens // 64)
        def _(i):
            r = ds(i * 64, 64)
            values = xf[r].astype(F32)
            n1[r] = rms_forward(values, gain_rows[0:1, :])[0].astype(BF16)

        put(n1, n1_out)

    def project():
        @pl.loop(0, o_at // 256)
        def _(n):
            tile = dot_nn(n1[...], wa[:, ds(n * 256, 256)])
            raw[2 * n] = tile[:, :LANES]
            raw[2 * n + 1] = tile[:, LANES:]

        put(raw, raw_out)

    def rope(n, gain_row, r):
        values = raw[n, r]
        normed = values * lax.rsqrt(head_mean(values * values) + EPSILON) * gain_row
        early = first_quarter(normed.shape)
        turned = jnp.where(early, -pltpu.roll(normed, LANES - HD // 2, 1), pltpu.roll(normed, HD // 2, 1))
        return normed * cos[r] + turned * sin[r]

    def doubled(tile):
        swapped = pltpu.roll(tile, HD, 1)
        lows = low_half(tile.shape)
        return jnp.where(lows, tile, swapped).astype(BF16), jnp.where(lows, swapped, tile).astype(BF16)

    def rotate():
        @pl.loop(0, tokens // blk)
        def _(i):
            r = ds(i * blk, blk)
            for n in range(groups):
                qrot[n, r] = rope(n, gain["q"], r).astype(BF16)
            for n in range(groups // 2):
                kdup[2 * n, r], kdup[2 * n + 1, r] = doubled(rope(groups + n, gain["k"], r))
                vdup[2 * n, r], vdup[2 * n + 1, r] = doubled(raw[groups + groups // 2 + n, r])

        put(qrot, qrot_out)
        put(kdup, kdup_out)
        put(vdup, vdup_out)

    def attend(base):
        @pl.loop(0, groups * (half // blk))
        def _(step):
            g = step // (half // blk)
            start = base + lax.rem(step, half // blk) * blk
            r = ds(start, blk)
            q = qrot[g, r]
            lows = low_half(q.shape)
            index = lax.broadcasted_iota(jnp.int32, (blk, tokens), 0) + start
            allowed = (segc[r, 0:1] == seg_ref[...].astype(F32)) & (lane_of((blk, tokens)) <= index)
            result = []
            for hh in range(2):
                picked = jnp.where(lows if hh == 0 else jnp.logical_not(lows), q, jnp.zeros_like(q))
                scores = dot_nt(picked, kdup[g]) * (1.0 / math.sqrt(HD))
                scores = jnp.where(allowed, scores, NEG_FILL)
                e = jnp.exp(scores - jnp.max(scores, axis=1, keepdims=True))
                p = (e / jnp.sum(e, axis=1, keepdims=True)).astype(BF16)
                prob[g, ds(hh * tokens + start, blk)] = p
                result.append(dot_nn(p, vdup[g]))
            att[r, ds(g * LANES, LANES)] = jnp.where(lows, result[0], result[1]).astype(BF16)

    def send_partial():
        @pl.loop(0, wide // 256)
        def _(n):
            cols = ds(n * 256, 256)
            part_out[:, cols] = dot_nt(att[ds(theirs, half)], wa[cols, o_at:g_at]).astype(BF16)

        out_copy.start()

    def attend_mine():
        attend(mine)
        put(prob, p_out)
        put(att, att_out)

    def own_partial():
        @pl.loop(0, wide // 256)
        def _(n):
            cols = ds(n * 256, 256)
            hidden[:, cols] = x_ref[:, cols].astype(F32) + dot_nt(att[ds(mine, half)], wa[cols, o_at:g_at])

        out_copy.wait_recv()

    def norm2():
        @pl.loop(0, half // 64)
        def _(i):
            r = ds(i * 64, 64)
            values = hidden[r] + part_in[r].astype(F32)
            hidden[r] = values
            n2[ds(mine + i * 64, 64)] = rms_forward(values, gain_rows[1:2, :])[0].astype(BF16)

        put(hidden, hidden_out)
        n2_copy.start()

    def hidden_units(j, base):
        chunk, before = chunks[j], sum(chunks[:j])

        @pl.loop(0, chunk // 256)
        def _(n):
            r = ds(base, half)
            gate = dot_nn(n2[r], wf[j][:, ds(n * 256, 256)])
            up = dot_nn(n2[r], wf[j][:, ds(chunk + n * 256, 256)])
            gact = dot_nn(dyf[r], wf[j][:, ds(2 * chunk + n * 256, 256)])
            sig = jax.nn.sigmoid(gate)
            silu = gate * sig
            cols = ds(before + n * 256, 256)
            act[r, cols] = (silu * up).astype(BF16)
            dg[r, cols] = (gact * up * sig * (1.0 + gate * (1.0 - sig))).astype(BF16)
            du[r, cols] = (gact * silu).astype(BF16)

    def partner_units(j):
        if j == 0:
            dy_copy.wait_recv()
            put(dyf, dyf_out)
            n2_copy.wait_recv()
            put(n2, n2_out)
        hidden_units(j, theirs)

    def combine(j):
        chunk = chunks[j]
        cols = slice(sum(chunks[:j]), sum(chunks[: j + 1]))

        @pl.loop(0, wide // 256)
        def _(n):
            r = ds(n * 256, 256)
            down = dot_nt(act[:, cols], wf[j][r, 2 * chunk :])
            back = dot_nt(dg[:, cols], wf[j][r, :chunk]) + dot_nt(du[:, cols], wf[j][r, chunk : 2 * chunk])
            if j == 0:
                op[:, r] = down
                gn[:, r] = back
            else:
                op[:, r] += down
                gn[:, r] += back

    def close():
        put(act, act_out)
        put(dg, dg_out)
        put(du, du_out)
        put(gn.at[ds(mine, half)], gnm_out)

        @pl.loop(0, half // 64)
        def _(i):
            r = ds(i * 64, 64)
            gno[r] = gn[ds(theirs + i * 64, 64)].astype(BF16)
            oo[r] = op[ds(theirs + i * 64, 64)].astype(BF16)
            om[r] = op[ds(mine + i * 64, 64)] + hidden[r]

        put(gno, gno_out)
        put(oo, oo_out)
        put(om, om_out)

    def joined(stage):
        def act(k, *s):
            if k == 0:
                stage(CHUNKS + 1, *s)
            stage(k, *s)

        return act

    steps = {
        "fill": fill, "tables": tables, "gains": gains, "norm1": norm1, "project": project, "rotate": rotate,
        "attend0": lambda: attend(theirs), "partial0": send_partial, "attend1": attend_mine,
        "partial1": own_partial, "norm2": norm2, "own": lambda j: hidden_units(j, mine),
        "other": partner_units, "combine": combine, "close": close,
        "M": joined(gather.main), "D": joined(gather.side), "F": joined(gather.final),
    }
    for name, *which in FORWARD_ORDER:
        steps[name](*which)
    for copy in (x_copy, dy_copy, out_copy, n2_copy):
        copy.wait_send()
    for k in range(CHUNKS + 2):
        gather.finish(k)
    for copy in outs:
        copy.wait()


def forward(dp, x, dy, seg, pos, freq, norms, qks, wq, wkv, wo_t, wgu, wd_t):
    rows, half = wq.shape[0], x.shape[0]
    tokens, wide = 2 * half, dp * rows
    q_wide, kv_wide, ff_wide = wq.shape[1], wkv.shape[2], wd_t.shape[1]
    groups = q_wide // LANES
    attn_wide = 2 * q_wide + 2 * kv_wide
    shapes = [
        ((wide, attn_wide), BF16),
        ((dp * GAIN_ROWS, LANES), BF16),
        ((tokens, wide), BF16),
        ((2 * groups, tokens, LANES), F32),
        ((groups, 2 * tokens, tokens), BF16),
        ((groups, tokens, LANES), BF16),
        ((groups, tokens, LANES), BF16),
        ((groups, tokens, LANES), BF16),
        ((tokens, q_wide), BF16),
        ((half, wide), F32),
        ((tokens, wide), BF16),
        ((tokens, wide), BF16),
        ((tokens, ff_wide), BF16),
        ((tokens, ff_wide), BF16),
        ((tokens, ff_wide), BF16),
        ((tokens, LANES), F32),
        ((tokens, LANES), F32),
        ((half, wide), F32),
        ((half, wide), BF16),
        ((half, wide), F32),
        ((half, wide), BF16),
    ]
    (wa, wg, n1, raw, p, qrot, kdup, vdup, att, hidden, n2, dyf, act, dg, du, cos, sin, gnm, gno, om, oo) = shapes
    vmem = [
        wa, wg, *[((wide, 3 * w), BF16) for w in chunk_widths(ff_wide)], n2, dyf, n1, n2, raw, p, qrot, kdup, vdup, att,
        hidden, act, dg, du, cos, sin, cos, ((tokens, wide), F32), ((tokens, wide), F32), oo, oo, gno, oo, om,
        ((8, wide), F32),
    ]
    return pl.pallas_call(
        functools.partial(fwd_kernel, dp, rows, half),
        out_shape=[jax.ShapeDtypeStruct(*s) for s in shapes],
        in_specs=[pl.BlockSpec(memory_space=pltpu.VMEM)] * 12,
        out_specs=[pl.BlockSpec(memory_space=pl.ANY)] * len(shapes),
        scratch_shapes=[pltpu.VMEM(*s) for s in vmem]
        + [
            pltpu.SemaphoreType.DMA((CHUNKS + 2, dp // 2, 4)),
            pltpu.SemaphoreType.DMA((CHUNKS + 2, dp)),
            pltpu.SemaphoreType.DMA((4, 2)),
            pltpu.SemaphoreType.DMA((len(shapes),)),
        ],
        compiler_params=pltpu.CompilerParams(
            collective_id=3, has_side_effects=True, vmem_limit_bytes=62 * 1024 * 1024
        ),
        name="forward",
    )(x, dy, seg, pos, freq, norms, qks, wq, wkv, wo_t, wgu, wd_t)


class Scatter:
    def __init__(self, at, rows, slabs, flipped, first, second, chained, emit, sems):
        self.at, self.rows, self.slabs, self.flipped, self.emit = at, rows, slabs, flipped, emit
        self.first, self.second, self.chained = first, second, chained
        self.sent1, self.sent2, self.sent4, self.got1, self.got2, self.got_up, self.got_down = sems

    def slab(self, k, o):
        return self.slabs[k](ds(o * self.rows[k], self.rows[k]))

    def swap(self, k, t, ox):
        at, q = self.at, t * 2 + ox
        src = self.slab(k, at.device(t, ox, 1 - at.c))
        return remote(src, self.first[k].at[q], self.sent1.at[k, q], self.got1.at[k, q], at.sibling)

    def cross(self, k, t):
        at = self.at
        q, slot = t * 2 + 1 - at.x, 0 if k in self.flipped else t
        return remote(
            self.first[k].at[q], self.second[k].at[slot], self.sent2.at[k, t], self.got2.at[k, slot], at.beside
        )

    def crossed(self, k, t):
        at = self.at
        slot = 0 if k in self.flipped else t
        block = self.second[k].at[slot]
        remote(block, block, self.sent2.at[k, t], self.got2.at[k, slot], at.beside).wait_recv()

    def slot(self, t, ox, last_down):
        return ox * (self.at.length + 1) + (self.at.length if last_down else t)

    def along(self, k, t, ox, up, distance):
        at, lane = self.at, ox * self.at.length + t
        src = self.first[k].at[t * 2 + ox] if k in self.flipped else self.second[k].at[t]
        dst = self.chained[k].at[self.slot(t, ox, distance == 1 and not up)]
        got = self.got_up if up else self.got_down
        return remote(src, dst, self.sent4.at[k, lane], got.at[k, lane], at.above if up else at.below)

    def arrive(self, k, t, ox, up, last):
        at, lane = self.at, ox * self.at.length + t
        block = self.chained[k].at[self.slot(t, ox, last and not up)]
        got = self.got_up if up else self.got_down
        remote(block, block, self.sent4.at[k, lane], got.at[k, lane], at.above).wait_recv()

    def lanes(self, k):
        return (1 - self.at.x, self.at.x) if k in self.flipped else (0,)

    def targets(self, act, distances=None):
        at = self.at
        for d in range(at.length - 1, -1, -1) if distances is None else distances:
            for sign in (1, -1) if d else (0,):
                t = at.z + d * sign
                if d:
                    pl.when((t >= 0) & (t < at.length))(lambda t=t, sign=sign, d=d: act(t, sign, d))
                else:
                    act(t, 0, 0)

    def each(self, k, act):
        @pl.loop(0, self.rows[k] // 16)
        def _(i):
            act(ds(i * 16, 16))

    def start(self, k):
        def act(t, sign, d):
            for ox in (1 - self.at.x, self.at.x):
                self.swap(k, t, ox).start()

        self.targets(act)

    def chip(self, k):
        at, first = self.at, self.first[k]

        def act(t, sign, d):
            for ox in (1 - at.x, at.x):
                q = t * 2 + ox
                self.swap(k, t, ox).wait_recv()
                base = at.device(t, ox, at.c) * self.rows[k]

                @pl.loop(0, self.rows[k] // 16)
                def _(i, q=q, base=base):
                    r = ds(i * 16, 16)
                    first[q, r] = first[q, r] + self.slabs[k](ds(base + i * 16, 16))[...]

                if ox is not at.x and k not in self.flipped:
                    self.cross(k, t).start()

        self.targets(act)

    def chain(self, k, d):
        at, first, second, chained = self.at, self.first[k], self.second[k], self.chained[k]
        flipped = k in self.flipped

        def ends(up, down, q, t, ox, other, put):
            def row(r):
                value = first[q, r].astype(F32)
                if other is not None:
                    value += second[other, r].astype(F32)
                if up:
                    value += chained[self.slot(t, ox, False), r].astype(F32)
                if down:
                    value += chained[self.slot(t, ox, True), r].astype(F32)
                put(r, value)

            self.each(k, row)

        def sums(*args):
            pl.when((at.z > 0) & (at.z < at.length - 1))(lambda: ends(True, True, *args))
            pl.when(at.z == 0)(lambda: ends(False, True, *args))
            pl.when(at.z == at.length - 1)(lambda: ends(True, False, *args))

        def last(t, ox):
            pl.when(at.z > 0)(lambda: self.arrive(k, t, ox, True, True))
            pl.when(at.z < at.length - 1)(lambda: self.arrive(k, t, ox, False, True))

        def out(r, value):
            self.emit(k, r, value)

        def act(t, sign, d):
            if d == 0 and flipped:
                q = t * 2 + 1 - at.x

                def keep(r, value):
                    first[q, r] = value.astype(BF16)

                last(t, 1 - at.x)
                sums(q, t, 1 - at.x, None, keep)
                self.cross(k, t).start()
                return
            if d < 0:
                last(t, at.x)
                self.crossed(k, t)
                sums(t * 2 + at.x, t, at.x, 0, out)
                return
            if not flipped:
                self.crossed(k, t)
            if d == 0:
                last(t, 0)
                sums(t * 2 + at.x, t, 0, t, out)
                return
            up = sign > 0
            inner = at.z > 0 if up else at.z < at.length - 1
            for ox in self.lanes(k):
                q = t * 2 + (ox if flipped else at.x)

                def middle(ox=ox, q=q):
                    self.arrive(k, t, ox, up, False)

                    def row(r):
                        value = first[q, r].astype(F32) + chained[self.slot(t, ox, False), r].astype(F32)
                        if flipped:
                            first[q, r] = value.astype(BF16)
                        else:
                            second[t, r] = (value + second[t, r].astype(F32)).astype(BF16)

                    self.each(k, row)

                def edge(q=q):
                    def row(r):
                        second[t, r] = second[t, r] + first[q, r]

                    self.each(k, row)

                pl.when(inner)(middle)
                if not flipped:
                    pl.when(jnp.logical_not(inner))(edge)
                self.along(k, t, ox, up, d).start()

        if d < 0:
            act(at.z, 0, d)
        else:
            self.targets(act, (d,))

    def swapped(self, k):
        def act(t, sign, d):
            for ox in range(2):
                self.swap(k, t, ox).wait_send()

        self.targets(act)

    def finish(self, k):
        def act(t, sign, d):
            if k not in self.flipped or d == 0:
                self.cross(k, t).wait_send()
            if sign:
                for ox in self.lanes(k):
                    self.along(k, t, ox, sign > 0, d).wait_send()

        self.targets(act)


BACKWARD_ORDER = (
    ("weights", 1), ("S", 1), ("weights", 0), ("S", 0), ("P", 1), ("C", 1, 3), ("P", 0), ("C", 1, 2),
    ("residual",), ("weights", 2), ("S", 2), ("C", 0, 3), ("C", 1, 1), ("P", 2), ("attended",), ("S", 3),
    ("heads", 0), ("C", 0, 2), ("heads", 1), ("heads", 2), ("heads", 3), ("C", 2, 3), ("unrotate",),
    ("send",), ("C", 2, 2), ("projection",), ("S", 4), ("P", 3), ("C", 0, 1), ("output",), ("own",), ("P", 4),
    ("input",), ("C", 2, 1), ("C", 0, 0), ("C", 4, 3), ("C", 3, 3), ("C", 4, 2), ("gains",), ("S", 5),
    ("C", 2, 0), ("C", 3, 2), ("P", 5), ("C", 5, 3), ("C", 1, 0), ("C", 4, 1), ("C", 5, 2), ("C", 3, 1),
    ("C", 4, 0), ("C", 5, 1), ("C", 1, -1), ("C", 3, 0), ("C", 5, 0),
)


def bwd_kernel(
    dp, rows, half, x_ref, dy_ref,
    wa_in, wg_in, n1_in, raw_in, p_in, qrot_in, kdup_in, vdup_in, att_in, hidden_in, n2_in,
    dyf_in, act_in, dg_in, du_in, cos_in, sin_in, gnm_in, gno_in, om_in, oo_in,
    bo_out, gi_out, gain_out, gq_out, gkv_out, go_out, ggu_out, gdn_out,
    parts0, parts1, pa, pg, stage, turned, turned2, tiles, prob, raw, qrot, kdup, vdup, att, weights, gains, gain_rows, cos, sin,
    hidden, gh, grecv, orecv, grows, n1recv, n1send, ga, qs, dos, dq, dk, dv, dqkv, terms, terms_in,
    *rest,
):
    count = CHUNKS + 3
    first, second, chained = rest[:count], rest[count : 2 * count], rest[2 * count : 3 * count]
    sems = rest[3 * count : 3 * count + 7]
    ysem, loads, tilesem = rest[3 * count + 7 :]
    at = Spot(dp)
    wide, tokens = dp * rows, 2 * half
    q_wide, kv_wide, ff_wide = gq_out.shape[1], gkv_out.shape[2], gdn_out.shape[1]
    chunks = chunk_widths(ff_wide)
    parts = (parts0, parts1, parts1)
    o_at, g_at = q_wide + 2 * kv_wide, 2 * q_wide + 2 * kv_wide
    groups = q_wide // LANES
    mine, theirs = at.t * half, (1 - at.t) * half
    used = []

    def load(src, dst):
        copy = pltpu.make_async_copy(src, dst, loads.at[len(used)])
        copy.start()
        used.append(copy)
        return copy

    def emit(k, r, value):
        if k < CHUNKS:
            chunk = chunks[k]
            cols = slice(sum(chunks[:k]), sum(chunks[: k + 1]))
            ggu_out[0, r, cols] = value[:, :chunk]
            ggu_out[1, r, cols] = value[:, chunk : 2 * chunk]
            gdn_out[r, cols] = value[:, 2 * chunk :]
        elif k == CHUNKS:
            go_out[r] = value
        elif k == CHUNKS + 1:
            gq_out[r] = value[:, :q_wide]
            gkv_out[0, r] = value[:, q_wide : q_wide + kv_wide]
            gkv_out[1, r] = value[:, q_wide + kv_wide :]
        else:
            gain_out[r] = value

    slabs = [lambda r, j=j: parts[j].at[r, : 3 * chunks[j]] for j in range(CHUNKS)]
    slabs += [lambda r: pa.at[r, o_at:g_at], lambda r: pa.at[r, 0:o_at], lambda r: pg.at[r]]
    scatter = Scatter(at, [rows] * (CHUNKS + 2) + [GAIN_ROWS], slabs, (FLIPPED,), first, second, chained, emit, sems)

    at.greet()
    g_copy = partner(at, gno_in, grecv, ysem.at[0])
    g_copy.start()
    o_copy = partner(at, oo_in, orecv, ysem.at[1])
    dy_load = load(dyf_in, stage.at[0])
    n2_load = load(n2_in, stage.at[1])

    def tile_copies(i, slot):
        cols = ds(i * 256, 256)
        return [
            pltpu.make_async_copy(src.at[:, cols], tiles.at[slot, n], tilesem.at[slot, n])
            for n, src in enumerate((act_in, dg_in, du_in))
        ]

    order = [FLIPPED, 0, 2]
    sequence = [(j, n) for j in order for n in range(chunks[j] // 256)]

    def tile_of(i):
        j, n = sequence[i]
        return sum(chunks[:j]) // 256 + n

    for copy in tile_copies(tile_of(0), 0):
        copy.start()
    wo_load = load(wa_in.at[:, o_at:g_at], weights.at[:, : g_at - o_at])
    gain_load = load(wg_in, gains)
    hidden_load = load(hidden_in, hidden)
    gnm_load = load(gnm_in, gh)
    cos_load, sin_load = load(cos_in, cos), load(sin_in, sin)
    att_load, raw_load = load(att_in, att), load(raw_in.at[0 : groups + groups // 2], raw)
    q_load, k_load, v_load = load(qrot_in, qrot), load(kdup_in, kdup), load(vdup_in, vdup)
    om_load = load(om_in, gi_out)
    p_loads = [load(p_in.at[0], prob.at[0])]

    def transpose(src, dst):
        @pl.loop(0, wide // 128)
        def _(i):
            c = ds(i * 128, 128)
            dst[c] = src[:, c].T

    dy_load.wait()
    transpose(stage.at[0], turned)
    n2_load.wait()
    transpose(stage.at[1], turned2)
    n1_load = load(n1_in, stage.at[0])

    def weight_grads(j):
        chunk = chunks[j]
        for n in range(chunk // 256):
            i = sequence.index((j, n))
            slot = i % 2
            if i + 1 < len(sequence):
                for copy in tile_copies(tile_of(i + 1), 1 - slot):
                    copy.start()
            for copy in tile_copies(tile_of(i), slot):
                copy.wait()

            @pl.loop(0, wide // 256)
            def _(m, n=n, slot=slot):
                r = ds(m * 256, 256)
                for part, left, which in ((0, turned2, 1), (1, turned2, 2), (2, turned, 0)):
                    cols = slice(part * chunk + n * 256, part * chunk + (n + 1) * 256)
                    parts[j][r, cols] = dot_nn(left[r], tiles[slot, which]).astype(BF16)


    r_copy = partner(at, grows.at[ds(mine, half)], grows.at[ds(mine, half)], ysem.at[2])
    n_copy = partner(at, n1send, n1recv, ysem.at[3])
    t_copy = partner(at, terms, terms_in, ysem.at[4])
    blk = 128
    gain = {}

    def residual():
        gain_load.wait()
        qk_gain = spread_gains(gains, dp, gain_rows)
        lows1 = low_half((1, LANES))
        gain["q"] = jnp.where(lows1, qk_gain, pltpu.roll(qk_gain, HD, 1))
        gain["k"] = jnp.where(lows1, pltpu.roll(qk_gain, HD, 1), qk_gain)
        gain["attn"], gain["ffn"] = gain_rows[0:1, :], gain_rows[1:2, :]
        hidden_load.wait()
        gnm_load.wait()
        g_copy.wait_recv()
        terms[...] = jnp.zeros_like(terms)

        @pl.loop(0, half // 32)
        def _(i):
            r = ds(i * 32, 32)
            grad = gh[r] + grecv[r].astype(F32)
            values = hidden[r]
            scale = lax.rsqrt(jnp.mean(values * values, axis=-1, keepdims=True) + EPSILON)
            terms[1:2, :wide] += jnp.sum(grad * values * scale, axis=0, keepdims=True)
            result = dy_ref[r].astype(F32) + rms_backward(values, scale, gain["ffn"], grad)
            gh[r] = result
            grows[ds(mine + i * 32, 32)] = result.astype(BF16)

        r_copy.start()
        o_copy.start()

    def attended_grads():
        wo_load.wait()
        r_copy.wait_recv()

        @pl.loop(0, q_wide // 256)
        def _(n):
            tile = dot_nn(grows[...], weights[:, ds(n * 256, 256)]).astype(BF16)
            ga[2 * n] = tile[:, :LANES]
            ga[2 * n + 1] = tile[:, LANES:]

        gain["weights"] = load(wa_in.at[:, :o_at], weights)
        transpose(grows, turned)
        att_load.wait()

        @pl.loop(0, wide // 256)
        def _(m):
            r = ds(m * 256, 256)
            pa[r, o_at:g_at] = dot_nn(turned[r], att[...]).astype(BF16)

        q_load.wait()
        k_load.wait()
        v_load.wait()

    def heads(g):
        if g + 1 < groups:
            p_loads.append(load(p_in.at[g + 1], prob.at[(g + 1) % 2]))
        p_loads[g].wait()
        pg = prob.at[g % 2]

        @pl.loop(0, tokens // blk)
        def _(i, g=g):
            r, r2 = ds(i * blk, blk), ds(tokens + i * blk, blk)
            lows = low_half((blk, LANES))
            q, do = qrot[g, r], ga[g, r]
            zero = jnp.zeros_like(q)
            qs[r], qs[r2] = jnp.where(lows, q, zero), jnp.where(lows, zero, q)
            dos[r], dos[r2] = jnp.where(lows, do, zero), jnp.where(lows, zero, do)

        dv[g] = dot_tn(pg[...], dos[...])

        @pl.loop(0, tokens // blk)
        def _(i, g=g, pg=pg):
            lows = low_half((blk, LANES))
            result = []
            for hh in range(2):
                r = ds(hh * tokens + i * blk, blk)
                p = pg[r].astype(F32)
                grad_p = dot_nt(dos[r], vdup[g])
                delta = jnp.sum(p * grad_p, axis=1, keepdims=True)
                scores = (p * (grad_p - delta) * (1.0 / math.sqrt(HD))).astype(BF16)
                pg[r] = scores
                result.append(dot_nn(scores, kdup[g]))
            dq[g, ds(i * blk, blk)] = jnp.where(lows, result[0], result[1])

        dk[g] = dot_tn(pg[...], qs[...])

    def fold(value):
        return value + pltpu.roll(value, HD, 1)

    def turn_back(values, grad_rot, gain, r):
        u = grad_rot * sin[r]
        early = first_quarter(u.shape)
        grad = grad_rot * cos[r] + jnp.where(
            early, pltpu.roll(u, LANES - HD // 2, 1), -pltpu.roll(u, HD // 2, 1)
        )
        scale = lax.rsqrt(head_mean(values * values) + EPSILON)
        weighted = grad * gain
        inner = head_mean(weighted * values)
        term = jnp.sum(grad * values * scale, axis=0, keepdims=True)
        return scale * (weighted - values * scale * scale * inner), fold(term)

    def unrotate():
        cos_load.wait()
        sin_load.wait()
        raw_load.wait()

        @pl.loop(0, tokens // blk)
        def _(i):
            r = ds(i * blk, blk)
            lows = low_half((blk, LANES))
            q_term = k_term = jnp.zeros((1, LANES), F32)
            for n in range(groups):
                grad, term = turn_back(raw[n, r], dq[n, r], gain["q"], r)
                dqkv[r, n * LANES : (n + 1) * LANES] = grad.astype(BF16)
                q_term += term
            for n in range(groups // 2):
                pair = jnp.where(lows, fold(dk[2 * n, r]), fold(dk[2 * n + 1, r]))
                grad, term = turn_back(raw[groups + n, r], pair, gain["k"], r)
                dqkv[r, q_wide + n * LANES : q_wide + (n + 1) * LANES] = grad.astype(BF16)
                k_term += term
                pair = jnp.where(lows, fold(dv[2 * n, r]), fold(dv[2 * n + 1, r]))
                dqkv[r, q_wide + kv_wide + n * LANES : q_wide + kv_wide + (n + 1) * LANES] = pair.astype(BF16)
            terms[0:1, wide:] += jnp.where(low_half((1, LANES)), q_term, k_term)

    def send_input():
        gain["weights"].wait()

        @pl.loop(0, wide // 256)
        def _(n):
            r = ds(n * 256, 256)
            n1send[:, r] = dot_nt(dqkv[ds(theirs, half)], weights[r]).astype(BF16)

        n_copy.start()

    def projection_grads():
        n1_load.wait()
        transpose(stage.at[0], turned2)

        @pl.loop(0, wide // 256)
        def _(m):
            r = ds(m * 256, 256)
            for n in range(o_at // 256):
                cols = slice(n * 256, (n + 1) * 256)
                pa[r, cols] = dot_nn(turned2[r], dqkv[:, cols]).astype(BF16)

    def output():
        om_load.wait()
        o_copy.wait_recv()

        @pl.loop(0, half // 64)
        def _(i):
            r = ds(i * 64, 64)
            bo_out[r] = (gi_out[r] + orecv[r].astype(F32)).astype(BF16)

    def own_input():
        @pl.loop(0, wide // 256)
        def _(n):
            r = ds(n * 256, 256)
            gi_out[:, r] = dot_nt(dqkv[ds(mine, half)], weights[r])

    def input_grads():
        n_copy.wait_recv()

        @pl.loop(0, half // 32)
        def _(i):
            r = ds(i * 32, 32)
            grad = gi_out[r] + n1recv[r].astype(F32)
            values = x_ref[r].astype(F32)
            scale = lax.rsqrt(jnp.mean(values * values, axis=-1, keepdims=True) + EPSILON)
            terms[0:1, :wide] += jnp.sum(grad * values * scale, axis=0, keepdims=True)
            gi_out[r] = gh[r] + rms_backward(values, scale, gain["attn"], grad)

        t_copy.start()

    def gain_grads():
        t_copy.wait_recv()

        both = terms[...] + terms_in[...]
        lows = low_half((1, LANES))
        rest_rows = jnp.zeros((GAIN_ROWS - 2, LANES), F32)
        for i in range(dp // 2):
            block = both[:, i * LANES : (i + 1) * LANES]
            swapped = pltpu.roll(block, HD, 1)
            even = jnp.where(lows, block[0:1], swapped[1:2])
            odd = jnp.where(lows, swapped[0:1], block[1:2])
            for o, row in ((2 * i, even), (2 * i + 1, odd)):
                packed = jnp.concatenate([row, both[0:1, wide:], rest_rows], axis=0)
                pg[o * GAIN_ROWS : (o + 1) * GAIN_ROWS] = packed.astype(BF16)

    steps = {
        "weights": weight_grads, "residual": residual, "attended": attended_grads, "heads": heads,
        "unrotate": unrotate, "send": send_input, "projection": projection_grads, "output": output,
        "own": own_input, "input": input_grads, "gains": gain_grads,
        "S": scatter.start, "P": scatter.chip, "C": scatter.chain,
    }
    waited = set()
    for name, *which in BACKWARD_ORDER:
        if name == "weights" and which[0] == 2:
            scatter.swapped(FLIPPED)
            waited.add(FLIPPED)
        steps[name](*which)
    for copy in (g_copy, o_copy, r_copy, n_copy, t_copy):
        copy.wait_send()
    for k in range(count):
        if k not in waited:
            scatter.swapped(k)
        scatter.finish(k)


def backward(dp, x, dy, saved, q_wide, kv_wide, ff_wide):
    half, wide = x.shape
    rows, tokens = wide // dp, 2 * half
    groups = q_wide // LANES
    length = layout_of(dp)[0]
    chunks = chunk_widths(ff_wide)
    widths = [3 * w for w in chunks] + [q_wide, q_wide + 2 * kv_wide, LANES]
    heights = [rows] * (CHUNKS + 2) + [GAIN_ROWS]
    shapes = [
        ((half, wide), BF16),
        ((half, wide), F32),
        ((GAIN_ROWS, LANES), F32),
        ((rows, q_wide), F32),
        ((2, rows, kv_wide), F32),
        ((rows, q_wide), F32),
        ((2, rows, ff_wide), F32),
        ((rows, ff_wide), F32),
    ]
    vmem = [
        ((wide, widths[0]), BF16),
        ((wide, max(widths[1:3])), BF16),
        ((wide, sum(widths[CHUNKS:-1])), BF16),
        ((dp * GAIN_ROWS, LANES), BF16),
        ((2, tokens, wide), BF16),
        ((wide, tokens), BF16),
        ((wide, tokens), BF16),
        ((2, 3, tokens, 256), BF16),
        ((2, 2 * tokens, tokens), BF16),
        ((groups + groups // 2, tokens, LANES), F32),
        ((groups, tokens, LANES), BF16),
        ((groups, tokens, LANES), BF16),
        ((groups, tokens, LANES), BF16),
        ((tokens, q_wide), BF16),
        ((wide, q_wide + 2 * kv_wide), BF16),
        ((dp * GAIN_ROWS, LANES), BF16),
        ((8, wide), F32),
        ((tokens, LANES), F32),
        ((tokens, LANES), F32),
        ((half, wide), F32),
        ((half, wide), F32),
        ((half, wide), BF16),
        ((half, wide), BF16),
        ((tokens, wide), BF16),
        ((half, wide), BF16),
        ((half, wide), BF16),
        ((groups, tokens, LANES), BF16),
        ((2 * tokens, LANES), BF16),
        ((2 * tokens, LANES), BF16),
        ((groups, tokens, LANES), F32),
        ((groups, tokens, LANES), F32),
        ((groups, tokens, LANES), F32),
        ((tokens, q_wide + 2 * kv_wide), BF16),
        ((8, wide + LANES), F32),
        ((8, wide + LANES), F32),
    ]
    for slots, turned in ((dp // 2, dp // 2), (length, 1), (length + 1, 2 * length + 2)):
        vmem += [((turned if k == FLIPPED else slots, heights[k], w), BF16) for k, w in enumerate(widths)]
    count = len(widths)
    return pl.pallas_call(
        functools.partial(bwd_kernel, dp, rows, half),
        out_shape=[jax.ShapeDtypeStruct(*s) for s in shapes],
        in_specs=[pl.BlockSpec(memory_space=pltpu.VMEM)] * 2
        + [pl.BlockSpec(memory_space=pl.ANY)] * len(saved),
        out_specs=[pl.BlockSpec(memory_space=pltpu.VMEM)] * len(shapes),
        scratch_shapes=[pltpu.VMEM(*s) for s in vmem]
        + [
            pltpu.SemaphoreType.DMA((count, n))
            for n in (dp // 2, length, 2 * length, dp // 2, length, 2 * length, 2 * length)
        ]
        + [
            pltpu.SemaphoreType.DMA((5, 2)),
            pltpu.SemaphoreType.DMA((24,)),
            pltpu.SemaphoreType.DMA((2, 3)),
        ],
        compiler_params=pltpu.CompilerParams(
            collective_id=4, has_side_effects=True, vmem_limit_bytes=63 * 1024 * 1024
        ),
        name="backward",
    )(x, dy, *saved)


def finish_kernel(dp, rows, qk_shard, count, gain_ref, *refs):
    ins, norm_out, qk_out, outs, sem = refs[:count], refs[count], refs[count + 1], refs[count + 2 : -1], refs[-1]
    copies = [pltpu.make_async_copy(a, b, sem.at[i]) for i, (a, b) in enumerate(zip(ins, outs))]
    for copy in copies:
        copy.start()
    block = gain_ref[0:8]
    norm_out[0:1] = block[0:1, :rows]
    norm_out[1:2] = pltpu.roll(block, LANES - rows, 1)[0:1, :rows]
    own = lax.axis_index("dp") * qk_shard
    for i in range(2):
        moved = pltpu.roll(block, lax.rem(2 * LANES - own - i * HD, LANES), 1)
        qk_out[i : i + 1] = moved[1:2, :qk_shard]
    for copy in copies:
        copy.wait()


def finish(dp, rows, gains, qk_shard, arrays):
    return pl.pallas_call(
        functools.partial(finish_kernel, dp, rows, qk_shard, len(arrays)),
        out_shape=[jax.ShapeDtypeStruct((2, rows), F32), jax.ShapeDtypeStruct((2, qk_shard), F32)]
        + [jax.ShapeDtypeStruct(a.shape, a.dtype) for a in arrays],
        in_specs=[pl.BlockSpec(memory_space=pltpu.VMEM)] * (1 + len(arrays)),
        out_specs=[pl.BlockSpec(memory_space=pltpu.VMEM)] * 2
        + [pl.BlockSpec(memory_space=pl.ANY)] * len(arrays),
        scratch_shapes=[pltpu.SemaphoreType.DMA((len(arrays),))],
        name="finish",
    )(gains, *arrays)


def fast_device(
    block_input, cotangent, segment_ids, positions, norm_gains, qk_gains, w_query, w_keyval, w_output,
    w_gate_up, w_down,
):
    dp = lax.axis_size("dp")
    q_wide = w_query.shape[1]
    kv_wide, ff_wide = w_keyval.shape[2], w_gate_up.shape[2]
    qk_shard = qk_gains.shape[1]
    freq = np.tile(ROPE_BASE ** (-np.arange(0, HD, 2) / HD), 4)[None].astype(np.float32)
    saved = forward(
        dp, block_input, cotangent, segment_ids, positions, freq, norm_gains, qk_gains,
        w_query, w_keyval, w_output.T, w_gate_up, w_down.T,
    )
    block_output, grad_input, gains, grad_query, grad_keyval, grad_out, grad_gate_up, grad_down = backward(
        dp, block_input, cotangent, saved, q_wide, kv_wide, ff_wide
    )
    norm, qk, *rest = finish(
        dp, w_query.shape[0], gains, qk_shard,
        [block_output, grad_input, grad_query, grad_keyval, grad_out, grad_gate_up, grad_down],
    )
    block_output, grad_input, grad_query, grad_keyval, grad_out, grad_gate_up, grad_down = rest
    return (
        block_output,
        grad_input,
        norm,
        qk,
        grad_query,
        grad_keyval,
        grad_out.T,
        grad_gate_up,
        grad_down.T,
    )


def solution(mesh):
    return jax.shard_map(
        fast_device if mesh.shape["tensor"] == 2 and mesh.shape["dp"] == 16 else on_device,
        mesh=mesh,
        in_specs=(
            P(("dp", "tensor"), None),
            P(("dp", "tensor"), None),
            P("dp", None),
            P("dp", None),
            P(None, "dp"),
            P(None, "dp"),
            P("dp", "tensor"),
            P(None, "dp", "tensor"),
            P("tensor", "dp"),
            P(None, "dp", "tensor"),
            P("tensor", "dp"),
        ),
        out_specs=(
            P(("dp", "tensor"), None),
            P(("dp", "tensor"), None),
            P(None, "dp"),
            P(None, "dp"),
            P("dp", "tensor"),
            P(None, "dp", "tensor"),
            P("tensor", "dp"),
            P(None, "dp", "tensor"),
            P("tensor", "dp"),
        ),
        check_vma=False,
    )
```

```python
import functools
import math

import jax
import jax.numpy as jnp
import numpy as np
from jax import lax
from jax.experimental import pallas as pl
from jax.experimental.pallas import tpu as pltpu
from jax.sharding import PartitionSpec as P

HD = 64


EPSILON = 1e-05
ROPE_BASE = 1000000.0
NEG_FILL = -1e30


def rms_forward(values, gain):
    scale = lax.rsqrt(jnp.mean(values * values, axis=-1, keepdims=True) + EPSILON)
    return (values * scale * gain, scale)


def rms_backward(values, scale, gain, grad):
    weighted = grad * gain
    inner = jnp.mean(weighted * values, axis=-1, keepdims=True)
    return scale * (weighted - values * scale * scale * inner)


def rope_tables(places):
    freqs = ROPE_BASE ** (-jnp.arange(0, HD, 2).astype(jnp.float32) / HD)
    angles = places.astype(jnp.float32)[..., None] * freqs
    angles = jnp.concatenate([angles, angles], axis=-1)
    return (jnp.cos(angles), jnp.sin(angles))


def rotate_half(values):
    half = values.shape[-1] // 2
    return jnp.concatenate([-values[..., half:], values[..., :half]], axis=-1)


def rotate_back(values):
    half = values.shape[-1] // 2
    return jnp.concatenate([values[..., half:], -values[..., :half]], axis=-1)


def allowed_mask(segs):
    length = segs.shape[0]
    index = jnp.arange(length, dtype=jnp.int32)
    return (segs[:, None] == segs[None, :]) & (index[None, :] <= index[:, None])


def contract(left, right, left_dim, right_dim):
    return lax.dot_general(
        left, right, (((left_dim,), (right_dim,)), ((), ())), preferred_element_type=jnp.float32
    )


def fdot(left, right):
    return jnp.dot(left, right, preferred_element_type=jnp.float32)


def row_scores(q_rot, k_rot):
    kv_heads = k_rot.shape[1]
    groups = q_rot.shape[1] // kv_heads
    q_four = q_rot.reshape(q_rot.shape[0], kv_heads, groups, HD)
    scores = jnp.einsum("ikgd,jkd->kgij", q_four, k_rot, preferred_element_type=jnp.float32)
    return (scores / math.sqrt(HD), q_four)


def attend_row(q_rot, k_rot, values, segs):
    scores, q_four = row_scores(q_rot, k_rot)
    allowed = allowed_mask(segs)[None, None]
    masked = jnp.where(allowed, scores, NEG_FILL)
    top = jnp.max(masked, axis=-1, keepdims=True)
    expd = jnp.where(allowed, jnp.exp(masked - top), 0.0)
    total = jnp.sum(expd, axis=-1, keepdims=True)
    probs = (expd / total).astype(jnp.bfloat16)
    log_total = top[..., 0] + jnp.log(total[..., 0])
    attended = jnp.einsum("kgij,jkd->ikgd", probs, values, preferred_element_type=jnp.float32)
    return (attended.reshape(q_rot.shape).astype(jnp.bfloat16), log_total)


def back_row(q_rot, k_rot, values, grad_att, log_total, segs):
    scores, q_four = row_scores(q_rot, k_rot)
    allowed = allowed_mask(segs)[None, None]
    masked = jnp.where(allowed, scores, NEG_FILL)
    probs = jnp.where(allowed, jnp.exp(masked - log_total[..., None]), 0.0)
    probs_b = probs.astype(jnp.bfloat16)
    grad_four = grad_att.reshape(q_four.shape)
    grad_values = jnp.einsum(
        "kgij,ikgd->jkd", probs_b, grad_four, preferred_element_type=jnp.float32
    )
    grad_p = jnp.einsum("ikgd,jkd->kgij", grad_four, values, preferred_element_type=jnp.float32)
    delta = jnp.sum(probs * grad_p, axis=-1, keepdims=True)
    d_scores = (probs * (grad_p - delta) / math.sqrt(HD)).astype(jnp.bfloat16)
    grad_q = jnp.einsum(
        "kgij,jkd->ikgd", d_scores, k_rot, preferred_element_type=jnp.float32
    ).reshape(q_rot.shape)
    grad_k = jnp.einsum("kgij,ikgd->jkd", d_scores, q_four, preferred_element_type=jnp.float32)
    return (grad_q, grad_k, grad_values)


def layout_of(dp):
    if dp == 16:
        return (4, 4, 2)
    return (dp // 4, 2, dp // 2)


class Place:
    def __init__(self, dp):
        self.length, self.zs, self.xs = layout_of(dp)
        me = lax.axis_index("dp")
        self.z = lax.rem(me // self.zs, self.length)
        self.x = lax.rem(me // self.xs, 2)
        self.c = lax.rem(me, 2)

    def device(self, z, x, c):
        return z * self.zs + x * self.xs + c

    def greet(self):
        z, x, c = self.z, self.x, self.c
        barrier = pltpu.get_barrier_semaphore()

        def signal(target):
            pl.semaphore_signal(
                barrier, inc=1, device_id={"dp": target}, device_id_type=pl.DeviceIdType.MESH
            )

        signal(self.device(z, x, 1 - c))
        signal(self.device(z, 1 - x, c))
        pl.when(z > 0)(lambda: signal(self.device(z - 1, x, c)))
        pl.when(z < self.length - 1)(lambda: signal(self.device(z + 1, x, c)))
        ends = jnp.where(z > 0, 1, 0) + jnp.where(z < self.length - 1, 1, 0)
        pl.semaphore_wait(barrier, 2 + ends)


def remote(src, dst, send, recv, target):
    return pltpu.make_async_remote_copy(
        src_ref=src,
        dst_ref=dst,
        send_sem=send,
        recv_sem=recv,
        device_id={"dp": target},
        device_id_type=pl.DeviceIdType.MESH,
    )


def gather_kernel(dp, count, rows, *refs):
    ins, outs = refs[:count], refs[count : 2 * count]
    send, recv, local = refs[2 * count :]
    at = Place(dp)
    z, x, c, length = at.z, at.x, at.c, at.length
    below, above = at.device(z - 1, x, c), at.device(z + 1, x, c)
    beside, sibling = at.device(z, 1 - x, c), at.device(z, x, 1 - c)
    at.greet()
    own = at.device(z, x, c)

    def slab(k, o):
        return outs[k].at[pl.ds(pl.multiple_of(o * rows, rows), rows)]

    for k in range(count):
        pltpu.make_async_copy(ins[k], slab(k, own), local.at[k]).start()

    def move(k, oz, ox, way, target, first):
        o = at.device(oz, ox, c)
        src = ins[k] if first else slab(k, o)
        return remote(src, slab(k, o), send.at[k, oz * 2 + ox, way], recv.at[k, o], target)

    def arrived(k, o):
        remote(slab(k, o), slab(k, o), send.at[k, 0, 0], recv.at[k, o], sibling).wait_recv()

    def steps(act):
        for s in range(length):
            for sign in (1, -1) if s else (0,):
                oz = z - s * sign

                def event(oz=oz, s=s, sign=sign):
                    for k in range(count):
                        act(k, oz, s, sign)

                if s:
                    pl.when((oz >= 0) & (oz < length))(event)
                else:
                    event()
            if s:
                side(s - 1, act)
        side(length - 1, act)

    def side(s, act):
        for sign in (1, -1) if s else (0,):
            oz = z - s * sign

            def event(oz=oz):
                for k in range(count):
                    act(k, oz, None, 0)

            if s:
                pl.when((oz >= 0) & (oz < length))(event)
            else:
                event()

    def begin(k, oz, s, sign):
        if s is None:
            arrived(k, at.device(oz, 1 - x, c))
            move(k, oz, 1 - x, 3, sibling, False).start()
            return
        first = s == 0
        if not first:
            arrived(k, at.device(oz, x, c))
        if sign >= 0:
            pl.when(z < length - 1)(lambda: move(k, oz, x, 0, above, first).start())
        if sign <= 0:
            pl.when(z > 0)(lambda: move(k, oz, x, 1, below, first).start())
        move(k, oz, x, 2, beside, first).start()
        move(k, oz, x, 3, sibling, first).start()

    def finish(k, oz, s, sign):
        if s is None:
            move(k, oz, 1 - x, 3, sibling, False).wait_send()
            return
        first = s == 0
        if sign >= 0:
            pl.when(z < length - 1)(lambda: move(k, oz, x, 0, above, first).wait_send())
        if sign <= 0:
            pl.when(z > 0)(lambda: move(k, oz, x, 1, below, first).wait_send())
        move(k, oz, x, 2, beside, first).wait_send()
        move(k, oz, x, 3, sibling, first).wait_send()

    steps(begin)
    for oz in range(length):
        for ox in range(2):
            for k in range(count):
                arrived(k, at.device(oz, ox, 1 - c))
    steps(finish)
    for k in range(count):
        pltpu.make_async_copy(ins[k], slab(k, own), local.at[k]).wait()


def gather_rows(arrays, dp):
    count, rows = len(arrays), arrays[0].shape[0]
    return pl.pallas_call(
        functools.partial(gather_kernel, dp, count, rows),
        out_shape=[jax.ShapeDtypeStruct((dp * rows, a.shape[1]), a.dtype) for a in arrays],
        in_specs=[pl.BlockSpec(memory_space=pltpu.VMEM)] * count,
        out_specs=[pl.BlockSpec(memory_space=pl.ANY)] * count,
        scratch_shapes=[
            pltpu.SemaphoreType.DMA((count, dp // 2, 4)),
            pltpu.SemaphoreType.DMA((count, dp)),
            pltpu.SemaphoreType.DMA((count,)),
        ],
        compiler_params=pltpu.CompilerParams(collective_id=1, has_side_effects=True),
        name="gather_rows",
    )(*arrays)


def scatter_kernel(dp, count, rows, *refs):
    parts, outs = refs[:count], refs[count : 2 * count]
    mine, first, second, upward, downward = (
        refs[(2 + i) * count : (3 + i) * count] for i in range(5)
    )
    sent1, sent2, sent4, got1, got2, got_up, got_down, local = refs[7 * count :]
    at = Place(dp)
    z, x, c, length = at.z, at.x, at.c, at.length
    below, above = at.device(z - 1, x, c), at.device(z + 1, x, c)
    beside, sibling = at.device(z, 1 - x, c), at.device(z, x, 1 - c)
    at.greet()

    def slab(k, o):
        return parts[k].at[pl.ds(pl.multiple_of(o * rows, rows), rows)]

    def swap(k, t, ox):
        q = t * 2 + ox
        return remote(
            slab(k, at.device(t, ox, 1 - c)), first[k].at[q], sent1.at[k, q], got1.at[k, q], sibling
        )

    def keep(k, t, ox):
        q = t * 2 + ox
        return pltpu.make_async_copy(slab(k, at.device(t, ox, c)), mine[k].at[q], local.at[k, q])

    def cross(k, t):
        q = t * 2 + 1 - x
        return remote(first[k].at[q], second[k].at[t], sent2.at[k, t], got2.at[k, t], beside)

    def rise(k, t):
        return remote(second[k].at[t], upward[k].at[t], sent4.at[k, t], got_up.at[k, t], above)

    def fall(k, t):
        return remote(second[k].at[t], downward[k].at[t], sent4.at[k, t], got_down.at[k, t], below)

    def targets(act):
        for d in range(length - 1, -1, -1):
            for sign in (1, -1) if d else (0,):
                t = z + d * sign

                def event(t=t, sign=sign):
                    for k in range(count):
                        act(k, t, sign)

                if d:
                    pl.when((t >= 0) & (t < length))(event)
                else:
                    event()

    def wide(value):
        return value.astype(jnp.float32)

    def start(k, t, sign):
        for ox in (1 - x, x):
            swap(k, t, ox).start()
            keep(k, t, ox).start()

    def chip_sum(k, t, sign):
        for ox in (1 - x, x):
            q = t * 2 + ox
            keep(k, t, ox).wait()
            swap(k, t, ox).wait_recv()
            first[k][q] = (wide(first[k][q]) + wide(mine[k][q])).astype(jnp.bfloat16)
            if ox is not x:
                cross(k, t).start()

    def chain(k, t, sign):
        cross(k, t).wait_recv()
        if sign == 0:
            outs[k][...] = wide(second[k][t]) + wide(first[k][t * 2 + x])

            def add_up():
                rise(k, t).wait_recv()
                outs[k][...] += wide(upward[k][t])

            def add_down():
                fall(k, t).wait_recv()
                outs[k][...] += wide(downward[k][t])

            pl.when(z > 0)(add_up)
            pl.when(z < length - 1)(add_down)
            return
        base, move = (upward, rise) if sign > 0 else (downward, fall)
        inner = z > 0 if sign > 0 else z < length - 1

        def middle():
            move(k, t).wait_recv()
            second[k][t] = (
                wide(second[k][t]) + wide(first[k][t * 2 + x]) + wide(base[k][t])
            ).astype(jnp.bfloat16)

        def edge():
            second[k][t] = (wide(second[k][t]) + wide(first[k][t * 2 + x])).astype(jnp.bfloat16)

        pl.when(inner)(middle)
        pl.when(jnp.logical_not(inner))(edge)
        move(k, t).start()

    def finish(k, t, sign):
        swap(k, t, 0).wait_send()
        swap(k, t, 1).wait_send()
        cross(k, t).wait_send()
        if sign:
            (rise if sign > 0 else fall)(k, t).wait_send()

    targets(start)
    targets(chip_sum)
    targets(chain)
    targets(finish)


def scatter_rows(arrays, dp):
    count, rows = len(arrays), arrays[0].shape[0] // dp
    length = layout_of(dp)[0]
    slots = [dp // 2, dp // 2, length, length, length]
    return pl.pallas_call(
        functools.partial(scatter_kernel, dp, count, rows),
        out_shape=[jax.ShapeDtypeStruct((rows, a.shape[1]), jnp.float32) for a in arrays],
        in_specs=[pl.BlockSpec(memory_space=pl.ANY)] * count,
        out_specs=[pl.BlockSpec(memory_space=pltpu.VMEM)] * count,
        scratch_shapes=[
            pltpu.VMEM((n, rows, a.shape[1]), a.dtype) for n in slots for a in arrays
        ]
        + [
            pltpu.SemaphoreType.DMA((count, n))
            for n in (dp // 2, length, length, dp // 2, length, length, length, dp // 2)
        ],
        compiler_params=pltpu.CompilerParams(
            collective_id=2, has_side_effects=True, vmem_limit_bytes=60 * 1024 * 1024
        ),
        name="scatter_rows",
    )(*arrays)


def exchange(values):
    return lax.ppermute(values, "tensor", ((0, 1), (1, 0)))


def collect(values):
    if lax.axis_size("tensor") != 2:
        return lax.all_gather(values, "tensor", axis=0, tiled=True)
    other = exchange(values)
    low = lax.axis_index("tensor") == 0
    return jnp.concatenate([jnp.where(low, values, other), jnp.where(low, other, values)])


def spread(values):
    if lax.axis_size("tensor") != 2:
        return lax.psum_scatter(values, "tensor", scatter_dimension=0, tiled=True)
    half = values.shape[0] // 2
    low = lax.axis_index("tensor") == 0
    head, tail = values[:half], values[half:]
    other = exchange(jnp.where(low, tail, head).astype(jnp.bfloat16))
    return jnp.where(low, head, tail) + other.astype(jnp.float32)


def total(values):
    if lax.axis_size("tensor") != 2:
        return lax.psum(values, "tensor")
    return values + exchange(values)


def on_device(
    block_input,
    cotangent,
    segment_ids,
    positions,
    norm_gains,
    qk_gains,
    w_query,
    w_keyval,
    w_output,
    w_gate_up,
    w_down,
):
    dp = lax.axis_size("dp")
    rows_here, row_len = segment_ids.shape
    tokens_here = rows_here * row_len
    shard, q_wide = w_query.shape
    kv_wide, ff_wide = w_keyval.shape[2], w_gate_up.shape[2]
    qk_shard = qk_gains.shape[1]
    gains = jnp.concatenate(
        [norm_gains.T, jnp.pad(qk_gains.T, ((0, shard - qk_shard), (0, 0)))], axis=1
    )
    gains = jnp.pad(gains, ((0, 0), (0, 124)))
    attn_pack = jnp.concatenate([w_query, w_keyval[0], w_keyval[1], w_output.T, gains], axis=1)
    gate_up_pack = jnp.concatenate([w_gate_up[0], w_gate_up[1]], axis=1)
    attn_full, gate_up_full, down_full = gather_rows([attn_pack, gate_up_pack, w_down.T], dp)
    qkv_wide = q_wide + 2 * kv_wide
    qkv_full = attn_full[:, :qkv_wide]
    output_full = attn_full[:, qkv_wide : qkv_wide + q_wide]
    gain_cols = attn_full[:, qkv_wide + q_wide :].astype(jnp.float32)
    gain_attn, gain_ffn = gain_cols[:, 0], gain_cols[:, 1]
    qk_cols = gain_cols.reshape(dp, shard, 128)[:, :qk_shard, 2:4].reshape(dp * qk_shard, 2)
    gain_q, gain_k = qk_cols[:, 0], qk_cols[:, 1]
    heads_here = q_wide // HD
    kv_here = kv_wide // HD
    dy_rows = collect(cotangent)
    xlocal = block_input.astype(jnp.float32)
    normed_f, scale1 = rms_forward(xlocal, gain_attn)
    normed1 = collect(normed_f.astype(jnp.bfloat16))
    qkv = fdot(normed1, qkv_full)
    query = qkv[:, :q_wide].reshape(rows_here, row_len, heads_here, HD)
    keys = qkv[:, q_wide : q_wide + kv_wide].reshape(rows_here, row_len, kv_here, HD)
    values = (
        qkv[:, q_wide + kv_wide :].astype(jnp.bfloat16).reshape(rows_here, row_len, kv_here, HD)
    )
    q_norm, q_scale = rms_forward(query, gain_q)
    k_norm, k_scale = rms_forward(keys, gain_k)
    cosv, sinv = rope_tables(positions)
    cosv = cosv[:, :, None, :]
    sinv = sinv[:, :, None, :]
    q_rot = (q_norm * cosv + rotate_half(q_norm) * sinv).astype(jnp.bfloat16)
    k_rot = (k_norm * cosv + rotate_half(k_norm) * sinv).astype(jnp.bfloat16)
    attended, log_total = jax.vmap(attend_row)(q_rot, k_rot, values, segment_ids)
    att_flat = attended.reshape(tokens_here, heads_here * HD)
    hidden = xlocal + spread(contract(att_flat, output_full, 1, 1))
    normed_g, scale2 = rms_forward(hidden, gain_ffn)
    normed2 = collect(normed_g.astype(jnp.bfloat16))
    gate_up = fdot(normed2, gate_up_full)
    gate_proj, up_proj = gate_up[:, :ff_wide], gate_up[:, ff_wide:]
    sigmoid_gate = jax.nn.sigmoid(gate_proj)
    silu_gate = gate_proj * sigmoid_gate
    act = (silu_gate * up_proj).astype(jnp.bfloat16)
    block_output = (hidden + spread(contract(act, down_full, 1, 1))).astype(jnp.bfloat16)
    grad_act = fdot(dy_rows, down_full)
    grad_down = contract(dy_rows, act, 0, 0).astype(jnp.bfloat16)
    d_gate = grad_act * up_proj * sigmoid_gate * (1.0 + gate_proj * (1.0 - sigmoid_gate))
    d_gate_up = jnp.concatenate(
        [d_gate.astype(jnp.bfloat16), (grad_act * silu_gate).astype(jnp.bfloat16)], axis=1
    )
    grad_gate_up = contract(normed2, d_gate_up, 0, 0).astype(jnp.bfloat16)
    grad_n2 = spread(contract(d_gate_up, gate_up_full, 1, 1))
    gain_ffn_grad = jnp.sum(grad_n2 * hidden * scale2, axis=0)
    grad_hidden = cotangent.astype(jnp.float32) + rms_backward(hidden, scale2, gain_ffn, grad_n2)
    grad_rows = collect(grad_hidden.astype(jnp.bfloat16))
    grad_att = (
        fdot(grad_rows, output_full)
        .astype(jnp.bfloat16)
        .reshape(rows_here, row_len, heads_here, HD)
    )
    grad_out = contract(grad_rows, att_flat, 0, 0).astype(jnp.bfloat16)
    grad_qrot, grad_krot, grad_vals = jax.vmap(back_row)(
        q_rot, k_rot, values, grad_att, log_total, segment_ids
    )
    grad_qn = grad_qrot * cosv + rotate_back(grad_qrot * sinv)
    grad_kn = grad_krot * cosv + rotate_back(grad_krot * sinv)
    gain_q_grad = jnp.sum(grad_qn * query * q_scale, axis=(0, 1, 2))
    gain_k_grad = jnp.sum(grad_kn * keys * k_scale, axis=(0, 1, 2))
    d_query = rms_backward(query, q_scale, gain_q, grad_qn).astype(jnp.bfloat16)
    d_keys = rms_backward(keys, k_scale, gain_k, grad_kn).astype(jnp.bfloat16)
    d_qkv = jnp.concatenate(
        [
            d_query.reshape(tokens_here, q_wide),
            d_keys.reshape(tokens_here, kv_wide),
            grad_vals.astype(jnp.bfloat16).reshape(tokens_here, kv_wide),
        ],
        axis=1,
    )
    grad_qkv = contract(normed1, d_qkv, 0, 0).astype(jnp.bfloat16)
    grad_n1 = spread(contract(d_qkv, qkv_full, 1, 1))
    gain_attn_grad = jnp.sum(grad_n1 * xlocal * scale1, axis=0)
    grad_input = grad_hidden + rms_backward(xlocal, scale1, gain_attn, grad_n1)
    gain_terms = total(
        jnp.concatenate([gain_attn_grad, gain_ffn_grad, gain_q_grad, gain_k_grad])[None]
    )[0]
    wide = dp * shard
    norm_terms = gain_terms[: 2 * wide].reshape(2, wide).T
    qk_terms = gain_terms[2 * wide :].reshape(2, dp, qk_shard).transpose(1, 2, 0)
    qk_terms = jnp.pad(qk_terms, ((0, 0), (0, shard - qk_shard), (0, 0))).reshape(wide, 2)
    gain_pack = jnp.concatenate([norm_terms, qk_terms], axis=1).astype(jnp.bfloat16)
    gain_pack = jnp.pad(gain_pack, ((0, 0), (0, 124)))
    grad_attn = jnp.concatenate([grad_qkv, grad_out, gain_pack], axis=1)
    attn_sum, gate_up_sum, down_sum = scatter_rows([grad_attn, grad_gate_up, grad_down], dp)
    gain_sum = attn_sum[:, qkv_wide + q_wide :]
    return (
        block_output,
        grad_input,
        gain_sum[:, 0:2].T,
        gain_sum[:qk_shard, 2:4].T,
        attn_sum[:, :q_wide],
        jnp.stack([attn_sum[:, q_wide : q_wide + kv_wide], attn_sum[:, q_wide + kv_wide : qkv_wide]]),
        attn_sum[:, qkv_wide : qkv_wide + q_wide].T,
        jnp.stack([gate_up_sum[:, :ff_wide], gate_up_sum[:, ff_wide:]]),
        down_sum.T,
    )


MESH = pl.DeviceIdType.MESH
LANES = 128
F32, BF16 = jnp.float32, jnp.bfloat16


def dot_nn(a, b):
    return lax.dot_general(a, b, (((1,), (0,)), ((), ())), preferred_element_type=F32)


def dot_nt(a, b):
    return lax.dot_general(a, b, (((1,), (1,)), ((), ())), preferred_element_type=F32)


def dot_tn(a, b):
    return lax.dot_general(a, b, (((0,), (0,)), ((), ())), preferred_element_type=F32)


def lane_of(shape):
    return lax.broadcasted_iota(jnp.int32, shape, len(shape) - 1)


def head_mean(values):
    row = lax.broadcasted_iota(jnp.int32, (LANES, LANES), 0) // HD
    ones = jnp.where(row == lane_of((LANES, LANES)) // HD, 1.0 / HD, 0.0).astype(BF16)
    high = values.astype(BF16)
    low = (values - high.astype(F32)).astype(BF16)
    return dot_nn(high, ones) + dot_nn(low, ones)


def low_half(shape):
    return lane_of(shape) < HD


def first_quarter(shape):
    return lax.rem(lane_of(shape), HD) < HD // 2


def ds(start, size):
    if isinstance(start, int):
        return pl.ds(start, size)
    return pl.ds(pl.multiple_of(start, size), size)


class Gather:
    def __init__(self, at, rows, slabs, flipped, send, recv):
        self.at, self.rows, self.slabs, self.flipped = at, rows, slabs, flipped
        self.send, self.recv = send, recv

    def slab(self, k, o):
        return self.slabs[k](ds(o * self.rows[k], self.rows[k]))

    def move(self, k, oz, ox, way, target):
        at = self.at
        o = at.device(oz, ox, at.c)
        return remote(
            self.slab(k, o), self.slab(k, o), self.send.at[k, oz * 2 + ox, way], self.recv.at[k, o], target
        )

    def arrived(self, k, o):
        at = self.at
        slab = self.slab(k, o)
        remote(slab, slab, self.send.at[k, 0, 0], self.recv.at[k, o], at.sibling).wait_recv()

    def sources(self, s, act):
        at = self.at
        for sign in (1, -1) if s else (0,):
            oz = at.z - s * sign
            if s:
                pl.when((oz >= 0) & (oz < at.length))(lambda oz=oz, sign=sign: act(oz, sign))
            else:
                act(oz, 0)

    def along(self, k, oz, ox, sign, act):
        at = self.at
        if sign >= 0:
            pl.when(at.z < at.length - 1)(lambda: act(self.move(k, oz, ox, 0, at.above)))
        if sign <= 0:
            pl.when(at.z > 0)(lambda: act(self.move(k, oz, ox, 1, at.below)))

    def outgoing(self, k, s, oz, sign, act):
        at = self.at
        self.along(k, oz, at.x, sign, act)
        if not s or k not in self.flipped:
            act(self.move(k, oz, at.x, 2, at.beside))
        act(self.move(k, oz, at.x, 3, at.sibling))

    def onward(self, k, oz, sign, act):
        at = self.at
        if k in self.flipped:
            self.along(k, oz, 1 - at.x, sign, act)
        act(self.move(k, oz, 1 - at.x, 3, at.sibling))

    def main(self, k, s):
        at = self.at

        def act(oz, sign):
            if s:
                self.arrived(k, at.device(oz, at.x, at.c))
            self.outgoing(k, s, oz, sign, lambda m: m.start())

        self.sources(s, act)

    def side(self, k, s):
        at = self.at

        def act(oz, sign):
            self.arrived(k, at.device(oz, 1 - at.x, at.c))
            self.onward(k, oz, sign, lambda m: m.start())

        self.sources(s, act)

    def final(self, k):
        at = self.at
        for oz in range(at.length):
            for ox in range(2):
                self.arrived(k, at.device(oz, ox, 1 - at.c))

    def finish(self, k):
        at = self.at
        for s in range(at.length):
            self.sources(s, lambda oz, sign: self.outgoing(k, s, oz, sign, lambda m: m.wait_send()))
            self.sources(s, lambda oz, sign: self.onward(k, oz, sign, lambda m: m.wait_send()))


class Spot(Place):
    def __init__(self, dp):
        super().__init__(dp)
        z, x, c = self.z, self.x, self.c
        self.below, self.above = self.device(z - 1, x, c), self.device(z + 1, x, c)
        self.beside, self.sibling = self.device(z, 1 - x, c), self.device(z, x, 1 - c)
        self.own = self.device(z, x, c)
        self.t = lax.axis_index("tensor")

    def greet(self):
        barrier = pltpu.get_barrier_semaphore()

        def signal(target):
            pl.semaphore_signal(barrier, inc=1, device_id=target, device_id_type=MESH)

        signal({"dp": self.sibling})
        signal({"dp": self.beside})
        signal({"tensor": 1 - self.t})
        pl.when(self.z > 0)(lambda: signal({"dp": self.below}))
        pl.when(self.z < self.length - 1)(lambda: signal({"dp": self.above}))
        ends = jnp.where(self.z > 0, 1, 0) + jnp.where(self.z < self.length - 1, 1, 0)
        pl.semaphore_wait(barrier, 3 + ends)


def partner(at, src, dst, sems):
    return pltpu.make_async_remote_copy(
        src_ref=src,
        dst_ref=dst,
        send_sem=sems.at[0],
        recv_sem=sems.at[1],
        device_id={"tensor": 1 - at.t},
        device_id_type=MESH,
    )


CHUNKS = 3
GAIN_ROWS = 16
FLIPPED = 1


def chunk_widths(ff_wide):
    tiles = ff_wide // 256
    sizes = [tiles * 4 // 9, tiles * 2 // 9]
    return [256 * n for n in sizes + [tiles - sum(sizes)]]


FORWARD_ORDER = (
    ("M", 0, 0), ("fill",), ("M", 2, 0), ("D", 0, 0), ("M", 0, 1), ("D", 2, 0), ("M", 0, 2), ("M", 3, 0),
    ("tables",), ("M", 0, 3), ("D", 0, 1), ("M", 1, 0), ("D", 0, 2), ("M", 3, 1), ("D", 0, 3), ("F", 0),
    ("gains",), ("norm1",), ("project",), ("M", 1, 1), ("rotate",), ("attend0",), ("partial0",), ("M", 1, 2),
    ("attend1",), ("partial1",), ("D", 1, 0), ("M", 1, 3), ("norm2",), ("D", 2, 1), ("D", 3, 0), ("M", 3, 2),
    ("M", 2, 1), ("D", 1, 1), ("D", 2, 2), ("D", 1, 2), ("D", 1, 3), ("M", 3, 3), ("M", 2, 2), ("D", 3, 1),
    ("F", 1), ("own", 0), ("other", 0), ("D", 2, 3), ("combine", 0), ("M", 2, 3), ("D", 3, 2), ("D", 3, 3),
    ("F", 2), ("own", 1), ("other", 1), ("combine", 1), ("F", 3), ("own", 2), ("other", 2), ("combine", 2),
    ("close",),
)


def transpose(src, dst):
    @pl.loop(0, src.shape[1] // LANES)
    def _(i):
        c = ds(i * LANES, LANES)
        dst[c] = src[:, c].T


def spread_gains(packed, dp, gain_rows):
    lows = low_half((1, LANES))
    qk = jnp.zeros((1, LANES), F32)
    for i in range(dp // 2):
        even = packed[2 * i * GAIN_ROWS : (2 * i + 1) * GAIN_ROWS].astype(F32)
        odd = packed[(2 * i + 1) * GAIN_ROWS : (2 * i + 2) * GAIN_ROWS].astype(F32)
        cols = slice(i * LANES, (i + 1) * LANES)
        gain_rows[0:1, cols] = jnp.where(lows, even[0:1], pltpu.roll(odd, HD, 1)[0:1])
        gain_rows[1:2, cols] = jnp.where(lows, pltpu.roll(even, HD, 1)[0:1], odd[0:1])
        qk += even[1:2] + odd[1:2]
    return qk


def fwd_kernel(
    dp, rows, half, x_ref, dy_ref, seg_ref, pos_ref, freq_ref, norm_ref, qk_ref, wq_ref, wkv_ref, wo_ref,
    wgu_ref, wd_ref,
    wa_out, wg_out, n1_out, raw_out, p_out, qrot_out, kdup_out, vdup_out, att_out, hidden_out, n2_out,
    dyf_out, act_out, dg_out, du_out, cos_out, sin_out, gnm_out, gno_out, om_out, oo_out,
    wa, wg, wf0, wf1, wf2, xf, dyf, n1, n2, raw, prob, qrot, kdup, vdup, att, hidden, act, dg, du, cos, sin,
    segc, gn, op, part_out, part_in, gno, oo, om, gain_rows, n1t, n2t, dyt,
    send, recv, ysem, outsem,
):
    at = Spot(dp)
    wide = dp * rows
    tokens = 2 * half
    q_wide, kv_wide, ff_wide = wq_ref.shape[1], wkv_ref.shape[2], wd_ref.shape[1]
    chunks = chunk_widths(ff_wide)
    wf = (wf0, wf1, wf2)
    o_at, g_at = q_wide + 2 * kv_wide, 2 * q_wide + 2 * kv_wide
    groups = q_wide // LANES
    mine, theirs = at.t * half, (1 - at.t) * half
    own_rows = ds(at.own * rows, rows)
    outs = []

    def put(src, dst):
        copy = pltpu.make_async_copy(src, dst, outsem.at[len(outs)])
        copy.start()
        outs.append(copy)

    at.greet()
    gather = Gather(
        at,
        [rows] * (CHUNKS + 1) + [GAIN_ROWS],
        [lambda r: wa.at[r]] + [lambda r, j=j: wf[j].at[r] for j in range(CHUNKS)] + [lambda r: wg.at[r]],
        (1 + FLIPPED,),
        send,
        recv,
    )
    wa[own_rows, 0:q_wide] = wq_ref[...]
    wa[own_rows, q_wide : q_wide + kv_wide] = wkv_ref[0]
    wa[own_rows, q_wide + kv_wide : o_at] = wkv_ref[1]
    wa[own_rows, o_at:g_at] = wo_ref[...]
    norms = jnp.concatenate([norm_ref[...].astype(F32), jnp.zeros((2, LANES - rows), F32)], axis=1)
    norms = jnp.concatenate([norms, jnp.zeros((6, LANES), F32)], axis=0)
    qk_shard = qk_ref.shape[1]
    qk = jnp.concatenate([qk_ref[...].astype(F32), jnp.zeros((2, LANES - qk_shard), F32)], axis=1)
    qk = jnp.concatenate([qk, jnp.zeros((6, LANES), F32)], axis=0)
    wg[ds(at.own * GAIN_ROWS, GAIN_ROWS)] = jnp.concatenate(
        [
            norms[0:1] + pltpu.roll(norms, rows, 1)[1:2],
            pltpu.roll(qk, at.own * qk_shard, 1)[0:1] + pltpu.roll(qk, at.own * qk_shard + HD, 1)[1:2],
            jnp.zeros((GAIN_ROWS - 2, LANES), F32),
        ],
        axis=0,
    ).astype(BF16)
    x_copy = partner(at, x_ref, xf.at[ds(mine, half)], ysem.at[0])
    dy_copy = partner(at, dy_ref, dyf.at[ds(mine, half)], ysem.at[1])
    out_copy = partner(at, part_out, part_in, ysem.at[2])
    n2_copy = partner(at, n2.at[ds(mine, half)], n2.at[ds(mine, half)], ysem.at[3])
    gain = {}
    blk = 128

    def fill():
        x_copy.start()
        dy_copy.start()
        for j, chunk in enumerate(chunks):
            cols = slice(sum(chunks[:j]), sum(chunks[: j + 1]))
            wf[j][own_rows, 0:chunk] = wgu_ref[0, :, cols]
            wf[j][own_rows, chunk : 2 * chunk] = wgu_ref[1, :, cols]
            wf[j][own_rows, 2 * chunk :] = wd_ref[:, cols]

    def tables():
        xf[ds(mine, half)] = x_ref[...]
        dyf[ds(mine, half)] = dy_ref[...]
        segc[...] = jnp.broadcast_to(seg_ref[...].astype(F32), (LANES, tokens)).T
        cos[...] = jnp.broadcast_to(pos_ref[...].astype(F32), (LANES, tokens)).T

        @pl.loop(0, tokens // 64)
        def _(i):
            r = ds(i * 64, 64)
            angles = cos[r] * freq_ref[...]
            cos[r] = jnp.cos(angles)
            sin[r] = jnp.sin(angles)

        put(cos, cos_out)
        put(sin, sin_out)

    def gains():
        put(wa, wa_out)
        put(wg, wg_out)
        qk = spread_gains(wg, dp, gain_rows)
        lows = low_half((1, LANES))
        gain["q"] = jnp.where(lows, qk, pltpu.roll(qk, HD, 1))
        gain["k"] = jnp.where(lows, pltpu.roll(qk, HD, 1), qk)
        x_copy.wait_recv()

    def norm1():
        @pl.loop(0, tokens // 64)
        def _(i):
            r = ds(i * 64, 64)
            values = xf[r].astype(F32)
            n1[r] = rms_forward(values, gain_rows[0:1, :])[0].astype(BF16)


    def project():
        @pl.loop(0, o_at // 256)
        def _(n):
            tile = dot_nn(n1[...], wa[:, ds(n * 256, 256)])
            raw[2 * n] = tile[:, :LANES]
            raw[2 * n + 1] = tile[:, LANES:]

        put(raw, raw_out)

    def rope(n, gain_row, r):
        values = raw[n, r]
        normed = values * lax.rsqrt(head_mean(values * values) + EPSILON) * gain_row
        early = first_quarter(normed.shape)
        turned = jnp.where(early, -pltpu.roll(normed, LANES - HD // 2, 1), pltpu.roll(normed, HD // 2, 1))
        return normed * cos[r] + turned * sin[r]

    def doubled(tile):
        swapped = pltpu.roll(tile, HD, 1)
        lows = low_half(tile.shape)
        return jnp.where(lows, tile, swapped).astype(BF16), jnp.where(lows, swapped, tile).astype(BF16)

    def rotate():
        @pl.loop(0, tokens // blk)
        def _(i):
            r = ds(i * blk, blk)
            for n in range(groups):
                qrot[n, r] = rope(n, gain["q"], r).astype(BF16)
            for n in range(groups // 2):
                kdup[2 * n, r], kdup[2 * n + 1, r] = doubled(rope(groups + n, gain["k"], r))
                vdup[2 * n, r], vdup[2 * n + 1, r] = doubled(raw[groups + groups // 2 + n, r])

        put(qrot, qrot_out)
        put(kdup, kdup_out)
        put(vdup, vdup_out)
        transpose(n1, n1t)
        put(n1t, n1_out)

    def attend(base):
        @pl.loop(0, groups * (half // blk))
        def _(step):
            g = step // (half // blk)
            start = base + lax.rem(step, half // blk) * blk
            r = ds(start, blk)
            q = qrot[g, r]
            lows = low_half(q.shape)
            index = lax.broadcasted_iota(jnp.int32, (blk, tokens), 0) + start
            allowed = (segc[r, 0:1] == seg_ref[...].astype(F32)) & (lane_of((blk, tokens)) <= index)
            result = []
            for hh in range(2):
                picked = jnp.where(lows if hh == 0 else jnp.logical_not(lows), q, jnp.zeros_like(q))
                scores = dot_nt(picked, kdup[g]) * (1.0 / math.sqrt(HD))
                scores = jnp.where(allowed, scores, NEG_FILL)
                e = jnp.exp(scores - jnp.max(scores, axis=1, keepdims=True))
                p = (e / jnp.sum(e, axis=1, keepdims=True)).astype(BF16)
                prob[g, ds(hh * tokens + start, blk)] = p
                result.append(dot_nn(p, vdup[g]))
            att[r, ds(g * LANES, LANES)] = jnp.where(lows, result[0], result[1]).astype(BF16)

    def send_partial():
        @pl.loop(0, wide // 256)
        def _(n):
            cols = ds(n * 256, 256)
            part_out[:, cols] = dot_nt(att[ds(theirs, half)], wa[cols, o_at:g_at]).astype(BF16)

        out_copy.start()
        dy_copy.wait_recv()
        transpose(dyf, dyt)
        put(dyt, dyf_out)

    def attend_mine():
        attend(mine)
        put(prob, p_out)
        put(att, att_out)

    def own_partial():
        @pl.loop(0, wide // 256)
        def _(n):
            cols = ds(n * 256, 256)
            hidden[:, cols] = x_ref[:, cols].astype(F32) + dot_nt(att[ds(mine, half)], wa[cols, o_at:g_at])

        out_copy.wait_recv()

    def norm2():
        @pl.loop(0, half // 64)
        def _(i):
            r = ds(i * 64, 64)
            values = hidden[r] + part_in[r].astype(F32)
            hidden[r] = values
            n2[ds(mine + i * 64, 64)] = rms_forward(values, gain_rows[1:2, :])[0].astype(BF16)

        put(hidden, hidden_out)
        n2_copy.start()

    def hidden_units(j, base):
        chunk, before = chunks[j], sum(chunks[:j])

        @pl.loop(0, chunk // 256)
        def _(n):
            r = ds(base, half)
            gate = dot_nn(n2[r], wf[j][:, ds(n * 256, 256)])
            up = dot_nn(n2[r], wf[j][:, ds(chunk + n * 256, 256)])
            gact = dot_nn(dyf[r], wf[j][:, ds(2 * chunk + n * 256, 256)])
            sig = jax.nn.sigmoid(gate)
            silu = gate * sig
            cols = ds(before + n * 256, 256)
            act[r, cols] = (silu * up).astype(BF16)
            dg[r, cols] = (gact * up * sig * (1.0 + gate * (1.0 - sig))).astype(BF16)
            du[r, cols] = (gact * silu).astype(BF16)

    def partner_units(j):
        if j == 0:
            n2_copy.wait_recv()
        hidden_units(j, theirs)
        cols = slice(sum(chunks[:j]), sum(chunks[: j + 1]))
        for src, dst in ((act, act_out), (dg, dg_out), (du, du_out)):
            put(src.at[:, cols], dst.at[:, cols])

    def combine(j):
        chunk = chunks[j]
        cols = slice(sum(chunks[:j]), sum(chunks[: j + 1]))

        @pl.loop(0, wide // 256)
        def _(n):
            r = ds(n * 256, 256)
            down = dot_nt(act[:, cols], wf[j][r, 2 * chunk :])
            back = dot_nt(dg[:, cols], wf[j][r, :chunk]) + dot_nt(du[:, cols], wf[j][r, chunk : 2 * chunk])
            if j == 0:
                op[:, r] = down
                gn[:, r] = back
            else:
                op[:, r] += down
                gn[:, r] += back

        if j == 1:
            transpose(n2, n2t)
            put(n2t, n2_out)

    def close():
        put(gn.at[ds(mine, half)], gnm_out)

        @pl.loop(0, half // 64)
        def _(i):
            r = ds(i * 64, 64)
            gno[r] = gn[ds(theirs + i * 64, 64)].astype(BF16)
            oo[r] = op[ds(theirs + i * 64, 64)].astype(BF16)
            om[r] = op[ds(mine + i * 64, 64)] + hidden[r]

        put(gno, gno_out)
        put(oo, oo_out)
        put(om, om_out)

    def joined(stage):
        def act(k, *s):
            if k == 0:
                stage(CHUNKS + 1, *s)
            stage(k, *s)

        return act

    steps = {
        "fill": fill, "tables": tables, "gains": gains, "norm1": norm1, "project": project, "rotate": rotate,
        "attend0": lambda: attend(theirs), "partial0": send_partial, "attend1": attend_mine,
        "partial1": own_partial, "norm2": norm2, "own": lambda j: hidden_units(j, mine),
        "other": partner_units, "combine": combine, "close": close,
        "M": joined(gather.main), "D": joined(gather.side), "F": joined(gather.final),
    }
    for name, *which in FORWARD_ORDER:
        steps[name](*which)
    for copy in (x_copy, dy_copy, out_copy, n2_copy):
        copy.wait_send()
    for k in range(CHUNKS + 2):
        gather.finish(k)
    for copy in outs:
        copy.wait()


def forward(dp, x, dy, seg, pos, freq, norms, qks, wq, wkv, wo_t, wgu, wd_t):
    rows, half = wq.shape[0], x.shape[0]
    tokens, wide = 2 * half, dp * rows
    q_wide, kv_wide, ff_wide = wq.shape[1], wkv.shape[2], wd_t.shape[1]
    groups = q_wide // LANES
    attn_wide = 2 * q_wide + 2 * kv_wide
    shapes = [
        ((wide, attn_wide), BF16),
        ((dp * GAIN_ROWS, LANES), BF16),
        ((wide, tokens), BF16),
        ((2 * groups, tokens, LANES), F32),
        ((groups, 2 * tokens, tokens), BF16),
        ((groups, tokens, LANES), BF16),
        ((groups, tokens, LANES), BF16),
        ((groups, tokens, LANES), BF16),
        ((tokens, q_wide), BF16),
        ((half, wide), F32),
        ((wide, tokens), BF16),
        ((wide, tokens), BF16),
        ((tokens, ff_wide), BF16),
        ((tokens, ff_wide), BF16),
        ((tokens, ff_wide), BF16),
        ((tokens, LANES), F32),
        ((tokens, LANES), F32),
        ((half, wide), F32),
        ((half, wide), BF16),
        ((half, wide), F32),
        ((half, wide), BF16),
    ]
    (wa, wg, n1, raw, p, qrot, kdup, vdup, att, hidden, n2, dyf, act, dg, du, cos, sin, gnm, gno, om, oo) = shapes
    flat = ((tokens, wide), BF16)
    vmem = [
        wa, wg, *[((wide, 3 * w), BF16) for w in chunk_widths(ff_wide)], flat, flat, flat, flat, raw, p, qrot, kdup, vdup, att,
        hidden, act, dg, du, cos, sin, cos, ((tokens, wide), F32), ((tokens, wide), F32), oo, oo, gno, oo, om,
        ((8, wide), F32), n1, n2, dyf,
    ]
    return pl.pallas_call(
        functools.partial(fwd_kernel, dp, rows, half),
        out_shape=[jax.ShapeDtypeStruct(*s) for s in shapes],
        in_specs=[pl.BlockSpec(memory_space=pltpu.VMEM)] * 12,
        out_specs=[pl.BlockSpec(memory_space=pl.ANY)] * len(shapes),
        scratch_shapes=[pltpu.VMEM(*s) for s in vmem]
        + [
            pltpu.SemaphoreType.DMA((CHUNKS + 2, dp // 2, 4)),
            pltpu.SemaphoreType.DMA((CHUNKS + 2, dp)),
            pltpu.SemaphoreType.DMA((4, 2)),
            pltpu.SemaphoreType.DMA((len(shapes) + 3 * CHUNKS,)),
        ],
        compiler_params=pltpu.CompilerParams(
            collective_id=3, has_side_effects=True, vmem_limit_bytes=62 * 1024 * 1024
        ),
        name="forward",
    )(x, dy, seg, pos, freq, norms, qks, wq, wkv, wo_t, wgu, wd_t)


class Scatter:
    def __init__(self, at, rows, slabs, flipped, first, second, chained, emit, sems):
        self.at, self.rows, self.slabs, self.flipped, self.emit = at, rows, slabs, flipped, emit
        self.first, self.second, self.chained = first, second, chained
        self.sent1, self.sent2, self.sent4, self.got1, self.got2, self.got_up, self.got_down = sems

    def slab(self, k, o):
        return self.slabs[k](ds(o * self.rows[k], self.rows[k]))

    def swap(self, k, t, ox):
        at, q = self.at, t * 2 + ox
        src = self.slab(k, at.device(t, ox, 1 - at.c))
        return remote(src, self.first[k].at[q], self.sent1.at[k, q], self.got1.at[k, q], at.sibling)

    def cross(self, k, t):
        at = self.at
        q, slot = t * 2 + 1 - at.x, 0 if k in self.flipped else t
        return remote(
            self.first[k].at[q], self.second[k].at[slot], self.sent2.at[k, t], self.got2.at[k, slot], at.beside
        )

    def crossed(self, k, t):
        at = self.at
        slot = 0 if k in self.flipped else t
        block = self.second[k].at[slot]
        remote(block, block, self.sent2.at[k, t], self.got2.at[k, slot], at.beside).wait_recv()

    def slot(self, t, ox, last_down):
        return ox * (self.at.length + 1) + (self.at.length if last_down else t)

    def along(self, k, t, ox, up, distance):
        at, lane = self.at, ox * self.at.length + t
        src = self.first[k].at[t * 2 + ox] if k in self.flipped else self.second[k].at[t]
        dst = self.chained[k].at[self.slot(t, ox, distance == 1 and not up)]
        got = self.got_up if up else self.got_down
        return remote(src, dst, self.sent4.at[k, lane], got.at[k, lane], at.above if up else at.below)

    def arrive(self, k, t, ox, up, last):
        at, lane = self.at, ox * self.at.length + t
        block = self.chained[k].at[self.slot(t, ox, last and not up)]
        got = self.got_up if up else self.got_down
        remote(block, block, self.sent4.at[k, lane], got.at[k, lane], at.above).wait_recv()

    def lanes(self, k):
        return (1 - self.at.x, self.at.x) if k in self.flipped else (0,)

    def targets(self, act, distances=None):
        at = self.at
        for d in range(at.length - 1, -1, -1) if distances is None else distances:
            for sign in (1, -1) if d else (0,):
                t = at.z + d * sign
                if d:
                    pl.when((t >= 0) & (t < at.length))(lambda t=t, sign=sign, d=d: act(t, sign, d))
                else:
                    act(t, 0, 0)

    def each(self, k, act):
        @pl.loop(0, self.rows[k] // 16)
        def _(i):
            act(ds(i * 16, 16))

    def start(self, k):
        def act(t, sign, d):
            for ox in (1 - self.at.x, self.at.x):
                self.swap(k, t, ox).start()

        self.targets(act)

    def chip(self, k):
        at, first = self.at, self.first[k]

        def act(t, sign, d):
            for ox in (1 - at.x, at.x):
                q = t * 2 + ox
                self.swap(k, t, ox).wait_recv()
                base = at.device(t, ox, at.c) * self.rows[k]

                @pl.loop(0, self.rows[k] // 16)
                def _(i, q=q, base=base):
                    r = ds(i * 16, 16)
                    first[q, r] = first[q, r] + self.slabs[k](ds(base + i * 16, 16))[...]

                if ox is not at.x and k not in self.flipped:
                    self.cross(k, t).start()

        self.targets(act)

    def chain(self, k, d):
        at, first, second, chained = self.at, self.first[k], self.second[k], self.chained[k]
        flipped = k in self.flipped

        def ends(up, down, q, t, ox, other, put):
            def row(r):
                value = first[q, r].astype(F32)
                if other is not None:
                    value += second[other, r].astype(F32)
                if up:
                    value += chained[self.slot(t, ox, False), r].astype(F32)
                if down:
                    value += chained[self.slot(t, ox, True), r].astype(F32)
                put(r, value)

            self.each(k, row)

        def sums(*args):
            pl.when((at.z > 0) & (at.z < at.length - 1))(lambda: ends(True, True, *args))
            pl.when(at.z == 0)(lambda: ends(False, True, *args))
            pl.when(at.z == at.length - 1)(lambda: ends(True, False, *args))

        def last(t, ox):
            pl.when(at.z > 0)(lambda: self.arrive(k, t, ox, True, True))
            pl.when(at.z < at.length - 1)(lambda: self.arrive(k, t, ox, False, True))

        def out(r, value):
            self.emit(k, r, value)

        def act(t, sign, d):
            if d == 0 and flipped:
                q = t * 2 + 1 - at.x

                def keep(r, value):
                    first[q, r] = value.astype(BF16)

                last(t, 1 - at.x)
                sums(q, t, 1 - at.x, None, keep)
                self.cross(k, t).start()
                return
            if d < 0:
                last(t, at.x)
                self.crossed(k, t)
                sums(t * 2 + at.x, t, at.x, 0, out)
                return
            if not flipped:
                self.crossed(k, t)
            if d == 0:
                last(t, 0)
                sums(t * 2 + at.x, t, 0, t, out)
                return
            up = sign > 0
            inner = at.z > 0 if up else at.z < at.length - 1
            for ox in self.lanes(k):
                q = t * 2 + (ox if flipped else at.x)

                def middle(ox=ox, q=q):
                    self.arrive(k, t, ox, up, False)

                    def row(r):
                        value = first[q, r].astype(F32) + chained[self.slot(t, ox, False), r].astype(F32)
                        if flipped:
                            first[q, r] = value.astype(BF16)
                        else:
                            second[t, r] = (value + second[t, r].astype(F32)).astype(BF16)

                    self.each(k, row)

                def edge(q=q):
                    def row(r):
                        second[t, r] = second[t, r] + first[q, r]

                    self.each(k, row)

                pl.when(inner)(middle)
                if not flipped:
                    pl.when(jnp.logical_not(inner))(edge)
                self.along(k, t, ox, up, d).start()

        if d < 0:
            act(at.z, 0, d)
        else:
            self.targets(act, (d,))

    def swapped(self, k):
        def act(t, sign, d):
            for ox in range(2):
                self.swap(k, t, ox).wait_send()

        self.targets(act)

    def finish(self, k):
        def act(t, sign, d):
            if k not in self.flipped or d == 0:
                self.cross(k, t).wait_send()
            if sign:
                for ox in self.lanes(k):
                    self.along(k, t, ox, sign > 0, d).wait_send()

        self.targets(act)


BACKWARD_ORDER = (
    ("weights", 1), ("S", 1), ("weights", 0), ("S", 0), ("P", 1), ("C", 1, 3), ("P", 0), ("residual",),
    ("C", 1, 2), ("weights", 2), ("S", 2), ("C", 0, 3), ("attended",), ("S", 3), ("C", 1, 1), ("P", 2),
    ("C", 0, 2), ("heads", 0), ("heads", 1), ("heads", 2), ("heads", 3), ("C", 0, 1), ("unrotate",),
    ("send",), ("projection",), ("S", 4), ("P", 3), ("C", 2, 3), ("C", 2, 2), ("output",), ("own",),
    ("C", 0, 0), ("input",), ("P", 4), ("C", 2, 1), ("C", 4, 3), ("C", 3, 3), ("C", 4, 2), ("gains",),
    ("S", 5), ("C", 3, 2), ("P", 5), ("C", 1, 0), ("C", 5, 3), ("C", 4, 1), ("C", 5, 2), ("C", 3, 1),
    ("C", 4, 0), ("C", 5, 1), ("C", 2, 0), ("C", 1, -1), ("C", 3, 0), ("C", 5, 0),
)


def bwd_kernel(
    dp, rows, half, x_ref, dy_ref,
    wa_in, wg_in, n1_in, raw_in, p_in, qrot_in, kdup_in, vdup_in, att_in, hidden_in, n2_in,
    dyf_in, act_in, dg_in, du_in, cos_in, sin_in, gnm_in, gno_in, om_in, oo_in,
    bo_out, gi_out, gain_out, gq_out, gkv_out, go_out, ggu_out, gdn_out,
    parts0, parts1, pa, pg, stage, turned, turned2, tiles, prob, raw, qrot, kdup, vdup, att, weights, gains, gain_rows, cos, sin,
    hidden, gh, grecv, orecv, grows, n1recv, n1send, ga, qs, dos, dq, dk, dv, dqkv, terms, terms_in,
    *rest,
):
    count = CHUNKS + 3
    first, second, chained = rest[:count], rest[count : 2 * count], rest[2 * count : 3 * count]
    sems = rest[3 * count : 3 * count + 7]
    ysem, loads, tilesem = rest[3 * count + 7 :]
    at = Spot(dp)
    wide, tokens = dp * rows, 2 * half
    q_wide, kv_wide, ff_wide = gq_out.shape[1], gkv_out.shape[2], gdn_out.shape[1]
    chunks = chunk_widths(ff_wide)
    parts = (parts0, parts1, parts1)
    o_at, g_at = q_wide + 2 * kv_wide, 2 * q_wide + 2 * kv_wide
    groups = q_wide // LANES
    mine, theirs = at.t * half, (1 - at.t) * half
    used = []

    def load(src, dst):
        copy = pltpu.make_async_copy(src, dst, loads.at[len(used)])
        copy.start()
        used.append(copy)
        return copy

    def emit(k, r, value):
        if k < CHUNKS:
            chunk = chunks[k]
            cols = slice(sum(chunks[:k]), sum(chunks[: k + 1]))
            ggu_out[0, r, cols] = value[:, :chunk]
            ggu_out[1, r, cols] = value[:, chunk : 2 * chunk]
            gdn_out[r, cols] = value[:, 2 * chunk :]
        elif k == CHUNKS:
            go_out[r] = value
        elif k == CHUNKS + 1:
            gq_out[r] = value[:, :q_wide]
            gkv_out[0, r] = value[:, q_wide : q_wide + kv_wide]
            gkv_out[1, r] = value[:, q_wide + kv_wide :]
        else:
            gain_out[r] = value

    slabs = [lambda r, j=j: parts[j].at[r, : 3 * chunks[j]] for j in range(CHUNKS)]
    slabs += [lambda r: pa.at[r, o_at:g_at], lambda r: pa.at[r, 0:o_at], lambda r: pg.at[r]]
    scatter = Scatter(at, [rows] * (CHUNKS + 2) + [GAIN_ROWS], slabs, (FLIPPED,), first, second, chained, emit, sems)

    at.greet()
    g_copy = partner(at, gno_in, grecv, ysem.at[0])
    g_copy.start()
    o_copy = partner(at, oo_in, orecv, ysem.at[1])
    dy_load, n2_load = load(dyf_in, turned), load(n2_in, turned2)

    def tile_copies(i, slot):
        cols = ds(i * 256, 256)
        return [
            pltpu.make_async_copy(src.at[:, cols], tiles.at[slot, n], tilesem.at[slot, n])
            for n, src in enumerate((act_in, dg_in, du_in))
        ]

    order = [FLIPPED, 0, 2]
    sequence = [(j, n) for j in order for n in range(chunks[j] // 256)]

    def tile_of(i):
        j, n = sequence[i]
        return sum(chunks[:j]) // 256 + n

    for copy in tile_copies(tile_of(0), 0):
        copy.start()
    wo_load = load(wa_in.at[:, o_at:g_at], weights.at[:, : g_at - o_at])
    gain_load = load(wg_in, gains)
    hidden_load = load(hidden_in, hidden)
    gnm_load = load(gnm_in, gh)
    cos_load, sin_load = load(cos_in, cos), load(sin_in, sin)
    att_load, raw_load = load(att_in, att), load(raw_in.at[0 : groups + groups // 2], raw)
    q_load, k_load, v_load = load(qrot_in, qrot), load(kdup_in, kdup), load(vdup_in, vdup)
    om_load = load(om_in, gi_out)
    p_loads = [load(p_in.at[0], prob.at[0])]

    n1_load = load(n1_in, stage)
    dy_load.wait()
    n2_load.wait()

    def weight_grads(j):
        chunk = chunks[j]
        for n in range(chunk // 256):
            i = sequence.index((j, n))
            slot = i % 2
            if i + 1 < len(sequence):
                for copy in tile_copies(tile_of(i + 1), 1 - slot):
                    copy.start()
            for copy in tile_copies(tile_of(i), slot):
                copy.wait()

            @pl.loop(0, wide // 256)
            def _(m, n=n, slot=slot):
                r = ds(m * 256, 256)
                for part, left, which in ((0, turned2, 1), (1, turned2, 2), (2, turned, 0)):
                    cols = slice(part * chunk + n * 256, part * chunk + (n + 1) * 256)
                    parts[j][r, cols] = dot_nn(left[r], tiles[slot, which]).astype(BF16)


    r_copy = partner(at, grows.at[ds(mine, half)], grows.at[ds(mine, half)], ysem.at[2])
    n_copy = partner(at, n1send, n1recv, ysem.at[3])
    t_copy = partner(at, terms, terms_in, ysem.at[4])
    blk = 128
    gain = {}

    def residual():
        gain_load.wait()
        qk_gain = spread_gains(gains, dp, gain_rows)
        lows1 = low_half((1, LANES))
        gain["q"] = jnp.where(lows1, qk_gain, pltpu.roll(qk_gain, HD, 1))
        gain["k"] = jnp.where(lows1, pltpu.roll(qk_gain, HD, 1), qk_gain)
        gain["attn"], gain["ffn"] = gain_rows[0:1, :], gain_rows[1:2, :]
        hidden_load.wait()
        gnm_load.wait()
        g_copy.wait_recv()
        terms[...] = jnp.zeros_like(terms)

        @pl.loop(0, half // 32)
        def _(i):
            r = ds(i * 32, 32)
            grad = gh[r] + grecv[r].astype(F32)
            values = hidden[r]
            scale = lax.rsqrt(jnp.mean(values * values, axis=-1, keepdims=True) + EPSILON)
            terms[1:2, :wide] += jnp.sum(grad * values * scale, axis=0, keepdims=True)
            result = dy_ref[r].astype(F32) + rms_backward(values, scale, gain["ffn"], grad)
            gh[r] = result
            grows[ds(mine + i * 32, 32)] = result.astype(BF16)

        r_copy.start()
        o_copy.start()

    def attended_grads():
        wo_load.wait()
        r_copy.wait_recv()

        @pl.loop(0, q_wide // 256)
        def _(n):
            tile = dot_nn(grows[...], weights[:, ds(n * 256, 256)]).astype(BF16)
            ga[2 * n] = tile[:, :LANES]
            ga[2 * n + 1] = tile[:, LANES:]

        gain["weights"] = load(wa_in.at[:, :o_at], weights)
        transpose(grows, turned)
        att_load.wait()

        @pl.loop(0, wide // 256)
        def _(m):
            r = ds(m * 256, 256)
            pa[r, o_at:g_at] = dot_nn(turned[r], att[...]).astype(BF16)

        q_load.wait()
        k_load.wait()
        v_load.wait()

    def heads(g):
        if g + 1 < groups:
            p_loads.append(load(p_in.at[g + 1], prob.at[(g + 1) % 2]))
        p_loads[g].wait()
        pg = prob.at[g % 2]

        @pl.loop(0, tokens // blk)
        def _(i, g=g):
            r, r2 = ds(i * blk, blk), ds(tokens + i * blk, blk)
            lows = low_half((blk, LANES))
            q, do = qrot[g, r], ga[g, r]
            zero = jnp.zeros_like(q)
            qs[r], qs[r2] = jnp.where(lows, q, zero), jnp.where(lows, zero, q)
            dos[r], dos[r2] = jnp.where(lows, do, zero), jnp.where(lows, zero, do)

        dv[g] = dot_tn(pg[...], dos[...])

        @pl.loop(0, tokens // blk)
        def _(i, g=g, pg=pg):
            lows = low_half((blk, LANES))
            result = []
            for hh in range(2):
                r = ds(hh * tokens + i * blk, blk)
                p = pg[r].astype(F32)
                grad_p = dot_nt(dos[r], vdup[g])
                delta = jnp.sum(p * grad_p, axis=1, keepdims=True)
                scores = (p * (grad_p - delta) * (1.0 / math.sqrt(HD))).astype(BF16)
                pg[r] = scores
                result.append(dot_nn(scores, kdup[g]))
            dq[g, ds(i * blk, blk)] = jnp.where(lows, result[0], result[1])

        dk[g] = dot_tn(pg[...], qs[...])

    def fold(value):
        return value + pltpu.roll(value, HD, 1)

    def turn_back(values, grad_rot, gain, r):
        u = grad_rot * sin[r]
        early = first_quarter(u.shape)
        grad = grad_rot * cos[r] + jnp.where(
            early, pltpu.roll(u, LANES - HD // 2, 1), -pltpu.roll(u, HD // 2, 1)
        )
        scale = lax.rsqrt(head_mean(values * values) + EPSILON)
        weighted = grad * gain
        inner = head_mean(weighted * values)
        term = jnp.sum(grad * values * scale, axis=0, keepdims=True)
        return scale * (weighted - values * scale * scale * inner), fold(term)

    def unrotate():
        cos_load.wait()
        sin_load.wait()
        raw_load.wait()

        @pl.loop(0, tokens // blk)
        def _(i):
            r = ds(i * blk, blk)
            lows = low_half((blk, LANES))
            q_term = k_term = jnp.zeros((1, LANES), F32)
            for n in range(groups):
                grad, term = turn_back(raw[n, r], dq[n, r], gain["q"], r)
                dqkv[r, n * LANES : (n + 1) * LANES] = grad.astype(BF16)
                q_term += term
            for n in range(groups // 2):
                pair = jnp.where(lows, fold(dk[2 * n, r]), fold(dk[2 * n + 1, r]))
                grad, term = turn_back(raw[groups + n, r], pair, gain["k"], r)
                dqkv[r, q_wide + n * LANES : q_wide + (n + 1) * LANES] = grad.astype(BF16)
                k_term += term
                pair = jnp.where(lows, fold(dv[2 * n, r]), fold(dv[2 * n + 1, r]))
                dqkv[r, q_wide + kv_wide + n * LANES : q_wide + kv_wide + (n + 1) * LANES] = pair.astype(BF16)
            terms[0:1, wide:] += jnp.where(low_half((1, LANES)), q_term, k_term)

    def send_input():
        gain["weights"].wait()

        @pl.loop(0, wide // 256)
        def _(n):
            r = ds(n * 256, 256)
            n1send[:, r] = dot_nt(dqkv[ds(theirs, half)], weights[r]).astype(BF16)

        n_copy.start()

    def projection_grads():
        n1_load.wait()

        @pl.loop(0, wide // 256)
        def _(m):
            r = ds(m * 256, 256)
            for n in range(o_at // 256):
                cols = slice(n * 256, (n + 1) * 256)
                pa[r, cols] = dot_nn(stage[r], dqkv[:, cols]).astype(BF16)

    def output():
        om_load.wait()
        o_copy.wait_recv()

        @pl.loop(0, half // 64)
        def _(i):
            r = ds(i * 64, 64)
            bo_out[r] = (gi_out[r] + orecv[r].astype(F32)).astype(BF16)

    def own_input():
        @pl.loop(0, wide // 256)
        def _(n):
            r = ds(n * 256, 256)
            gi_out[:, r] = dot_nt(dqkv[ds(mine, half)], weights[r])

    def input_grads():
        n_copy.wait_recv()

        @pl.loop(0, half // 32)
        def _(i):
            r = ds(i * 32, 32)
            grad = gi_out[r] + n1recv[r].astype(F32)
            values = x_ref[r].astype(F32)
            scale = lax.rsqrt(jnp.mean(values * values, axis=-1, keepdims=True) + EPSILON)
            terms[0:1, :wide] += jnp.sum(grad * values * scale, axis=0, keepdims=True)
            gi_out[r] = gh[r] + rms_backward(values, scale, gain["attn"], grad)

        t_copy.start()

    def gain_grads():
        t_copy.wait_recv()

        both = terms[...] + terms_in[...]
        lows = low_half((1, LANES))
        rest_rows = jnp.zeros((GAIN_ROWS - 2, LANES), F32)
        for i in range(dp // 2):
            block = both[:, i * LANES : (i + 1) * LANES]
            swapped = pltpu.roll(block, HD, 1)
            even = jnp.where(lows, block[0:1], swapped[1:2])
            odd = jnp.where(lows, swapped[0:1], block[1:2])
            for o, row in ((2 * i, even), (2 * i + 1, odd)):
                packed = jnp.concatenate([row, both[0:1, wide:], rest_rows], axis=0)
                pg[o * GAIN_ROWS : (o + 1) * GAIN_ROWS] = packed.astype(BF16)

    steps = {
        "weights": weight_grads, "residual": residual, "attended": attended_grads, "heads": heads,
        "unrotate": unrotate, "send": send_input, "projection": projection_grads, "output": output,
        "own": own_input, "input": input_grads, "gains": gain_grads,
        "S": scatter.start, "P": scatter.chip, "C": scatter.chain,
    }
    waited = set()
    for name, *which in BACKWARD_ORDER:
        if name == "weights" and which[0] == 2:
            scatter.swapped(FLIPPED)
            waited.add(FLIPPED)
        steps[name](*which)
    for copy in (g_copy, o_copy, r_copy, n_copy, t_copy):
        copy.wait_send()
    for k in range(count):
        if k not in waited:
            scatter.swapped(k)
        scatter.finish(k)


def backward(dp, x, dy, saved, q_wide, kv_wide, ff_wide):
    half, wide = x.shape
    rows, tokens = wide // dp, 2 * half
    groups = q_wide // LANES
    length = layout_of(dp)[0]
    chunks = chunk_widths(ff_wide)
    widths = [3 * w for w in chunks] + [q_wide, q_wide + 2 * kv_wide, LANES]
    heights = [rows] * (CHUNKS + 2) + [GAIN_ROWS]
    shapes = [
        ((half, wide), BF16),
        ((half, wide), F32),
        ((GAIN_ROWS, LANES), F32),
        ((rows, q_wide), F32),
        ((2, rows, kv_wide), F32),
        ((rows, q_wide), F32),
        ((2, rows, ff_wide), F32),
        ((rows, ff_wide), F32),
    ]
    vmem = [
        ((wide, widths[0]), BF16),
        ((wide, max(widths[1:3])), BF16),
        ((wide, sum(widths[CHUNKS:-1])), BF16),
        ((dp * GAIN_ROWS, LANES), BF16),
        ((wide, tokens), BF16),
        ((wide, tokens), BF16),
        ((wide, tokens), BF16),
        ((2, 3, tokens, 256), BF16),
        ((2, 2 * tokens, tokens), BF16),
        ((groups + groups // 2, tokens, LANES), F32),
        ((groups, tokens, LANES), BF16),
        ((groups, tokens, LANES), BF16),
        ((groups, tokens, LANES), BF16),
        ((tokens, q_wide), BF16),
        ((wide, q_wide + 2 * kv_wide), BF16),
        ((dp * GAIN_ROWS, LANES), BF16),
        ((8, wide), F32),
        ((tokens, LANES), F32),
        ((tokens, LANES), F32),
        ((half, wide), F32),
        ((half, wide), F32),
        ((half, wide), BF16),
        ((half, wide), BF16),
        ((tokens, wide), BF16),
        ((half, wide), BF16),
        ((half, wide), BF16),
        ((groups, tokens, LANES), BF16),
        ((2 * tokens, LANES), BF16),
        ((2 * tokens, LANES), BF16),
        ((groups, tokens, LANES), F32),
        ((groups, tokens, LANES), F32),
        ((groups, tokens, LANES), F32),
        ((tokens, q_wide + 2 * kv_wide), BF16),
        ((8, wide + LANES), F32),
        ((8, wide + LANES), F32),
    ]
    for slots, turned in ((dp // 2, dp // 2), (length, 1), (length + 1, 2 * length + 2)):
        vmem += [((turned if k == FLIPPED else slots, heights[k], w), BF16) for k, w in enumerate(widths)]
    count = len(widths)
    return pl.pallas_call(
        functools.partial(bwd_kernel, dp, rows, half),
        out_shape=[jax.ShapeDtypeStruct(*s) for s in shapes],
        in_specs=[pl.BlockSpec(memory_space=pltpu.VMEM)] * 2
        + [pl.BlockSpec(memory_space=pl.ANY)] * len(saved),
        out_specs=[pl.BlockSpec(memory_space=pltpu.VMEM)] * len(shapes),
        scratch_shapes=[pltpu.VMEM(*s) for s in vmem]
        + [
            pltpu.SemaphoreType.DMA((count, n))
            for n in (dp // 2, length, 2 * length, dp // 2, length, 2 * length, 2 * length)
        ]
        + [
            pltpu.SemaphoreType.DMA((5, 2)),
            pltpu.SemaphoreType.DMA((24,)),
            pltpu.SemaphoreType.DMA((2, 3)),
        ],
        compiler_params=pltpu.CompilerParams(
            collective_id=4, has_side_effects=True, vmem_limit_bytes=63 * 1024 * 1024
        ),
        name="backward",
    )(x, dy, *saved)


def finish_kernel(dp, rows, qk_shard, count, gain_ref, *refs):
    ins, norm_out, qk_out, outs = refs[:count], refs[count], refs[count + 1], refs[count + 2 : 2 * count + 2]
    held, sem = refs[2 * count + 2 : -1], refs[-1]
    loads = [pltpu.make_async_copy(a, b, sem.at[0, i]) for i, (a, b) in enumerate(zip(ins, held))]
    copies = [pltpu.make_async_copy(a, b, sem.at[1, i]) for i, (a, b) in enumerate(zip(held, outs))]
    for copy in loads:
        copy.start()
    for load, copy in zip(loads, copies):
        load.wait()
        copy.start()
    block = gain_ref[0:8]
    norm_out[0:1] = block[0:1, :rows]
    norm_out[1:2] = pltpu.roll(block, LANES - rows, 1)[0:1, :rows]
    own = lax.axis_index("dp") * qk_shard
    for i in range(2):
        moved = pltpu.roll(block, lax.rem(2 * LANES - own - i * HD, LANES), 1)
        qk_out[i : i + 1] = moved[1:2, :qk_shard]
    for copy in copies:
        copy.wait()


def finish(dp, rows, gains, qk_shard, arrays):
    return pl.pallas_call(
        functools.partial(finish_kernel, dp, rows, qk_shard, len(arrays)),
        out_shape=[jax.ShapeDtypeStruct((2, rows), F32), jax.ShapeDtypeStruct((2, qk_shard), F32)]
        + [jax.ShapeDtypeStruct(a.shape, a.dtype) for a in arrays],
        in_specs=[pl.BlockSpec(memory_space=pltpu.VMEM)]
        + [pl.BlockSpec(memory_space=pl.ANY)] * len(arrays),
        out_specs=[pl.BlockSpec(memory_space=pltpu.VMEM)] * 2
        + [pl.BlockSpec(memory_space=pl.ANY)] * len(arrays),
        scratch_shapes=[pltpu.VMEM(a.shape, a.dtype) for a in arrays]
        + [pltpu.SemaphoreType.DMA((2, len(arrays)))],
        compiler_params=pltpu.CompilerParams(vmem_limit_bytes=32 * 1024 * 1024),
        name="finish",
    )(gains, *arrays)


def fast_device(
    block_input, cotangent, segment_ids, positions, norm_gains, qk_gains, w_query, w_keyval, w_output,
    w_gate_up, w_down,
):
    dp = lax.axis_size("dp")
    q_wide = w_query.shape[1]
    kv_wide, ff_wide = w_keyval.shape[2], w_gate_up.shape[2]
    qk_shard = qk_gains.shape[1]
    freq = np.tile(ROPE_BASE ** (-np.arange(0, HD, 2) / HD), 4)[None].astype(np.float32)
    saved = forward(
        dp, block_input, cotangent, segment_ids, positions, freq, norm_gains, qk_gains,
        w_query, w_keyval, w_output.T, w_gate_up, w_down.T,
    )
    block_output, grad_input, gains, grad_query, grad_keyval, grad_out, grad_gate_up, grad_down = backward(
        dp, block_input, cotangent, saved, q_wide, kv_wide, ff_wide
    )
    norm, qk, *rest = finish(
        dp, w_query.shape[0], gains, qk_shard,
        [block_output, grad_input, grad_query, grad_keyval, grad_out, grad_gate_up, grad_down],
    )
    block_output, grad_input, grad_query, grad_keyval, grad_out, grad_gate_up, grad_down = rest
    return (
        block_output,
        grad_input,
        norm,
        qk,
        grad_query,
        grad_keyval,
        grad_out.T,
        grad_gate_up,
        grad_down.T,
    )


def solution(mesh):
    return jax.shard_map(
        fast_device if mesh.shape["tensor"] == 2 and mesh.shape["dp"] == 16 else on_device,
        mesh=mesh,
        in_specs=(
            P(("dp", "tensor"), None),
            P(("dp", "tensor"), None),
            P("dp", None),
            P("dp", None),
            P(None, "dp"),
            P(None, "dp"),
            P("dp", "tensor"),
            P(None, "dp", "tensor"),
            P("tensor", "dp"),
            P(None, "dp", "tensor"),
            P("tensor", "dp"),
        ),
        out_specs=(
            P(("dp", "tensor"), None),
            P(("dp", "tensor"), None),
            P(None, "dp"),
            P(None, "dp"),
            P("dp", "tensor"),
            P(None, "dp", "tensor"),
            P("tensor", "dp"),
            P(None, "dp", "tensor"),
            P("tensor", "dp"),
        ),
        check_vma=False,
    )
```

```python
import functools
import math

import jax
import jax.numpy as jnp
import numpy as np
from jax import lax
from jax.experimental import pallas as pl
from jax.experimental.pallas import tpu as pltpu
from jax.sharding import PartitionSpec as P

HD = 64


EPSILON = 1e-05
ROPE_BASE = 1000000.0
NEG_FILL = -1e30


def rms_forward(values, gain):
    scale = lax.rsqrt(jnp.mean(values * values, axis=-1, keepdims=True) + EPSILON)
    return (values * scale * gain, scale)


def rms_backward(values, scale, gain, grad):
    weighted = grad * gain
    inner = jnp.mean(weighted * values, axis=-1, keepdims=True)
    return scale * (weighted - values * scale * scale * inner)


def rope_tables(places):
    freqs = ROPE_BASE ** (-jnp.arange(0, HD, 2).astype(jnp.float32) / HD)
    angles = places.astype(jnp.float32)[..., None] * freqs
    angles = jnp.concatenate([angles, angles], axis=-1)
    return (jnp.cos(angles), jnp.sin(angles))


def rotate_half(values):
    half = values.shape[-1] // 2
    return jnp.concatenate([-values[..., half:], values[..., :half]], axis=-1)


def rotate_back(values):
    half = values.shape[-1] // 2
    return jnp.concatenate([values[..., half:], -values[..., :half]], axis=-1)


def allowed_mask(segs):
    length = segs.shape[0]
    index = jnp.arange(length, dtype=jnp.int32)
    return (segs[:, None] == segs[None, :]) & (index[None, :] <= index[:, None])


def contract(left, right, left_dim, right_dim):
    return lax.dot_general(
        left, right, (((left_dim,), (right_dim,)), ((), ())), preferred_element_type=jnp.float32
    )


def fdot(left, right):
    return jnp.dot(left, right, preferred_element_type=jnp.float32)


def row_scores(q_rot, k_rot):
    kv_heads = k_rot.shape[1]
    groups = q_rot.shape[1] // kv_heads
    q_four = q_rot.reshape(q_rot.shape[0], kv_heads, groups, HD)
    scores = jnp.einsum("ikgd,jkd->kgij", q_four, k_rot, preferred_element_type=jnp.float32)
    return (scores / math.sqrt(HD), q_four)


def attend_row(q_rot, k_rot, values, segs):
    scores, q_four = row_scores(q_rot, k_rot)
    allowed = allowed_mask(segs)[None, None]
    masked = jnp.where(allowed, scores, NEG_FILL)
    top = jnp.max(masked, axis=-1, keepdims=True)
    expd = jnp.where(allowed, jnp.exp(masked - top), 0.0)
    total = jnp.sum(expd, axis=-1, keepdims=True)
    probs = (expd / total).astype(jnp.bfloat16)
    log_total = top[..., 0] + jnp.log(total[..., 0])
    attended = jnp.einsum("kgij,jkd->ikgd", probs, values, preferred_element_type=jnp.float32)
    return (attended.reshape(q_rot.shape).astype(jnp.bfloat16), log_total)


def back_row(q_rot, k_rot, values, grad_att, log_total, segs):
    scores, q_four = row_scores(q_rot, k_rot)
    allowed = allowed_mask(segs)[None, None]
    masked = jnp.where(allowed, scores, NEG_FILL)
    probs = jnp.where(allowed, jnp.exp(masked - log_total[..., None]), 0.0)
    probs_b = probs.astype(jnp.bfloat16)
    grad_four = grad_att.reshape(q_four.shape)
    grad_values = jnp.einsum(
        "kgij,ikgd->jkd", probs_b, grad_four, preferred_element_type=jnp.float32
    )
    grad_p = jnp.einsum("ikgd,jkd->kgij", grad_four, values, preferred_element_type=jnp.float32)
    delta = jnp.sum(probs * grad_p, axis=-1, keepdims=True)
    d_scores = (probs * (grad_p - delta) / math.sqrt(HD)).astype(jnp.bfloat16)
    grad_q = jnp.einsum(
        "kgij,jkd->ikgd", d_scores, k_rot, preferred_element_type=jnp.float32
    ).reshape(q_rot.shape)
    grad_k = jnp.einsum("kgij,ikgd->jkd", d_scores, q_four, preferred_element_type=jnp.float32)
    return (grad_q, grad_k, grad_values)


def layout_of(dp):
    if dp == 16:
        return (4, 4, 2)
    return (dp // 4, 2, dp // 2)


class Place:
    def __init__(self, dp):
        self.length, self.zs, self.xs = layout_of(dp)
        me = lax.axis_index("dp")
        self.z = lax.rem(me // self.zs, self.length)
        self.x = lax.rem(me // self.xs, 2)
        self.c = lax.rem(me, 2)

    def device(self, z, x, c):
        return z * self.zs + x * self.xs + c

    def greet(self):
        z, x, c = self.z, self.x, self.c
        barrier = pltpu.get_barrier_semaphore()

        def signal(target):
            pl.semaphore_signal(
                barrier, inc=1, device_id={"dp": target}, device_id_type=pl.DeviceIdType.MESH
            )

        signal(self.device(z, x, 1 - c))
        signal(self.device(z, 1 - x, c))
        pl.when(z > 0)(lambda: signal(self.device(z - 1, x, c)))
        pl.when(z < self.length - 1)(lambda: signal(self.device(z + 1, x, c)))
        ends = jnp.where(z > 0, 1, 0) + jnp.where(z < self.length - 1, 1, 0)
        pl.semaphore_wait(barrier, 2 + ends)


def remote(src, dst, send, recv, target):
    return pltpu.make_async_remote_copy(
        src_ref=src,
        dst_ref=dst,
        send_sem=send,
        recv_sem=recv,
        device_id={"dp": target},
        device_id_type=pl.DeviceIdType.MESH,
    )


def gather_kernel(dp, count, rows, *refs):
    ins, outs = refs[:count], refs[count : 2 * count]
    send, recv, local = refs[2 * count :]
    at = Place(dp)
    z, x, c, length = at.z, at.x, at.c, at.length
    below, above = at.device(z - 1, x, c), at.device(z + 1, x, c)
    beside, sibling = at.device(z, 1 - x, c), at.device(z, x, 1 - c)
    at.greet()
    own = at.device(z, x, c)

    def slab(k, o):
        return outs[k].at[pl.ds(pl.multiple_of(o * rows, rows), rows)]

    for k in range(count):
        pltpu.make_async_copy(ins[k], slab(k, own), local.at[k]).start()

    def move(k, oz, ox, way, target, first):
        o = at.device(oz, ox, c)
        src = ins[k] if first else slab(k, o)
        return remote(src, slab(k, o), send.at[k, oz * 2 + ox, way], recv.at[k, o], target)

    def arrived(k, o):
        remote(slab(k, o), slab(k, o), send.at[k, 0, 0], recv.at[k, o], sibling).wait_recv()

    def steps(act):
        for s in range(length):
            for sign in (1, -1) if s else (0,):
                oz = z - s * sign

                def event(oz=oz, s=s, sign=sign):
                    for k in range(count):
                        act(k, oz, s, sign)

                if s:
                    pl.when((oz >= 0) & (oz < length))(event)
                else:
                    event()
            if s:
                side(s - 1, act)
        side(length - 1, act)

    def side(s, act):
        for sign in (1, -1) if s else (0,):
            oz = z - s * sign

            def event(oz=oz):
                for k in range(count):
                    act(k, oz, None, 0)

            if s:
                pl.when((oz >= 0) & (oz < length))(event)
            else:
                event()

    def begin(k, oz, s, sign):
        if s is None:
            arrived(k, at.device(oz, 1 - x, c))
            move(k, oz, 1 - x, 3, sibling, False).start()
            return
        first = s == 0
        if not first:
            arrived(k, at.device(oz, x, c))
        if sign >= 0:
            pl.when(z < length - 1)(lambda: move(k, oz, x, 0, above, first).start())
        if sign <= 0:
            pl.when(z > 0)(lambda: move(k, oz, x, 1, below, first).start())
        move(k, oz, x, 2, beside, first).start()
        move(k, oz, x, 3, sibling, first).start()

    def finish(k, oz, s, sign):
        if s is None:
            move(k, oz, 1 - x, 3, sibling, False).wait_send()
            return
        first = s == 0
        if sign >= 0:
            pl.when(z < length - 1)(lambda: move(k, oz, x, 0, above, first).wait_send())
        if sign <= 0:
            pl.when(z > 0)(lambda: move(k, oz, x, 1, below, first).wait_send())
        move(k, oz, x, 2, beside, first).wait_send()
        move(k, oz, x, 3, sibling, first).wait_send()

    steps(begin)
    for oz in range(length):
        for ox in range(2):
            for k in range(count):
                arrived(k, at.device(oz, ox, 1 - c))
    steps(finish)
    for k in range(count):
        pltpu.make_async_copy(ins[k], slab(k, own), local.at[k]).wait()


def gather_rows(arrays, dp):
    count, rows = len(arrays), arrays[0].shape[0]
    return pl.pallas_call(
        functools.partial(gather_kernel, dp, count, rows),
        out_shape=[jax.ShapeDtypeStruct((dp * rows, a.shape[1]), a.dtype) for a in arrays],
        in_specs=[pl.BlockSpec(memory_space=pltpu.VMEM)] * count,
        out_specs=[pl.BlockSpec(memory_space=pl.ANY)] * count,
        scratch_shapes=[
            pltpu.SemaphoreType.DMA((count, dp // 2, 4)),
            pltpu.SemaphoreType.DMA((count, dp)),
            pltpu.SemaphoreType.DMA((count,)),
        ],
        compiler_params=pltpu.CompilerParams(collective_id=1, has_side_effects=True),
        name="gather_rows",
    )(*arrays)


def scatter_kernel(dp, count, rows, *refs):
    parts, outs = refs[:count], refs[count : 2 * count]
    mine, first, second, upward, downward = (
        refs[(2 + i) * count : (3 + i) * count] for i in range(5)
    )
    sent1, sent2, sent4, got1, got2, got_up, got_down, local = refs[7 * count :]
    at = Place(dp)
    z, x, c, length = at.z, at.x, at.c, at.length
    below, above = at.device(z - 1, x, c), at.device(z + 1, x, c)
    beside, sibling = at.device(z, 1 - x, c), at.device(z, x, 1 - c)
    at.greet()

    def slab(k, o):
        return parts[k].at[pl.ds(pl.multiple_of(o * rows, rows), rows)]

    def swap(k, t, ox):
        q = t * 2 + ox
        return remote(
            slab(k, at.device(t, ox, 1 - c)), first[k].at[q], sent1.at[k, q], got1.at[k, q], sibling
        )

    def keep(k, t, ox):
        q = t * 2 + ox
        return pltpu.make_async_copy(slab(k, at.device(t, ox, c)), mine[k].at[q], local.at[k, q])

    def cross(k, t):
        q = t * 2 + 1 - x
        return remote(first[k].at[q], second[k].at[t], sent2.at[k, t], got2.at[k, t], beside)

    def rise(k, t):
        return remote(second[k].at[t], upward[k].at[t], sent4.at[k, t], got_up.at[k, t], above)

    def fall(k, t):
        return remote(second[k].at[t], downward[k].at[t], sent4.at[k, t], got_down.at[k, t], below)

    def targets(act):
        for d in range(length - 1, -1, -1):
            for sign in (1, -1) if d else (0,):
                t = z + d * sign

                def event(t=t, sign=sign):
                    for k in range(count):
                        act(k, t, sign)

                if d:
                    pl.when((t >= 0) & (t < length))(event)
                else:
                    event()

    def wide(value):
        return value.astype(jnp.float32)

    def start(k, t, sign):
        for ox in (1 - x, x):
            swap(k, t, ox).start()
            keep(k, t, ox).start()

    def chip_sum(k, t, sign):
        for ox in (1 - x, x):
            q = t * 2 + ox
            keep(k, t, ox).wait()
            swap(k, t, ox).wait_recv()
            first[k][q] = (wide(first[k][q]) + wide(mine[k][q])).astype(jnp.bfloat16)
            if ox is not x:
                cross(k, t).start()

    def chain(k, t, sign):
        cross(k, t).wait_recv()
        if sign == 0:
            outs[k][...] = wide(second[k][t]) + wide(first[k][t * 2 + x])

            def add_up():
                rise(k, t).wait_recv()
                outs[k][...] += wide(upward[k][t])

            def add_down():
                fall(k, t).wait_recv()
                outs[k][...] += wide(downward[k][t])

            pl.when(z > 0)(add_up)
            pl.when(z < length - 1)(add_down)
            return
        base, move = (upward, rise) if sign > 0 else (downward, fall)
        inner = z > 0 if sign > 0 else z < length - 1

        def middle():
            move(k, t).wait_recv()
            second[k][t] = (
                wide(second[k][t]) + wide(first[k][t * 2 + x]) + wide(base[k][t])
            ).astype(jnp.bfloat16)

        def edge():
            second[k][t] = (wide(second[k][t]) + wide(first[k][t * 2 + x])).astype(jnp.bfloat16)

        pl.when(inner)(middle)
        pl.when(jnp.logical_not(inner))(edge)
        move(k, t).start()

    def finish(k, t, sign):
        swap(k, t, 0).wait_send()
        swap(k, t, 1).wait_send()
        cross(k, t).wait_send()
        if sign:
            (rise if sign > 0 else fall)(k, t).wait_send()

    targets(start)
    targets(chip_sum)
    targets(chain)
    targets(finish)


def scatter_rows(arrays, dp):
    count, rows = len(arrays), arrays[0].shape[0] // dp
    length = layout_of(dp)[0]
    slots = [dp // 2, dp // 2, length, length, length]
    return pl.pallas_call(
        functools.partial(scatter_kernel, dp, count, rows),
        out_shape=[jax.ShapeDtypeStruct((rows, a.shape[1]), jnp.float32) for a in arrays],
        in_specs=[pl.BlockSpec(memory_space=pl.ANY)] * count,
        out_specs=[pl.BlockSpec(memory_space=pltpu.VMEM)] * count,
        scratch_shapes=[
            pltpu.VMEM((n, rows, a.shape[1]), a.dtype) for n in slots for a in arrays
        ]
        + [
            pltpu.SemaphoreType.DMA((count, n))
            for n in (dp // 2, length, length, dp // 2, length, length, length, dp // 2)
        ],
        compiler_params=pltpu.CompilerParams(
            collective_id=2, has_side_effects=True, vmem_limit_bytes=60 * 1024 * 1024
        ),
        name="scatter_rows",
    )(*arrays)


def exchange(values):
    return lax.ppermute(values, "tensor", ((0, 1), (1, 0)))


def collect(values):
    if lax.axis_size("tensor") != 2:
        return lax.all_gather(values, "tensor", axis=0, tiled=True)
    other = exchange(values)
    low = lax.axis_index("tensor") == 0
    return jnp.concatenate([jnp.where(low, values, other), jnp.where(low, other, values)])


def spread(values):
    if lax.axis_size("tensor") != 2:
        return lax.psum_scatter(values, "tensor", scatter_dimension=0, tiled=True)
    half = values.shape[0] // 2
    low = lax.axis_index("tensor") == 0
    head, tail = values[:half], values[half:]
    other = exchange(jnp.where(low, tail, head).astype(jnp.bfloat16))
    return jnp.where(low, head, tail) + other.astype(jnp.float32)


def total(values):
    if lax.axis_size("tensor") != 2:
        return lax.psum(values, "tensor")
    return values + exchange(values)


def on_device(
    block_input,
    cotangent,
    segment_ids,
    positions,
    norm_gains,
    qk_gains,
    w_query,
    w_keyval,
    w_output,
    w_gate_up,
    w_down,
):
    dp = lax.axis_size("dp")
    rows_here, row_len = segment_ids.shape
    tokens_here = rows_here * row_len
    shard, q_wide = w_query.shape
    kv_wide, ff_wide = w_keyval.shape[2], w_gate_up.shape[2]
    qk_shard = qk_gains.shape[1]
    gains = jnp.concatenate(
        [norm_gains.T, jnp.pad(qk_gains.T, ((0, shard - qk_shard), (0, 0)))], axis=1
    )
    gains = jnp.pad(gains, ((0, 0), (0, 124)))
    attn_pack = jnp.concatenate([w_query, w_keyval[0], w_keyval[1], w_output.T, gains], axis=1)
    gate_up_pack = jnp.concatenate([w_gate_up[0], w_gate_up[1]], axis=1)
    attn_full, gate_up_full, down_full = gather_rows([attn_pack, gate_up_pack, w_down.T], dp)
    qkv_wide = q_wide + 2 * kv_wide
    qkv_full = attn_full[:, :qkv_wide]
    output_full = attn_full[:, qkv_wide : qkv_wide + q_wide]
    gain_cols = attn_full[:, qkv_wide + q_wide :].astype(jnp.float32)
    gain_attn, gain_ffn = gain_cols[:, 0], gain_cols[:, 1]
    qk_cols = gain_cols.reshape(dp, shard, 128)[:, :qk_shard, 2:4].reshape(dp * qk_shard, 2)
    gain_q, gain_k = qk_cols[:, 0], qk_cols[:, 1]
    heads_here = q_wide // HD
    kv_here = kv_wide // HD
    dy_rows = collect(cotangent)
    xlocal = block_input.astype(jnp.float32)
    normed_f, scale1 = rms_forward(xlocal, gain_attn)
    normed1 = collect(normed_f.astype(jnp.bfloat16))
    qkv = fdot(normed1, qkv_full)
    query = qkv[:, :q_wide].reshape(rows_here, row_len, heads_here, HD)
    keys = qkv[:, q_wide : q_wide + kv_wide].reshape(rows_here, row_len, kv_here, HD)
    values = (
        qkv[:, q_wide + kv_wide :].astype(jnp.bfloat16).reshape(rows_here, row_len, kv_here, HD)
    )
    q_norm, q_scale = rms_forward(query, gain_q)
    k_norm, k_scale = rms_forward(keys, gain_k)
    cosv, sinv = rope_tables(positions)
    cosv = cosv[:, :, None, :]
    sinv = sinv[:, :, None, :]
    q_rot = (q_norm * cosv + rotate_half(q_norm) * sinv).astype(jnp.bfloat16)
    k_rot = (k_norm * cosv + rotate_half(k_norm) * sinv).astype(jnp.bfloat16)
    attended, log_total = jax.vmap(attend_row)(q_rot, k_rot, values, segment_ids)
    att_flat = attended.reshape(tokens_here, heads_here * HD)
    hidden = xlocal + spread(contract(att_flat, output_full, 1, 1))
    normed_g, scale2 = rms_forward(hidden, gain_ffn)
    normed2 = collect(normed_g.astype(jnp.bfloat16))
    gate_up = fdot(normed2, gate_up_full)
    gate_proj, up_proj = gate_up[:, :ff_wide], gate_up[:, ff_wide:]
    sigmoid_gate = jax.nn.sigmoid(gate_proj)
    silu_gate = gate_proj * sigmoid_gate
    act = (silu_gate * up_proj).astype(jnp.bfloat16)
    block_output = (hidden + spread(contract(act, down_full, 1, 1))).astype(jnp.bfloat16)
    grad_act = fdot(dy_rows, down_full)
    grad_down = contract(dy_rows, act, 0, 0).astype(jnp.bfloat16)
    d_gate = grad_act * up_proj * sigmoid_gate * (1.0 + gate_proj * (1.0 - sigmoid_gate))
    d_gate_up = jnp.concatenate(
        [d_gate.astype(jnp.bfloat16), (grad_act * silu_gate).astype(jnp.bfloat16)], axis=1
    )
    grad_gate_up = contract(normed2, d_gate_up, 0, 0).astype(jnp.bfloat16)
    grad_n2 = spread(contract(d_gate_up, gate_up_full, 1, 1))
    gain_ffn_grad = jnp.sum(grad_n2 * hidden * scale2, axis=0)
    grad_hidden = cotangent.astype(jnp.float32) + rms_backward(hidden, scale2, gain_ffn, grad_n2)
    grad_rows = collect(grad_hidden.astype(jnp.bfloat16))
    grad_att = (
        fdot(grad_rows, output_full)
        .astype(jnp.bfloat16)
        .reshape(rows_here, row_len, heads_here, HD)
    )
    grad_out = contract(grad_rows, att_flat, 0, 0).astype(jnp.bfloat16)
    grad_qrot, grad_krot, grad_vals = jax.vmap(back_row)(
        q_rot, k_rot, values, grad_att, log_total, segment_ids
    )
    grad_qn = grad_qrot * cosv + rotate_back(grad_qrot * sinv)
    grad_kn = grad_krot * cosv + rotate_back(grad_krot * sinv)
    gain_q_grad = jnp.sum(grad_qn * query * q_scale, axis=(0, 1, 2))
    gain_k_grad = jnp.sum(grad_kn * keys * k_scale, axis=(0, 1, 2))
    d_query = rms_backward(query, q_scale, gain_q, grad_qn).astype(jnp.bfloat16)
    d_keys = rms_backward(keys, k_scale, gain_k, grad_kn).astype(jnp.bfloat16)
    d_qkv = jnp.concatenate(
        [
            d_query.reshape(tokens_here, q_wide),
            d_keys.reshape(tokens_here, kv_wide),
            grad_vals.astype(jnp.bfloat16).reshape(tokens_here, kv_wide),
        ],
        axis=1,
    )
    grad_qkv = contract(normed1, d_qkv, 0, 0).astype(jnp.bfloat16)
    grad_n1 = spread(contract(d_qkv, qkv_full, 1, 1))
    gain_attn_grad = jnp.sum(grad_n1 * xlocal * scale1, axis=0)
    grad_input = grad_hidden + rms_backward(xlocal, scale1, gain_attn, grad_n1)
    gain_terms = total(
        jnp.concatenate([gain_attn_grad, gain_ffn_grad, gain_q_grad, gain_k_grad])[None]
    )[0]
    wide = dp * shard
    norm_terms = gain_terms[: 2 * wide].reshape(2, wide).T
    qk_terms = gain_terms[2 * wide :].reshape(2, dp, qk_shard).transpose(1, 2, 0)
    qk_terms = jnp.pad(qk_terms, ((0, 0), (0, shard - qk_shard), (0, 0))).reshape(wide, 2)
    gain_pack = jnp.concatenate([norm_terms, qk_terms], axis=1).astype(jnp.bfloat16)
    gain_pack = jnp.pad(gain_pack, ((0, 0), (0, 124)))
    grad_attn = jnp.concatenate([grad_qkv, grad_out, gain_pack], axis=1)
    attn_sum, gate_up_sum, down_sum = scatter_rows([grad_attn, grad_gate_up, grad_down], dp)
    gain_sum = attn_sum[:, qkv_wide + q_wide :]
    return (
        block_output,
        grad_input,
        gain_sum[:, 0:2].T,
        gain_sum[:qk_shard, 2:4].T,
        attn_sum[:, :q_wide],
        jnp.stack([attn_sum[:, q_wide : q_wide + kv_wide], attn_sum[:, q_wide + kv_wide : qkv_wide]]),
        attn_sum[:, qkv_wide : qkv_wide + q_wide].T,
        jnp.stack([gate_up_sum[:, :ff_wide], gate_up_sum[:, ff_wide:]]),
        down_sum.T,
    )


MESH = pl.DeviceIdType.MESH
LANES = 128
F32, BF16 = jnp.float32, jnp.bfloat16


def dot_nn(a, b):
    return lax.dot_general(a, b, (((1,), (0,)), ((), ())), preferred_element_type=F32)


def dot_nt(a, b):
    return lax.dot_general(a, b, (((1,), (1,)), ((), ())), preferred_element_type=F32)


def dot_tn(a, b):
    return lax.dot_general(a, b, (((0,), (0,)), ((), ())), preferred_element_type=F32)


def lane_of(shape):
    return lax.broadcasted_iota(jnp.int32, shape, len(shape) - 1)


def head_mean(values):
    row = lax.broadcasted_iota(jnp.int32, (LANES, LANES), 0) // HD
    ones = jnp.where(row == lane_of((LANES, LANES)) // HD, 1.0 / HD, 0.0).astype(BF16)
    high = values.astype(BF16)
    low = (values - high.astype(F32)).astype(BF16)
    return dot_nn(high, ones) + dot_nn(low, ones)


def low_half(shape):
    return lane_of(shape) < HD


def first_quarter(shape):
    return lax.rem(lane_of(shape), HD) < HD // 2


def ds(start, size):
    if isinstance(start, int):
        return pl.ds(start, size)
    return pl.ds(pl.multiple_of(start, size), size)


class Gather:
    def __init__(self, at, rows, slabs, flipped, send, recv):
        self.at, self.rows, self.slabs, self.flipped = at, rows, slabs, flipped
        self.send, self.recv = send, recv

    def slab(self, k, o):
        return self.slabs[k](ds(o * self.rows[k], self.rows[k]))

    def move(self, k, oz, ox, way, target):
        at = self.at
        o = at.device(oz, ox, at.c)
        return remote(
            self.slab(k, o), self.slab(k, o), self.send.at[k, oz * 2 + ox, way], self.recv.at[k, o], target
        )

    def arrived(self, k, o):
        at = self.at
        slab = self.slab(k, o)
        remote(slab, slab, self.send.at[k, 0, 0], self.recv.at[k, o], at.sibling).wait_recv()

    def sources(self, s, act):
        at = self.at
        for sign in (1, -1) if s else (0,):
            oz = at.z - s * sign
            if s:
                pl.when((oz >= 0) & (oz < at.length))(lambda oz=oz, sign=sign: act(oz, sign))
            else:
                act(oz, 0)

    def along(self, k, oz, ox, sign, act):
        at = self.at
        if sign >= 0:
            pl.when(at.z < at.length - 1)(lambda: act(self.move(k, oz, ox, 0, at.above)))
        if sign <= 0:
            pl.when(at.z > 0)(lambda: act(self.move(k, oz, ox, 1, at.below)))

    def outgoing(self, k, s, oz, sign, act):
        at = self.at
        self.along(k, oz, at.x, sign, act)
        if not s or k not in self.flipped:
            act(self.move(k, oz, at.x, 2, at.beside))
        act(self.move(k, oz, at.x, 3, at.sibling))

    def onward(self, k, oz, sign, act):
        at = self.at
        if k in self.flipped:
            self.along(k, oz, 1 - at.x, sign, act)
        act(self.move(k, oz, 1 - at.x, 3, at.sibling))

    def main(self, k, s):
        at = self.at

        def act(oz, sign):
            if s:
                self.arrived(k, at.device(oz, at.x, at.c))
            self.outgoing(k, s, oz, sign, lambda m: m.start())

        self.sources(s, act)

    def side(self, k, s):
        at = self.at

        def act(oz, sign):
            self.arrived(k, at.device(oz, 1 - at.x, at.c))
            self.onward(k, oz, sign, lambda m: m.start())

        self.sources(s, act)

    def final(self, k):
        at = self.at
        for oz in range(at.length):
            for ox in range(2):
                self.arrived(k, at.device(oz, ox, 1 - at.c))

    def finish(self, k):
        at = self.at
        for s in range(at.length):
            self.sources(s, lambda oz, sign: self.outgoing(k, s, oz, sign, lambda m: m.wait_send()))
            self.sources(s, lambda oz, sign: self.onward(k, oz, sign, lambda m: m.wait_send()))


class Spot(Place):
    def __init__(self, dp):
        super().__init__(dp)
        z, x, c = self.z, self.x, self.c
        self.below, self.above = self.device(z - 1, x, c), self.device(z + 1, x, c)
        self.beside, self.sibling = self.device(z, 1 - x, c), self.device(z, x, 1 - c)
        self.own = self.device(z, x, c)
        self.t = lax.axis_index("tensor")

    def greet(self):
        barrier = pltpu.get_barrier_semaphore()

        def signal(target):
            pl.semaphore_signal(barrier, inc=1, device_id=target, device_id_type=MESH)

        signal({"dp": self.sibling})
        signal({"dp": self.beside})
        signal({"tensor": 1 - self.t})
        pl.when(self.z > 0)(lambda: signal({"dp": self.below}))
        pl.when(self.z < self.length - 1)(lambda: signal({"dp": self.above}))
        ends = jnp.where(self.z > 0, 1, 0) + jnp.where(self.z < self.length - 1, 1, 0)
        pl.semaphore_wait(barrier, 3 + ends)


def partner(at, src, dst, sems):
    return pltpu.make_async_remote_copy(
        src_ref=src,
        dst_ref=dst,
        send_sem=sems.at[0],
        recv_sem=sems.at[1],
        device_id={"tensor": 1 - at.t},
        device_id_type=MESH,
    )


CHUNKS = 3
GAIN_ROWS = 16
FLIPPED = 1


def chunk_widths(ff_wide):
    tiles = ff_wide // 256
    sizes = [tiles * 4 // 9, tiles * 2 // 9]
    return [256 * n for n in sizes + [tiles - sum(sizes)]]


FORWARD_ORDER = (
    ("M", 0, 0), ("fill",), ("M", 2, 0), ("D", 0, 0), ("M", 0, 1), ("D", 2, 0), ("M", 0, 2), ("M", 3, 0),
    ("tables",), ("M", 0, 3), ("D", 0, 1), ("M", 1, 0), ("D", 0, 2), ("M", 3, 1), ("D", 0, 3), ("F", 0),
    ("gains",), ("norm1",), ("project",), ("M", 1, 1), ("rotate",), ("attend0",), ("partial0",), ("M", 1, 2),
    ("attend1",), ("partial1",), ("D", 1, 0), ("M", 1, 3), ("norm2",), ("D", 2, 1), ("D", 3, 0), ("M", 3, 2),
    ("M", 2, 1), ("D", 1, 1), ("D", 2, 2), ("D", 1, 2), ("D", 1, 3), ("M", 3, 3), ("M", 2, 2), ("D", 3, 1),
    ("F", 1), ("own", 0), ("other", 0), ("D", 2, 3), ("combine", 0), ("M", 2, 3), ("D", 3, 2), ("D", 3, 3),
    ("F", 2), ("own", 1), ("other", 1), ("combine", 1), ("F", 3), ("own", 2), ("other", 2), ("combine", 2),
    ("close",),
)


def transpose(src, dst):
    @pl.loop(0, src.shape[1] // LANES)
    def _(i):
        c = ds(i * LANES, LANES)
        dst[c] = src[:, c].T


def spread_gains(packed, dp, gain_rows):
    lows = low_half((1, LANES))
    qk = jnp.zeros((1, LANES), F32)
    for i in range(dp // 2):
        even = packed[2 * i * GAIN_ROWS : (2 * i + 1) * GAIN_ROWS].astype(F32)
        odd = packed[(2 * i + 1) * GAIN_ROWS : (2 * i + 2) * GAIN_ROWS].astype(F32)
        cols = slice(i * LANES, (i + 1) * LANES)
        gain_rows[0:1, cols] = jnp.where(lows, even[0:1], pltpu.roll(odd, HD, 1)[0:1])
        gain_rows[1:2, cols] = jnp.where(lows, pltpu.roll(even, HD, 1)[0:1], odd[0:1])
        qk += even[1:2] + odd[1:2]
    return qk


def fwd_kernel(
    dp, rows, half, x_ref, dy_ref, seg_ref, pos_ref, freq_ref, norm_ref, qk_ref, wq_ref, wkv_ref, wo_ref,
    wgu_ref, wd_ref,
    wa_out, wg_out, n1_out, raw_out, p_out, qrot_out, kdup_out, vdup_out, att_out, hidden_out, n2_out,
    dyf_out, act_out, dg_out, du_out, cos_out, sin_out, gnm_out, gno_out, om_out, oo_out,
    wa, wg, wf0, wf1, wf2, xf, dyf, n1, n2, raw, prob, qrot, kdup, vdup, att, hidden, act, dg, du, cos, sin,
    segc, gn, op, part_out, part_in, gno, oo, om, gain_rows, n1t, n2t, dyt,
    send, recv, ysem, outsem,
):
    at = Spot(dp)
    wide = dp * rows
    tokens = 2 * half
    q_wide, kv_wide, ff_wide = wq_ref.shape[1], wkv_ref.shape[2], wd_ref.shape[1]
    chunks = chunk_widths(ff_wide)
    wf = (wf0, wf1, wf2)
    o_at, g_at = q_wide + 2 * kv_wide, 2 * q_wide + 2 * kv_wide
    groups = q_wide // LANES
    mine, theirs = at.t * half, (1 - at.t) * half
    own_rows = ds(at.own * rows, rows)
    outs = []

    def put(src, dst):
        copy = pltpu.make_async_copy(src, dst, outsem.at[len(outs)])
        copy.start()
        outs.append(copy)

    at.greet()
    gather = Gather(
        at,
        [rows] * (CHUNKS + 1) + [GAIN_ROWS],
        [lambda r: wa.at[r]] + [lambda r, j=j: wf[j].at[r] for j in range(CHUNKS)] + [lambda r: wg.at[r]],
        (1 + FLIPPED,),
        send,
        recv,
    )
    wa[own_rows, 0:q_wide] = wq_ref[...]
    wa[own_rows, q_wide : q_wide + kv_wide] = wkv_ref[0]
    wa[own_rows, q_wide + kv_wide : o_at] = wkv_ref[1]
    wa[own_rows, o_at:g_at] = wo_ref[...]
    norms = jnp.concatenate([norm_ref[...].astype(F32), jnp.zeros((2, LANES - rows), F32)], axis=1)
    norms = jnp.concatenate([norms, jnp.zeros((6, LANES), F32)], axis=0)
    qk_shard = qk_ref.shape[1]
    qk = jnp.concatenate([qk_ref[...].astype(F32), jnp.zeros((2, LANES - qk_shard), F32)], axis=1)
    qk = jnp.concatenate([qk, jnp.zeros((6, LANES), F32)], axis=0)
    wg[ds(at.own * GAIN_ROWS, GAIN_ROWS)] = jnp.concatenate(
        [
            norms[0:1] + pltpu.roll(norms, rows, 1)[1:2],
            pltpu.roll(qk, at.own * qk_shard, 1)[0:1] + pltpu.roll(qk, at.own * qk_shard + HD, 1)[1:2],
            jnp.zeros((GAIN_ROWS - 2, LANES), F32),
        ],
        axis=0,
    ).astype(BF16)
    x_copy = partner(at, x_ref, xf.at[ds(mine, half)], ysem.at[0])
    dy_copy = partner(at, dy_ref, dyf.at[ds(mine, half)], ysem.at[1])
    out_copy = partner(at, part_out, part_in, ysem.at[2])
    n2_copy = partner(at, n2.at[ds(mine, half)], n2.at[ds(mine, half)], ysem.at[3])
    gain = {}
    blk = 128

    def fill():
        x_copy.start()
        dy_copy.start()
        for j, chunk in enumerate(chunks):
            cols = slice(sum(chunks[:j]), sum(chunks[: j + 1]))
            wf[j][own_rows, 0:chunk] = wgu_ref[0, :, cols]
            wf[j][own_rows, chunk : 2 * chunk] = wgu_ref[1, :, cols]
            wf[j][own_rows, 2 * chunk :] = wd_ref[:, cols]

    def tables():
        xf[ds(mine, half)] = x_ref[...]
        dyf[ds(mine, half)] = dy_ref[...]
        segc[...] = jnp.broadcast_to(seg_ref[...].astype(F32), (LANES, tokens)).T
        cos[...] = jnp.broadcast_to(pos_ref[...].astype(F32), (LANES, tokens)).T

        @pl.loop(0, tokens // 64)
        def _(i):
            r = ds(i * 64, 64)
            angles = cos[r] * freq_ref[...]
            cos[r] = jnp.cos(angles)
            sin[r] = jnp.sin(angles)

        put(cos, cos_out)
        put(sin, sin_out)

    def gains():
        put(wa, wa_out)
        put(wg, wg_out)
        qk = spread_gains(wg, dp, gain_rows)
        lows = low_half((1, LANES))
        gain["q"] = jnp.where(lows, qk, pltpu.roll(qk, HD, 1))
        gain["k"] = jnp.where(lows, pltpu.roll(qk, HD, 1), qk)
        x_copy.wait_recv()

    def norm1():
        @pl.loop(0, tokens // 64)
        def _(i):
            r = ds(i * 64, 64)
            values = xf[r].astype(F32)
            n1[r] = rms_forward(values, gain_rows[0:1, :])[0].astype(BF16)


    def project():
        @pl.loop(0, o_at // 256)
        def _(n):
            tile = dot_nn(n1[...], wa[:, ds(n * 256, 256)])
            raw[2 * n] = tile[:, :LANES]
            raw[2 * n + 1] = tile[:, LANES:]

        put(raw, raw_out)

    def rope(n, gain_row, r):
        values = raw[n, r]
        normed = values * lax.rsqrt(head_mean(values * values) + EPSILON) * gain_row
        early = first_quarter(normed.shape)
        turned = jnp.where(early, -pltpu.roll(normed, LANES - HD // 2, 1), pltpu.roll(normed, HD // 2, 1))
        return normed * cos[r] + turned * sin[r]

    def doubled(tile):
        swapped = pltpu.roll(tile, HD, 1)
        lows = low_half(tile.shape)
        return jnp.where(lows, tile, swapped).astype(BF16), jnp.where(lows, swapped, tile).astype(BF16)

    def rotate():
        @pl.loop(0, tokens // blk)
        def _(i):
            r = ds(i * blk, blk)
            for n in range(groups):
                qrot[n, r] = rope(n, gain["q"], r).astype(BF16)
            for n in range(groups // 2):
                kdup[2 * n, r], kdup[2 * n + 1, r] = doubled(rope(groups + n, gain["k"], r))
                vdup[2 * n, r], vdup[2 * n + 1, r] = doubled(raw[groups + groups // 2 + n, r])

        put(qrot, qrot_out)
        put(kdup, kdup_out)
        put(vdup, vdup_out)
        transpose(n1, n1t)
        put(n1t, n1_out)

    def attend(base):
        @pl.loop(0, groups * (half // blk))
        def _(step):
            g = step // (half // blk)
            start = base + lax.rem(step, half // blk) * blk
            r = ds(start, blk)
            q = qrot[g, r]
            lows = low_half(q.shape)
            index = lax.broadcasted_iota(jnp.int32, (blk, tokens), 0) + start
            allowed = (segc[r, 0:1] == seg_ref[...].astype(F32)) & (lane_of((blk, tokens)) <= index)
            result = []
            for hh in range(2):
                picked = jnp.where(lows if hh == 0 else jnp.logical_not(lows), q, jnp.zeros_like(q))
                scores = dot_nt(picked, kdup[g]) * (1.0 / math.sqrt(HD))
                scores = jnp.where(allowed, scores, NEG_FILL)
                e = jnp.exp(scores - jnp.max(scores, axis=1, keepdims=True))
                p = (e / jnp.sum(e, axis=1, keepdims=True)).astype(BF16)
                prob[g, ds(hh * tokens + start, blk)] = p
                result.append(dot_nn(p, vdup[g]))
            att[r, ds(g * LANES, LANES)] = jnp.where(lows, result[0], result[1]).astype(BF16)

    def send_partial():
        @pl.loop(0, wide // 256)
        def _(n):
            cols = ds(n * 256, 256)
            part_out[:, cols] = dot_nt(att[ds(theirs, half)], wa[cols, o_at:g_at]).astype(BF16)

        out_copy.start()
        dy_copy.wait_recv()
        transpose(dyf, dyt)
        put(dyt, dyf_out)

    def attend_mine():
        attend(mine)
        put(prob, p_out)
        put(att, att_out)

    def own_partial():
        @pl.loop(0, wide // 256)
        def _(n):
            cols = ds(n * 256, 256)
            hidden[:, cols] = x_ref[:, cols].astype(F32) + dot_nt(att[ds(mine, half)], wa[cols, o_at:g_at])

        out_copy.wait_recv()

    def norm2():
        @pl.loop(0, half // 64)
        def _(i):
            r = ds(i * 64, 64)
            values = hidden[r] + part_in[r].astype(F32)
            hidden[r] = values
            n2[ds(mine + i * 64, 64)] = rms_forward(values, gain_rows[1:2, :])[0].astype(BF16)

        put(hidden, hidden_out)
        n2_copy.start()

    def hidden_units(j, base):
        chunk, before = chunks[j], sum(chunks[:j])

        @pl.loop(0, chunk // 256)
        def _(n):
            r = ds(base, half)
            gate = dot_nn(n2[r], wf[j][:, ds(n * 256, 256)])
            up = dot_nn(n2[r], wf[j][:, ds(chunk + n * 256, 256)])
            gact = dot_nn(dyf[r], wf[j][:, ds(2 * chunk + n * 256, 256)])
            sig = jax.nn.sigmoid(gate)
            silu = gate * sig
            cols = ds(before + n * 256, 256)
            act[r, cols] = (silu * up).astype(BF16)
            dg[r, cols] = (gact * up * sig * (1.0 + gate * (1.0 - sig))).astype(BF16)
            du[r, cols] = (gact * silu).astype(BF16)

    def partner_units(j):
        if j == 0:
            n2_copy.wait_recv()
        hidden_units(j, theirs)
        cols = slice(sum(chunks[:j]), sum(chunks[: j + 1]))
        for src, dst in ((act, act_out), (dg, dg_out), (du, du_out)):
            put(src.at[:, cols], dst.at[:, cols])

    def combine(j):
        chunk = chunks[j]
        cols = slice(sum(chunks[:j]), sum(chunks[: j + 1]))

        @pl.loop(0, wide // 256)
        def _(n):
            r = ds(n * 256, 256)
            down = dot_nt(act[:, cols], wf[j][r, 2 * chunk :])
            back = dot_nt(dg[:, cols], wf[j][r, :chunk]) + dot_nt(du[:, cols], wf[j][r, chunk : 2 * chunk])
            if j == 0:
                op[:, r] = down
                gn[:, r] = back
            else:
                op[:, r] += down
                gn[:, r] += back

        if j == 1:
            transpose(n2, n2t)
            put(n2t, n2_out)

    def close():
        put(gn.at[ds(mine, half)], gnm_out)

        @pl.loop(0, half // 64)
        def _(i):
            r = ds(i * 64, 64)
            gno[r] = gn[ds(theirs + i * 64, 64)].astype(BF16)
            oo[r] = op[ds(theirs + i * 64, 64)].astype(BF16)
            om[r] = op[ds(mine + i * 64, 64)] + hidden[r]

        put(gno, gno_out)
        put(oo, oo_out)
        put(om, om_out)

    def joined(stage):
        def act(k, *s):
            if k == 0:
                stage(CHUNKS + 1, *s)
            stage(k, *s)

        return act

    steps = {
        "fill": fill, "tables": tables, "gains": gains, "norm1": norm1, "project": project, "rotate": rotate,
        "attend0": lambda: attend(theirs), "partial0": send_partial, "attend1": attend_mine,
        "partial1": own_partial, "norm2": norm2, "own": lambda j: hidden_units(j, mine),
        "other": partner_units, "combine": combine, "close": close,
        "M": joined(gather.main), "D": joined(gather.side), "F": joined(gather.final),
    }
    for name, *which in FORWARD_ORDER:
        steps[name](*which)
    for copy in (x_copy, dy_copy, out_copy, n2_copy):
        copy.wait_send()
    for k in range(CHUNKS + 2):
        gather.finish(k)
    for copy in outs:
        copy.wait()


def forward(dp, x, dy, seg, pos, freq, norms, qks, wq, wkv, wo_t, wgu, wd_t):
    rows, half = wq.shape[0], x.shape[0]
    tokens, wide = 2 * half, dp * rows
    q_wide, kv_wide, ff_wide = wq.shape[1], wkv.shape[2], wd_t.shape[1]
    groups = q_wide // LANES
    attn_wide = 2 * q_wide + 2 * kv_wide
    shapes = [
        ((wide, attn_wide), BF16),
        ((dp * GAIN_ROWS, LANES), BF16),
        ((wide, tokens), BF16),
        ((2 * groups, tokens, LANES), F32),
        ((groups, 2 * tokens, tokens), BF16),
        ((groups, tokens, LANES), BF16),
        ((groups, tokens, LANES), BF16),
        ((groups, tokens, LANES), BF16),
        ((tokens, q_wide), BF16),
        ((half, wide), F32),
        ((wide, tokens), BF16),
        ((wide, tokens), BF16),
        ((tokens, ff_wide), BF16),
        ((tokens, ff_wide), BF16),
        ((tokens, ff_wide), BF16),
        ((tokens, LANES), F32),
        ((tokens, LANES), F32),
        ((half, wide), F32),
        ((half, wide), BF16),
        ((half, wide), F32),
        ((half, wide), BF16),
    ]
    (wa, wg, n1, raw, p, qrot, kdup, vdup, att, hidden, n2, dyf, act, dg, du, cos, sin, gnm, gno, om, oo) = shapes
    flat = ((tokens, wide), BF16)
    vmem = [
        wa, wg, *[((wide, 3 * w), BF16) for w in chunk_widths(ff_wide)], flat, flat, flat, flat, raw, p, qrot, kdup, vdup, att,
        hidden, act, dg, du, cos, sin, cos, ((tokens, wide), F32), ((tokens, wide), F32), oo, oo, gno, oo, om,
        ((8, wide), F32), n1, n2, dyf,
    ]
    return pl.pallas_call(
        functools.partial(fwd_kernel, dp, rows, half),
        out_shape=[jax.ShapeDtypeStruct(*s) for s in shapes],
        in_specs=[pl.BlockSpec(memory_space=pltpu.VMEM)] * 12,
        out_specs=[pl.BlockSpec(memory_space=pl.ANY)] * len(shapes),
        scratch_shapes=[pltpu.VMEM(*s) for s in vmem]
        + [
            pltpu.SemaphoreType.DMA((CHUNKS + 2, dp // 2, 4)),
            pltpu.SemaphoreType.DMA((CHUNKS + 2, dp)),
            pltpu.SemaphoreType.DMA((4, 2)),
            pltpu.SemaphoreType.DMA((len(shapes) + 3 * CHUNKS,)),
        ],
        compiler_params=pltpu.CompilerParams(
            collective_id=3, has_side_effects=True, vmem_limit_bytes=62 * 1024 * 1024
        ),
        name="forward",
    )(x, dy, seg, pos, freq, norms, qks, wq, wkv, wo_t, wgu, wd_t)


class Scatter:
    def __init__(self, at, rows, slabs, flipped, first, second, chained, emit, sems):
        self.at, self.rows, self.slabs, self.flipped, self.emit = at, rows, slabs, flipped, emit
        self.first, self.second, self.chained = first, second, chained
        self.sent1, self.sent2, self.sent4, self.got1, self.got2, self.got_up, self.got_down = sems

    def slab(self, k, o):
        return self.slabs[k](ds(o * self.rows[k], self.rows[k]))

    def swap(self, k, t, ox):
        at, q = self.at, t * 2 + ox
        src = self.slab(k, at.device(t, ox, 1 - at.c))
        return remote(src, self.first[k].at[q], self.sent1.at[k, q], self.got1.at[k, q], at.sibling)

    def cross(self, k, t):
        at = self.at
        q, slot = t * 2 + 1 - at.x, 0 if k in self.flipped else t
        return remote(
            self.first[k].at[q], self.second[k].at[slot], self.sent2.at[k, t], self.got2.at[k, slot], at.beside
        )

    def crossed(self, k, t):
        at = self.at
        slot = 0 if k in self.flipped else t
        block = self.second[k].at[slot]
        remote(block, block, self.sent2.at[k, t], self.got2.at[k, slot], at.beside).wait_recv()

    def slot(self, t, ox, last_down):
        return ox * (self.at.length + 1) + (self.at.length if last_down else t)

    def along(self, k, t, ox, up, distance):
        at, lane = self.at, ox * self.at.length + t
        src = self.first[k].at[t * 2 + ox] if k in self.flipped else self.second[k].at[t]
        dst = self.chained[k].at[self.slot(t, ox, distance == 1 and not up)]
        got = self.got_up if up else self.got_down
        return remote(src, dst, self.sent4.at[k, lane], got.at[k, lane], at.above if up else at.below)

    def arrive(self, k, t, ox, up, last):
        at, lane = self.at, ox * self.at.length + t
        block = self.chained[k].at[self.slot(t, ox, last and not up)]
        got = self.got_up if up else self.got_down
        remote(block, block, self.sent4.at[k, lane], got.at[k, lane], at.above).wait_recv()

    def lanes(self, k):
        return (1 - self.at.x, self.at.x) if k in self.flipped else (0,)

    def targets(self, act, distances=None):
        at = self.at
        for d in range(at.length - 1, -1, -1) if distances is None else distances:
            for sign in (1, -1) if d else (0,):
                t = at.z + d * sign
                if d:
                    pl.when((t >= 0) & (t < at.length))(lambda t=t, sign=sign, d=d: act(t, sign, d))
                else:
                    act(t, 0, 0)

    def each(self, k, act):
        @pl.loop(0, self.rows[k] // 16)
        def _(i):
            act(ds(i * 16, 16))

    def start(self, k):
        def act(t, sign, d):
            for ox in (1 - self.at.x, self.at.x):
                self.swap(k, t, ox).start()

        self.targets(act)

    def chip(self, k):
        at, first = self.at, self.first[k]

        def act(t, sign, d):
            for ox in (1 - at.x, at.x):
                q = t * 2 + ox
                self.swap(k, t, ox).wait_recv()
                base = at.device(t, ox, at.c) * self.rows[k]

                @pl.loop(0, self.rows[k] // 16)
                def _(i, q=q, base=base):
                    r = ds(i * 16, 16)
                    first[q, r] = first[q, r] + self.slabs[k](ds(base + i * 16, 16))[...]

                if ox is not at.x and k not in self.flipped:
                    self.cross(k, t).start()

        self.targets(act)

    def chain(self, k, d):
        at, first, second, chained = self.at, self.first[k], self.second[k], self.chained[k]
        flipped = k in self.flipped

        def ends(up, down, q, t, ox, other, put):
            def row(r):
                value = first[q, r].astype(F32)
                if other is not None:
                    value += second[other, r].astype(F32)
                if up:
                    value += chained[self.slot(t, ox, False), r].astype(F32)
                if down:
                    value += chained[self.slot(t, ox, True), r].astype(F32)
                put(r, value)

            self.each(k, row)

        def sums(*args):
            pl.when((at.z > 0) & (at.z < at.length - 1))(lambda: ends(True, True, *args))
            pl.when(at.z == 0)(lambda: ends(False, True, *args))
            pl.when(at.z == at.length - 1)(lambda: ends(True, False, *args))

        def last(t, ox):
            pl.when(at.z > 0)(lambda: self.arrive(k, t, ox, True, True))
            pl.when(at.z < at.length - 1)(lambda: self.arrive(k, t, ox, False, True))

        def out(r, value):
            self.emit(k, r, value)

        def act(t, sign, d):
            if d == 0 and flipped:
                q = t * 2 + 1 - at.x

                def keep(r, value):
                    first[q, r] = value.astype(BF16)

                last(t, 1 - at.x)
                sums(q, t, 1 - at.x, None, keep)
                self.cross(k, t).start()
                return
            if d < 0:
                last(t, at.x)
                self.crossed(k, t)
                sums(t * 2 + at.x, t, at.x, 0, out)
                return
            if not flipped:
                self.crossed(k, t)
            if d == 0:
                last(t, 0)
                sums(t * 2 + at.x, t, 0, t, out)
                return
            up = sign > 0
            inner = at.z > 0 if up else at.z < at.length - 1
            for ox in self.lanes(k):
                q = t * 2 + (ox if flipped else at.x)

                def middle(ox=ox, q=q):
                    self.arrive(k, t, ox, up, False)

                    def row(r):
                        value = first[q, r].astype(F32) + chained[self.slot(t, ox, False), r].astype(F32)
                        if flipped:
                            first[q, r] = value.astype(BF16)
                        else:
                            second[t, r] = (value + second[t, r].astype(F32)).astype(BF16)

                    self.each(k, row)

                def edge(q=q):
                    def row(r):
                        second[t, r] = second[t, r] + first[q, r]

                    self.each(k, row)

                pl.when(inner)(middle)
                if not flipped:
                    pl.when(jnp.logical_not(inner))(edge)
                self.along(k, t, ox, up, d).start()

        if d < 0:
            act(at.z, 0, d)
        else:
            self.targets(act, (d,))

    def swapped(self, k):
        def act(t, sign, d):
            for ox in range(2):
                self.swap(k, t, ox).wait_send()

        self.targets(act)

    def finish(self, k):
        def act(t, sign, d):
            if k not in self.flipped or d == 0:
                self.cross(k, t).wait_send()
            if sign:
                for ox in self.lanes(k):
                    self.along(k, t, ox, sign > 0, d).wait_send()

        self.targets(act)


BACKWARD_ORDER = (
    ("weights", 1), ("S", 1), ("weights", 0), ("S", 0), ("P", 1), ("C", 1, 3), ("P", 0), ("residual",),
    ("C", 1, 2), ("weights", 2), ("S", 2), ("C", 0, 3), ("attended",), ("S", 3), ("C", 1, 1), ("P", 2),
    ("C", 0, 2), ("heads", 0), ("heads", 1), ("heads", 2), ("heads", 3), ("C", 0, 1), ("unrotate",),
    ("send",), ("projection",), ("S", 4), ("P", 3), ("C", 2, 3), ("C", 2, 2), ("output",), ("own",),
    ("C", 0, 0), ("input",), ("P", 4), ("C", 2, 1), ("C", 4, 3), ("C", 3, 3), ("C", 4, 2), ("gains",),
    ("S", 5), ("C", 3, 2), ("P", 5), ("C", 1, 0), ("C", 5, 3), ("C", 4, 1), ("C", 5, 2), ("C", 3, 1),
    ("C", 4, 0), ("C", 5, 1), ("C", 2, 0), ("C", 1, -1), ("C", 3, 0), ("C", 5, 0),
)


def bwd_kernel(
    dp, rows, half, x_ref, dy_ref,
    wa_in, wg_in, n1_in, raw_in, p_in, qrot_in, kdup_in, vdup_in, att_in, hidden_in, n2_in,
    dyf_in, act_in, dg_in, du_in, cos_in, sin_in, gnm_in, gno_in, om_in, oo_in,
    bo_out, gi_out, gain_out, gq_out, gkv_out, go_out, ggu_out, gdn_out,
    parts0, parts1, pa, pg, stage, turned, turned2, tiles, prob, raw, qrot, kdup, vdup, att, weights, gains, gain_rows, cos, sin,
    hidden, gh, grecv, orecv, grows, n1recv, n1send, ga, qs, dos, dq, dk, dv, dqkv, terms, terms_in,
    *rest,
):
    count = CHUNKS + 3
    first, second, chained = rest[:count], rest[count : 2 * count], rest[2 * count : 3 * count]
    sems = rest[3 * count : 3 * count + 7]
    ysem, loads, tilesem = rest[3 * count + 7 :]
    at = Spot(dp)
    wide, tokens = dp * rows, 2 * half
    q_wide, kv_wide, ff_wide = gq_out.shape[1], gkv_out.shape[2], gdn_out.shape[1]
    chunks = chunk_widths(ff_wide)
    parts = (parts0, parts1, parts1)
    o_at, g_at = q_wide + 2 * kv_wide, 2 * q_wide + 2 * kv_wide
    groups = q_wide // LANES
    mine, theirs = at.t * half, (1 - at.t) * half
    used = []

    def load(src, dst):
        copy = pltpu.make_async_copy(src, dst, loads.at[len(used)])
        copy.start()
        used.append(copy)
        return copy

    def emit(k, r, value):
        if k < CHUNKS:
            chunk = chunks[k]
            cols = slice(sum(chunks[:k]), sum(chunks[: k + 1]))
            ggu_out[0, r, cols] = value[:, :chunk]
            ggu_out[1, r, cols] = value[:, chunk : 2 * chunk]
            gdn_out[r, cols] = value[:, 2 * chunk :]
        elif k == CHUNKS:
            go_out[r] = value
        elif k == CHUNKS + 1:
            gq_out[r] = value[:, :q_wide]
            gkv_out[0, r] = value[:, q_wide : q_wide + kv_wide]
            gkv_out[1, r] = value[:, q_wide + kv_wide :]
        else:
            gain_out[r] = value

    slabs = [lambda r, j=j: parts[j].at[r, : 3 * chunks[j]] for j in range(CHUNKS)]
    slabs += [lambda r: pa.at[r, o_at:g_at], lambda r: pa.at[r, 0:o_at], lambda r: pg.at[r]]
    scatter = Scatter(at, [rows] * (CHUNKS + 2) + [GAIN_ROWS], slabs, (FLIPPED,), first, second, chained, emit, sems)

    at.greet()
    g_copy = partner(at, gno_in, grecv, ysem.at[0])
    g_copy.start()
    o_copy = partner(at, oo_in, orecv, ysem.at[1])
    dy_load, n2_load = load(dyf_in, turned), load(n2_in, turned2)

    def tile_copies(i, slot):
        cols = ds(i * 256, 256)
        return [
            pltpu.make_async_copy(src.at[:, cols], tiles.at[slot, n], tilesem.at[slot, n])
            for n, src in enumerate((act_in, dg_in, du_in))
        ]

    order = [FLIPPED, 0, 2]
    sequence = [(j, n) for j in order for n in range(chunks[j] // 256)]

    def tile_of(i):
        j, n = sequence[i]
        return sum(chunks[:j]) // 256 + n

    for copy in tile_copies(tile_of(0), 0):
        copy.start()
    wo_load = load(wa_in.at[:, o_at:g_at], weights.at[:, : g_at - o_at])
    gain_load = load(wg_in, gains)
    hidden_load = load(hidden_in, hidden)
    gnm_load = load(gnm_in, gh)
    cos_load, sin_load = load(cos_in, cos), load(sin_in, sin)
    att_load, raw_load = load(att_in, att), load(raw_in.at[0 : groups + groups // 2], raw)
    q_load, k_load, v_load = load(qrot_in, qrot), load(kdup_in, kdup), load(vdup_in, vdup)
    om_load = load(om_in, gi_out)
    p_loads = [load(p_in.at[0], prob.at[0])]

    n1_load = load(n1_in, stage)
    dy_load.wait()
    n2_load.wait()

    def weight_grads(j):
        chunk = chunks[j]
        for n in range(chunk // 256):
            i = sequence.index((j, n))
            slot = i % 2
            if i + 1 < len(sequence):
                for copy in tile_copies(tile_of(i + 1), 1 - slot):
                    copy.start()
            for copy in tile_copies(tile_of(i), slot):
                copy.wait()

            @pl.loop(0, wide // 256)
            def _(m, n=n, slot=slot):
                r = ds(m * 256, 256)
                for part, left, which in ((0, turned2, 1), (1, turned2, 2), (2, turned, 0)):
                    cols = slice(part * chunk + n * 256, part * chunk + (n + 1) * 256)
                    parts[j][r, cols] = dot_nn(left[r], tiles[slot, which]).astype(BF16)


    r_copy = partner(at, grows.at[ds(mine, half)], grows.at[ds(mine, half)], ysem.at[2])
    n_copy = partner(at, n1send, n1recv, ysem.at[3])
    t_copy = partner(at, terms, terms_in, ysem.at[4])
    blk = 128
    gain = {}

    def residual():
        gain_load.wait()
        qk_gain = spread_gains(gains, dp, gain_rows)
        lows1 = low_half((1, LANES))
        gain["q"] = jnp.where(lows1, qk_gain, pltpu.roll(qk_gain, HD, 1))
        gain["k"] = jnp.where(lows1, pltpu.roll(qk_gain, HD, 1), qk_gain)
        gain["attn"], gain["ffn"] = gain_rows[0:1, :], gain_rows[1:2, :]
        hidden_load.wait()
        gnm_load.wait()
        g_copy.wait_recv()
        terms[...] = jnp.zeros_like(terms)

        @pl.loop(0, half // 32)
        def _(i):
            r = ds(i * 32, 32)
            grad = gh[r] + grecv[r].astype(F32)
            values = hidden[r]
            scale = lax.rsqrt(jnp.mean(values * values, axis=-1, keepdims=True) + EPSILON)
            terms[1:2, :wide] += jnp.sum(grad * values * scale, axis=0, keepdims=True)
            result = dy_ref[r].astype(F32) + rms_backward(values, scale, gain["ffn"], grad)
            gh[r] = result
            grows[ds(mine + i * 32, 32)] = result.astype(BF16)

        r_copy.start()
        o_copy.start()

    def attended_grads():
        wo_load.wait()
        r_copy.wait_recv()

        @pl.loop(0, q_wide // 256)
        def _(n):
            tile = dot_nn(grows[...], weights[:, ds(n * 256, 256)]).astype(BF16)
            ga[2 * n] = tile[:, :LANES]
            ga[2 * n + 1] = tile[:, LANES:]

        gain["weights"] = load(wa_in.at[:, :o_at], weights)
        transpose(grows, turned)
        att_load.wait()

        @pl.loop(0, wide // 256)
        def _(m):
            r = ds(m * 256, 256)
            pa[r, o_at:g_at] = dot_nn(turned[r], att[...]).astype(BF16)

        q_load.wait()
        k_load.wait()
        v_load.wait()

    def heads(g):
        if g + 1 < groups:
            p_loads.append(load(p_in.at[g + 1], prob.at[(g + 1) % 2]))
        p_loads[g].wait()
        pg = prob.at[g % 2]

        @pl.loop(0, tokens // blk)
        def _(i, g=g):
            r, r2 = ds(i * blk, blk), ds(tokens + i * blk, blk)
            lows = low_half((blk, LANES))
            q, do = qrot[g, r], ga[g, r]
            zero = jnp.zeros_like(q)
            qs[r], qs[r2] = jnp.where(lows, q, zero), jnp.where(lows, zero, q)
            dos[r], dos[r2] = jnp.where(lows, do, zero), jnp.where(lows, zero, do)

        dv[g] = dot_tn(pg[...], dos[...])

        @pl.loop(0, tokens // blk)
        def _(i, g=g, pg=pg):
            lows = low_half((blk, LANES))
            result = []
            for hh in range(2):
                r = ds(hh * tokens + i * blk, blk)
                p = pg[r].astype(F32)
                grad_p = dot_nt(dos[r], vdup[g])
                delta = jnp.sum(p * grad_p, axis=1, keepdims=True)
                scores = (p * (grad_p - delta) * (1.0 / math.sqrt(HD))).astype(BF16)
                pg[r] = scores
                result.append(dot_nn(scores, kdup[g]))
            dq[g, ds(i * blk, blk)] = jnp.where(lows, result[0], result[1])

        dk[g] = dot_tn(pg[...], qs[...])

    def fold(value):
        return value + pltpu.roll(value, HD, 1)

    def turn_back(values, grad_rot, gain, r):
        u = grad_rot * sin[r]
        early = first_quarter(u.shape)
        grad = grad_rot * cos[r] + jnp.where(
            early, pltpu.roll(u, LANES - HD // 2, 1), -pltpu.roll(u, HD // 2, 1)
        )
        scale = lax.rsqrt(head_mean(values * values) + EPSILON)
        weighted = grad * gain
        inner = head_mean(weighted * values)
        term = jnp.sum(grad * values * scale, axis=0, keepdims=True)
        return scale * (weighted - values * scale * scale * inner), fold(term)

    def unrotate():
        cos_load.wait()
        sin_load.wait()
        raw_load.wait()

        @pl.loop(0, tokens // blk)
        def _(i):
            r = ds(i * blk, blk)
            lows = low_half((blk, LANES))
            q_term = k_term = jnp.zeros((1, LANES), F32)
            for n in range(groups):
                grad, term = turn_back(raw[n, r], dq[n, r], gain["q"], r)
                dqkv[r, n * LANES : (n + 1) * LANES] = grad.astype(BF16)
                q_term += term
            for n in range(groups // 2):
                pair = jnp.where(lows, fold(dk[2 * n, r]), fold(dk[2 * n + 1, r]))
                grad, term = turn_back(raw[groups + n, r], pair, gain["k"], r)
                dqkv[r, q_wide + n * LANES : q_wide + (n + 1) * LANES] = grad.astype(BF16)
                k_term += term
                pair = jnp.where(lows, fold(dv[2 * n, r]), fold(dv[2 * n + 1, r]))
                dqkv[r, q_wide + kv_wide + n * LANES : q_wide + kv_wide + (n + 1) * LANES] = pair.astype(BF16)
            terms[0:1, wide:] += jnp.where(low_half((1, LANES)), q_term, k_term)

    def send_input():
        gain["weights"].wait()

        @pl.loop(0, wide // 256)
        def _(n):
            r = ds(n * 256, 256)
            n1send[:, r] = dot_nt(dqkv[ds(theirs, half)], weights[r]).astype(BF16)

        n_copy.start()

    def projection_grads():
        n1_load.wait()

        @pl.loop(0, wide // 256)
        def _(m):
            r = ds(m * 256, 256)
            for n in range(o_at // 256):
                cols = slice(n * 256, (n + 1) * 256)
                pa[r, cols] = dot_nn(stage[r], dqkv[:, cols]).astype(BF16)

    def output():
        om_load.wait()
        o_copy.wait_recv()

        @pl.loop(0, half // 64)
        def _(i):
            r = ds(i * 64, 64)
            bo_out[r] = (gi_out[r] + orecv[r].astype(F32)).astype(BF16)

    def own_input():
        @pl.loop(0, wide // 256)
        def _(n):
            r = ds(n * 256, 256)
            gi_out[:, r] = dot_nt(dqkv[ds(mine, half)], weights[r])

    def input_grads():
        n_copy.wait_recv()

        @pl.loop(0, half // 32)
        def _(i):
            r = ds(i * 32, 32)
            grad = gi_out[r] + n1recv[r].astype(F32)
            values = x_ref[r].astype(F32)
            scale = lax.rsqrt(jnp.mean(values * values, axis=-1, keepdims=True) + EPSILON)
            terms[0:1, :wide] += jnp.sum(grad * values * scale, axis=0, keepdims=True)
            gi_out[r] = gh[r] + rms_backward(values, scale, gain["attn"], grad)

        t_copy.start()

    def gain_grads():
        t_copy.wait_recv()

        both = terms[...] + terms_in[...]
        lows = low_half((1, LANES))
        rest_rows = jnp.zeros((GAIN_ROWS - 2, LANES), F32)
        for i in range(dp // 2):
            block = both[:, i * LANES : (i + 1) * LANES]
            swapped = pltpu.roll(block, HD, 1)
            even = jnp.where(lows, block[0:1], swapped[1:2])
            odd = jnp.where(lows, swapped[0:1], block[1:2])
            for o, row in ((2 * i, even), (2 * i + 1, odd)):
                packed = jnp.concatenate([row, both[0:1, wide:], rest_rows], axis=0)
                pg[o * GAIN_ROWS : (o + 1) * GAIN_ROWS] = packed.astype(BF16)

    steps = {
        "weights": weight_grads, "residual": residual, "attended": attended_grads, "heads": heads,
        "unrotate": unrotate, "send": send_input, "projection": projection_grads, "output": output,
        "own": own_input, "input": input_grads, "gains": gain_grads,
        "S": scatter.start, "P": scatter.chip, "C": scatter.chain,
    }
    waited = set()
    for name, *which in BACKWARD_ORDER:
        if name == "weights" and which[0] == 2:
            scatter.swapped(FLIPPED)
            waited.add(FLIPPED)
        steps[name](*which)
    for copy in (g_copy, o_copy, r_copy, n_copy, t_copy):
        copy.wait_send()
    for k in range(count):
        if k not in waited:
            scatter.swapped(k)
        scatter.finish(k)


def backward(dp, x, dy, saved, q_wide, kv_wide, ff_wide):
    half, wide = x.shape
    rows, tokens = wide // dp, 2 * half
    groups = q_wide // LANES
    length = layout_of(dp)[0]
    chunks = chunk_widths(ff_wide)
    widths = [3 * w for w in chunks] + [q_wide, q_wide + 2 * kv_wide, LANES]
    heights = [rows] * (CHUNKS + 2) + [GAIN_ROWS]
    shapes = [
        ((half, wide), BF16),
        ((half, wide), F32),
        ((GAIN_ROWS, LANES), F32),
        ((rows, q_wide), F32),
        ((2, rows, kv_wide), F32),
        ((rows, q_wide), F32),
        ((2, rows, ff_wide), F32),
        ((rows, ff_wide), F32),
    ]
    vmem = [
        ((wide, widths[0]), BF16),
        ((wide, max(widths[1:3])), BF16),
        ((wide, sum(widths[CHUNKS:-1])), BF16),
        ((dp * GAIN_ROWS, LANES), BF16),
        ((wide, tokens), BF16),
        ((wide, tokens), BF16),
        ((wide, tokens), BF16),
        ((2, 3, tokens, 256), BF16),
        ((2, 2 * tokens, tokens), BF16),
        ((groups + groups // 2, tokens, LANES), F32),
        ((groups, tokens, LANES), BF16),
        ((groups, tokens, LANES), BF16),
        ((groups, tokens, LANES), BF16),
        ((tokens, q_wide), BF16),
        ((wide, q_wide + 2 * kv_wide), BF16),
        ((dp * GAIN_ROWS, LANES), BF16),
        ((8, wide), F32),
        ((tokens, LANES), F32),
        ((tokens, LANES), F32),
        ((half, wide), F32),
        ((half, wide), F32),
        ((half, wide), BF16),
        ((half, wide), BF16),
        ((tokens, wide), BF16),
        ((half, wide), BF16),
        ((half, wide), BF16),
        ((groups, tokens, LANES), BF16),
        ((2 * tokens, LANES), BF16),
        ((2 * tokens, LANES), BF16),
        ((groups, tokens, LANES), F32),
        ((groups, tokens, LANES), F32),
        ((groups, tokens, LANES), F32),
        ((tokens, q_wide + 2 * kv_wide), BF16),
        ((8, wide + LANES), F32),
        ((8, wide + LANES), F32),
    ]
    for slots, turned in ((dp // 2, dp // 2), (length, 1), (length + 1, 2 * length + 2)):
        vmem += [((turned if k == FLIPPED else slots, heights[k], w), BF16) for k, w in enumerate(widths)]
    count = len(widths)
    return pl.pallas_call(
        functools.partial(bwd_kernel, dp, rows, half),
        out_shape=[jax.ShapeDtypeStruct(*s) for s in shapes],
        in_specs=[pl.BlockSpec(memory_space=pltpu.VMEM)] * 2
        + [pl.BlockSpec(memory_space=pl.ANY)] * len(saved),
        out_specs=[pl.BlockSpec(memory_space=pltpu.VMEM)] * len(shapes),
        scratch_shapes=[pltpu.VMEM(*s) for s in vmem]
        + [
            pltpu.SemaphoreType.DMA((count, n))
            for n in (dp // 2, length, 2 * length, dp // 2, length, 2 * length, 2 * length)
        ]
        + [
            pltpu.SemaphoreType.DMA((5, 2)),
            pltpu.SemaphoreType.DMA((24,)),
            pltpu.SemaphoreType.DMA((2, 3)),
        ],
        compiler_params=pltpu.CompilerParams(
            collective_id=4, has_side_effects=True, vmem_limit_bytes=63 * 1024 * 1024
        ),
        name="backward",
    )(x, dy, *saved)


def finish_kernel(dp, rows, qk_shard, count, gain_ref, *refs):
    ins, norm_out, qk_out, outs, sem = refs[:count], refs[count], refs[count + 1], refs[count + 2 : -1], refs[-1]
    copies = [pltpu.make_async_copy(a, b, sem.at[i]) for i, (a, b) in enumerate(zip(ins, outs))]
    for copy in copies:
        copy.start()
    block = gain_ref[0:8]
    norm_out[0:1] = block[0:1, :rows]
    norm_out[1:2] = pltpu.roll(block, LANES - rows, 1)[0:1, :rows]
    own = lax.axis_index("dp") * qk_shard
    for i in range(2):
        moved = pltpu.roll(block, lax.rem(2 * LANES - own - i * HD, LANES), 1)
        qk_out[i : i + 1] = moved[1:2, :qk_shard]
    for copy in copies:
        copy.wait()


def finish(dp, rows, gains, qk_shard, arrays):
    return pl.pallas_call(
        functools.partial(finish_kernel, dp, rows, qk_shard, len(arrays)),
        out_shape=[jax.ShapeDtypeStruct((2, rows), F32), jax.ShapeDtypeStruct((2, qk_shard), F32)]
        + [jax.ShapeDtypeStruct(a.shape, a.dtype) for a in arrays],
        in_specs=[pl.BlockSpec(memory_space=pltpu.VMEM)] * (1 + len(arrays)),
        out_specs=[pl.BlockSpec(memory_space=pltpu.VMEM)] * 2
        + [pl.BlockSpec(memory_space=pl.ANY)] * len(arrays),
        scratch_shapes=[pltpu.SemaphoreType.DMA((len(arrays),))],
        name="finish",
    )(gains, *arrays)


def fast_device(
    block_input, cotangent, segment_ids, positions, norm_gains, qk_gains, w_query, w_keyval, w_output,
    w_gate_up, w_down,
):
    dp = lax.axis_size("dp")
    q_wide = w_query.shape[1]
    kv_wide, ff_wide = w_keyval.shape[2], w_gate_up.shape[2]
    qk_shard = qk_gains.shape[1]
    freq = np.tile(ROPE_BASE ** (-np.arange(0, HD, 2) / HD), 4)[None].astype(np.float32)
    saved = forward(
        dp, block_input, cotangent, segment_ids, positions, freq, norm_gains, qk_gains,
        w_query, w_keyval, w_output.T, w_gate_up, w_down.T,
    )
    block_output, grad_input, gains, grad_query, grad_keyval, grad_out, grad_gate_up, grad_down = backward(
        dp, block_input, cotangent, saved, q_wide, kv_wide, ff_wide
    )
    norm, qk, *rest = finish(
        dp, w_query.shape[0], gains, qk_shard,
        [block_output, grad_input, grad_query, grad_keyval, grad_out, grad_gate_up, grad_down],
    )
    block_output, grad_input, grad_query, grad_keyval, grad_out, grad_gate_up, grad_down = rest
    return (
        block_output,
        grad_input,
        norm,
        qk,
        grad_query,
        grad_keyval,
        grad_out.T,
        grad_gate_up,
        grad_down.T,
    )


def solution(mesh):
    return jax.shard_map(
        fast_device if mesh.shape["tensor"] == 2 and mesh.shape["dp"] == 16 else on_device,
        mesh=mesh,
        in_specs=(
            P(("dp", "tensor"), None),
            P(("dp", "tensor"), None),
            P("dp", None),
            P("dp", None),
            P(None, "dp"),
            P(None, "dp"),
            P("dp", "tensor"),
            P(None, "dp", "tensor"),
            P("tensor", "dp"),
            P(None, "dp", "tensor"),
            P("tensor", "dp"),
        ),
        out_specs=(
            P(("dp", "tensor"), None),
            P(("dp", "tensor"), None),
            P(None, "dp"),
            P(None, "dp"),
            P("dp", "tensor"),
            P(None, "dp", "tensor"),
            P("tensor", "dp"),
            P(None, "dp", "tensor"),
            P("tensor", "dp"),
        ),
        check_vma=False,
    )
```
